32 devices in a mesh: seq: 8 (over y, x, core), row: 4 (over z).
Axes of the slice: x: 2, y: 2, z: 4, core: 2. Of those that a mesh axis runs over, the one named last changes fastest.
Arguments:
- long_tokens: bfloat16 [4, 1024, 1024], P('row', 'seq'), may hold values from -6 to 6
- short_tokens: bfloat16 [32, 512, 1024], P(('seq', 'row')), may hold values from -6 to 6
- long_length: int32 [4], P('row'), may hold values from 256 to 1024, as said below
- long_cotangent: bfloat16 [4, 1024, 1024], P('row', 'seq'), may hold values from -6 to 6
- short_cotangent: bfloat16 [32, 512, 1024], P(('seq', 'row')), may hold values from -6 to 6
- first_gain: float32 [1024], replicated, may hold values from 0.1 to 1.9
- gate_weight: bfloat16 [1024, 1536], P(None, ('seq', 'row')), may hold values from -0.1875 to 0.1875
- gate_bias: float32 [1536], replicated, may hold values from -3 to 3
- input_weight: bfloat16 [1024, 1536], P(None, ('seq', 'row')), may hold values from -0.1875 to 0.1875
- input_bias: float32 [1536], replicated, may hold values from -3 to 3
- conv_weight: float32 [4, 1536], replicated, may hold values from -3 to 3
- conv_bias: float32 [1536], replicated, may hold values from -2 to 2
- decay_gate_weight: bfloat16 [8, 192, 192], replicated, may hold values from -0.4375 to 0.4375
- decay_gate_bias: float32 [1536], replicated, may hold values from -3 to 3
- input_gate_weight: bfloat16 [8, 192, 192], replicated, may hold values from -0.4375 to 0.4375
- input_gate_bias: float32 [1536], replicated, may hold values from -3 to 3
- decay_param: float32 [1536], replicated, may hold values from -16 to -4
- out_weight: bfloat16 [1536, 1024], P(('seq', 'row')), may hold values from -0.4375 to 0.4375
- second_gain: float32 [1024], replicated, may hold values from 0.1 to 1.9
- mlp_gate_weight: bfloat16 [1024, 3072], P(None, ('seq', 'row')), may hold values from -0.1875 to 0.1875
- mlp_up_weight: bfloat16 [1024, 3072], P(None, ('seq', 'row')), may hold values from -0.1875 to 0.1875
- mlp_down_weight: bfloat16 [3072, 1024], P(('seq', 'row')), may hold values from -0.21875 to 0.21875
Outputs:
- long_output: bfloat16 [4, 1024, 1024], P('row', 'seq')
- short_output: bfloat16 [32, 512, 1024], P(('seq', 'row'))
- long_input_grad: float32 [4, 1024, 1024], P('row', 'seq')
- short_input_grad: float32 [32, 512, 1024], P(('seq', 'row'))
- first_gain_grad: float32 [1024], replicated
- gate_weight_grad: float32 [1024, 1536], P(None, ('seq', 'row'))
- gate_bias_grad: float32 [1536], replicated
- input_weight_grad: float32 [1024, 1536], P(None, ('seq', 'row'))
- input_bias_grad: float32 [1536], replicated
- conv_weight_grad: float32 [4, 1536], replicated
- conv_bias_grad: float32 [1536], replicated
- decay_gate_weight_grad: float32 [8, 192, 192], replicated
- decay_gate_bias_grad: float32 [1536], replicated
- input_gate_weight_grad: float32 [8, 192, 192], replicated
- input_gate_bias_grad: float32 [1536], replicated
- decay_param_grad: float32 [1536], replicated
- out_weight_grad: float32 [1536, 1024], P(('seq', 'row'))
- second_gain_grad: float32 [1024], replicated
- mlp_gate_weight_grad: float32 [1024, 3072], P(None, ('seq', 'row'))
- mlp_up_weight_grad: float32 [1024, 3072], P(None, ('seq', 'row'))
- mlp_down_weight_grad: float32 [3072, 1024], P(('seq', 'row'))
The draws below stay inside these ranges and needn't reach their ends.
Inputs may be any that keep to these rules, and one draw needn't show every extreme that they name: Positions at or beyond long_length of a long row carry no cotangent; some long row has all 1024 positions real.
All inputs are finite; a program needn't handle non-finite values.
Results may differ from the reference program's by a relative error of at most 0.014.
Values may be sent and summed in bfloat16 or wider, within the bound.
A program may use at most 320 MiB of HBM per device.

```python
import math
import jax
import jax.numpy as jnp
from jax import lax

D = 1024
R = 1536
F = 3072
BLOCKS = 8
BW = 192
CONV = 4
SHORT_LEN = 512
LONG_LEN = 1024
NLONG = 4
NSHORT = 32


def draw_long_length(key, part):
    key_one, key_two = jax.random.split(jax.random.fold_in(key, 11))
    span_draw = jax.random.randint(key_one, (NLONG,), LONG_LEN // 4, LONG_LEN + 1)
    chosen = jax.random.randint(key_two, (), 0, NLONG)
    return jnp.where(jnp.arange(NLONG) == chosen, LONG_LEN, span_draw).astype(jnp.int32)


def draw_decay_param(key, part):
    key_one, key_two, key_three = jax.random.split(jax.random.fold_in(key, 23), 3)
    slow_share = 0.5
    slow_mask = jax.random.uniform(key_one, (R,), jnp.float32) < slow_share
    slow_rate = jnp.exp(jax.random.uniform(key_two, (R,), jnp.float32, math.log(0.5 / LONG_LEN), math.log(2.5 / LONG_LEN)))
    fast_rate = jnp.exp(jax.random.uniform(key_three, (R,), jnp.float32, math.log(0.03), math.log(0.1)))
    gate_rate = jnp.where(slow_mask, slow_rate, fast_rate)
    return jnp.log(jnp.expm1(gate_rate / 6.0)).astype(jnp.float32)


def levels(stream_key, dims, cuts, least, largest):
    factor_of = 1.0
    for position, parts in cuts:
        steps = jax.random.uniform(jax.random.fold_in(jax.random.fold_in(stream_key, 6), position), (parts,), jnp.float32, least / len(cuts), largest / len(cuts))
        factor_of = factor_of * jnp.repeat(jnp.exp(steps), dims[position] // parts).reshape((-1,) + (1,) * (len(dims) - 1 - position))
    return factor_of


def scatter_about(own_key, extent, deviation, limit, cuts=(), kind=jnp.bfloat16):
    drawn = jax.random.normal(own_key, extent, jnp.float32) * deviation
    if len(cuts) > 0:
        drawn = levels(own_key, extent, cuts, -0.22, 0.18) * drawn
    return jnp.clip(drawn, min=-limit, max=limit).astype(kind)


def setup_inputs(seed: int = 0) -> dict:
    splits = jax.random.split(jax.random.key(seed), 23)
    long_tokens = scatter_about(splits[0], (NLONG, LONG_LEN, D), 1.0, 6.0, ((0, 4), (1, 8)))
    short_tokens = scatter_about(splits[1], (NSHORT, SHORT_LEN, D), 1.0, 6.0, ((0, 32),))
    long_length = draw_long_length(jax.random.fold_in(splits[22], 71), 0)
    long_cotangent = scatter_about(splits[3], (NLONG, LONG_LEN, D), 1.0, 6.0, ((0, 4), (1, 8)))
    short_cotangent = scatter_about(splits[4], (NSHORT, SHORT_LEN, D), 1.0, 6.0, ((0, 32),))
    first_gain = jnp.clip(1.0 + 0.18 * jax.random.normal(splits[5], (D,), jnp.float32), 0.1, 1.9)
    gate_weight = scatter_about(splits[6], (D, R), D ** -0.5, 0.1875, ((1, 32),))
    gate_bias = scatter_about(splits[7], (R,), 0.5, 3.0, (), jnp.float32)
    input_weight = scatter_about(splits[8], (D, R), D ** -0.5, 0.1875, ((1, 32),))
    input_bias = scatter_about(splits[9], (R,), 0.5, 3.0, (), jnp.float32)
    conv_weight = scatter_about(splits[10], (CONV, R), 0.5, 3.0, (), jnp.float32)
    conv_bias = scatter_about(splits[11], (R,), 0.3, 2.0, (), jnp.float32)
    decay_gate_weight = scatter_about(splits[12], (BLOCKS, BW, BW), BW ** -0.5, 0.4375)
    decay_gate_bias = scatter_about(splits[13], (R,), 0.5, 3.0, (), jnp.float32)
    input_gate_weight = scatter_about(splits[14], (BLOCKS, BW, BW), BW ** -0.5, 0.4375)
    input_gate_bias = scatter_about(splits[15], (R,), 0.5, 3.0, (), jnp.float32)
    decay_param = draw_decay_param(jax.random.fold_in(splits[22], 71), 0)
    out_weight = scatter_about(splits[17], (R, D), (R // 8) ** -0.5, 0.4375, ((0, 32),))
    second_gain = jnp.clip(1.0 + 0.18 * jax.random.normal(splits[18], (D,), jnp.float32), 0.1, 1.9)
    mlp_gate_weight = scatter_about(splits[19], (D, F), D ** -0.5, 0.1875, ((1, 32),))
    mlp_up_weight = scatter_about(splits[20], (D, F), D ** -0.5, 0.1875, ((1, 32),))
    mlp_down_weight = scatter_about(splits[21], (F, D), (F // 4) ** -0.5, 0.21875, ((0, 32),))
    return {"long_tokens": long_tokens, "short_tokens": short_tokens, "long_length": long_length, "long_cotangent": long_cotangent, "short_cotangent": short_cotangent, "first_gain": first_gain, "gate_weight": gate_weight, "gate_bias": gate_bias, "input_weight": input_weight, "input_bias": input_bias, "conv_weight": conv_weight, "conv_bias": conv_bias, "decay_gate_weight": decay_gate_weight, "decay_gate_bias": decay_gate_bias, "input_gate_weight": input_gate_weight, "input_gate_bias": input_gate_bias, "decay_param": decay_param, "out_weight": out_weight, "second_gain": second_gain, "mlp_gate_weight": mlp_gate_weight, "mlp_up_weight": mlp_up_weight, "mlp_down_weight": mlp_down_weight}


@jax.custom_vjp
def low(v):
    return lax.optimization_barrier(v.astype(jnp.bfloat16)).astype(jnp.float32)

@jax.custom_vjp
def low_back(v):
    return v

def low_keep(v):
    return (low(v), None)

def low_pass(kept, grad):
    return (grad,)

def back_keep(v):
    return (v, None)

def back_low(kept, grad):
    return (low(grad),)
low.defvjp(low_keep, low_pass)
low_back.defvjp(back_keep, back_low)

def rms_norm(values, norm_gain):
    inverse = lax.rsqrt(lax.optimization_barrier(jnp.mean(values * values, axis=-1, keepdims=True)) + 1e-06)
    return values * inverse * norm_gain

def matmul(left, right):
    return jnp.einsum('bsd,df->bsf', left, right, precision=lax.Precision.HIGHEST)

def pair_combine(earlier, later):
    return (earlier[0] * later[0], earlier[1] * later[0] + later[1])

def recurrence_gates(decay_pre, input_pre, conv_out, decay_param):
    gate_rate = jax.nn.sigmoid(decay_pre)
    opening = jax.nn.sigmoid(input_pre)
    log_decay = -8.0 * jax.nn.softplus(decay_param) * (0.25 + gate_rate)
    return (jnp.exp(log_decay), jnp.sqrt(-jnp.expm1(2.0 * log_decay)) * opening * conv_out)

def blockwise(values, weight):
    batch_size, length, channels = values.shape
    blocks = weight.shape[0]
    split_conv = values.reshape(batch_size, length, blocks, channels // blocks)
    product = jnp.einsum('bshi,hij->bshj', split_conv, weight, precision=lax.Precision.HIGHEST)
    return product.reshape(batch_size, length, channels)

def block_layer(params, values):
    first_gain, gate_weight, gate_bias, input_weight, input_bias, conv_weight, conv_bias, decay_gate_weight, decay_gate_bias, input_gate_weight, input_gate_bias, decay_param, out_weight, second_gain, mlp_gate_weight, mlp_up_weight, mlp_down_weight = params
    length = values.shape[1]
    normed = low(rms_norm(values, first_gain))
    gate_pre = low_back(matmul(normed, gate_weight)) + gate_bias
    gate_out = jax.nn.gelu(gate_pre, approximate=True)
    inner = low_back(matmul(normed, input_weight)) + input_bias
    conv_taps = conv_weight.shape[0]
    padded = jnp.pad(inner, ((0, 0), (conv_taps - 1, 0), (0, 0)))
    conv_out = conv_bias + conv_weight[0] * padded[:, conv_taps - 1:conv_taps - 1 + length]
    for tap_index in range(1, conv_taps):
        start = conv_taps - 1 - tap_index
        conv_out = conv_out + conv_weight[tap_index] * padded[:, start:start + length]
    conv_low = low(conv_out)
    decay_pre = low_back(blockwise(conv_low, decay_gate_weight)) + decay_gate_bias
    input_pre = low_back(blockwise(conv_low, input_gate_weight)) + input_gate_bias
    decays, drives = recurrence_gates(decay_pre, input_pre, conv_out, decay_param)
    _, states = lax.associative_scan(pair_combine, (decays, drives), axis=1)
    mix_out = low(states * gate_out)
    residual = values + low_back(matmul(mix_out, out_weight))
    normed2 = low(rms_norm(residual, second_gain))
    mlp_gate_out = low_back(matmul(normed2, mlp_gate_weight))
    mlp_up_out = low_back(matmul(normed2, mlp_up_weight))
    hidden = low(jax.nn.gelu(mlp_gate_out, approximate=True) * mlp_up_out)
    return residual + low_back(matmul(hidden, mlp_down_weight))

def reference(long_tokens, short_tokens, long_length, long_cotangent, short_cotangent, first_gain, gate_weight, gate_bias, input_weight, input_bias, conv_weight, conv_bias, decay_gate_weight, decay_gate_bias, input_gate_weight, input_gate_bias, decay_param, out_weight, second_gain, mlp_gate_weight, mlp_up_weight, mlp_down_weight):
    params = tuple((p.astype(jnp.float32) for p in (first_gain, gate_weight, gate_bias, input_weight, input_bias, conv_weight, conv_bias, decay_gate_weight, decay_gate_bias, input_gate_weight, input_gate_bias, decay_param, out_weight, second_gain, mlp_gate_weight, mlp_up_weight, mlp_down_weight)))
    long_values = long_tokens.astype(jnp.float32)
    short_values = short_tokens.astype(jnp.float32)

    def forward(params, long_values, short_values):
        checked_layer = jax.checkpoint(lambda rows: block_layer(params, rows))
        long_result = lax.map(lambda one_row: checked_layer(one_row[None])[0], long_values)
        grouped = short_values.reshape(-1, 8, SHORT_LEN, D)
        short_result = lax.map(checked_layer, grouped).reshape(short_values.shape)
        return (long_result, short_result)
    (long_result, short_result), pullback = jax.vjp(forward, params, long_values, short_values)
    keep_mask = (jnp.arange(LONG_LEN, dtype=jnp.int32)[None, :] < long_length[:, None]).astype(jnp.float32)
    long_upstream = long_cotangent.astype(jnp.float32) * keep_mask[:, :, None]
    grads, long_grad, short_grad = pullback((long_upstream, short_cotangent.astype(jnp.float32)))
    return (long_result.astype(jnp.bfloat16), short_result.astype(jnp.bfloat16), long_grad, short_grad, grads[0], grads[1], grads[2], grads[3], grads[4], grads[5], grads[6], grads[7], grads[8], grads[9], grads[10], grads[11], grads[12], grads[13], grads[14], grads[15], grads[16])
```

```python
import functools

import jax
import jax.numpy as jnp
from jax import lax
from jax.experimental import pallas as pl
from jax.experimental.pallas import tpu as pltpu
from jax.sharding import PartitionSpec as P

EPSILON = 1e-06
F32 = jnp.float32
BF16 = jnp.bfloat16
SLOTS = 32
TILE = 16
HALO = 16
MIB = 1024 * 1024
GELU_A = 0.7978845608028654
GELU_B = 0.044715


def dot_nn(a, b):
    return lax.dot_general(a, b, (((1,), (0,)), ((), ())), preferred_element_type=F32)


def dot_nt(a, b):
    return lax.dot_general(a, b, (((1,), (1,)), ((), ())), preferred_element_type=F32)


def dot_tn(a, b):
    return lax.dot_general(a, b, (((0,), (0,)), ((), ())), preferred_element_type=F32)


def sigmoid(v):
    return 0.5 * jnp.tanh(0.5 * v) + 0.5


def gelu(v):
    t = jnp.tanh(v * (GELU_A + (GELU_A * GELU_B) * (v * v)))
    h = 0.5 * v
    return h + h * t


def gelu_pair(v):
    w = v * v
    t = jnp.tanh(v * (GELU_A + (GELU_A * GELU_B) * w))
    h = 0.5 * v
    slope = 0.5 + 0.5 * t + (h - h * (t * t)) * (GELU_A + (3.0 * GELU_A * GELU_B) * w)
    return h + h * t, slope


def row_iota(shape):
    return lax.broadcasted_iota(jnp.int32, shape, 0)


def at(j):
    return pl.ds(pl.multiple_of(j * TILE, TILE), TILE)


def scan_tile(a, b, reverse):
    rows = row_iota(a.shape)
    step = 1
    while step < TILE:
        if reverse:
            keep, shift = rows < TILE - step, TILE - step
        else:
            keep, shift = rows >= step, step
        b = jnp.where(keep, a * pltpu.roll(b, shift, 0) + b, b)
        a = jnp.where(keep, a * pltpu.roll(a, shift, 0), a)
        step *= 2
    return a, b


def shift_down(cur, prev, k):
    if k == 0:
        return cur
    rows = row_iota(cur.shape)
    return jnp.where(rows < k, pltpu.roll(prev, k, 0), pltpu.roll(cur, k, 0))


def shift_up(cur, later, k):
    if k == 0:
        return cur
    rows = row_iota(cur.shape)
    return jnp.where(
        rows >= TILE - k, pltpu.roll(later, TILE - k, 0), pltpu.roll(cur, TILE - k, 0)
    )


def fold(v):
    return v[0:8] + v[8:16]


def flat(block):
    return block.reshape(block.shape[0] * block.shape[1], block.shape[2])


def gates(dp, ip, c8):
    rate = sigmoid(dp)
    opening = sigmoid(ip)
    log_decay = -c8 * (0.25 + rate)
    decay = jnp.exp(log_decay)
    square = -jnp.tanh(log_decay) * (1.0 + decay * decay)
    return rate, opening, decay, square


GB, IB, CW, CB, DB, OB, C8, S8 = 0, 1, 2, 6, 7, 8, 9, 10


def conv_tile(in_ref, pc_ref, j, live):
    cur = in_ref[at(j), :]
    prev = in_ref[at(j - 1), :] * live
    out = pc_ref[CB : CB + 1, :] + pc_ref[CW : CW + 1, :] * cur
    moved = [cur]
    for k in range(1, 4):
        m = shift_down(cur, prev, k)
        moved.append(m)
        out = out + pc_ref[CW + k : CW + k + 1, :] * m
    return out, moved


def front_kernel(
    ltiles, tiles, first_ref, x_ref, gain_ref, wg_ref, wi_ref, wd_ref, wo_ref, pc_ref,
    gp_ref, in_ref, dp_ref, ip_ref, st_ref, pr_ref, mix_ref, end_ref, nm_ref, cv_ref, cl_ref,
):
    @pl.when(pl.program_id(0) == 0)
    def _():
        @pl.loop(0, tiles)
        def _(j):
            v = x_ref[at(j), :].astype(F32)
            s = lax.rsqrt(jnp.mean(v * v, axis=1, keepdims=True) + EPSILON)
            nm_ref[at(j), :] = (v * s * gain_ref[...]).astype(BF16)

    nm = nm_ref[...]
    gp_ref[...] = dot_nt(nm, flat(wg_ref[...])) + pc_ref[GB : GB + 1, :]
    in_ref[...] = dot_nt(nm, flat(wi_ref[...])) + pc_ref[IB : IB + 1, :]
    in_ref[0:HALO, :] = in_ref[0:HALO, :] * first_ref[0, 0]
    cl_ref[0:HALO, :] = jnp.zeros((HALO, cl_ref.shape[1]), BF16)

    @pl.loop(1, tiles)
    def _(j):
        live = jnp.where(j == 1 + ltiles, 0.0, 1.0)
        out, _ = conv_tile(in_ref, pc_ref, j, live)
        cv_ref[at(j), :] = out
        cl_ref[at(j), :] = out.astype(BF16)

    low = cl_ref[...]
    dp_ref[...] = dot_nn(low, wd_ref[0]) + pc_ref[DB : DB + 1, :]
    ip_ref[...] = dot_nn(low, wo_ref[0]) + pc_ref[OB : OB + 1, :]

    def scanned(j):
        _, opening, a, square = gates(dp_ref[at(j), :], ip_ref[at(j), :], pc_ref[C8 : C8 + 1, :])
        b = (square * lax.rsqrt(square)) * opening * cv_ref[at(j), :]
        return scan_tile(a, b, False)

    width = gp_ref.shape[1]

    def long_step(i, carry):
        state, reach = carry
        a, b = scanned(1 + i)
        s = b + a * state
        r = a * reach
        st_ref[at(1 + i), :] = s
        pr_ref[at(1 + i), :] = r
        return s[TILE - 1 : TILE], r[TILE - 1 : TILE]

    state, reach = lax.fori_loop(
        0, ltiles, long_step, (jnp.zeros((1, width), F32), jnp.ones((1, width), F32))
    )
    end_ref[...] = jnp.concatenate([reach, state, jnp.zeros((6, width), F32)], axis=0)

    def short_step(i, state):
        j = 1 + ltiles + i
        a, b = scanned(j)
        s = b + a * state
        st_ref[at(j), :] = s
        mix_ref[at(i), :] = (s * gelu(gp_ref[at(j), :])).astype(BF16)
        return s[TILE - 1 : TILE]

    lax.fori_loop(0, tiles - 1 - ltiles, short_step, jnp.zeros((1, width), F32))


def mlp_kernel(
    ltiles, tiles, x_ref, cot_ref, st_ref, pr_ref, gp_ref, sin_ref, mixs_ref, wo_ref, gain_ref,
    w_ref, out_ref, dres_ref, rlow_ref, mixl_ref, gain_grad_ref, dw_ref,
    n2_ref, acc_o, acc_n, g_ref, u_ref, d_ref, h_ref, dg_ref, du_ref,
):
    step = pl.program_id(0)
    lrows = ltiles * TILE
    half = g_ref.shape[1] // 2
    share = w_ref.shape[1] // 3

    @pl.when(step == 0)
    def _():
        s_in = sin_ref[0:1, :]

        @pl.loop(0, ltiles)
        def _(i):
            s = st_ref[at(1 + i), :] + pr_ref[at(1 + i), :] * s_in
            mixl_ref[at(i), :] = (s * gelu(gp_ref[at(1 + i), :])).astype(BF16)

        wo = flat(wo_ref[...])
        dres_ref[0:lrows, :] = dot_nn(mixl_ref[...], wo)
        dres_ref[lrows:, :] = dot_nn(mixs_ref[...], wo)

        @pl.loop(0, tiles)
        def _(i):
            r = dres_ref[at(i), :] + x_ref[at(1 + i), :].astype(F32)
            dres_ref[at(i), :] = r
            acc_o[at(i), :] = r
            s = lax.rsqrt(jnp.mean(r * r, axis=1, keepdims=True) + EPSILON)
            n2_ref[at(i), :] = (r * s * gain_ref[...]).astype(BF16)

        acc_n[...] = jnp.zeros_like(acc_n)

    n2 = n2_ref[...]
    wg = flat(w_ref[:, 0:share, :])
    wu = flat(w_ref[:, share : 2 * share, :])
    wd = flat(w_ref[:, 2 * share :, :])
    g_ref[...] = dot_nt(n2, wg)
    u_ref[...] = dot_nt(n2, wu)
    d_ref[...] = dot_nt(cot_ref[...], wd)

    @pl.loop(0, tiles)
    def _(i):
        for k in range(2):
            cols = slice(k * half, (k + 1) * half)
            ge, slope = gelu_pair(g_ref[at(i), cols])
            u = u_ref[at(i), cols]
            d = d_ref[at(i), cols]
            h_ref[at(i), cols] = (ge * u).astype(BF16)
            dg_ref[at(i), cols] = (d * u * slope).astype(BF16)
            du_ref[at(i), cols] = (d * ge).astype(BF16)

    acc_o[...] += dot_nn(h_ref[...], wd)
    acc_n[...] += dot_nn(dg_ref[...], wg) + dot_nn(du_ref[...], wu)
    shape = (dw_ref.shape[0], share, dw_ref.shape[2])
    dw_ref[:, 0:share, :] = dot_tn(dg_ref[...], n2).astype(BF16).reshape(shape)
    dw_ref[:, share : 2 * share, :] = dot_tn(du_ref[...], n2).astype(BF16).reshape(shape)
    dw_ref[:, 2 * share :, :] = dot_tn(h_ref[...], cot_ref[...]).astype(BF16).reshape(shape)

    @pl.when(step == pl.num_programs(0) - 1)
    def _():
        def one(i, total):
            r = dres_ref[at(i), :]
            out_ref[at(i), :] = acc_o[at(i), :].astype(BF16)
            dn = acc_n[at(i), :]
            s = lax.rsqrt(jnp.mean(r * r, axis=1, keepdims=True) + EPSILON)
            e = dn * gain_ref[...]
            inner = jnp.mean(e * r, axis=1, keepdims=True)
            dr = cot_ref[at(i), :].astype(F32) + s * e - r * (s * s * s * inner)
            dres_ref[at(i), :] = dr
            rlow_ref[at(i), :] = dr.astype(BF16)
            return total + fold(dn * (r * s))

        gain_grad_ref[...] = lax.fori_loop(0, tiles, one, jnp.zeros(gain_grad_ref.shape, F32))


def back_kernel(
    ltiles, tiles, rlow_ref, wo_ref, mixl_ref, mixs_ref, gp_ref, st_ref, pr_ref, sin_ref, dp_ref,
    pc_ref, dwo_ref, gl_ref, tot_ref, rch_ref, end_ref, bias_ref, dm_ref,
):
    lrows = ltiles * TILE
    width = gp_ref.shape[1]
    rlow = rlow_ref[...]
    dm_ref[...] = dot_nt(rlow, flat(wo_ref[...]))
    grad = dot_tn(mixl_ref[...], rlow_ref[0:lrows, :]) + dot_tn(mixs_ref[...], rlow_ref[lrows:, :])
    dwo_ref[...] = grad.astype(BF16).reshape(dwo_ref.shape)
    gl_ref[0:HALO, :] = jnp.zeros((HALO, width), BF16)
    last = row_iota((TILE, width)) == TILE - 1

    def local(j, states):
        dm = dm_ref[at(j - 1), :]
        ge, slope = gelu_pair(gp_ref[at(j), :])
        dgate = dm * states * slope
        gl_ref[at(j), :] = dgate.astype(BF16)
        ds = dm * ge
        rate = sigmoid(dp_ref[at(j), :])
        decay = jnp.exp(-pc_ref[C8 : C8 + 1, :] * (0.25 + rate))
        a, b = scan_tile(decay, decay * ds, True)
        return a, b, ds, fold(dgate)

    def short_step(i, carry):
        c, bias = carry
        j = tiles - 1 - i
        a, b, ds, part = local(j, st_ref[at(j), :])
        cs = b + a * c
        tot_ref[at(j), :] = ds + jnp.where(last, c, pltpu.roll(cs, TILE - 1, 0))
        return cs[0:1], bias + part

    _, bias = lax.fori_loop(
        0,
        tiles - 1 - ltiles,
        short_step,
        (jnp.zeros((1, width), F32), jnp.zeros((8, width), F32)),
    )
    s_in = sin_ref[0:1, :]

    def long_step(i, carry):
        c, reach, bias = carry
        j = ltiles - i
        a, b, ds, part = local(j, st_ref[at(j), :] + pr_ref[at(j), :] * s_in)
        cs = b + a * c
        rs = a * reach
        tot_ref[at(j), :] = ds + jnp.where(last, c, pltpu.roll(cs, TILE - 1, 0))
        rch_ref[at(j), :] = jnp.where(last, reach, pltpu.roll(rs, TILE - 1, 0))
        return cs[0:1], rs[0:1], bias + part

    c, reach, bias = lax.fori_loop(
        0, ltiles, long_step, (jnp.zeros((1, width), F32), jnp.ones((1, width), F32), bias)
    )
    end_ref[...] = jnp.concatenate([reach, c, jnp.zeros((6, width), F32)], axis=0)
    bias_ref[...] = bias


def last_kernel(
    ltiles, tiles, first_ref, x_ref, gain_ref, nm_ref, dres_ref, wg_ref, wi_ref, wd_ref, wo_ref,
    pc_ref, in_ref, dp_ref, ip_ref, st_ref, pr_ref, sin_ref, tot_ref, rch_ref, cin_ref, gl_ref,
    dx_ref, halo_ref, gain_grad_ref, dwg_ref, dwi_ref, gd_ref, go_ref, small_ref,
    acc, dc_ref, cl_ref, dl_ref, ol_ref, il_ref,
):
    width = in_ref.shape[1]
    step = pl.program_id(0)
    zero8 = jnp.zeros((8, width), F32)
    cl_ref[0:HALO, :] = jnp.zeros((HALO, width), BF16)
    dl_ref[0:HALO, :] = jnp.zeros((HALO, width), BF16)
    ol_ref[0:HALO, :] = jnp.zeros((HALO, width), BF16)
    dc_ref[0:HALO, :] = jnp.zeros((HALO, width), F32)

    def gate_step(j, states, total, live, carry):
        before, sum_d, sum_o, sum_p = carry
        rows = row_iota((TILE, width))
        prior = jnp.where(rows == 0, before, pltpu.roll(states, 1, 0))
        conv, _ = conv_tile(in_ref, pc_ref, j, live)
        rate, opening, decay, square = gates(
            dp_ref[at(j), :], ip_ref[at(j), :], pc_ref[C8 : C8 + 1, :]
        )
        inv = lax.rsqrt(square)
        mult = square * inv
        weighted = total * opening
        d_open = total * mult * conv
        d_log = decay * (total * prior - (weighted * conv) * (decay * inv))
        d_rate = -pc_ref[C8 : C8 + 1, :] * d_log
        d_dp = d_rate * (rate - rate * rate)
        d_ip = d_open * (opening - opening * opening)
        cl_ref[at(j), :] = conv.astype(BF16)
        dl_ref[at(j), :] = d_dp.astype(BF16)
        ol_ref[at(j), :] = d_ip.astype(BF16)
        dc_ref[at(j), :] = weighted * mult
        return (
            states[TILE - 1 : TILE],
            sum_d + fold(d_dp),
            sum_o + fold(d_ip),
            sum_p - fold((0.25 + rate) * d_log),
        )

    s_in = sin_ref[0:1, :]
    c_in = cin_ref[0:1, :]

    def long_step(i, carry):
        j = 1 + i
        states = st_ref[at(j), :] + pr_ref[at(j), :] * s_in
        total = tot_ref[at(j), :] + rch_ref[at(j), :] * c_in
        return gate_step(j, states, total, 1.0, carry)

    def short_step(i, carry):
        j = 1 + ltiles + i
        return gate_step(j, st_ref[at(j), :], tot_ref[at(j), :], jnp.where(i == 0, 0.0, 1.0), carry)

    carry = lax.fori_loop(0, ltiles, long_step, (s_in, zero8, zero8, zero8))
    carry = lax.fori_loop(
        0, tiles - 1 - ltiles, short_step, (jnp.zeros((1, width), F32),) + carry[1:]
    )
    _, sum_d, sum_o, sum_p = carry

    low, dlow, olow = cl_ref[...], dl_ref[...], ol_ref[...]
    gd_ref[0] = dot_tn(low, dlow)
    go_ref[0] = dot_tn(low, olow)
    dc_ref[...] += dot_nt(dlow, wd_ref[0]) + dot_nt(olow, wo_ref[0])

    def conv_step(j, carry):
        sum_c, sum_i, sums = carry
        live = jnp.where(j == 1 + ltiles, 0.0, 1.0)
        cur = dc_ref[at(j), :]
        up = jnp.where((j == ltiles) | (j == tiles - 1), 0.0, 1.0)
        later = dc_ref[at(jnp.minimum(j + 1, tiles - 1)), :] * up
        _, moved = conv_tile(in_ref, pc_ref, jnp.maximum(j, 1), live)
        d_in = pc_ref[CW : CW + 1, :] * cur
        for k in range(1, 4):
            d_in = d_in + pc_ref[CW + k : CW + k + 1, :] * shift_up(cur, later, k)
        d_in = d_in * jnp.where(j == 0, first_ref[0, 0], 1.0)
        il_ref[at(j), :] = d_in.astype(BF16)
        return (
            sum_c + fold(cur),
            sum_i + fold(d_in),
            tuple(s + fold(cur * m) for s, m in zip(sums, moved)),
        )

    sum_c, sum_i, sums = lax.fori_loop(0, tiles, conv_step, (zero8, zero8, (zero8,) * 4))
    parts = [sum_i, *sums, sum_c, sum_d, sum_o, sum_p * pc_ref[S8 : S8 + 1, :]]
    rows = [jnp.sum(p, axis=0, keepdims=True) for p in parts]
    small_ref[...] = jnp.concatenate(rows + [jnp.zeros((16 - len(rows), width), F32)], axis=0)

    nm = nm_ref[...]
    dwi_ref[...] = dot_tn(il_ref[...], nm).astype(BF16).reshape(dwi_ref.shape)
    dwg_ref[...] = dot_tn(gl_ref[...], nm).astype(BF16).reshape(dwg_ref.shape)
    part = dot_nn(gl_ref[...], flat(wg_ref[...])) + dot_nn(il_ref[...], flat(wi_ref[...]))

    @pl.when(step == 0)
    def _():
        acc[...] = part

    @pl.when(step > 0)
    def _():
        acc[...] += part

    @pl.when(step == pl.num_programs(0) - 1)
    def _():
        def norm_back(j):
            v = x_ref[at(j), :].astype(F32)
            dn = acc[at(j), :]
            s = lax.rsqrt(jnp.mean(v * v, axis=1, keepdims=True) + EPSILON)
            e = dn * gain_ref[...]
            inner = jnp.mean(e * v, axis=1, keepdims=True)
            return s * e - v * (s * s * s * inner), fold(dn * (v * s))

        halo, total = norm_back(0)
        halo_ref[...] = halo

        def one(i, total):
            d, part = norm_back(1 + i)
            dx_ref[at(i), :] = dres_ref[at(i), :] + d
            return total + part

        gain_grad_ref[...] = lax.fori_loop(0, tiles - 1, one, total)


def shape_of(shape, dtype):
    return jax.ShapeDtypeStruct(shape, dtype)


def whole(shape):
    return pl.BlockSpec(shape, lambda g: (0,) * len(shape), pipeline_mode=pl.Buffered(1))


def kept(shape):
    return pl.BlockSpec(shape, lambda g: (0,) * len(shape))


def columns(rows, width):
    return pl.BlockSpec((rows, width), lambda g: (0, g))


def params(limit):
    return pltpu.CompilerParams(
        dimension_semantics=("arbitrary",), vmem_limit_bytes=int(limit * MIB)
    )


def pair_blocks(weight):
    blocks, width, _ = weight.shape
    pairs = weight.reshape(blocks // 2, 2, width, width)
    zero = jnp.zeros_like(pairs[:, 0])
    top = jnp.concatenate([pairs[:, 0], zero], axis=2)
    low = jnp.concatenate([zero, pairs[:, 1]], axis=2)
    return jnp.concatenate([top, low], axis=1)


def unpair(grads):
    width = grads.shape[1] // 2
    both = jnp.stack([grads[:, :width, :width], grads[:, width:, width:]], axis=1)
    return both.reshape(-1, width, width)


def to_slots(parts, count):
    rows = parts[0].shape[0]
    depth = parts[0].shape[1]
    got = lax.all_gather(jnp.concatenate(parts, axis=0), ("seq", "row"), axis=0, tiled=False)
    if count != SLOTS:
        got = got.reshape(count, len(parts), rows, depth).transpose(1, 0, 2, 3)
        got = got.reshape(len(parts), SLOTS, rows * count // SLOTS, depth).transpose(1, 0, 2, 3)
    return got.reshape(SLOTS, -1, depth)


def scatter_slots(grads, number, count):
    slots, rows, depth = grads.shape
    if count != SLOTS:
        grads = grads.reshape(slots, number, rows // number, depth).transpose(1, 0, 2, 3)
        grads = grads.reshape(number, count, -1, depth).transpose(1, 0, 2, 3)
    flat_grads = grads.reshape(slots * rows, depth)
    own = lax.psum_scatter(flat_grads, ("seq", "row"), scatter_dimension=0, tiled=True)
    own = own.astype(F32).reshape(number, -1, depth)
    return [own[i] for i in range(number)]


def entering(ends, reverse):
    count = lax.axis_size("seq")
    place = lax.axis_index("seq")
    got = lax.all_gather(ends, "seq")
    state = jnp.zeros_like(ends[0])
    for hop in range(count - 1):
        source = count - 1 - hop if reverse else hop
        ahead = source > place if reverse else source < place
        state = jnp.where(ahead, got[source, 0] * state + got[source, 1], state)
    return jnp.broadcast_to(state[None], (8, state.shape[0]))


def hop(value, axis, steps):
    count = lax.axis_size(axis)
    first, last = (max(0, -steps), min(count, count - steps))
    return lax.ppermute(value, axis, [(source, source + steps) for source in range(first, last)])


def shards(
    long_tokens,
    short_tokens,
    long_length,
    long_cotangent,
    short_cotangent,
    first_gain,
    gate_weight,
    gate_bias,
    input_weight,
    input_bias,
    conv_weight,
    conv_bias,
    decay_gate_weight,
    decay_gate_bias,
    input_gate_weight,
    input_gate_bias,
    decay_param,
    out_weight,
    second_gain,
    mlp_gate_weight,
    mlp_up_weight,
    mlp_down_weight,
):
    count = lax.axis_size("seq") * lax.axis_size("row")
    lrows, srows, depth = long_tokens.shape[1], short_tokens.shape[1], long_tokens.shape[2]
    chans = gate_bias.shape[0]
    units = mlp_gate_weight.shape[1] * count
    tokens = lrows + srows
    total = HALO + tokens
    ltiles, tiles = lrows // TILE, total // TILE
    cshare, ushare = chans // SLOTS, units // SLOTS
    groups = 4
    width = chans // groups
    per = SLOTS // groups

    long_x = long_tokens.reshape(lrows, depth)
    halo_x = hop(long_x[lrows - HALO :], "seq", 1)
    mixw = to_slots([gate_weight.T, input_weight.T, out_weight], count)
    mlpw = to_slots([mlp_gate_weight.T, mlp_up_weight.T, mlp_down_weight], count)
    x = jnp.concatenate([halo_x, long_x, short_tokens.reshape(srows, depth)], axis=0)
    place = lax.axis_index("seq")
    first = jnp.where(place > 0, 1.0, 0.0).astype(F32).reshape(1, 1)
    positions = place * lrows + jnp.arange(lrows, dtype=jnp.int32)
    keep = positions[:, None] < long_length[0]
    masked = jnp.where(keep, long_cotangent.reshape(lrows, depth), jnp.zeros((), BF16))
    cot = jnp.concatenate([masked, short_cotangent.reshape(srows, depth)], axis=0)
    chan = jnp.concatenate(
        [
            jnp.stack([gate_bias, input_bias]),
            conv_weight,
            jnp.stack(
                [
                    conv_bias,
                    decay_gate_bias,
                    input_gate_bias,
                    8.0 * jax.nn.softplus(decay_param),
                    8.0 * jax.nn.sigmoid(decay_param),
                ]
            ),
            jnp.zeros((5, chans), F32),
        ],
        axis=0,
    )
    pair_d = pair_blocks(decay_gate_weight)
    pair_o = pair_blocks(input_gate_weight)
    gain1 = first_gain[None]
    gain2 = second_gain[None]
    scalar = pl.BlockSpec(memory_space=pltpu.SMEM)

    def mix_part(which):
        return pl.BlockSpec((per, cshare, depth), lambda g: (g, which, 0))

    pair_spec = pl.BlockSpec((1, width, width), lambda g: (g, 0, 0))
    col = columns(total, width)
    col_long = columns(HALO + lrows, width)
    pc_spec = columns(16, width)
    col8 = columns(8, width)

    wide = shape_of((total, chans), F32)
    narrow = shape_of((HALO + lrows, chans), F32)
    gp, inner, dp, ip, states, reach, mix_s, ends, normed = pl.pallas_call(
        functools.partial(front_kernel, ltiles, tiles),
        grid=(groups,),
        in_specs=[
            scalar, whole((total, depth)), whole((1, depth)), mix_part(0), mix_part(1),
            pair_spec, pair_spec, pc_spec,
        ],
        out_specs=[
            col, col, col, col, col, col_long, columns(srows, width), col8,
            kept((total, depth)),
        ],
        out_shape=[
            wide, wide, wide, wide, wide, narrow, shape_of((srows, chans), BF16),
            shape_of((8, chans), F32), shape_of((total, depth), BF16),
        ],
        scratch_shapes=[pltpu.VMEM((total, width), F32), pltpu.VMEM((total, width), BF16)],
        compiler_params=params(48),
        name="front",
    )(first, x, gain1, mixw, mixw, pair_d, pair_o, chan)

    s_in = entering(ends[0:2], False)

    steps = 4
    hid = units // steps
    slots = SLOTS // steps
    share = 3 * ushare
    out, d_res, rlow, mix_l, gain2_grad, dmlp = pl.pallas_call(
        functools.partial(mlp_kernel, ltiles, tokens // TILE),
        grid=(steps,),
        in_specs=[
            whole((total, depth)), whole((tokens, depth)), whole((HALO + lrows, chans)),
            whole((HALO + lrows, chans)), whole((HALO + lrows, chans)), whole((8, chans)),
            whole((srows, chans)),
            pl.BlockSpec((SLOTS, cshare, depth), lambda g: (0, 2, 0), pipeline_mode=pl.Buffered(1)),
            whole((1, depth)),
            pl.BlockSpec((slots, share, depth), lambda g: (g, 0, 0)),
        ],
        out_specs=[
            whole((tokens, depth)), whole((tokens, depth)), whole((tokens, depth)),
            whole((lrows, chans)), whole((8, depth)),
            pl.BlockSpec((slots, share, depth), lambda g: (g, 0, 0)),
        ],
        out_shape=[
            shape_of((tokens, depth), BF16), shape_of((tokens, depth), F32),
            shape_of((tokens, depth), BF16), shape_of((lrows, chans), BF16),
            shape_of((8, depth), F32), shape_of((SLOTS, share, depth), BF16),
        ],
        scratch_shapes=[
            pltpu.VMEM((tokens, depth), BF16), pltpu.VMEM((tokens, depth), F32),
            pltpu.VMEM((tokens, depth), F32), pltpu.VMEM((tokens, hid), F32),
            pltpu.VMEM((tokens, hid), F32), pltpu.VMEM((tokens, hid), F32),
            pltpu.VMEM((tokens, hid), BF16), pltpu.VMEM((tokens, hid), BF16),
            pltpu.VMEM((tokens, hid), BF16),
        ],
        compiler_params=params(60),
        name="mlp",
    )(x, cot, states, reach, gp, s_in, mix_s, mixw, gain2, mlpw)

    slot_spec = pl.BlockSpec((per, cshare, depth), lambda g: (g, 0, 0))
    slot_shape = shape_of((SLOTS, cshare, depth), BF16)
    d_out, gate_low, total_grad, back_reach, back_ends, gate_bias_part = pl.pallas_call(
        functools.partial(back_kernel, ltiles, tiles),
        grid=(groups,),
        in_specs=[
            whole((tokens, depth)), mix_part(2), columns(lrows, width), columns(srows, width),
            col, col, col_long, col8, col, pc_spec,
        ],
        out_specs=[slot_spec, col, col, col_long, col8, col8],
        out_shape=[
            slot_shape, shape_of((total, chans), BF16), wide, narrow,
            shape_of((8, chans), F32), shape_of((8, chans), F32),
        ],
        scratch_shapes=[pltpu.VMEM((tokens, width), F32)],
        compiler_params=params(48),
        name="back",
    )(rlow, mixw, mix_l, mix_s, gp, states, reach, s_in, dp, chan)

    c_in = entering(back_ends[0:2], True)

    grad_pair = shape_of((groups, width, width), F32)
    d_x, d_halo, gain1_grad, d_gate, d_input, d_decay, d_open, small = pl.pallas_call(
        functools.partial(last_kernel, ltiles, tiles),
        grid=(groups,),
        in_specs=[
            scalar, whole((total, depth)), whole((1, depth)), whole((total, depth)),
            whole((tokens, depth)), mix_part(0), mix_part(1), pair_spec, pair_spec, pc_spec,
            col, col, col, col, col_long, col8, col, col_long, col8, col,
        ],
        out_specs=[
            whole((tokens, depth)), whole((HALO, depth)), whole((8, depth)), slot_spec, slot_spec,
            pair_spec, pair_spec, pc_spec,
        ],
        out_shape=[
            shape_of((tokens, depth), F32), shape_of((HALO, depth), F32), shape_of((8, depth), F32),
            slot_shape, slot_shape, grad_pair, grad_pair, shape_of((16, chans), F32),
        ],
        scratch_shapes=[
            pltpu.VMEM((total, depth), F32), pltpu.VMEM((total, width), F32),
            pltpu.VMEM((total, width), BF16), pltpu.VMEM((total, width), BF16),
            pltpu.VMEM((total, width), BF16), pltpu.VMEM((total, width), BF16),
        ],
        compiler_params=params(60),
        name="last",
    )(
        first, x, gain1, normed, d_res, mixw, mixw, pair_d, pair_o, chan,
        inner, dp, ip, states, reach, s_in, total_grad, back_reach, c_in, gate_low,
    )

    late = hop(d_halo, "seq", -1)
    long_grad = d_x[:lrows].at[lrows - HALO :].add(late)
    short_grad = d_x[lrows:]

    g_mgate, g_mup, g_down = scatter_slots(dmlp, 3, count)
    dmix = jnp.concatenate([d_gate, d_input, d_out], axis=1)
    g_gate, g_input, g_out = scatter_slots(dmix, 3, count)
    sums = lax.psum(
        (
            jnp.sum(gain1_grad, axis=0),
            jnp.sum(gain2_grad, axis=0),
            jnp.sum(gate_bias_part, axis=0),
            small[0:9],
            unpair(d_decay),
            unpair(d_open),
        ),
        ("seq", "row"),
    )
    gain1_sum, gain2_sum, gate_bias_sum, rows, decay_sum, open_sum = sums
    return (
        out[:lrows].reshape(long_tokens.shape),
        out[lrows:].reshape(short_tokens.shape),
        long_grad.reshape(long_tokens.shape),
        short_grad.reshape(short_tokens.shape),
        gain1_sum,
        g_gate.T,
        gate_bias_sum,
        g_input.T,
        rows[0],
        rows[1:5],
        rows[5],
        decay_sum,
        rows[6],
        open_sum,
        rows[7],
        rows[8],
        g_out,
        gain2_sum,
        g_mgate.T,
        g_mup.T,
        g_down,
    )


def solution(mesh):
    both = ("seq", "row")
    long_spec = P("row", "seq", None)
    short_spec = P(both, None, None)
    cols = P(None, both)
    rows = P(both, None)
    return jax.shard_map(
        shards,
        mesh=mesh,
        in_specs=(
            long_spec, short_spec, P("row"), long_spec, short_spec, P(), cols, P(), cols, P(),
            P(), P(), P(), P(), P(), P(), P(), rows, P(), cols, cols, rows,
        ),
        out_specs=(
            long_spec, short_spec, long_spec, short_spec, P(), cols, P(), cols, P(), P(), P(),
            P(), P(), P(), P(), P(), rows, P(), cols, cols, rows,
        ),
        check_vma=False,
    )
```

```python
import functools

import jax
import jax.numpy as jnp
from jax import lax
from jax.experimental import pallas as pl
from jax.experimental.pallas import tpu as pltpu
from jax.sharding import PartitionSpec as P

EPSILON = 1e-06
F32 = jnp.float32
BF16 = jnp.bfloat16
SLOTS = 32
TILE = 16
HALO = 16
MIB = 1024 * 1024
GELU_A = 0.7978845608028654
GELU_B = 0.044715


def dot_nn(a, b):
    return lax.dot_general(a, b, (((1,), (0,)), ((), ())), preferred_element_type=F32)


def dot_nt(a, b):
    return lax.dot_general(a, b, (((1,), (1,)), ((), ())), preferred_element_type=F32)


def dot_tn(a, b):
    return lax.dot_general(a, b, (((0,), (0,)), ((), ())), preferred_element_type=F32)


def sigmoid(v):
    return 0.5 * jnp.tanh(0.5 * v) + 0.5


def gelu(v):
    t = jnp.tanh(v * (GELU_A + (GELU_A * GELU_B) * (v * v)))
    h = 0.5 * v
    return h + h * t


def gelu_pair(v):
    w = v * v
    t = jnp.tanh(v * (GELU_A + (GELU_A * GELU_B) * w))
    h = 0.5 * v
    slope = 0.5 + 0.5 * t + (h - h * (t * t)) * (GELU_A + (3.0 * GELU_A * GELU_B) * w)
    return h + h * t, slope


def row_iota(shape):
    return lax.broadcasted_iota(jnp.int32, shape, 0)


def at(j):
    return pl.ds(pl.multiple_of(j * TILE, TILE), TILE)


def scan_tile(a, b, reverse):
    rows = row_iota(a.shape)
    step = 1
    while step < TILE:
        if reverse:
            keep, shift = rows < TILE - step, TILE - step
        else:
            keep, shift = rows >= step, step
        b = jnp.where(keep, a * pltpu.roll(b, shift, 0) + b, b)
        a = jnp.where(keep, a * pltpu.roll(a, shift, 0), a)
        step *= 2
    return a, b


def shift_down(cur, prev, k):
    if k == 0:
        return cur
    rows = row_iota(cur.shape)
    return jnp.where(rows < k, pltpu.roll(prev, k, 0), pltpu.roll(cur, k, 0))


def shift_up(cur, later, k):
    if k == 0:
        return cur
    rows = row_iota(cur.shape)
    return jnp.where(
        rows >= TILE - k, pltpu.roll(later, TILE - k, 0), pltpu.roll(cur, TILE - k, 0)
    )


def fold(v):
    return v[0:8] + v[8:16]


def flat(block):
    return block.reshape(block.shape[0] * block.shape[1], block.shape[2])


def gates(dp, ip, c8):
    rate = sigmoid(dp)
    opening = sigmoid(ip)
    log_decay = -c8 * (0.25 + rate)
    decay = jnp.exp(log_decay)
    square = -jnp.tanh(log_decay) * (1.0 + decay * decay)
    return rate, opening, decay, square


GB, IB, CW, CB, DB, OB, C8, S8 = 0, 1, 2, 6, 7, 8, 9, 10


def conv_tile(in_ref, pc_ref, j, live):
    cur = in_ref[at(j), :]
    prev = in_ref[at(j - 1), :] * live
    out = pc_ref[CB : CB + 1, :] + pc_ref[CW : CW + 1, :] * cur
    moved = [cur]
    for k in range(1, 4):
        m = shift_down(cur, prev, k)
        moved.append(m)
        out = out + pc_ref[CW + k : CW + k + 1, :] * m
    return out, moved


def front_kernel(
    ltiles, tiles, first_ref, x_ref, gain_ref, wg_ref, wi_ref, wd_ref, wo_ref, pc_ref,
    gp_ref, in_ref, dp_ref, ip_ref, st_ref, pr_ref, mix_ref, end_ref, nm_ref, cv_ref, cl_ref,
):
    @pl.when(pl.program_id(0) == 0)
    def _():
        @pl.loop(0, tiles)
        def _(j):
            v = x_ref[at(j), :].astype(F32)
            s = lax.rsqrt(jnp.mean(v * v, axis=1, keepdims=True) + EPSILON)
            nm_ref[at(j), :] = (v * s * gain_ref[...]).astype(BF16)

    nm = nm_ref[...]
    gp_ref[...] = dot_nt(nm, flat(wg_ref[...])) + pc_ref[GB : GB + 1, :]
    in_ref[...] = dot_nt(nm, flat(wi_ref[...])) + pc_ref[IB : IB + 1, :]
    in_ref[0:HALO, :] = in_ref[0:HALO, :] * first_ref[0, 0]
    cl_ref[0:HALO, :] = jnp.zeros((HALO, cl_ref.shape[1]), BF16)

    @pl.loop(1, tiles)
    def _(j):
        live = jnp.where(j == 1 + ltiles, 0.0, 1.0)
        out, _ = conv_tile(in_ref, pc_ref, j, live)
        cv_ref[at(j), :] = out
        cl_ref[at(j), :] = out.astype(BF16)

    low = cl_ref[...]
    dp_ref[...] = dot_nn(low, wd_ref[0]) + pc_ref[DB : DB + 1, :]
    ip_ref[...] = dot_nn(low, wo_ref[0]) + pc_ref[OB : OB + 1, :]

    def scanned(j):
        _, opening, a, square = gates(dp_ref[at(j), :], ip_ref[at(j), :], pc_ref[C8 : C8 + 1, :])
        b = (square * lax.rsqrt(square)) * opening * cv_ref[at(j), :]
        return scan_tile(a, b, False)

    width = gp_ref.shape[1]

    def long_step(i, carry):
        state, reach = carry
        a, b = scanned(1 + i)
        s = b + a * state
        r = a * reach
        st_ref[at(1 + i), :] = s
        pr_ref[at(1 + i), :] = r
        return s[TILE - 1 : TILE], r[TILE - 1 : TILE]

    state, reach = lax.fori_loop(
        0, ltiles, long_step, (jnp.zeros((1, width), F32), jnp.ones((1, width), F32))
    )
    end_ref[...] = jnp.concatenate([reach, state, jnp.zeros((6, width), F32)], axis=0)

    def short_step(i, state):
        j = 1 + ltiles + i
        a, b = scanned(j)
        s = b + a * state
        st_ref[at(j), :] = s
        mix_ref[at(i), :] = (s * gelu(gp_ref[at(j), :])).astype(BF16)
        return s[TILE - 1 : TILE]

    lax.fori_loop(0, tiles - 1 - ltiles, short_step, jnp.zeros((1, width), F32))


def mlp_kernel(
    ltiles, tiles, x_ref, cot_ref, st_ref, pr_ref, gp_ref, sin_ref, mixs_ref, wo_ref, gain_ref,
    w_ref, out_ref, dres_ref, rlow_ref, mixl_ref, gain_grad_ref, dw_ref,
    n2_ref, acc_o, acc_n, g_ref, u_ref, d_ref, h_ref, dg_ref, du_ref,
):
    step = pl.program_id(0)
    lrows = ltiles * TILE
    half = g_ref.shape[1] // 2
    share = w_ref.shape[1] // 3

    @pl.when(step == 0)
    def _():
        s_in = sin_ref[0:1, :]

        @pl.loop(0, ltiles)
        def _(i):
            s = st_ref[at(1 + i), :] + pr_ref[at(1 + i), :] * s_in
            mixl_ref[at(i), :] = (s * gelu(gp_ref[at(1 + i), :])).astype(BF16)

        wo = flat(wo_ref[...])
        dres_ref[0:lrows, :] = dot_nn(mixl_ref[...], wo)
        dres_ref[lrows:, :] = dot_nn(mixs_ref[...], wo)

        @pl.loop(0, tiles)
        def _(i):
            r = dres_ref[at(i), :] + x_ref[at(1 + i), :].astype(F32)
            dres_ref[at(i), :] = r
            acc_o[at(i), :] = r
            s = lax.rsqrt(jnp.mean(r * r, axis=1, keepdims=True) + EPSILON)
            n2_ref[at(i), :] = (r * s * gain_ref[...]).astype(BF16)

        acc_n[...] = jnp.zeros_like(acc_n)

    n2 = n2_ref[...]
    wg = flat(w_ref[:, 0:share, :])
    wu = flat(w_ref[:, share : 2 * share, :])
    wd = flat(w_ref[:, 2 * share :, :])
    g_ref[...] = dot_nt(n2, wg)
    u_ref[...] = dot_nt(n2, wu)
    d_ref[...] = dot_nt(cot_ref[...], wd)

    @pl.loop(0, tiles)
    def _(i):
        for k in range(2):
            cols = slice(k * half, (k + 1) * half)
            ge, slope = gelu_pair(g_ref[at(i), cols])
            u = u_ref[at(i), cols]
            d = d_ref[at(i), cols]
            h_ref[at(i), cols] = (ge * u).astype(BF16)
            dg_ref[at(i), cols] = (d * u * slope).astype(BF16)
            du_ref[at(i), cols] = (d * ge).astype(BF16)

    acc_o[...] += dot_nn(h_ref[...], wd)
    acc_n[...] += dot_nn(dg_ref[...], wg) + dot_nn(du_ref[...], wu)
    shape = (dw_ref.shape[0], share, dw_ref.shape[2])
    dw_ref[:, 0:share, :] = dot_tn(dg_ref[...], n2).astype(BF16).reshape(shape)
    dw_ref[:, share : 2 * share, :] = dot_tn(du_ref[...], n2).astype(BF16).reshape(shape)
    dw_ref[:, 2 * share :, :] = dot_tn(h_ref[...], cot_ref[...]).astype(BF16).reshape(shape)

    @pl.when(step == pl.num_programs(0) - 1)
    def _():
        def one(i, total):
            r = dres_ref[at(i), :]
            out_ref[at(i), :] = acc_o[at(i), :].astype(BF16)
            dn = acc_n[at(i), :]
            s = lax.rsqrt(jnp.mean(r * r, axis=1, keepdims=True) + EPSILON)
            e = dn * gain_ref[...]
            inner = jnp.mean(e * r, axis=1, keepdims=True)
            dr = cot_ref[at(i), :].astype(F32) + s * e - r * (s * s * s * inner)
            dres_ref[at(i), :] = dr
            rlow_ref[at(i), :] = dr.astype(BF16)
            return total + fold(dn * (r * s))

        gain_grad_ref[...] = lax.fori_loop(0, tiles, one, jnp.zeros(gain_grad_ref.shape, F32))


def back_kernel(
    ltiles, tiles, rlow_ref, wo_ref, mixl_ref, mixs_ref, gp_ref, st_ref, pr_ref, sin_ref, dp_ref,
    pc_ref, dwo_ref, gl_ref, tot_ref, rch_ref, end_ref, bias_ref, dm_ref,
):
    lrows = ltiles * TILE
    width = gp_ref.shape[1]
    rlow = rlow_ref[...]
    dm_ref[...] = dot_nt(rlow, flat(wo_ref[...]))
    grad = dot_tn(mixl_ref[...], rlow_ref[0:lrows, :]) + dot_tn(mixs_ref[...], rlow_ref[lrows:, :])
    dwo_ref[...] = grad.astype(BF16).reshape(dwo_ref.shape)
    gl_ref[0:HALO, :] = jnp.zeros((HALO, width), BF16)
    last = row_iota((TILE, width)) == TILE - 1

    def local(j, states):
        dm = dm_ref[at(j - 1), :]
        ge, slope = gelu_pair(gp_ref[at(j), :])
        dgate = dm * states * slope
        gl_ref[at(j), :] = dgate.astype(BF16)
        ds = dm * ge
        rate = sigmoid(dp_ref[at(j), :])
        decay = jnp.exp(-pc_ref[C8 : C8 + 1, :] * (0.25 + rate))
        a, b = scan_tile(decay, decay * ds, True)
        return a, b, ds, fold(dgate)

    def short_step(i, carry):
        c, bias = carry
        j = tiles - 1 - i
        a, b, ds, part = local(j, st_ref[at(j), :])
        cs = b + a * c
        tot_ref[at(j), :] = ds + jnp.where(last, c, pltpu.roll(cs, TILE - 1, 0))
        return cs[0:1], bias + part

    _, bias = lax.fori_loop(
        0,
        tiles - 1 - ltiles,
        short_step,
        (jnp.zeros((1, width), F32), jnp.zeros((8, width), F32)),
    )
    s_in = sin_ref[0:1, :]

    def long_step(i, carry):
        c, reach, bias = carry
        j = ltiles - i
        a, b, ds, part = local(j, st_ref[at(j), :] + pr_ref[at(j), :] * s_in)
        cs = b + a * c
        rs = a * reach
        tot_ref[at(j), :] = ds + jnp.where(last, c, pltpu.roll(cs, TILE - 1, 0))
        rch_ref[at(j), :] = jnp.where(last, reach, pltpu.roll(rs, TILE - 1, 0))
        return cs[0:1], rs[0:1], bias + part

    c, reach, bias = lax.fori_loop(
        0, ltiles, long_step, (jnp.zeros((1, width), F32), jnp.ones((1, width), F32), bias)
    )
    end_ref[...] = jnp.concatenate([reach, c, jnp.zeros((6, width), F32)], axis=0)
    bias_ref[...] = bias


def last_kernel(
    ltiles, tiles, first_ref, x_ref, gain_ref, nm_ref, dres_ref, wg_ref, wi_ref, wd_ref, wo_ref,
    pc_ref, in_ref, dp_ref, ip_ref, st_ref, pr_ref, sin_ref, tot_ref, rch_ref, cin_ref, gl_ref,
    bias_ref, dx_ref, halo_ref, gain_grad_ref, dwg_ref, dwi_ref, gg_ref, small_ref,
    acc, dc_ref, cl_ref, dl_ref, ol_ref, il_ref,
):
    width = in_ref.shape[1]
    step = pl.program_id(0)
    zero8 = jnp.zeros((8, width), F32)
    cl_ref[0:HALO, :] = jnp.zeros((HALO, width), BF16)
    dl_ref[0:HALO, :] = jnp.zeros((HALO, width), BF16)
    ol_ref[0:HALO, :] = jnp.zeros((HALO, width), BF16)
    dc_ref[0:HALO, :] = jnp.zeros((HALO, width), F32)

    def gate_step(j, states, total, live, carry):
        before, sum_d, sum_o, sum_p = carry
        rows = row_iota((TILE, width))
        prior = jnp.where(rows == 0, before, pltpu.roll(states, 1, 0))
        conv, _ = conv_tile(in_ref, pc_ref, j, live)
        rate, opening, decay, square = gates(
            dp_ref[at(j), :], ip_ref[at(j), :], pc_ref[C8 : C8 + 1, :]
        )
        inv = lax.rsqrt(square)
        mult = square * inv
        weighted = total * opening
        d_open = total * mult * conv
        d_log = decay * (total * prior - (weighted * conv) * (decay * inv))
        d_rate = -pc_ref[C8 : C8 + 1, :] * d_log
        d_dp = d_rate * (rate - rate * rate)
        d_ip = d_open * (opening - opening * opening)
        cl_ref[at(j), :] = conv.astype(BF16)
        dl_ref[at(j), :] = d_dp.astype(BF16)
        ol_ref[at(j), :] = d_ip.astype(BF16)
        dc_ref[at(j), :] = weighted * mult
        return (
            states[TILE - 1 : TILE],
            sum_d + fold(d_dp),
            sum_o + fold(d_ip),
            sum_p - fold((0.25 + rate) * d_log),
        )

    s_in = sin_ref[0:1, :]
    c_in = cin_ref[0:1, :]

    def long_step(i, carry):
        j = 1 + i
        states = st_ref[at(j), :] + pr_ref[at(j), :] * s_in
        total = tot_ref[at(j), :] + rch_ref[at(j), :] * c_in
        return gate_step(j, states, total, 1.0, carry)

    def short_step(i, carry):
        j = 1 + ltiles + i
        return gate_step(j, st_ref[at(j), :], tot_ref[at(j), :], jnp.where(i == 0, 0.0, 1.0), carry)

    carry = lax.fori_loop(0, ltiles, long_step, (s_in, zero8, zero8, zero8))
    carry = lax.fori_loop(
        0, tiles - 1 - ltiles, short_step, (jnp.zeros((1, width), F32),) + carry[1:]
    )
    _, sum_d, sum_o, sum_p = carry

    low, dlow, olow = cl_ref[...], dl_ref[...], ol_ref[...]
    half = width // 2
    for which, grads in ((0, dlow), (1, olow)):
        product = dot_tn(low, grads).astype(BF16)
        gg_ref[which, 0] = product[:half, :half]
        gg_ref[which, 1] = product[half:, half:]
    dc_ref[...] += dot_nt(dlow, wd_ref[0]) + dot_nt(olow, wo_ref[0])

    def conv_step(j, carry):
        sum_c, sum_i, sums = carry
        live = jnp.where(j == 1 + ltiles, 0.0, 1.0)
        cur = dc_ref[at(j), :]
        up = jnp.where((j == ltiles) | (j == tiles - 1), 0.0, 1.0)
        later = dc_ref[at(jnp.minimum(j + 1, tiles - 1)), :] * up
        _, moved = conv_tile(in_ref, pc_ref, jnp.maximum(j, 1), live)
        d_in = pc_ref[CW : CW + 1, :] * cur
        for k in range(1, 4):
            d_in = d_in + pc_ref[CW + k : CW + k + 1, :] * shift_up(cur, later, k)
        d_in = d_in * jnp.where(j == 0, first_ref[0, 0], 1.0)
        il_ref[at(j), :] = d_in.astype(BF16)
        return (
            sum_c + fold(cur),
            sum_i + fold(d_in),
            tuple(s + fold(cur * m) for s, m in zip(sums, moved)),
        )

    sum_c, sum_i, sums = lax.fori_loop(0, tiles, conv_step, (zero8, zero8, (zero8,) * 4))
    parts = [sum_i, *sums, sum_c, sum_d, sum_o, sum_p * pc_ref[S8 : S8 + 1, :], bias_ref[...]]
    rows = [jnp.sum(p, axis=0, keepdims=True) for p in parts]
    small_ref[...] = jnp.concatenate(rows + [jnp.zeros((16 - len(rows), width), F32)], axis=0)

    nm = nm_ref[...]
    dwi_ref[...] = dot_tn(il_ref[...], nm).astype(BF16).reshape(dwi_ref.shape)
    dwg_ref[...] = dot_tn(gl_ref[...], nm).astype(BF16).reshape(dwg_ref.shape)
    part = dot_nn(gl_ref[...], flat(wg_ref[...])) + dot_nn(il_ref[...], flat(wi_ref[...]))

    @pl.when(step == 0)
    def _():
        acc[...] = part

    @pl.when(step > 0)
    def _():
        acc[...] += part

    @pl.when(step == pl.num_programs(0) - 1)
    def _():
        def norm_back(j):
            v = x_ref[at(j), :].astype(F32)
            dn = acc[at(j), :]
            s = lax.rsqrt(jnp.mean(v * v, axis=1, keepdims=True) + EPSILON)
            e = dn * gain_ref[...]
            inner = jnp.mean(e * v, axis=1, keepdims=True)
            return s * e - v * (s * s * s * inner), fold(dn * (v * s))

        halo, total = norm_back(0)
        halo_ref[...] = halo

        def one(i, total):
            d, part = norm_back(1 + i)
            dx_ref[at(i), :] = dres_ref[at(i), :] + d
            return total + part

        gain_grad_ref[...] = lax.fori_loop(0, tiles - 1, one, total)


def shape_of(shape, dtype):
    return jax.ShapeDtypeStruct(shape, dtype)


def whole(shape):
    return pl.BlockSpec(shape, lambda g: (0,) * len(shape), pipeline_mode=pl.Buffered(1))


def kept(shape):
    return pl.BlockSpec(shape, lambda g: (0,) * len(shape))


def columns(rows, width):
    return pl.BlockSpec((rows, width), lambda g: (0, g))


def params(limit):
    return pltpu.CompilerParams(
        dimension_semantics=("arbitrary",), vmem_limit_bytes=int(limit * MIB)
    )


def pair_blocks(weight):
    blocks, width, _ = weight.shape
    pairs = weight.reshape(blocks // 2, 2, width, width)
    zero = jnp.zeros_like(pairs[:, 0])
    top = jnp.concatenate([pairs[:, 0], zero], axis=2)
    low = jnp.concatenate([zero, pairs[:, 1]], axis=2)
    return jnp.concatenate([top, low], axis=1)


def place_of():
    s = lax.axis_index("seq")
    return s // 4, (s // 2) % 2, s % 2, lax.axis_index("row")


def device_at(y, x, c, z):
    return ((y * 2 + x) * 2 + c, z)


class Peers:
    def __init__(self, zcount):
        y, x, c, z = self.place = place_of()
        self.far = [(z + k) % zcount for k in range(1, zcount)]
        self.along = [device_at(y, x, c, q) for q in self.far]
        self.near = ((y + c) % 2, (x + 1 - c) % 2)
        self.first = device_at(*self.near, c, z)
        self.second = device_at((y + 1 - c) % 2, (x + c) % 2, c, z)
        self.other = device_at(y, x, 1 - c, z)

    def meet(self):
        everyone = [*self.along, self.first, self.second, self.other]
        barrier = pltpu.get_barrier_semaphore()
        for peer in everyone:
            pl.semaphore_signal(
                barrier, inc=1, device_id=peer, device_id_type=pl.DeviceIdType.MESH
            )
        pl.semaphore_wait(barrier, len(everyone))


def remote(source, target, send, recv, device):
    return pltpu.make_async_remote_copy(
        src_ref=source,
        dst_ref=target,
        send_sem=send,
        recv_sem=recv,
        device_id=device,
        device_id_type=pl.DeviceIdType.MESH,
    )


class Spread:
    def __init__(self, peers, own, full, send, recv):
        self.peers, self.own, self.full, self.send, self.recv = peers, own, full, send, recv

    def go(self, stage, act):
        y, x, c, z = self.peers.place
        p, full = self.peers, self.full
        if stage == 0:
            for k, device in enumerate(p.along):
                act(remote(self.own, full(y, x, c, z), self.send(k), self.recv(k), device))
            return
        k = len(p.along) + stage - 1
        if stage == 2:

            @pl.when(c == 0)
            def _():
                part = full(y, slice(None), c, slice(None))
                act(remote(part, part, self.send(k), self.recv(k), p.second))

            @pl.when(c == 1)
            def _():
                part = full(slice(None), x, c, slice(None))
                act(remote(part, part, self.send(k), self.recv(k), p.second))

            return
        if stage == 1:
            part, device = full(y, x, c, slice(None)), p.first
        else:
            part, device = full(slice(None), slice(None), c, slice(None)), p.other
        act(remote(part, part, self.send(k), self.recv(k), device))

    def start(self, stage):
        self.go(stage, lambda d: d.start())

    def arrive(self, stage):
        self.go(stage, lambda d: d.wait_recv())

    def drain(self):
        for stage in range(4):
            self.go(stage, lambda d: d.wait_send())


def waves(count, lags):
    for t in range(count + sum(lags) + 1):
        for stage in range(len(lags), -1, -1):
            piece = t - sum(lags[:stage])
            if 0 <= piece < count:
                yield piece, stage


def gather_kernel(zcount, chunks, lags, number, *refs):
    ins, outs = refs[:number], refs[number : 2 * number]
    csem, ssem, rsem = refs[2 * number :]
    peers = Peers(zcount)
    y, x, c, z = peers.place
    peers.meet()
    spreads, copies = [], []
    for i, (which, start, size) in enumerate(chunks):
        rows = pl.ds(start, size)
        own = ins[which].at[rows]

        def full(a, b, d, e, ref=outs[which], rows=rows):
            return ref.at[a, b, d, e, rows]

        spreads.append(
            Spread(peers, own, full, lambda k, i=i: ssem.at[i, k], lambda k, i=i: rsem.at[i, k])
        )
        copies.append(pltpu.make_async_copy(own, full(y, x, c, z), csem.at[i]))
    for i, stage in waves(len(chunks), lags):
        if stage == 0:
            copies[i].start()
        elif stage == 1:
            copies[i].wait()
        if stage > 0:
            spreads[i].arrive(stage - 1)
        if stage < 4:
            spreads[i].start(stage)
    for spread in spreads:
        spread.drain()


def gather_call(parts, zcount):
    size = 16
    chunks = [
        (which, start, size)
        for which, part in enumerate(parts)
        for start in range(0, part.shape[0], size)
    ]
    hbm = pl.BlockSpec(memory_space=pl.ANY)
    links = pltpu.SemaphoreType.DMA((len(chunks), zcount + 2))
    return pl.pallas_call(
        functools.partial(gather_kernel, zcount, chunks, (2, 2, 3, 2), len(parts)),
        out_shape=[shape_of((2, 2, 2, zcount) + p.shape, p.dtype) for p in parts],
        in_specs=[hbm] * len(parts),
        out_specs=[hbm] * len(parts),
        scratch_shapes=[pltpu.SemaphoreType.DMA((len(chunks),)), links, links],
        compiler_params=pltpu.CompilerParams(collective_id=0, has_side_effects=True),
        name="gather",
    )(*parts)


def scatter_kernel(zcount, chunks, lags, nin, nout, *refs):
    ins, outs = refs[:nin], refs[nin : nin + nout]
    scratch = refs[nin + nout :]
    buffers = [scratch[0:5], scratch[5:10], scratch[10:15]]
    csem, ssem, rsem, ssem2, rsem2 = scratch[15:]
    peers = Peers(zcount)
    y, x, c, z = peers.place
    peers.meet()

    def add(into, i, part, j):
        into[i] = (into[i].astype(F32) + part[j].astype(F32)).astype(into.dtype)

    class Piece:
        def __init__(self, i, kind, slot, which, start, rows, target, offset):
            self.i, self.kind, self.slot = i, kind, slot
            self.a, self.r0, self.r1, self.r2, self.r3 = buffers[kind]
            self.source, self.rows = ins[which], pl.ds(start, rows)
            self.target, self.span = outs[target], pl.ds(offset, rows)
            self.spread = None
            if kind > 0:

                def full(*place):
                    return self.target.at[place]

                self.spread = Spread(
                    peers, full(y, x, c, z), full, lambda k: ssem2.at[i, k], lambda k: rsem2.at[i, k]
                )

        def local(self):
            mine = self.source.at[:, :, c, :, self.rows]
            return pltpu.make_async_copy(mine, self.a.at[self.slot], csem.at[self.i])

        def send(self, stage, act):
            s = self.slot

            def go(source, target, k, device):
                act(remote(source, target, ssem.at[self.i, k], rsem.at[self.i, k], device))

            if stage == 0:
                theirs = self.source.at[:, :, 1 - c, :, self.rows]
                go(theirs, self.r0.at[s], 0, peers.other)
            elif stage == 1:

                @pl.when(c == 0)
                def _():
                    go(self.a.at[s, 1 - y], self.r1.at[s], 1, peers.second)

                @pl.when(c == 1)
                def _():
                    go(self.a.at[s, :, 1 - x], self.r1.at[s], 1, peers.second)

            elif stage == 2:
                go(self.a.at[(s, *peers.near)], self.r2.at[s], 2, peers.first)
            else:
                for k, device in enumerate(peers.along):
                    go(self.a.at[s, y, x, peers.far[k]], self.r3.at[s, k], 3 + k, device)

        def step(self, stage):
            s = self.slot
            if stage == 0:
                self.local().start()
            elif stage <= 4:
                self.send(stage - 1, lambda d: d.wait_recv())
            else:
                self.spread.arrive(stage - 5)
            if stage == 1:
                self.local().wait()

                @pl.loop(0, 4 * zcount)
                def _(q):
                    i = (s, q // (2 * zcount), (q // zcount) % 2, q % zcount)
                    add(self.a, i, self.r0, i)

            elif stage == 2:

                @pl.loop(0, 2 * zcount)
                def _(q):
                    h = q // zcount
                    i = (s, y * (1 - c) + h * c, h * (1 - c) + x * c, q % zcount)
                    add(self.a, i, self.r1, (s, h, q % zcount))

            elif stage == 3:

                @pl.loop(0, zcount)
                def _(q):
                    add(self.a, (s, y, x, q), self.r2, (s, q))

            elif stage == 4:
                total = self.a[s, y, x, z].astype(F32)
                for k in range(zcount - 1):
                    total = total + self.r3[s, k].astype(F32)
                if self.kind == 0:
                    self.target[self.span] = total
                else:
                    self.target[y, x, c, z] = total.astype(self.target.dtype)
            if stage < 4:
                self.send(stage, lambda d: d.start())
            elif stage < 8 and self.kind > 0:
                self.spread.start(stage - 4)

        def drain(self):
            for stage in range(4):
                self.send(stage, lambda d: d.wait_send())
            if self.spread is not None:
                self.spread.drain()

    pieces = [Piece(i, *chunk) for i, chunk in enumerate(chunks)]
    for i, stage in waves(len(pieces), lags):
        if stage <= 4 or pieces[i].kind > 0:
            pieces[i].step(stage)
    for piece in pieces:
        piece.drain()


def scatter_call(mains, gate_grads, sums, zcount):
    grid = (2, 2, 2, zcount)
    rows = 48
    nmain = len(mains)
    chunks = [
        (2, 0, nmain + 1, 0, sums.shape[1], None, 0),
        (1, 0, nmain, 0, gate_grads.shape[1], None, 0),
    ]
    outs = []
    ins = []
    for which, (array, number) in enumerate(mains):
        share, depth = array.shape[1] // number, array.shape[2]
        ins.append(array.reshape(grid + array.shape[1:]))
        for part in range(number):
            for start in range(0, share, rows):
                chunks.append(
                    (0, len(chunks) - 2, which, part * share + start, rows, len(outs), start)
                )
            outs.append(shape_of((share, depth), F32))
    chunks[0] = chunks[0][:5] + (len(outs) + 1, 0)
    chunks[1] = chunks[1][:5] + (len(outs), 0)
    for array in (gate_grads, sums):
        ins.append(array.reshape(grid + array.shape[1:]))
        outs.append(shape_of(ins[-1].shape, array.dtype))

    def five(number, shape, dtype):
        lead = [(2, 2, zcount), (2, 2, zcount), (2, zcount), (zcount,), (zcount - 1,)]
        return [pltpu.VMEM((number, *d, *shape), dtype) for d in lead]

    n = len(chunks)
    links = pltpu.SemaphoreType.DMA((n, zcount + 2))
    return pl.pallas_call(
        functools.partial(
            scatter_kernel, zcount, chunks, (2, 2, 2, 2, 1, 1, 1, 1), len(ins), len(outs)
        ),
        out_shape=outs,
        in_specs=[pl.BlockSpec(memory_space=pl.ANY)] * len(ins),
        out_specs=[pl.BlockSpec(memory_space=pltpu.VMEM)] * len(outs),
        scratch_shapes=[
            *five(n - 2, (rows, mains[0][0].shape[2]), BF16),
            *five(1, gate_grads.shape[1:], BF16),
            *five(1, sums.shape[1:], F32),
            pltpu.SemaphoreType.DMA((n,)),
            links, links, links, links,
        ],
        compiler_params=pltpu.CompilerParams(
            collective_id=1, has_side_effects=True, vmem_limit_bytes=62 * MIB
        ),
        name="scatter",
    )(*ins)


def to_slots(parts, count):
    rows = parts[0].shape[0]
    depth = parts[0].shape[1]
    got = lax.all_gather(jnp.concatenate(parts, axis=0), ("seq", "row"), axis=0, tiled=False)
    if count != SLOTS:
        got = got.reshape(count, len(parts), rows, depth).transpose(1, 0, 2, 3)
        got = got.reshape(len(parts), SLOTS, rows * count // SLOTS, depth).transpose(1, 0, 2, 3)
    return got.reshape(SLOTS, -1, depth)


def scatter_slots(grads, number, count):
    slots, rows, depth = grads.shape
    if count != SLOTS:
        grads = grads.reshape(slots, number, rows // number, depth).transpose(1, 0, 2, 3)
        grads = grads.reshape(number, count, -1, depth).transpose(1, 0, 2, 3)
    flat_grads = grads.reshape(slots * rows, depth)
    own = lax.psum_scatter(flat_grads, ("seq", "row"), scatter_dimension=0, tiled=True)
    own = own.astype(F32).reshape(number, -1, depth)
    return [own[i] for i in range(number)]


def entering(ends, reverse):
    count = lax.axis_size("seq")
    place = lax.axis_index("seq")
    got = lax.all_gather(ends, "seq")
    state = jnp.zeros_like(ends[0])
    for hop in range(count - 1):
        source = count - 1 - hop if reverse else hop
        ahead = source > place if reverse else source < place
        state = jnp.where(ahead, got[source, 0] * state + got[source, 1], state)
    return jnp.broadcast_to(state[None], (8, state.shape[0]))


def hop(value, axis, steps):
    count = lax.axis_size(axis)
    first, last = (max(0, -steps), min(count, count - steps))
    return lax.ppermute(value, axis, [(source, source + steps) for source in range(first, last)])


def shards(
    long_tokens,
    short_tokens,
    long_length,
    long_cotangent,
    short_cotangent,
    first_gain,
    gate_weight,
    gate_bias,
    input_weight,
    input_bias,
    conv_weight,
    conv_bias,
    decay_gate_weight,
    decay_gate_bias,
    input_gate_weight,
    input_gate_bias,
    decay_param,
    out_weight,
    second_gain,
    mlp_gate_weight,
    mlp_up_weight,
    mlp_down_weight,
):
    count = lax.axis_size("seq") * lax.axis_size("row")
    lrows, srows, depth = long_tokens.shape[1], short_tokens.shape[1], long_tokens.shape[2]
    chans = gate_bias.shape[0]
    units = mlp_gate_weight.shape[1] * count
    tokens = lrows + srows
    total = HALO + tokens
    ltiles, tiles = lrows // TILE, total // TILE
    cshare, ushare = chans // SLOTS, units // SLOTS
    groups = 4
    width = chans // groups
    per = SLOTS // groups

    long_x = long_tokens.reshape(lrows, depth)
    halo_x = hop(long_x[lrows - HALO :], "seq", 1)
    mix_own = [gate_weight.T, input_weight.T, out_weight]
    mlp_own = [mlp_gate_weight.T, mlp_up_weight.T, mlp_down_weight]
    zcount = lax.axis_size("row")
    fast = lax.axis_size("seq") == 8 and count == SLOTS
    if fast:
        own = [jnp.concatenate(mix_own, axis=0), jnp.concatenate(mlp_own, axis=0)]
        mixw, mlpw = [w.reshape(SLOTS, -1, depth) for w in gather_call(own, zcount)]
    else:
        mixw, mlpw = to_slots(mix_own, count), to_slots(mlp_own, count)
    x = jnp.concatenate([halo_x, long_x, short_tokens.reshape(srows, depth)], axis=0)
    place = lax.axis_index("seq")
    first = jnp.where(place > 0, 1.0, 0.0).astype(F32).reshape(1, 1)
    positions = place * lrows + jnp.arange(lrows, dtype=jnp.int32)
    keep = positions[:, None] < long_length[0]
    masked = jnp.where(keep, long_cotangent.reshape(lrows, depth), jnp.zeros((), BF16))
    cot = jnp.concatenate([masked, short_cotangent.reshape(srows, depth)], axis=0)
    chan = jnp.concatenate(
        [
            jnp.stack([gate_bias, input_bias]),
            conv_weight,
            jnp.stack(
                [
                    conv_bias,
                    decay_gate_bias,
                    input_gate_bias,
                    8.0 * jax.nn.softplus(decay_param),
                    8.0 * jax.nn.sigmoid(decay_param),
                ]
            ),
            jnp.zeros((5, chans), F32),
        ],
        axis=0,
    )
    pair_d = pair_blocks(decay_gate_weight)
    pair_o = pair_blocks(input_gate_weight)
    gain1 = first_gain[None]
    gain2 = second_gain[None]
    scalar = pl.BlockSpec(memory_space=pltpu.SMEM)

    def mix_part(which):
        return pl.BlockSpec((per, cshare, depth), lambda g: (g, which, 0))

    pair_spec = pl.BlockSpec((1, width, width), lambda g: (g, 0, 0))
    col = columns(total, width)
    col_long = columns(HALO + lrows, width)
    pc_spec = columns(16, width)
    col8 = columns(8, width)

    wide = shape_of((total, chans), F32)
    narrow = shape_of((HALO + lrows, chans), F32)
    gp, inner, dp, ip, states, reach, mix_s, ends, normed = pl.pallas_call(
        functools.partial(front_kernel, ltiles, tiles),
        grid=(groups,),
        in_specs=[
            scalar, whole((total, depth)), whole((1, depth)), mix_part(0), mix_part(1),
            pair_spec, pair_spec, pc_spec,
        ],
        out_specs=[
            col, col, col, col, col, col_long, columns(srows, width), col8,
            kept((total, depth)),
        ],
        out_shape=[
            wide, wide, wide, wide, wide, narrow, shape_of((srows, chans), BF16),
            shape_of((8, chans), F32), shape_of((total, depth), BF16),
        ],
        scratch_shapes=[pltpu.VMEM((total, width), F32), pltpu.VMEM((total, width), BF16)],
        compiler_params=params(48),
        name="front",
    )(first, x, gain1, mixw, mixw, pair_d, pair_o, chan)

    s_in = entering(ends[0:2], False)

    steps = 4
    hid = units // steps
    slots = SLOTS // steps
    share = 3 * ushare
    out, d_res, rlow, mix_l, gain2_grad, dmlp = pl.pallas_call(
        functools.partial(mlp_kernel, ltiles, tokens // TILE),
        grid=(steps,),
        in_specs=[
            whole((total, depth)), whole((tokens, depth)), whole((HALO + lrows, chans)),
            whole((HALO + lrows, chans)), whole((HALO + lrows, chans)), whole((8, chans)),
            whole((srows, chans)),
            pl.BlockSpec((SLOTS, cshare, depth), lambda g: (0, 2, 0), pipeline_mode=pl.Buffered(1)),
            whole((1, depth)),
            pl.BlockSpec((slots, share, depth), lambda g: (g, 0, 0)),
        ],
        out_specs=[
            whole((tokens, depth)), whole((tokens, depth)), whole((tokens, depth)),
            whole((lrows, chans)), whole((8, depth)),
            pl.BlockSpec((slots, share, depth), lambda g: (g, 0, 0)),
        ],
        out_shape=[
            shape_of((tokens, depth), BF16), shape_of((tokens, depth), F32),
            shape_of((tokens, depth), BF16), shape_of((lrows, chans), BF16),
            shape_of((8, depth), F32), shape_of((SLOTS, share, depth), BF16),
        ],
        scratch_shapes=[
            pltpu.VMEM((tokens, depth), BF16), pltpu.VMEM((tokens, depth), F32),
            pltpu.VMEM((tokens, depth), F32), pltpu.VMEM((tokens, hid), F32),
            pltpu.VMEM((tokens, hid), F32), pltpu.VMEM((tokens, hid), F32),
            pltpu.VMEM((tokens, hid), BF16), pltpu.VMEM((tokens, hid), BF16),
            pltpu.VMEM((tokens, hid), BF16),
        ],
        compiler_params=params(60),
        name="mlp",
    )(x, cot, states, reach, gp, s_in, mix_s, mixw, gain2, mlpw)

    slot_spec = pl.BlockSpec((per, cshare, depth), lambda g: (g, 0, 0))
    slot_shape = shape_of((SLOTS, cshare, depth), BF16)
    d_out, gate_low, total_grad, back_reach, back_ends, gate_bias_part = pl.pallas_call(
        functools.partial(back_kernel, ltiles, tiles),
        grid=(groups,),
        in_specs=[
            whole((tokens, depth)), mix_part(2), columns(lrows, width), columns(srows, width),
            col, col, col_long, col8, col, pc_spec,
        ],
        out_specs=[slot_spec, col, col, col_long, col8, col8],
        out_shape=[
            slot_shape, shape_of((total, chans), BF16), wide, narrow,
            shape_of((8, chans), F32), shape_of((8, chans), F32),
        ],
        scratch_shapes=[pltpu.VMEM((tokens, width), F32)],
        compiler_params=params(48),
        name="back",
    )(rlow, mixw, mix_l, mix_s, gp, states, reach, s_in, dp, chan)

    c_in = entering(back_ends[0:2], True)

    blocks, bwidth = decay_gate_weight.shape[0:2]
    d_x, d_halo, gain1_grad, d_gate, d_input, d_gates, small = pl.pallas_call(
        functools.partial(last_kernel, ltiles, tiles),
        grid=(groups,),
        in_specs=[
            scalar, whole((total, depth)), whole((1, depth)), whole((total, depth)),
            whole((tokens, depth)), mix_part(0), mix_part(1), pair_spec, pair_spec, pc_spec,
            col, col, col, col, col_long, col8, col, col_long, col8, col, col8,
        ],
        out_specs=[
            whole((tokens, depth)), whole((HALO, depth)), whole((8, depth)), slot_spec, slot_spec,
            pl.BlockSpec((2, 2, bwidth, bwidth), lambda g: (0, g, 0, 0)), pc_spec,
        ],
        out_shape=[
            shape_of((tokens, depth), F32), shape_of((HALO, depth), F32), shape_of((8, depth), F32),
            slot_shape, slot_shape, shape_of((2, blocks, bwidth, bwidth), BF16),
            shape_of((16, chans), F32),
        ],
        scratch_shapes=[
            pltpu.VMEM((total, depth), F32), pltpu.VMEM((total, width), F32),
            pltpu.VMEM((total, width), BF16), pltpu.VMEM((total, width), BF16),
            pltpu.VMEM((total, width), BF16), pltpu.VMEM((total, width), BF16),
        ],
        compiler_params=params(60),
        name="last",
    )(
        first, x, gain1, normed, d_res, mixw, mixw, pair_d, pair_o, chan,
        inner, dp, ip, states, reach, s_in, total_grad, back_reach, c_in, gate_low,
        gate_bias_part,
    )

    late = hop(d_halo, "seq", -1)
    long_grad = d_x[:lrows].at[lrows - HALO :].add(late)
    short_grad = d_x[lrows:]

    lanes = 2048
    gains = jnp.stack([jnp.sum(gain1_grad, axis=0), jnp.sum(gain2_grad, axis=0)])
    small = jnp.concatenate(
        [
            jnp.pad(small[0:10], ((0, 0), (0, lanes - chans))),
            jnp.pad(gains, ((0, 0), (0, lanes - depth))),
            jnp.zeros((4, lanes), F32),
        ],
        axis=0,
    )
    if fast:
        mains = [(dmlp, 3), (d_gate, 1), (d_input, 1), (d_out, 1)]
        tiled = small.reshape(2, 8, lanes // 128, 128).transpose(0, 2, 1, 3)
        *shares, gate_sums, sums = scatter_call(
            mains, d_gates.reshape(SLOTS, -1, bwidth), tiled.reshape(SLOTS, 8, 128), zcount
        )
        g_mgate, g_mup, g_down, g_gate, g_input, g_out = shares
        gate_sums = gate_sums.reshape(d_gates.shape)
        sums = sums.reshape(2, lanes // 128, 8, 128).transpose(0, 2, 1, 3).reshape(16, lanes)
    else:
        g_mgate, g_mup, g_down = scatter_slots(dmlp, 3, count)
        dmix = jnp.concatenate([d_gate, d_input, d_out], axis=1)
        g_gate, g_input, g_out = scatter_slots(dmix, 3, count)
        gate_sums, sums = lax.psum((d_gates.astype(F32), small), ("seq", "row"))
    gate_sums = gate_sums.astype(F32)
    rows = sums[0:10, :chans]
    return (
        out[:lrows].reshape(long_tokens.shape),
        out[lrows:].reshape(short_tokens.shape),
        long_grad.reshape(long_tokens.shape),
        short_grad.reshape(short_tokens.shape),
        sums[10, :depth],
        g_gate.T,
        rows[9],
        g_input.T,
        rows[0],
        rows[1:5],
        rows[5],
        gate_sums[0],
        rows[6],
        gate_sums[1],
        rows[7],
        rows[8],
        g_out,
        sums[11, :depth],
        g_mgate.T,
        g_mup.T,
        g_down,
    )


def solution(mesh):
    both = ("seq", "row")
    long_spec = P("row", "seq", None)
    short_spec = P(both, None, None)
    cols = P(None, both)
    rows = P(both, None)
    return jax.shard_map(
        shards,
        mesh=mesh,
        in_specs=(
            long_spec, short_spec, P("row"), long_spec, short_spec, P(), cols, P(), cols, P(),
            P(), P(), P(), P(), P(), P(), P(), rows, P(), cols, cols, rows,
        ),
        out_specs=(
            long_spec, short_spec, long_spec, short_spec, P(), cols, P(), cols, P(), P(), P(),
            P(), P(), P(), P(), P(), rows, P(), cols, cols, rows,
        ),
        check_vma=False,
    )
```

```python
import functools

import jax
import jax.numpy as jnp
from jax import lax
from jax.experimental import pallas as pl
from jax.experimental.pallas import tpu as pltpu
from jax.sharding import PartitionSpec as P

EPSILON = 1e-06
F32 = jnp.float32
BF16 = jnp.bfloat16
GRID = (2, 2, 2, 4)
SLOTS = 32
TILE = 16
HALO = 16
MIB = 1024 * 1024
GELU_A = 0.7978845608028654
GELU_B = 0.044715


def dot_nn(a, b):
    return lax.dot_general(a, b, (((1,), (0,)), ((), ())), preferred_element_type=F32)


def dot_nt(a, b):
    return lax.dot_general(a, b, (((1,), (1,)), ((), ())), preferred_element_type=F32)


def dot_tn(a, b):
    return lax.dot_general(a, b, (((0,), (0,)), ((), ())), preferred_element_type=F32)


def sigmoid(v):
    return 0.5 * jnp.tanh(0.5 * v) + 0.5


def gelu(v):
    t = jnp.tanh(v * (GELU_A + (GELU_A * GELU_B) * (v * v)))
    h = 0.5 * v
    return h + h * t


def gelu_pair(v):
    w = v * v
    t = jnp.tanh(v * (GELU_A + (GELU_A * GELU_B) * w))
    h = 0.5 * v
    slope = 0.5 + 0.5 * t + (h - h * (t * t)) * (GELU_A + (3.0 * GELU_A * GELU_B) * w)
    return h + h * t, slope


def row_iota(shape):
    return lax.broadcasted_iota(jnp.int32, shape, 0)


def at(j):
    return pl.ds(pl.multiple_of(j * TILE, TILE), TILE)


def scan_tile(a, b, reverse):
    rows = row_iota(a.shape)
    step = 1
    while step < TILE:
        if reverse:
            keep, shift = rows < TILE - step, TILE - step
        else:
            keep, shift = rows >= step, step
        b = jnp.where(keep, a * pltpu.roll(b, shift, 0) + b, b)
        a = jnp.where(keep, a * pltpu.roll(a, shift, 0), a)
        step *= 2
    return a, b


def shift_down(cur, prev, k):
    if k == 0:
        return cur
    rows = row_iota(cur.shape)
    return jnp.where(rows < k, pltpu.roll(prev, k, 0), pltpu.roll(cur, k, 0))


def shift_up(cur, later, k):
    if k == 0:
        return cur
    rows = row_iota(cur.shape)
    return jnp.where(
        rows >= TILE - k, pltpu.roll(later, TILE - k, 0), pltpu.roll(cur, TILE - k, 0)
    )


def fold(v):
    return v[0:8] + v[8:16]


def flat(block):
    return block.reshape(-1, block.shape[-1])


def gates(dp, ip, c8):
    rate = sigmoid(dp)
    opening = sigmoid(ip)
    log_decay = -c8 * (0.25 + rate)
    decay = jnp.exp(log_decay)
    square = -jnp.tanh(log_decay) * (1.0 + decay * decay)
    return rate, opening, decay, square


GB, IB, CW, CB, DB, OB, C8, S8 = 0, 1, 2, 6, 7, 8, 9, 10


def conv_tile(in_ref, pc_ref, j, live):
    cur = in_ref[at(j), :]
    prev = in_ref[at(j - 1), :] * live
    out = pc_ref[CB : CB + 1, :] + pc_ref[CW : CW + 1, :] * cur
    moved = [cur]
    for k in range(1, 4):
        m = shift_down(cur, prev, k)
        moved.append(m)
        out = out + pc_ref[CW + k : CW + k + 1, :] * m
    return out, moved


def place_of():
    s = lax.axis_index("seq")
    return s // 4, (s // 2) % 2, s % 2, lax.axis_index("row")


def device_at(y, x, c, z):
    return ((y * 2 + x) * 2 + c, z)


class Peers:
    def __init__(self, zcount):
        y, x, c, z = self.place = place_of()
        self.far = [(z + k) % zcount for k in range(1, zcount)]
        self.along = [device_at(y, x, c, q) for q in self.far]
        self.near = ((y + c) % 2, (x + 1 - c) % 2)
        self.first = device_at(*self.near, c, z)
        self.second = device_at((y + 1 - c) % 2, (x + c) % 2, c, z)
        self.other = device_at(y, x, 1 - c, z)

    def meet(self):
        everyone = [*self.along, self.first, self.second, self.other]
        barrier = pltpu.get_barrier_semaphore()
        for peer in everyone:
            pl.semaphore_signal(
                barrier, inc=1, device_id=peer, device_id_type=pl.DeviceIdType.MESH
            )
        pl.semaphore_wait(barrier, len(everyone))


def remote(source, target, send, recv, device):
    return pltpu.make_async_remote_copy(
        src_ref=source,
        dst_ref=target,
        send_sem=send,
        recv_sem=recv,
        device_id=device,
        device_id_type=pl.DeviceIdType.MESH,
    )


class Spread:
    def __init__(self, peers, own, full, send, recv):
        self.peers, self.own, self.full, self.send, self.recv = peers, own, full, send, recv

    def go(self, stage, act):
        y, x, c, z = self.peers.place
        p, full = self.peers, self.full
        if stage == 0:
            for k, device in enumerate(p.along):
                act(remote(self.own, full(y, x, c, z), self.send(k), self.recv(k), device))
            return
        k = len(p.along) + stage - 1
        if stage == 2:

            @pl.when(c == 0)
            def _():
                part = full(y, slice(None), c, slice(None))
                act(remote(part, part, self.send(k), self.recv(k), p.second))

            @pl.when(c == 1)
            def _():
                part = full(slice(None), x, c, slice(None))
                act(remote(part, part, self.send(k), self.recv(k), p.second))

            return
        if stage == 1:
            part, device = full(y, x, c, slice(None)), p.first
        else:
            part, device = full(slice(None), slice(None), c, slice(None)), p.other
        act(remote(part, part, self.send(k), self.recv(k), device))

    def start(self, stage):
        self.go(stage, lambda d: d.start())

    def arrive(self, stage):
        self.go(stage, lambda d: d.wait_recv())

    def drain(self):
        for stage in range(4):
            self.go(stage, lambda d: d.wait_send())


def wave_of(t, count, lags):
    for stage in range(len(lags), -1, -1):
        piece = t - sum(lags[:stage])
        if 0 <= piece < count:
            yield piece, stage


class Gather:
    def __init__(self, zcount, ins, outs, sems, chunks, lags):
        self.csem, self.ssem, self.rsem = sems
        self.peers = Peers(zcount)
        self.lags = lags
        y, x, c, z = self.peers.place
        self.spreads, self.copies = [], []
        for i, (which, start, size) in enumerate(chunks):
            rows = pl.ds(start, size)
            own = ins[which].at[rows]

            def full(a, b, d, e, ref=outs[which], rows=rows):
                return ref.at[a, b, d, e, rows]

            def send(k, i=i):
                return self.ssem.at[i, k]

            def recv(k, i=i):
                return self.rsem.at[i, k]

            self.spreads.append(Spread(self.peers, own, full, send, recv))
            self.copies.append(pltpu.make_async_copy(own, full(y, x, c, z), self.csem.at[i]))
        self.waves = len(chunks) + sum(lags) + 1

    def wave(self, t):
        for i, stage in wave_of(t, len(self.spreads), self.lags):
            if stage == 0:
                self.copies[i].start()
            elif stage == 1:
                self.copies[i].wait()
            if stage > 0:
                self.spreads[i].arrive(stage - 1)
            if stage < 4:
                self.spreads[i].start(stage)

    def drain(self):
        for spread in self.spreads:
            spread.drain()


def in_turn(weave, step, plan):
    def point(k):
        for s, points in enumerate(plan):
            if k < len(points) and points[k]:

                @pl.when(step == s)
                def _(todo=points[k]):
                    for t in todo:
                        weave.wave(t)

    return point


def spread_out(waves, ahead, steps, points):
    todo = list(range(waves))
    plan = []
    for s in range(steps):
        row = []
        for k in range(points):
            take = ahead if s == 0 and k == 0 else 1
            if s == steps - 1 and k == points - 1:
                take = len(todo)
            row.append(todo[:take])
            todo = todo[take:]
        plan.append(row)
    return plan


def row_chunks(parts, size):
    return [
        (which, start, size)
        for which, part in enumerate(parts)
        for start in range(0, part.shape[0], size)
    ]


def gather_sems(count, zcount):
    links = pltpu.SemaphoreType.DMA((count, zcount + 2))
    return [pltpu.SemaphoreType.DMA((count,)), links, links]


def gathered(part, zcount):
    return jax.ShapeDtypeStruct((2, 2, 2, zcount) + part.shape, part.dtype)


def gather_kernel(zcount, chunks, lags, number, *refs):
    gather = Gather(zcount, refs[:number], refs[number : 2 * number], refs[2 * number :], chunks, lags)
    gather.peers.meet()
    for t in range(gather.waves):
        gather.wave(t)
    gather.drain()


def gather_call(parts, zcount):
    chunks = row_chunks(parts, 16)
    hbm = pl.BlockSpec(memory_space=pl.ANY)
    return pl.pallas_call(
        functools.partial(gather_kernel, zcount, chunks, (2, 2, 3, 2), len(parts)),
        out_shape=[gathered(p, zcount) for p in parts],
        in_specs=[hbm] * len(parts),
        out_specs=[hbm] * len(parts),
        scratch_shapes=gather_sems(len(chunks), zcount),
        compiler_params=pltpu.CompilerParams(collective_id=0, has_side_effects=True),
        name="gather",
    )(*parts)


CORE, GATES, SUMS, HALVED = 0, 1, 2, 3


class Scatter:
    def __init__(self, zcount, ins, outs, buffers, sems, chunks, lags):
        self.peers = Peers(zcount)
        self.zcount, self.chunks, self.lags = zcount, chunks, lags
        self.ins, self.outs, self.buffers = ins, outs, buffers
        self.csem, self.ssem, self.rsem = sems[:3]
        self.pieces = [Piece(self, i, sems[3:], *chunk) for i, chunk in enumerate(chunks)]
        self.waves = len(chunks) + sum(lags) + 1

    def wave(self, t):
        for i, stage in wave_of(t, len(self.pieces), self.lags):
            if stage <= 4 or self.pieces[i].spread is not None:
                self.pieces[i].step(stage)

    def drain(self):
        for piece in self.pieces:
            piece.drain()


def add_into(into, i, part, j):
    into[i] = (into[i].astype(F32) + part[j].astype(F32)).astype(into.dtype)


class Piece:
    def __init__(self, owner, i, sems, kind, slot, which, source, span, target, place):
        self.o, self.i, self.kind, self.slot = owner, i, kind, slot
        self.a, self.r0, self.r1, self.r2, self.r3 = owner.buffers[kind]
        self.source, self.lead, self.rows = owner.ins[which], source, pl.ds(*span)
        self.target, self.place = owner.outs[target], place
        self.spread = None
        if kind in (GATES, SUMS):
            y, x, c, z = owner.peers.place

            def full(*at_place):
                return self.target.at[at_place]

            def send(k):
                return sems[0].at[i, k]

            def recv(k):
                return sems[1].at[i, k]

            self.spread = Spread(owner.peers, full(y, x, c, z), full, send, recv)

    def local(self):
        c = self.o.peers.place[2]
        if self.kind == HALVED:
            mine = self.source.at[self.lead, :, :, :, self.rows]
        else:
            mine = self.source.at[:, :, c, :, self.rows]
        return pltpu.make_async_copy(mine, self.a.at[self.slot], self.o.csem.at[self.i])

    def send(self, stage, act):
        s, peers = self.slot, self.o.peers
        y, x, c, z = peers.place

        def go(source, target, k, device):
            act(remote(source, target, self.o.ssem.at[self.i, k], self.o.rsem.at[self.i, k], device))

        if stage == 0:
            if self.kind != HALVED:
                theirs = self.source.at[:, :, 1 - c, :, self.rows]
                go(theirs, self.r0.at[s], 0, peers.other)
        elif stage == 1:

            @pl.when(c == 0)
            def _():
                go(self.a.at[s, 1 - y], self.r1.at[s], 1, peers.second)

            @pl.when(c == 1)
            def _():
                go(self.a.at[s, :, 1 - x], self.r1.at[s], 1, peers.second)

        elif stage == 2:
            go(self.a.at[(s, *peers.near)], self.r2.at[s], 2, peers.first)
        else:
            for k, device in enumerate(peers.along):
                go(self.a.at[s, y, x, peers.far[k]], self.r3.at[s, k], 3 + k, device)

    def step(self, stage):
        s, zcount = self.slot, self.o.zcount
        y, x, c, z = self.o.peers.place
        if stage == 0:
            self.local().start()
        elif stage <= 4:
            self.send(stage - 1, lambda d: d.wait_recv())
        else:
            self.spread.arrive(stage - 5)
        if stage == 1:
            self.local().wait()
            if self.kind != HALVED:

                @pl.loop(0, 4 * zcount)
                def _(q):
                    i = (s, q // (2 * zcount), (q // zcount) % 2, q % zcount)
                    add_into(self.a, i, self.r0, i)

        elif stage == 2:

            @pl.loop(0, 2 * zcount)
            def _(q):
                h = q // zcount
                i = (s, y * (1 - c) + h * c, h * (1 - c) + x * c, q % zcount)
                add_into(self.a, i, self.r1, (s, h, q % zcount))

        elif stage == 3:

            @pl.loop(0, zcount)
            def _(q):
                add_into(self.a, (s, y, x, q), self.r2, (s, q))

        elif stage == 4:
            total = self.a[s, y, x, z].astype(F32)
            for k in range(zcount - 1):
                total = total + self.r3[s, k].astype(F32)
            if self.spread is None:
                self.target[self.place : self.place + total.shape[0]] = total
            else:
                self.target[y, x, c, z] = total.astype(self.target.dtype)
        if stage < 4:
            self.send(stage, lambda d: d.start())
        elif stage < 8 and self.spread is not None:
            self.spread.start(stage - 4)

    def drain(self):
        for stage in range(4):
            self.send(stage, lambda d: d.wait_send())
        if self.spread is not None:
            self.spread.drain()


def five(number, shape, dtype, zcount):
    lead = [(2, 2, zcount), (2, 2, zcount), (2, zcount), (zcount,), (zcount - 1,)]
    return [pltpu.VMEM((number, *d, *shape), dtype) for d in lead]


def scatter_kernel(zcount, chunks, lags, nin, nout, *refs):
    ins, outs, rest = refs[:nin], refs[nin : nin + nout], refs[nin + nout :]
    halved = (rest[15], None, *rest[16:19])
    buffers = [rest[0:5], rest[5:10], rest[10:15], halved]
    scatter = Scatter(zcount, ins, outs, buffers, rest[19:], chunks, lags)
    scatter.peers.meet()
    for t in range(scatter.waves):
        scatter.wave(t)
    scatter.drain()


def scatter_call(halved, mains, gate_grads, sums, zcount):
    grid = (2, 2, 2, zcount)
    rows, depth = mains[0].shape[1:]
    nmain = len(mains)
    ins = [m.reshape(grid + m.shape[1:]) for m in mains]
    ins += [a.reshape(grid + a.shape[1:]) for a in (gate_grads, sums)]
    outs = [shape_of((rows, depth), F32) for _ in mains]
    outs += [shape_of(a.shape, a.dtype) for a in ins[nmain:]]
    chunks = [
        (SUMS, 0, nmain + 1, None, (0, sums.shape[1]), nmain + 1, 0),
        (GATES, 0, nmain, None, (0, gate_grads.shape[1]), nmain, 0),
    ]
    halves = halved.shape[0]
    number = 0
    ins.append(halved)
    for k in range(3):
        outs.append(shape_of((halves * rows, depth), F32))
        for h in range(halves):
            chunks.append(
                (HALVED, number, nmain + 2, h, (k * rows, rows), nmain + 2 + k, h * rows)
            )
            number += 1
    for i in range(nmain):
        chunks.append((CORE, i, i, None, (0, rows), i, 0))
    n = len(chunks)
    links = pltpu.SemaphoreType.DMA((n, zcount + 2))
    lone = five(number, (rows, depth), BF16, zcount)
    return pl.pallas_call(
        functools.partial(
            scatter_kernel, zcount, chunks, (2, 2, 2, 2, 1, 1, 1, 1), len(ins), len(outs)
        ),
        out_shape=outs,
        in_specs=[pl.BlockSpec(memory_space=pl.ANY)] * len(ins),
        out_specs=[pl.BlockSpec(memory_space=pltpu.VMEM)] * len(outs),
        scratch_shapes=[
            *five(nmain, (rows, depth), BF16, zcount),
            *five(1, gate_grads.shape[1:], BF16, zcount),
            *five(1, sums.shape[1:], F32, zcount),
            lone[0], *lone[2:],
            pltpu.SemaphoreType.DMA((n,)),
            links, links, links, links,
        ],
        compiler_params=pltpu.CompilerParams(
            collective_id=1, has_side_effects=True, vmem_limit_bytes=62 * MIB
        ),
        name="scatter",
    )(*ins)


def no_point(k):
    pass


def front_kernel(ltiles, tiles, links, *refs):
    (
        first_ref, x_ref, gain_ref, wg_ref, wi_ref, wd_ref, wo_ref, pc_ref
    ) = refs[:8]
    refs = refs[8:]
    point, gather = no_point, None
    step = pl.program_id(0)
    if links is not None:
        zcount, chunks, lags, plan, number = links
        gather = Gather(
            zcount, refs[:number], refs[number + 9 : 2 * number + 9], refs[2 * number + 11 :], chunks, lags
        )
        refs = refs[number : number + 9] + refs[2 * number + 9 : 2 * number + 11]
        point = in_turn(gather, step, plan)
    gp_ref, in_ref, dp_ref, ip_ref, st_ref, pr_ref, mix_ref, end_ref, nm_ref, cv_ref, cl_ref = refs

    @pl.when(step == 0)
    def _():
        if gather is not None:
            gather.peers.meet()

    point(0)

    @pl.when(step == 0)
    def _():
        @pl.loop(0, tiles)
        def _(j):
            v = x_ref[at(j), :].astype(F32)
            s = lax.rsqrt(jnp.mean(v * v, axis=1, keepdims=True) + EPSILON)
            nm_ref[at(j), :] = (v * s * gain_ref[...]).astype(BF16)

    nm = nm_ref[...]
    gp_ref[...] = dot_nt(nm, flat(wg_ref[...])) + pc_ref[GB : GB + 1, :]
    in_ref[...] = dot_nt(nm, flat(wi_ref[...])) + pc_ref[IB : IB + 1, :]
    point(1)
    in_ref[0:HALO, :] = in_ref[0:HALO, :] * first_ref[0, 0]
    cl_ref[0:HALO, :] = jnp.zeros((HALO, cl_ref.shape[1]), BF16)

    @pl.loop(1, tiles)
    def _(j):
        live = jnp.where(j == 1 + ltiles, 0.0, 1.0)
        out, _ = conv_tile(in_ref, pc_ref, j, live)
        cv_ref[at(j), :] = out
        cl_ref[at(j), :] = out.astype(BF16)

    point(2)
    low = cl_ref[...]
    dp_ref[...] = dot_nn(low, wd_ref[0]) + pc_ref[DB : DB + 1, :]
    ip_ref[...] = dot_nn(low, wo_ref[0]) + pc_ref[OB : OB + 1, :]

    def scanned(j):
        _, opening, a, square = gates(dp_ref[at(j), :], ip_ref[at(j), :], pc_ref[C8 : C8 + 1, :])
        b = (square * lax.rsqrt(square)) * opening * cv_ref[at(j), :]
        return scan_tile(a, b, False)

    width = gp_ref.shape[1]

    def long_step(i, carry):
        state, reach = carry
        a, b = scanned(1 + i)
        s = b + a * state
        r = a * reach
        st_ref[at(1 + i), :] = s
        pr_ref[at(1 + i), :] = r
        return s[TILE - 1 : TILE], r[TILE - 1 : TILE]

    state, reach = lax.fori_loop(
        0, ltiles, long_step, (jnp.zeros((1, width), F32), jnp.ones((1, width), F32))
    )
    end_ref[...] = jnp.concatenate([reach, state, jnp.zeros((6, width), F32)], axis=0)

    def short_step(i, state):
        j = 1 + ltiles + i
        a, b = scanned(j)
        s = b + a * state
        st_ref[at(j), :] = s
        mix_ref[at(i), :] = (s * gelu(gp_ref[at(j), :])).astype(BF16)
        return s[TILE - 1 : TILE]

    lax.fori_loop(0, tiles - 1 - ltiles, short_step, jnp.zeros((1, width), F32))
    point(3)
    if gather is not None:

        @pl.when(step == pl.num_programs(0) - 1)
        def _():
            gather.drain()


def mlp_kernel(ltiles, tiles, links, *refs):
    (
        x_ref, cot_ref, st_ref, pr_ref, gp_ref, sin_ref, mixs_ref, wo_ref, gain_ref, w1_ref, w2_ref
    ) = refs[:11]
    refs = refs[11:]
    point, gather = no_point, None
    step = pl.program_id(0)
    last = pl.num_programs(0) - 1
    out_ref, dres_ref, rlow_ref, mixl_ref, gain_grad_ref, dw_hbm = refs[:6]
    refs = refs[6:]
    if links is not None:
        zcount, chunks, lags, plan = links
        own_ref, w2_ref = w2_ref, refs[0]
        gather = Gather(zcount, [own_ref], [w2_ref], refs[-3:], chunks, lags)
        got_ref, sems, credit = refs[-6], refs[-5], refs[-4]
        refs = refs[1:-6]
        point = in_turn(gather, step, plan)
    (
        n2_ref, acc_o, acc_n, g_ref, u_ref, d_ref, h_ref, dg_ref, du_ref, wbuf, dwbuf, wsem, dsem
    ) = refs
    lrows = ltiles * TILE
    half = g_ref.shape[1] // 2
    share = wbuf.shape[-2] // 3
    steps = 2 * GRID[0]

    def load(s):
        source = w1_ref if s < steps // 2 else w2_ref
        return pltpu.make_async_copy(
            source.at[s % (steps // 2)], wbuf.at[s % 2], wsem.at[s % 2]
        )

    def each(todo, first=0):
        for s in range(first, steps):

            @pl.when(step == s)
            def _(s=s):
                todo(s)

    if gather is not None:
        y, x, c, z = gather.peers.place

    def store(s):
        h, q = s // (steps // 2), s % (steps // 2)
        mine = dwbuf if gather is None else dwbuf.at[:, c]
        return pltpu.make_async_copy(mine, dw_hbm.at[h, q], dsem)

    def swap():
        return remote(
            dwbuf.at[:, 1 - c], got_ref, sems.at[0], sems.at[1], gather.peers.other
        )

    def settle(s):
        if gather is not None:
            swap().wait_recv()

            @pl.loop(0, got_ref.shape[0] * got_ref.shape[1])
            def _(k):
                i, j = k // got_ref.shape[1], k % got_ref.shape[1]
                both = dwbuf[i, c, j].astype(F32) + got_ref[i, j].astype(F32)
                dwbuf[i, c, j] = both.astype(BF16)

            if s < steps - 1:
                pl.semaphore_signal(
                    credit,
                    inc=1,
                    device_id=gather.peers.other,
                    device_id_type=pl.DeviceIdType.MESH,
                )
        store(s).start()

    def clear(s):
        store(s).wait()
        if gather is not None:
            swap().wait_send()

    @pl.when(step == 0)
    def _():
        load(0).start()
        load(1).start()
        if gather is not None:
            gather.peers.meet()

    point(0)

    @pl.when(step == 0)
    def _():
        s_in = sin_ref[0:1, :]

        @pl.loop(0, ltiles)
        def _(i):
            s = st_ref[at(1 + i), :] + pr_ref[at(1 + i), :] * s_in
            mixl_ref[at(i), :] = (s * gelu(gp_ref[at(1 + i), :])).astype(BF16)

        wo = flat(wo_ref[...])
        dres_ref[0:lrows, :] = dot_nn(mixl_ref[...], wo)
        dres_ref[lrows:, :] = dot_nn(mixs_ref[...], wo)

        @pl.loop(0, tiles)
        def _(i):
            r = dres_ref[at(i), :] + x_ref[at(1 + i), :].astype(F32)
            dres_ref[at(i), :] = r
            acc_o[at(i), :] = r
            s = lax.rsqrt(jnp.mean(r * r, axis=1, keepdims=True) + EPSILON)
            n2_ref[at(i), :] = (r * s * gain_ref[...]).astype(BF16)

        acc_n[...] = jnp.zeros_like(acc_n)

    point(1)

    @pl.when(step == steps // 2)
    def _():
        load(steps // 2).start()
        load(steps // 2 + 1).start()

    each(lambda s: load(s).wait())
    slot = lax.rem(step, 2)
    n2 = n2_ref[...]
    wg = flat(wbuf[slot, ..., 0:share, :])
    wu = flat(wbuf[slot, ..., share : 2 * share, :])
    wd = flat(wbuf[slot, ..., 2 * share :, :])
    g_ref[...] = dot_nt(n2, wg)
    u_ref[...] = dot_nt(n2, wu)
    point(2)
    d_ref[...] = dot_nt(cot_ref[...], wd)
    each(lambda s: settle(s - 1), 1)
    point(3)

    @pl.loop(0, tiles)
    def _(i):
        for k in range(2):
            cols = slice(k * half, (k + 1) * half)
            ge, slope = gelu_pair(g_ref[at(i), cols])
            u = u_ref[at(i), cols]
            d = d_ref[at(i), cols]
            h_ref[at(i), cols] = (ge * u).astype(BF16)
            dg_ref[at(i), cols] = (d * u * slope).astype(BF16)
            du_ref[at(i), cols] = (d * ge).astype(BF16)

    point(4)
    acc_o[...] += dot_nn(h_ref[...], wd)
    acc_n[...] += dot_nn(dg_ref[...], wg) + dot_nn(du_ref[...], wu)
    point(5)
    each(lambda s: clear(s - 1), 1)
    lead = dwbuf.shape[:-2]
    rest = (share, dwbuf.shape[-1])
    for k, (left, right) in enumerate(((dg_ref, n2_ref), (du_ref, n2_ref), (h_ref, cot_ref))):
        grad = dot_tn(left[...], right[...]).astype(BF16)
        dwbuf[..., k * share : (k + 1) * share, :] = grad.reshape(lead + rest)
        if k < 2:
            point(6 + k)

    if gather is not None:
        @pl.when(step > 0)
        def _():
            pl.semaphore_wait(credit, 1)

        swap().start()

    @pl.when(step == last)
    def _():
        def one(i, total):
            r = dres_ref[at(i), :]
            out_ref[at(i), :] = acc_o[at(i), :].astype(BF16)
            dn = acc_n[at(i), :]
            s = lax.rsqrt(jnp.mean(r * r, axis=1, keepdims=True) + EPSILON)
            e = dn * gain_ref[...]
            inner = jnp.mean(e * r, axis=1, keepdims=True)
            dr = cot_ref[at(i), :].astype(F32) + s * e - r * (s * s * s * inner)
            dres_ref[at(i), :] = dr
            rlow_ref[at(i), :] = dr.astype(BF16)
            return total + fold(dn * (r * s))

        gain_grad_ref[...] = lax.fori_loop(0, tiles, one, jnp.zeros(gain_grad_ref.shape, F32))
        settle(steps - 1)
        clear(steps - 1)
        if gather is not None:
            gather.drain()


def back_kernel(
    ltiles, tiles, rlow_ref, wo_ref, mixl_ref, mixs_ref, gp_ref, st_ref, pr_ref, sin_ref, dp_ref,
    pc_ref, dwo_ref, gl_ref, tot_ref, rch_ref, end_ref, bias_ref, dm_ref,
):
    lrows = ltiles * TILE
    width = gp_ref.shape[1]
    rlow = rlow_ref[...]
    dm_ref[...] = dot_nt(rlow, flat(wo_ref[...]))
    grad = dot_tn(mixl_ref[...], rlow_ref[0:lrows, :]) + dot_tn(mixs_ref[...], rlow_ref[lrows:, :])
    dwo_ref[...] = grad.astype(BF16).reshape(dwo_ref.shape)
    gl_ref[0:HALO, :] = jnp.zeros((HALO, width), BF16)
    last = row_iota((TILE, width)) == TILE - 1

    def local(j, states):
        dm = dm_ref[at(j - 1), :]
        ge, slope = gelu_pair(gp_ref[at(j), :])
        dgate = dm * states * slope
        gl_ref[at(j), :] = dgate.astype(BF16)
        ds = dm * ge
        rate = sigmoid(dp_ref[at(j), :])
        decay = jnp.exp(-pc_ref[C8 : C8 + 1, :] * (0.25 + rate))
        a, b = scan_tile(decay, decay * ds, True)
        return a, b, ds, fold(dgate)

    def short_step(i, carry):
        c, bias = carry
        j = tiles - 1 - i
        a, b, ds, part = local(j, st_ref[at(j), :])
        cs = b + a * c
        tot_ref[at(j), :] = ds + jnp.where(last, c, pltpu.roll(cs, TILE - 1, 0))
        return cs[0:1], bias + part

    _, bias = lax.fori_loop(
        0,
        tiles - 1 - ltiles,
        short_step,
        (jnp.zeros((1, width), F32), jnp.zeros((8, width), F32)),
    )
    s_in = sin_ref[0:1, :]

    def long_step(i, carry):
        c, reach, bias = carry
        j = ltiles - i
        a, b, ds, part = local(j, st_ref[at(j), :] + pr_ref[at(j), :] * s_in)
        cs = b + a * c
        rs = a * reach
        tot_ref[at(j), :] = ds + jnp.where(last, c, pltpu.roll(cs, TILE - 1, 0))
        rch_ref[at(j), :] = jnp.where(last, reach, pltpu.roll(rs, TILE - 1, 0))
        return cs[0:1], rs[0:1], bias + part

    c, reach, bias = lax.fori_loop(
        0, ltiles, long_step, (jnp.zeros((1, width), F32), jnp.ones((1, width), F32), bias)
    )
    end_ref[...] = jnp.concatenate([reach, c, jnp.zeros((6, width), F32)], axis=0)
    bias_ref[...] = bias


def last_kernel(
    ltiles, tiles, first_ref, x_ref, gain_ref, nm_ref, dres_ref, wg_ref, wi_ref, wd_ref, wo_ref,
    pc_ref, in_ref, dp_ref, ip_ref, st_ref, pr_ref, sin_ref, tot_ref, rch_ref, cin_ref, gl_ref,
    bias_ref, dx_ref, halo_ref, gain_grad_ref, dwg_ref, dwi_ref, gg_ref, small_ref,
    acc, dc_ref, cl_ref, dl_ref, ol_ref, il_ref,
):
    width = in_ref.shape[1]
    step = pl.program_id(0)
    zero8 = jnp.zeros((8, width), F32)
    cl_ref[0:HALO, :] = jnp.zeros((HALO, width), BF16)
    dl_ref[0:HALO, :] = jnp.zeros((HALO, width), BF16)
    ol_ref[0:HALO, :] = jnp.zeros((HALO, width), BF16)
    dc_ref[0:HALO, :] = jnp.zeros((HALO, width), F32)

    def gate_step(j, states, total, live, carry):
        before, sum_d, sum_o, sum_p = carry
        rows = row_iota((TILE, width))
        prior = jnp.where(rows == 0, before, pltpu.roll(states, 1, 0))
        conv, _ = conv_tile(in_ref, pc_ref, j, live)
        rate, opening, decay, square = gates(
            dp_ref[at(j), :], ip_ref[at(j), :], pc_ref[C8 : C8 + 1, :]
        )
        inv = lax.rsqrt(square)
        mult = square * inv
        weighted = total * opening
        d_open = total * mult * conv
        d_log = decay * (total * prior - (weighted * conv) * (decay * inv))
        d_rate = -pc_ref[C8 : C8 + 1, :] * d_log
        d_dp = d_rate * (rate - rate * rate)
        d_ip = d_open * (opening - opening * opening)
        cl_ref[at(j), :] = conv.astype(BF16)
        dl_ref[at(j), :] = d_dp.astype(BF16)
        ol_ref[at(j), :] = d_ip.astype(BF16)
        dc_ref[at(j), :] = weighted * mult
        return (
            states[TILE - 1 : TILE],
            sum_d + fold(d_dp),
            sum_o + fold(d_ip),
            sum_p - fold((0.25 + rate) * d_log),
        )

    s_in = sin_ref[0:1, :]
    c_in = cin_ref[0:1, :]

    def long_step(i, carry):
        j = 1 + i
        states = st_ref[at(j), :] + pr_ref[at(j), :] * s_in
        total = tot_ref[at(j), :] + rch_ref[at(j), :] * c_in
        return gate_step(j, states, total, 1.0, carry)

    def short_step(i, carry):
        j = 1 + ltiles + i
        return gate_step(j, st_ref[at(j), :], tot_ref[at(j), :], jnp.where(i == 0, 0.0, 1.0), carry)

    carry = lax.fori_loop(0, ltiles, long_step, (s_in, zero8, zero8, zero8))
    carry = lax.fori_loop(
        0, tiles - 1 - ltiles, short_step, (jnp.zeros((1, width), F32),) + carry[1:]
    )
    _, sum_d, sum_o, sum_p = carry

    low, dlow, olow = cl_ref[...], dl_ref[...], ol_ref[...]
    half = width // 2
    for which, grads in ((0, dlow), (1, olow)):
        product = dot_tn(low, grads).astype(BF16)
        gg_ref[which, 0] = product[:half, :half]
        gg_ref[which, 1] = product[half:, half:]
    dc_ref[...] += dot_nt(dlow, wd_ref[0]) + dot_nt(olow, wo_ref[0])

    def conv_step(j, carry):
        sum_c, sum_i, sums = carry
        live = jnp.where(j == 1 + ltiles, 0.0, 1.0)
        cur = dc_ref[at(j), :]
        up = jnp.where((j == ltiles) | (j == tiles - 1), 0.0, 1.0)
        later = dc_ref[at(jnp.minimum(j + 1, tiles - 1)), :] * up
        _, moved = conv_tile(in_ref, pc_ref, jnp.maximum(j, 1), live)
        d_in = pc_ref[CW : CW + 1, :] * cur
        for k in range(1, 4):
            d_in = d_in + pc_ref[CW + k : CW + k + 1, :] * shift_up(cur, later, k)
        d_in = d_in * jnp.where(j == 0, first_ref[0, 0], 1.0)
        il_ref[at(j), :] = d_in.astype(BF16)
        return (
            sum_c + fold(cur),
            sum_i + fold(d_in),
            tuple(s + fold(cur * m) for s, m in zip(sums, moved)),
        )

    sum_c, sum_i, sums = lax.fori_loop(0, tiles, conv_step, (zero8, zero8, (zero8,) * 4))
    parts = [sum_i, *sums, sum_c, sum_d, sum_o, sum_p * pc_ref[S8 : S8 + 1, :], bias_ref[...]]
    rows = [jnp.sum(p, axis=0, keepdims=True) for p in parts]
    small_ref[...] = jnp.concatenate(rows + [jnp.zeros((16 - len(rows), width), F32)], axis=0)

    nm = nm_ref[...]
    dwi_ref[...] = dot_tn(il_ref[...], nm).astype(BF16).reshape(dwi_ref.shape)
    dwg_ref[...] = dot_tn(gl_ref[...], nm).astype(BF16).reshape(dwg_ref.shape)
    part = dot_nn(gl_ref[...], flat(wg_ref[...])) + dot_nn(il_ref[...], flat(wi_ref[...]))

    @pl.when(step == 0)
    def _():
        acc[...] = part

    @pl.when(step > 0)
    def _():
        acc[...] += part

    @pl.when(step == pl.num_programs(0) - 1)
    def _():
        def norm_back(j):
            v = x_ref[at(j), :].astype(F32)
            dn = acc[at(j), :]
            s = lax.rsqrt(jnp.mean(v * v, axis=1, keepdims=True) + EPSILON)
            e = dn * gain_ref[...]
            inner = jnp.mean(e * v, axis=1, keepdims=True)
            return s * e - v * (s * s * s * inner), fold(dn * (v * s))

        halo, total = norm_back(0)
        halo_ref[...] = halo

        def one(i, total):
            d, part = norm_back(1 + i)
            dx_ref[at(i), :] = dres_ref[at(i), :] + d
            return total + part

        gain_grad_ref[...] = lax.fori_loop(0, tiles - 1, one, total)


def shape_of(shape, dtype):
    return jax.ShapeDtypeStruct(shape, dtype)


def whole(shape):
    return pl.BlockSpec(shape, lambda g: (0,) * len(shape), pipeline_mode=pl.Buffered(1))


def kept(shape):
    return pl.BlockSpec(shape, lambda g: (0,) * len(shape))


def columns(rows, width):
    return pl.BlockSpec((rows, width), lambda g: (0, g))


def params(limit, **more):
    return pltpu.CompilerParams(
        dimension_semantics=("arbitrary",), vmem_limit_bytes=int(limit * MIB), **more
    )


def pair_blocks(weight):
    blocks, width, _ = weight.shape
    pairs = weight.reshape(blocks // 2, 2, width, width)
    zero = jnp.zeros_like(pairs[:, 0])
    top = jnp.concatenate([pairs[:, 0], zero], axis=2)
    low = jnp.concatenate([zero, pairs[:, 1]], axis=2)
    return jnp.concatenate([top, low], axis=1)


def to_slots(parts, count):
    rows = parts[0].shape[0]
    depth = parts[0].shape[1]
    got = lax.all_gather(jnp.concatenate(parts, axis=0), ("seq", "row"), axis=0, tiled=False)
    if count != SLOTS:
        got = got.reshape(count, len(parts), rows, depth).transpose(1, 0, 2, 3)
        got = got.reshape(len(parts), SLOTS, rows * count // SLOTS, depth).transpose(1, 0, 2, 3)
    return got.reshape(SLOTS, -1, depth)


def scatter_slots(grads, number, count):
    slots, rows, depth = grads.shape
    if count != SLOTS:
        grads = grads.reshape(slots, number, rows // number, depth).transpose(1, 0, 2, 3)
        grads = grads.reshape(number, count, -1, depth).transpose(1, 0, 2, 3)
    flat_grads = grads.reshape(slots * rows, depth)
    own = lax.psum_scatter(flat_grads, ("seq", "row"), scatter_dimension=0, tiled=True)
    own = own.astype(F32).reshape(number, -1, depth)
    return [own[i] for i in range(number)]


def entering(ends, reverse):
    count = lax.axis_size("seq")
    place = lax.axis_index("seq")
    got = lax.all_gather(ends, "seq")
    state = jnp.zeros_like(ends[0])
    for hop in range(count - 1):
        source = count - 1 - hop if reverse else hop
        ahead = source > place if reverse else source < place
        state = jnp.where(ahead, got[source, 0] * state + got[source, 1], state)
    return jnp.broadcast_to(state[None], (8, state.shape[0]))


def hop(value, axis, steps):
    count = lax.axis_size(axis)
    first, last = (max(0, -steps), min(count, count - steps))
    return lax.ppermute(value, axis, [(source, source + steps) for source in range(first, last)])


def shards(
    long_tokens,
    short_tokens,
    long_length,
    long_cotangent,
    short_cotangent,
    first_gain,
    gate_weight,
    gate_bias,
    input_weight,
    input_bias,
    conv_weight,
    conv_bias,
    decay_gate_weight,
    decay_gate_bias,
    input_gate_weight,
    input_gate_bias,
    decay_param,
    out_weight,
    second_gain,
    mlp_gate_weight,
    mlp_up_weight,
    mlp_down_weight,
):
    count = lax.axis_size("seq") * lax.axis_size("row")
    lrows, srows, depth = long_tokens.shape[1], short_tokens.shape[1], long_tokens.shape[2]
    chans = gate_bias.shape[0]
    units = mlp_gate_weight.shape[1] * count
    tokens = lrows + srows
    total = HALO + tokens
    ltiles, tiles = lrows // TILE, total // TILE
    cshare, ushare = chans // SLOTS, units // SLOTS
    groups = 4
    width = chans // groups
    per = SLOTS // groups

    long_x = long_tokens.reshape(lrows, depth)
    halo_x = hop(long_x[lrows - HALO :], "seq", 1)
    pair_own = [gate_weight.T, input_weight.T]
    mlp_own = [mlp_gate_weight.T, mlp_up_weight.T, mlp_down_weight]
    zcount = lax.axis_size("row")
    fast = lax.axis_size("seq") == 8 and count == SLOTS
    hbm = pl.BlockSpec(memory_space=pl.ANY)
    if fast:
        (pairw,) = gather_call([jnp.concatenate(pair_own, axis=0)], zcount)
        hshare = mlp_own[0].shape[0] // 2
        mlp_first, mlp_second = [
            jnp.concatenate([w[h * hshare : (h + 1) * hshare] for w in mlp_own]) for h in range(2)
        ]
        front_own = [out_weight, mlp_first]
        front_chunks = row_chunks(front_own, 16)
        lags = (2, 2, 3, 2)
        plan = spread_out(len(front_chunks) + sum(lags) + 1, 2, 4, 4)
        front_links = (zcount, front_chunks, lags, plan, len(front_own))
        front_extra = dict(
            specs=[hbm] * 2,
            shapes=[gathered(w, zcount) for w in front_own],
            scratch=gather_sems(len(front_chunks), zcount),
            params=dict(collective_id=2, has_side_effects=True),
        )
    else:
        pairw = to_slots(pair_own, count)
        outw = to_slots([out_weight], count)
        mlpw = to_slots(mlp_own, count).reshape(GRID + (3, 2, -1, depth))
        w_first, w_second = [mlpw[..., h, :, :].reshape(GRID + (-1, depth)) for h in range(2)]
        front_own, front_links = [], None
        front_extra = dict(specs=[], shapes=[], scratch=[], params={})
    pairw = pairw.reshape(SLOTS, -1, depth)
    x = jnp.concatenate([halo_x, long_x, short_tokens.reshape(srows, depth)], axis=0)
    place = lax.axis_index("seq")
    first = jnp.where(place > 0, 1.0, 0.0).astype(F32).reshape(1, 1)
    positions = place * lrows + jnp.arange(lrows, dtype=jnp.int32)
    keep = positions[:, None] < long_length[0]
    masked = jnp.where(keep, long_cotangent.reshape(lrows, depth), jnp.zeros((), BF16))
    cot = jnp.concatenate([masked, short_cotangent.reshape(srows, depth)], axis=0)
    chan = jnp.concatenate(
        [
            jnp.stack([gate_bias, input_bias]),
            conv_weight,
            jnp.stack(
                [
                    conv_bias,
                    decay_gate_bias,
                    input_gate_bias,
                    8.0 * jax.nn.softplus(decay_param),
                    8.0 * jax.nn.sigmoid(decay_param),
                ]
            ),
            jnp.zeros((5, chans), F32),
        ],
        axis=0,
    )
    pair_d = pair_blocks(decay_gate_weight)
    pair_o = pair_blocks(input_gate_weight)
    gain1 = first_gain[None]
    gain2 = second_gain[None]
    scalar = pl.BlockSpec(memory_space=pltpu.SMEM)

    def mix_part(which):
        return pl.BlockSpec((per, cshare, depth), lambda g: (g, which, 0))

    pair_spec = pl.BlockSpec((1, width, width), lambda g: (g, 0, 0))
    col = columns(total, width)
    col_long = columns(HALO + lrows, width)
    pc_spec = columns(16, width)
    col8 = columns(8, width)

    wide = shape_of((total, chans), F32)
    narrow = shape_of((HALO + lrows, chans), F32)
    gp, inner, dp, ip, states, reach, mix_s, ends, normed, *wide_w = pl.pallas_call(
        functools.partial(front_kernel, ltiles, tiles, front_links),
        grid=(groups,),
        in_specs=[
            scalar, whole((total, depth)), whole((1, depth)), mix_part(0), mix_part(1),
            pair_spec, pair_spec, pc_spec, *front_extra["specs"],
        ],
        out_specs=[
            col, col, col, col, col, col_long, columns(srows, width), col8,
            kept((total, depth)), *front_extra["specs"],
        ],
        out_shape=[
            wide, wide, wide, wide, wide, narrow, shape_of((srows, chans), BF16),
            shape_of((8, chans), F32), shape_of((total, depth), BF16), *front_extra["shapes"],
        ],
        scratch_shapes=[
            pltpu.VMEM((total, width), F32), pltpu.VMEM((total, width), BF16),
            *front_extra["scratch"],
        ],
        compiler_params=params(48, **front_extra["params"]),
        name="front",
    )(first, x, gain1, pairw, pairw, pair_d, pair_o, chan, *front_own)
    if fast:
        outw, w_first = wide_w
        outw = outw.reshape(SLOTS, -1, depth)

    s_in = entering(ends[0:2], False)

    steps = 4
    hid = units // steps
    block = GRID[1:] + (3 * ushare // 2, depth)
    wbuf = pltpu.VMEM((2,) + block, BF16)
    dwbuf = pltpu.VMEM(block, BF16)
    one_dma = pltpu.SemaphoreType.DMA
    if fast:
        chunks = row_chunks([mlp_second], 16)
        waves = len(chunks) + sum(lags) + 1
        plan = spread_out(waves, 3, 3, 8)
        mlp_links = (zcount, chunks, lags, plan)
        w_last, more_specs, more_shapes = mlp_second, [hbm], [gathered(mlp_second, zcount)]
        half_block = (block[0],) + block[2:]
        more_scratch = [
            pltpu.VMEM(half_block, BF16), one_dma((2,)), pltpu.SemaphoreType.REGULAR,
            *gather_sems(len(chunks), zcount),
        ]
        dw_shape = (2, 2) + half_block
        more_params = dict(collective_id=3, has_side_effects=True)
    else:
        mlp_links, w_last, more_specs, more_shapes, more_scratch = None, w_second, [], [], []
        dw_shape, more_params = (2, 2) + block, {}
    out, d_res, rlow, mix_l, gain2_grad, dmlp, *_ = pl.pallas_call(
        functools.partial(mlp_kernel, ltiles, tokens // TILE, mlp_links),
        grid=(steps,),
        in_specs=[
            whole((total, depth)), whole((tokens, depth)), whole((HALO + lrows, chans)),
            whole((HALO + lrows, chans)), whole((HALO + lrows, chans)), whole((8, chans)),
            whole((srows, chans)), whole((SLOTS, cshare, depth)), whole((1, depth)), hbm, hbm,
        ],
        out_specs=[
            whole((tokens, depth)), whole((tokens, depth)), whole((tokens, depth)),
            whole((lrows, chans)), whole((8, depth)), hbm, *more_specs,
        ],
        out_shape=[
            shape_of((tokens, depth), BF16), shape_of((tokens, depth), F32),
            shape_of((tokens, depth), BF16), shape_of((lrows, chans), BF16),
            shape_of((8, depth), F32), shape_of(dw_shape, BF16), *more_shapes,
        ],
        scratch_shapes=[
            pltpu.VMEM((tokens, depth), BF16), pltpu.VMEM((tokens, depth), F32),
            pltpu.VMEM((tokens, depth), F32), pltpu.VMEM((tokens, hid), F32),
            pltpu.VMEM((tokens, hid), F32), pltpu.VMEM((tokens, hid), F32),
            pltpu.VMEM((tokens, hid), BF16), pltpu.VMEM((tokens, hid), BF16),
            pltpu.VMEM((tokens, hid), BF16), wbuf, dwbuf, one_dma((2,)), one_dma, *more_scratch,
        ],
        compiler_params=params(62, **more_params),
        name="mlp",
    )(x, cot, states, reach, gp, s_in, mix_s, outw, gain2, w_first, w_last)

    slot_spec = pl.BlockSpec((per, cshare, depth), lambda g: (g, 0, 0))
    slot_shape = shape_of((SLOTS, cshare, depth), BF16)
    d_out, gate_low, total_grad, back_reach, back_ends, gate_bias_part = pl.pallas_call(
        functools.partial(back_kernel, ltiles, tiles),
        grid=(groups,),
        in_specs=[
            whole((tokens, depth)), mix_part(0), columns(lrows, width), columns(srows, width),
            col, col, col_long, col8, col, pc_spec,
        ],
        out_specs=[slot_spec, col, col, col_long, col8, col8],
        out_shape=[
            slot_shape, shape_of((total, chans), BF16), wide, narrow,
            shape_of((8, chans), F32), shape_of((8, chans), F32),
        ],
        scratch_shapes=[pltpu.VMEM((tokens, width), F32)],
        compiler_params=params(48),
        name="back",
    )(rlow, outw, mix_l, mix_s, gp, states, reach, s_in, dp, chan)

    c_in = entering(back_ends[0:2], True)

    blocks, bwidth = decay_gate_weight.shape[0:2]
    d_x, d_halo, gain1_grad, d_gate, d_input, d_gates, small = pl.pallas_call(
        functools.partial(last_kernel, ltiles, tiles),
        grid=(groups,),
        in_specs=[
            scalar, whole((total, depth)), whole((1, depth)), whole((total, depth)),
            whole((tokens, depth)), mix_part(0), mix_part(1), pair_spec, pair_spec, pc_spec,
            col, col, col, col, col_long, col8, col, col_long, col8, col, col8,
        ],
        out_specs=[
            whole((tokens, depth)), whole((HALO, depth)), whole((8, depth)), slot_spec, slot_spec,
            pl.BlockSpec((2, 2, bwidth, bwidth), lambda g: (0, g, 0, 0)), pc_spec,
        ],
        out_shape=[
            shape_of((tokens, depth), F32), shape_of((HALO, depth), F32), shape_of((8, depth), F32),
            slot_shape, slot_shape, shape_of((2, blocks, bwidth, bwidth), BF16),
            shape_of((16, chans), F32),
        ],
        scratch_shapes=[
            pltpu.VMEM((total, depth), F32), pltpu.VMEM((total, width), F32),
            pltpu.VMEM((total, width), BF16), pltpu.VMEM((total, width), BF16),
            pltpu.VMEM((total, width), BF16), pltpu.VMEM((total, width), BF16),
        ],
        compiler_params=params(60),
        name="last",
    )(
        first, x, gain1, normed, d_res, pairw, pairw, pair_d, pair_o, chan,
        inner, dp, ip, states, reach, s_in, total_grad, back_reach, c_in, gate_low,
        gate_bias_part,
    )

    late = hop(d_halo, "seq", -1)
    long_grad = d_x[:lrows].at[lrows - HALO :].add(late)
    short_grad = d_x[lrows:]

    lanes = 2048
    gains = jnp.stack([jnp.sum(gain1_grad, axis=0), jnp.sum(gain2_grad, axis=0)])
    small = jnp.concatenate(
        [
            jnp.pad(small[0:10], ((0, 0), (0, lanes - chans))),
            jnp.pad(gains, ((0, 0), (0, lanes - depth))),
            jnp.zeros((4, lanes), F32),
        ],
        axis=0,
    )
    if fast:
        mains = [d_gate, d_input, d_out]
        tiled = small.reshape(2, 8, lanes // 128, 128).transpose(0, 2, 1, 3)
        shares = scatter_call(
            dmlp, mains, d_gates.reshape(SLOTS, -1, bwidth), tiled.reshape(SLOTS, 8, 128), zcount
        )
        g_gate, g_input, g_out, gate_sums, sums, g_mgate, g_mup, g_down = shares
        gate_sums = gate_sums.reshape(d_gates.shape)
        sums = sums.reshape(2, lanes // 128, 8, 128).transpose(0, 2, 1, 3).reshape(16, lanes)
    else:
        dmlp = dmlp.reshape(2, SLOTS, 3, -1, depth).transpose(1, 2, 0, 3, 4)
        g_mgate, g_mup, g_down = scatter_slots(dmlp.reshape(SLOTS, -1, depth), 3, count)
        dmix = jnp.concatenate([d_gate, d_input, d_out], axis=1)
        g_gate, g_input, g_out = scatter_slots(dmix, 3, count)
        gate_sums, sums = lax.psum((d_gates.astype(F32), small), ("seq", "row"))
    gate_sums = gate_sums.astype(F32)
    rows = sums[0:10, :chans]
    return (
        out[:lrows].reshape(long_tokens.shape),
        out[lrows:].reshape(short_tokens.shape),
        long_grad.reshape(long_tokens.shape),
        short_grad.reshape(short_tokens.shape),
        sums[10, :depth],
        g_gate.T,
        rows[9],
        g_input.T,
        rows[0],
        rows[1:5],
        rows[5],
        gate_sums[0],
        rows[6],
        gate_sums[1],
        rows[7],
        rows[8],
        g_out,
        sums[11, :depth],
        g_mgate.T,
        g_mup.T,
        g_down,
    )


def solution(mesh):
    both = ("seq", "row")
    long_spec = P("row", "seq", None)
    short_spec = P(both, None, None)
    cols = P(None, both)
    rows = P(both, None)
    return jax.shard_map(
        shards,
        mesh=mesh,
        in_specs=(
            long_spec, short_spec, P("row"), long_spec, short_spec, P(), cols, P(), cols, P(),
            P(), P(), P(), P(), P(), P(), P(), rows, P(), cols, cols, rows,
        ),
        out_specs=(
            long_spec, short_spec, long_spec, short_spec, P(), cols, P(), cols, P(), P(), P(),
            P(), P(), P(), P(), P(), rows, P(), cols, cols, rows,
        ),
        check_vma=False,
    )
```

```python
import functools

import jax
import jax.numpy as jnp
from jax import lax
from jax.experimental import pallas as pl
from jax.experimental.pallas import tpu as pltpu
from jax.sharding import PartitionSpec as P

EPSILON = 1e-06
F32 = jnp.float32
BF16 = jnp.bfloat16
GRID = (2, 2, 2, 4)
SLOTS = 32
TILE = 16
HALO = 16
MIB = 1024 * 1024
TAIL_SLOTS = 11
GELU_A = 0.7978845608028654
GELU_B = 0.044715


def dot_nn(a, b):
    return lax.dot_general(a, b, (((1,), (0,)), ((), ())), preferred_element_type=F32)


def dot_nt(a, b):
    return lax.dot_general(a, b, (((1,), (1,)), ((), ())), preferred_element_type=F32)


def dot_tn(a, b):
    return lax.dot_general(a, b, (((0,), (0,)), ((), ())), preferred_element_type=F32)


def sigmoid(v):
    return 0.5 * jnp.tanh(0.5 * v) + 0.5


def gelu(v):
    t = jnp.tanh(v * (GELU_A + (GELU_A * GELU_B) * (v * v)))
    h = 0.5 * v
    return h + h * t


def gelu_pair(v):
    w = v * v
    t = jnp.tanh(v * (GELU_A + (GELU_A * GELU_B) * w))
    h = 0.5 * v
    slope = 0.5 + 0.5 * t + (h - h * (t * t)) * (GELU_A + (3.0 * GELU_A * GELU_B) * w)
    return h + h * t, slope


def row_iota(shape):
    return lax.broadcasted_iota(jnp.int32, shape, 0)


def at(j):
    return pl.ds(pl.multiple_of(j * TILE, TILE), TILE)


def scan_tile(a, b, reverse):
    rows = row_iota(a.shape)
    step = 1
    while step < TILE:
        if reverse:
            keep, shift = rows < TILE - step, TILE - step
        else:
            keep, shift = rows >= step, step
        b = jnp.where(keep, a * pltpu.roll(b, shift, 0) + b, b)
        a = jnp.where(keep, a * pltpu.roll(a, shift, 0), a)
        step *= 2
    return a, b


def shift_down(cur, prev, k):
    if k == 0:
        return cur
    rows = row_iota(cur.shape)
    return jnp.where(rows < k, pltpu.roll(prev, k, 0), pltpu.roll(cur, k, 0))


def shift_up(cur, later, k):
    if k == 0:
        return cur
    rows = row_iota(cur.shape)
    return jnp.where(
        rows >= TILE - k, pltpu.roll(later, TILE - k, 0), pltpu.roll(cur, TILE - k, 0)
    )


def fold(v):
    return v[0:8] + v[8:16]


def flat(block):
    return block.reshape(-1, block.shape[-1])


def gates(dp, ip, c8):
    rate = sigmoid(dp)
    opening = sigmoid(ip)
    log_decay = -c8 * (0.25 + rate)
    decay = jnp.exp(log_decay)
    square = -jnp.tanh(log_decay) * (1.0 + decay * decay)
    return rate, opening, decay, square


GB, IB, CW, CB, DB, OB, C8, S8 = 0, 1, 2, 6, 7, 8, 9, 10


def conv_tile(in_ref, pc_ref, j, live):
    cur = in_ref[at(j), :]
    prev = in_ref[at(j - 1), :] * live
    out = pc_ref[CB : CB + 1, :] + pc_ref[CW : CW + 1, :] * cur
    moved = [cur]
    for k in range(1, 4):
        m = shift_down(cur, prev, k)
        moved.append(m)
        out = out + pc_ref[CW + k : CW + k + 1, :] * m
    return out, moved


def place_of():
    s = lax.axis_index("seq")
    return s // 4, (s // 2) % 2, s % 2, lax.axis_index("row")


def device_at(y, x, c, z):
    return ((y * 2 + x) * 2 + c, z)


class Peers:
    def __init__(self, zcount):
        y, x, c, z = self.place = place_of()
        self.far = [(z + k) % zcount for k in range(1, zcount)]
        self.along = [device_at(y, x, c, q) for q in self.far]
        self.near = ((y + c) % 2, (x + 1 - c) % 2)
        self.first = device_at(*self.near, c, z)
        self.second = device_at((y + 1 - c) % 2, (x + c) % 2, c, z)
        self.other = device_at(y, x, 1 - c, z)

    def meet(self):
        everyone = [*self.along, self.first, self.second, self.other]
        barrier = pltpu.get_barrier_semaphore()
        for peer in everyone:
            pl.semaphore_signal(
                barrier, inc=1, device_id=peer, device_id_type=pl.DeviceIdType.MESH
            )
        pl.semaphore_wait(barrier, len(everyone))


def remote(source, target, send, recv, device):
    return pltpu.make_async_remote_copy(
        src_ref=source,
        dst_ref=target,
        send_sem=send,
        recv_sem=recv,
        device_id=device,
        device_id_type=pl.DeviceIdType.MESH,
    )


class Spread:
    def __init__(self, peers, own, full, send, recv):
        self.peers, self.own, self.full, self.send, self.recv = peers, own, full, send, recv

    def go(self, stage, act):
        y, x, c, z = self.peers.place
        p, full = self.peers, self.full
        if stage == 0:
            for k, device in enumerate(p.along):
                act(remote(self.own, full(y, x, c, z), self.send(k), self.recv(k), device))
            return
        k = len(p.along) + stage - 1
        if stage == 2:

            @pl.when(c == 0)
            def _():
                part = full(y, slice(None), c, slice(None))
                act(remote(part, part, self.send(k), self.recv(k), p.second))

            @pl.when(c == 1)
            def _():
                part = full(slice(None), x, c, slice(None))
                act(remote(part, part, self.send(k), self.recv(k), p.second))

            return
        if stage == 1:
            part, device = full(y, x, c, slice(None)), p.first
        else:
            part, device = full(slice(None), slice(None), c, slice(None)), p.other
        act(remote(part, part, self.send(k), self.recv(k), device))

    def start(self, stage):
        self.go(stage, lambda d: d.start())

    def arrive(self, stage):
        self.go(stage, lambda d: d.wait_recv())

    def drain(self):
        for stage in range(4):
            self.go(stage, lambda d: d.wait_send())


def wave_of(t, count, lags):
    for stage in range(len(lags), -1, -1):
        piece = t - sum(lags[:stage])
        if 0 <= piece < count:
            yield piece, stage


class Gather:
    def __init__(self, zcount, ins, outs, sems, chunks, lags):
        self.csem, self.ssem, self.rsem = sems
        self.peers = Peers(zcount)
        self.lags = lags
        y, x, c, z = self.peers.place
        self.spreads, self.copies = [], []
        for i, (which, start, size) in enumerate(chunks):
            rows = pl.ds(start, size)
            own = ins[which].at[rows]

            def full(a, b, d, e, ref=outs[which], rows=rows):
                return ref.at[a, b, d, e, rows]

            def send(k, i=i):
                return self.ssem.at[i, k]

            def recv(k, i=i):
                return self.rsem.at[i, k]

            self.spreads.append(Spread(self.peers, own, full, send, recv))
            self.copies.append(pltpu.make_async_copy(own, full(y, x, c, z), self.csem.at[i]))
        self.waves = len(chunks) + sum(lags) + 1

    def wave(self, t):
        for i, stage in wave_of(t, len(self.spreads), self.lags):
            if stage == 0:
                self.copies[i].start()
            elif stage == 1:
                self.copies[i].wait()
            if stage > 0:
                self.spreads[i].arrive(stage - 1)
            if stage < 4:
                self.spreads[i].start(stage)

    def drain(self):
        for spread in self.spreads:
            spread.drain()


def in_turn(weave, step, plan, first=0):
    def point(k):
        for s, points in enumerate(plan, first):
            if k < len(points) and points[k]:

                @pl.when(step == s)
                def _(todo=points[k]):
                    for t in todo:
                        weave.wave(t)

    return point


def spread_out(waves, ahead, steps, points):
    todo = list(range(waves))
    plan = []
    for s in range(steps):
        row = []
        for k in range(points):
            take = ahead if s == 0 and k == 0 else 1
            if s == steps - 1 and k == points - 1:
                take = len(todo)
            row.append(todo[:take])
            todo = todo[take:]
        plan.append(row)
    return plan


def paced(waves, ahead, marks):
    last = marks[-1][-1]
    plan = [[[] for _ in row] for row in marks]
    spots = [(t, s, k) for s, row in enumerate(marks) for k, t in enumerate(row)]
    for w in range(waves):
        due = last * max(0, w - ahead) / max(1, waves - ahead)
        _, s, k = next(spot for spot in spots if spot[0] >= due)
        plan[s][k].append(w)
    return plan


def row_chunks(parts, size):
    return [
        (which, start, size)
        for which, part in enumerate(parts)
        for start in range(0, part.shape[0], size)
    ]


def gather_sems(count, zcount):
    links = pltpu.SemaphoreType.DMA((count, zcount + 2))
    return [pltpu.SemaphoreType.DMA((count,)), links, links]


def gathered(part, zcount):
    return jax.ShapeDtypeStruct((2, 2, 2, zcount) + part.shape, part.dtype)


def gather_kernel(zcount, chunks, lags, number, *refs):
    gather = Gather(zcount, refs[:number], refs[number : 2 * number], refs[2 * number :], chunks, lags)
    gather.peers.meet()
    for t in range(gather.waves):
        gather.wave(t)
    gather.drain()


def gather_call(parts, zcount):
    chunks = row_chunks(parts, 16)
    hbm = pl.BlockSpec(memory_space=pl.ANY)
    return pl.pallas_call(
        functools.partial(gather_kernel, zcount, chunks, (2, 2, 3, 2), len(parts)),
        out_shape=[gathered(p, zcount) for p in parts],
        in_specs=[hbm] * len(parts),
        out_specs=[hbm] * len(parts),
        scratch_shapes=gather_sems(len(chunks), zcount),
        compiler_params=pltpu.CompilerParams(collective_id=0, has_side_effects=True),
        name="gather",
    )(*parts)


CORE, GATES, SUMS, HALVED = 0, 1, 2, 3


class Scatter:
    def __init__(self, zcount, ins, outs, buffers, sems, chunks, lags):
        self.peers = Peers(zcount)
        self.zcount, self.chunks, self.lags = zcount, chunks, lags
        self.ins, self.outs, self.buffers = ins, outs, buffers
        self.csem, self.ssem, self.rsem = sems[:3]
        self.pieces = [Piece(self, i, sems[3:], *chunk) for i, chunk in enumerate(chunks)]
        self.waves = len(chunks) + sum(lags) + 1

    def wave(self, t):
        for i, stage in wave_of(t, len(self.pieces), self.lags):
            if stage <= 4 or self.pieces[i].spread is not None:
                self.pieces[i].step(stage)

    def drain(self):
        for piece in self.pieces:
            piece.drain()


def add_into(into, i, part, j):
    into[i] = (into[i].astype(F32) + part[j].astype(F32)).astype(into.dtype)


class Piece:
    def __init__(self, owner, i, sems, kind, slot, which, source, span, target, place):
        self.o, self.i, self.kind, self.slot = owner, i, kind, slot
        self.a, self.r0, self.r1, self.r2, self.r3 = owner.buffers[kind]
        self.source, self.lead, self.rows = owner.ins[which], source, pl.ds(*span)
        self.target, self.place = owner.outs[target], place
        self.spread, self.drained = None, False
        if kind in (GATES, SUMS):
            y, x, c, z = owner.peers.place

            def full(*at_place):
                return self.target.at[at_place]

            def send(k):
                return sems[0].at[i, k]

            def recv(k):
                return sems[1].at[i, k]

            self.spread = Spread(owner.peers, full(y, x, c, z), full, send, recv)

    def local(self):
        c = self.o.peers.place[2]
        if self.kind == HALVED:
            mine = self.source.at[self.lead, :, :, :, self.rows]
        else:
            mine = self.source.at[:, :, c, :, self.rows]
        return pltpu.make_async_copy(mine, self.a.at[self.slot], self.o.csem.at[self.i])

    def send(self, stage, act):
        s, peers = self.slot, self.o.peers
        y, x, c, z = peers.place

        def go(source, target, k, device):
            act(remote(source, target, self.o.ssem.at[self.i, k], self.o.rsem.at[self.i, k], device))

        if stage == 0:
            if self.kind != HALVED:
                theirs = self.source.at[:, :, 1 - c, :, self.rows]
                go(theirs, self.r0.at[s], 0, peers.other)
        elif stage == 1:

            @pl.when(c == 0)
            def _():
                go(self.a.at[s, 1 - y], self.r1.at[s], 1, peers.second)

            @pl.when(c == 1)
            def _():
                go(self.a.at[s, :, 1 - x], self.r1.at[s], 1, peers.second)

        elif stage == 2:
            go(self.a.at[(s, *peers.near)], self.r2.at[s], 2, peers.first)
        else:
            for k, device in enumerate(peers.along):
                go(self.a.at[s, y, x, peers.far[k]], self.r3.at[s, k], 3 + k, device)

    def step(self, stage):
        s, zcount = self.slot, self.o.zcount
        y, x, c, z = self.o.peers.place
        if stage == 0:
            for earlier in self.o.pieces[: self.i]:
                if (earlier.kind, earlier.slot) == (self.kind, s):
                    earlier.drain()
            self.local().start()
        elif stage <= 4:
            self.send(stage - 1, lambda d: d.wait_recv())
        else:
            self.spread.arrive(stage - 5)
        if stage == 1:
            self.local().wait()
            if self.kind != HALVED:

                @pl.loop(0, 4 * zcount)
                def _(q):
                    i = (s, q // (2 * zcount), (q // zcount) % 2, q % zcount)
                    add_into(self.a, i, self.r0, i)

        elif stage == 2:

            @pl.loop(0, 2 * zcount)
            def _(q):
                h = q // zcount
                i = (s, y * (1 - c) + h * c, h * (1 - c) + x * c, q % zcount)
                add_into(self.a, i, self.r1, (s, h, q % zcount))

        elif stage == 3:

            @pl.loop(0, zcount)
            def _(q):
                add_into(self.a, (s, y, x, q), self.r2, (s, q))

        elif stage == 4:
            total = self.a[s, y, x, z].astype(F32)
            for k in range(zcount - 1):
                total = total + self.r3[s, k].astype(F32)
            if self.spread is None:
                self.target[self.place : self.place + total.shape[0]] = total
            else:
                self.target[y, x, c, z] = total.astype(self.target.dtype)
        if stage < 4:
            self.send(stage, lambda d: d.start())
        elif stage < 8 and self.spread is not None:
            self.spread.start(stage - 4)

    def drain(self):
        if self.drained:
            return
        self.drained = True
        for stage in range(4):
            self.send(stage, lambda d: d.wait_send())
        if self.spread is not None:
            self.spread.drain()


def five(number, shape, dtype, zcount):
    lead = [(2, 2, zcount), (2, 2, zcount), (2, zcount), (zcount,), (zcount - 1,)]
    return [pltpu.VMEM((number, *d, *shape), dtype) for d in lead]


def scatter_kernel(zcount, chunks, lags, nin, nout, *refs):
    ins, outs, rest = refs[:nin], refs[nin : nin + nout], refs[nin + nout :]
    buffers = [rest[0:5], rest[5:10], rest[10:15]]
    scatter = Scatter(zcount, ins, outs, buffers, rest[15:], chunks, lags)
    scatter.peers.meet()
    for t in range(scatter.waves):
        scatter.wave(t)
    scatter.drain()


def scatter_call(mains, gate_grads, sums, zcount):
    grid = (2, 2, 2, zcount)
    rows, depth = mains[0].shape[1:]
    nmain = len(mains)
    ins = [m.reshape(grid + m.shape[1:]) for m in mains]
    ins += [a.reshape(grid + a.shape[1:]) for a in (gate_grads, sums)]
    outs = [shape_of((rows, depth), F32) for _ in mains]
    outs += [shape_of(a.shape, a.dtype) for a in ins[nmain:]]
    chunks = [
        (SUMS, 0, nmain + 1, None, (0, sums.shape[1]), nmain + 1, 0),
        (GATES, 0, nmain, None, (0, gate_grads.shape[1]), nmain, 0),
    ]
    size = 16
    number = 0
    for i in range(nmain):
        for start in range(0, rows, size):
            chunks.append((CORE, number, i, None, (start, size), i, start))
            number += 1
    n = len(chunks)
    links = pltpu.SemaphoreType.DMA((n, zcount + 2))
    return pl.pallas_call(
        functools.partial(
            scatter_kernel, zcount, chunks, (2, 2, 2, 2, 1, 1, 1, 1), len(ins), len(outs)
        ),
        out_shape=outs,
        in_specs=[pl.BlockSpec(memory_space=pl.ANY)] * len(ins),
        out_specs=[pl.BlockSpec(memory_space=pltpu.VMEM)] * len(outs),
        scratch_shapes=[
            *five(number, (size, depth), BF16, zcount),
            *five(1, gate_grads.shape[1:], BF16, zcount),
            *five(1, sums.shape[1:], F32, zcount),
            pltpu.SemaphoreType.DMA((n,)),
            links, links, links, links,
        ],
        compiler_params=pltpu.CompilerParams(
            collective_id=1, has_side_effects=True, vmem_limit_bytes=62 * MIB
        ),
        name="scatter",
    )(*ins)


def no_point(k):
    pass


def front_kernel(ltiles, tiles, links, *refs):
    (
        first_ref, x_ref, gain_ref, wg_ref, wi_ref, wd_ref, wo_ref, pc_ref
    ) = refs[:8]
    refs = refs[8:]
    point, gather = no_point, None
    step = pl.program_id(0)
    if links is not None:
        zcount, chunks, lags, plan, number = links
        gather = Gather(
            zcount, refs[:number], refs[number + 9 : 2 * number + 9], refs[2 * number + 11 :], chunks, lags
        )
        refs = refs[number : number + 9] + refs[2 * number + 9 : 2 * number + 11]
        point = in_turn(gather, step, plan)
    gp_ref, in_ref, dp_ref, ip_ref, st_ref, pr_ref, mix_ref, end_ref, nm_ref, cv_ref, cl_ref = refs

    @pl.when(step == 0)
    def _():
        if gather is not None:
            gather.peers.meet()

    point(0)

    @pl.when(step == 0)
    def _():
        @pl.loop(0, tiles)
        def _(j):
            v = x_ref[at(j), :].astype(F32)
            s = lax.rsqrt(jnp.mean(v * v, axis=1, keepdims=True) + EPSILON)
            nm_ref[at(j), :] = (v * s * gain_ref[...]).astype(BF16)

    nm = nm_ref[...]
    gp_ref[...] = dot_nt(nm, flat(wg_ref[...])) + pc_ref[GB : GB + 1, :]
    in_ref[...] = dot_nt(nm, flat(wi_ref[...])) + pc_ref[IB : IB + 1, :]
    point(1)
    in_ref[0:HALO, :] = in_ref[0:HALO, :] * first_ref[0, 0]
    cl_ref[0:HALO, :] = jnp.zeros((HALO, cl_ref.shape[1]), BF16)

    @pl.loop(1, tiles)
    def _(j):
        live = jnp.where(j == 1 + ltiles, 0.0, 1.0)
        out, _ = conv_tile(in_ref, pc_ref, j, live)
        cv_ref[at(j), :] = out
        cl_ref[at(j), :] = out.astype(BF16)

    point(2)
    low = cl_ref[...]
    dp_ref[...] = dot_nn(low, wd_ref[0]) + pc_ref[DB : DB + 1, :]
    ip_ref[...] = dot_nn(low, wo_ref[0]) + pc_ref[OB : OB + 1, :]

    def scanned(j):
        _, opening, a, square = gates(dp_ref[at(j), :], ip_ref[at(j), :], pc_ref[C8 : C8 + 1, :])
        b = (square * lax.rsqrt(square)) * opening * cv_ref[at(j), :]
        return scan_tile(a, b, False)

    width = gp_ref.shape[1]

    def long_step(i, carry):
        state, reach = carry
        a, b = scanned(1 + i)
        s = b + a * state
        r = a * reach
        st_ref[at(1 + i), :] = s
        pr_ref[at(1 + i), :] = r
        return s[TILE - 1 : TILE], r[TILE - 1 : TILE]

    state, reach = lax.fori_loop(
        0, ltiles, long_step, (jnp.zeros((1, width), F32), jnp.ones((1, width), F32))
    )
    end_ref[...] = jnp.concatenate([reach, state, jnp.zeros((6, width), F32)], axis=0)

    def short_step(i, state):
        j = 1 + ltiles + i
        a, b = scanned(j)
        s = b + a * state
        st_ref[at(j), :] = s
        mix_ref[at(i), :] = (s * gelu(gp_ref[at(j), :])).astype(BF16)
        return s[TILE - 1 : TILE]

    lax.fori_loop(0, tiles - 1 - ltiles, short_step, jnp.zeros((1, width), F32))
    point(3)
    if gather is not None:

        @pl.when(step == pl.num_programs(0) - 1)
        def _():
            gather.drain()


def mlp_kernel(ltiles, tiles, links, *refs):
    (
        x_ref, cot_ref, st_ref, pr_ref, gp_ref, sin_ref, mixs_ref, wo_ref, gain_ref, w1_ref, w2_ref
    ) = refs[:11]
    refs = refs[11:]
    point, gather = no_point, None
    step = pl.program_id(0)
    last = pl.num_programs(0) - 1
    out_ref, dres_ref, rlow_ref, mixl_ref, gain_grad_ref, dw_hbm = refs[:6]
    refs = refs[6:]
    if links is not None:
        zcount, chunks, lags, plan = links
        own_ref, w2_ref = w2_ref, refs[0]
        gather = Gather(zcount, [own_ref], [w2_ref], refs[-3:], chunks, lags)
        got_ref, sems, credit = refs[-6], refs[-5], refs[-4]
        refs = refs[1:-6]
        point = in_turn(gather, step, plan)
    (
        n2_ref, acc_o, acc_n, g_ref, u_ref, d_ref, h_ref, dg_ref, du_ref, wbuf, dwbuf, wsem, dsem
    ) = refs
    lrows = ltiles * TILE
    half = g_ref.shape[1] // 2
    share = wbuf.shape[-2] // 3
    steps = 2 * GRID[0]

    def load(s):
        source = w1_ref if s < steps // 2 else w2_ref
        return pltpu.make_async_copy(
            source.at[s % (steps // 2)], wbuf.at[s % 2], wsem.at[s % 2]
        )

    def each(todo, first=0):
        for s in range(first, steps):

            @pl.when(step == s)
            def _(s=s):
                todo(s)

    if gather is not None:
        y, x, c, z = gather.peers.place

    def store(s):
        h, q = s // (steps // 2), s % (steps // 2)
        mine = dwbuf if gather is None else dwbuf.at[:, c]
        return pltpu.make_async_copy(mine, dw_hbm.at[h, q], dsem)

    def swap():
        return remote(
            dwbuf.at[:, 1 - c], got_ref, sems.at[0], sems.at[1], gather.peers.other
        )

    def settle(s):
        if gather is not None:
            swap().wait_recv()

            @pl.loop(0, got_ref.shape[0] * got_ref.shape[1])
            def _(k):
                i, j = k // got_ref.shape[1], k % got_ref.shape[1]
                both = dwbuf[i, c, j].astype(F32) + got_ref[i, j].astype(F32)
                dwbuf[i, c, j] = both.astype(BF16)

            if s < steps - 1:
                pl.semaphore_signal(
                    credit,
                    inc=1,
                    device_id=gather.peers.other,
                    device_id_type=pl.DeviceIdType.MESH,
                )
        store(s).start()

    def clear(s):
        store(s).wait()
        if gather is not None:
            swap().wait_send()

    @pl.when(step == 0)
    def _():
        load(0).start()
        load(1).start()
        if gather is not None:
            gather.peers.meet()

    point(0)

    @pl.when(step == 0)
    def _():
        s_in = sin_ref[0:1, :]

        @pl.loop(0, ltiles)
        def _(i):
            s = st_ref[at(1 + i), :] + pr_ref[at(1 + i), :] * s_in
            mixl_ref[at(i), :] = (s * gelu(gp_ref[at(1 + i), :])).astype(BF16)

        wo = flat(wo_ref[...])
        dres_ref[0:lrows, :] = dot_nn(mixl_ref[...], wo)
        dres_ref[lrows:, :] = dot_nn(mixs_ref[...], wo)

        @pl.loop(0, tiles)
        def _(i):
            r = dres_ref[at(i), :] + x_ref[at(1 + i), :].astype(F32)
            dres_ref[at(i), :] = r
            acc_o[at(i), :] = r
            s = lax.rsqrt(jnp.mean(r * r, axis=1, keepdims=True) + EPSILON)
            n2_ref[at(i), :] = (r * s * gain_ref[...]).astype(BF16)

        acc_n[...] = jnp.zeros_like(acc_n)

    point(1)

    @pl.when(step == steps // 2)
    def _():
        load(steps // 2).start()
        load(steps // 2 + 1).start()

    each(lambda s: load(s).wait())
    slot = lax.rem(step, 2)
    n2 = n2_ref[...]
    wg = flat(wbuf[slot, ..., 0:share, :])
    wu = flat(wbuf[slot, ..., share : 2 * share, :])
    wd = flat(wbuf[slot, ..., 2 * share :, :])
    g_ref[...] = dot_nt(n2, wg)
    u_ref[...] = dot_nt(n2, wu)
    point(2)
    d_ref[...] = dot_nt(cot_ref[...], wd)
    each(lambda s: settle(s - 1), 1)
    point(3)

    @pl.loop(0, tiles)
    def _(i):
        for k in range(2):
            cols = slice(k * half, (k + 1) * half)
            ge, slope = gelu_pair(g_ref[at(i), cols])
            u = u_ref[at(i), cols]
            d = d_ref[at(i), cols]
            h_ref[at(i), cols] = (ge * u).astype(BF16)
            dg_ref[at(i), cols] = (d * u * slope).astype(BF16)
            du_ref[at(i), cols] = (d * ge).astype(BF16)

    point(4)
    acc_o[...] += dot_nn(h_ref[...], wd)
    acc_n[...] += dot_nn(dg_ref[...], wg) + dot_nn(du_ref[...], wu)
    point(5)
    each(lambda s: clear(s - 1), 1)
    lead = dwbuf.shape[:-2]
    rest = (share, dwbuf.shape[-1])
    for k, (left, right) in enumerate(((dg_ref, n2_ref), (du_ref, n2_ref), (h_ref, cot_ref))):
        grad = dot_tn(left[...], right[...]).astype(BF16)
        dwbuf[..., k * share : (k + 1) * share, :] = grad.reshape(lead + rest)
        if k < 2:
            point(6 + k)

    if gather is not None:
        @pl.when(step > 0)
        def _():
            pl.semaphore_wait(credit, 1)

        swap().start()

    @pl.when(step == last)
    def _():
        def one(i, total):
            r = dres_ref[at(i), :]
            out_ref[at(i), :] = acc_o[at(i), :].astype(BF16)
            dn = acc_n[at(i), :]
            s = lax.rsqrt(jnp.mean(r * r, axis=1, keepdims=True) + EPSILON)
            e = dn * gain_ref[...]
            inner = jnp.mean(e * r, axis=1, keepdims=True)
            dr = cot_ref[at(i), :].astype(F32) + s * e - r * (s * s * s * inner)
            dres_ref[at(i), :] = dr
            rlow_ref[at(i), :] = dr.astype(BF16)
            return total + fold(dn * (r * s))

        gain_grad_ref[...] = lax.fori_loop(0, tiles, one, jnp.zeros(gain_grad_ref.shape, F32))
        settle(steps - 1)
        clear(steps - 1)
        if gather is not None:
            gather.drain()


def back_part(
    ltiles, tiles, point, rlow_ref, wo_ref, mixl_ref, mixs_ref, gp_ref, st_ref, pr_ref, sin_ref,
    dp_ref, pc_ref, dwo_ref, gl_ref, tot_ref, rch_ref, end_ref, bias_ref, dm_ref,
):
    point(0)
    lrows = ltiles * TILE
    width = gp_ref.shape[1]
    rlow = rlow_ref[...]
    dm_ref[...] = dot_nt(rlow, flat(wo_ref[...]))
    grad = dot_tn(mixl_ref[...], rlow_ref[0:lrows, :]) + dot_tn(mixs_ref[...], rlow_ref[lrows:, :])
    dwo_ref[...] = grad.astype(BF16).reshape(dwo_ref.shape)
    point(1)
    gl_ref[0:HALO, :] = jnp.zeros((HALO, width), BF16)
    last = row_iota((TILE, width)) == TILE - 1

    def local(j, states):
        dm = dm_ref[at(j - 1), :]
        ge, slope = gelu_pair(gp_ref[at(j), :])
        dgate = dm * states * slope
        gl_ref[at(j), :] = dgate.astype(BF16)
        ds = dm * ge
        rate = sigmoid(dp_ref[at(j), :])
        decay = jnp.exp(-pc_ref[C8 : C8 + 1, :] * (0.25 + rate))
        a, b = scan_tile(decay, decay * ds, True)
        return a, b, ds, fold(dgate)

    def short_step(i, carry):
        c, bias = carry
        j = tiles - 1 - i
        a, b, ds, part = local(j, st_ref[at(j), :])
        cs = b + a * c
        tot_ref[at(j), :] = ds + jnp.where(last, c, pltpu.roll(cs, TILE - 1, 0))
        return cs[0:1], bias + part

    _, bias = lax.fori_loop(
        0,
        tiles - 1 - ltiles,
        short_step,
        (jnp.zeros((1, width), F32), jnp.zeros((8, width), F32)),
    )
    point(2)
    s_in = sin_ref[0:1, :]

    def long_step(i, carry):
        c, reach, bias = carry
        j = ltiles - i
        a, b, ds, part = local(j, st_ref[at(j), :] + pr_ref[at(j), :] * s_in)
        cs = b + a * c
        rs = a * reach
        tot_ref[at(j), :] = ds + jnp.where(last, c, pltpu.roll(cs, TILE - 1, 0))
        rch_ref[at(j), :] = jnp.where(last, reach, pltpu.roll(rs, TILE - 1, 0))
        return cs[0:1], rs[0:1], bias + part

    c, reach, bias = lax.fori_loop(
        0, ltiles, long_step, (jnp.zeros((1, width), F32), jnp.ones((1, width), F32), bias)
    )
    end_ref[...] = jnp.concatenate([reach, c, jnp.zeros((6, width), F32)], axis=0)
    bias_ref[...] = bias


def last_part(
    ltiles, tiles, groups, point, exchange, residual, first_ref, x_ref, gain_ref, nm_ref,
    wg_ref, wi_ref, wd_ref, wo_ref, pc_ref, in_ref, dp_ref, ip_ref, st_ref, pr_ref, sin_ref,
    tot_ref, rch_ref, gl_ref, bias_ref, dx_ref, halo_ref, gain_grad_ref, dwg_ref, dwi_ref,
    gg_ref, small_ref, acc, dc_ref, cl_ref, dl_ref, ol_ref, il_ref,
):
    width = in_ref.shape[1]
    step = pl.program_id(0) - groups
    point(0)
    for g in range(groups):

        @pl.when(step == g)
        def _(g=g):
            dc_ref[0:1, :] = exchange.entering(g, True)

    c_in = dc_ref[0:1, :]

    @pl.when(step == groups - 1)
    def _():
        residual.start()

    zero8 = jnp.zeros((8, width), F32)
    cl_ref[0:HALO, :] = jnp.zeros((HALO, width), BF16)
    dl_ref[0:HALO, :] = jnp.zeros((HALO, width), BF16)
    ol_ref[0:HALO, :] = jnp.zeros((HALO, width), BF16)
    dc_ref[0:HALO, :] = jnp.zeros((HALO, width), F32)

    def gate_step(j, states, total, live, carry):
        before, sum_d, sum_o, sum_p = carry
        rows = row_iota((TILE, width))
        prior = jnp.where(rows == 0, before, pltpu.roll(states, 1, 0))
        conv, _ = conv_tile(in_ref, pc_ref, j, live)
        rate, opening, decay, square = gates(
            dp_ref[at(j), :], ip_ref[at(j), :], pc_ref[C8 : C8 + 1, :]
        )
        inv = lax.rsqrt(square)
        mult = square * inv
        weighted = total * opening
        d_open = total * mult * conv
        d_log = decay * (total * prior - (weighted * conv) * (decay * inv))
        d_rate = -pc_ref[C8 : C8 + 1, :] * d_log
        d_dp = d_rate * (rate - rate * rate)
        d_ip = d_open * (opening - opening * opening)
        cl_ref[at(j), :] = conv.astype(BF16)
        dl_ref[at(j), :] = d_dp.astype(BF16)
        ol_ref[at(j), :] = d_ip.astype(BF16)
        dc_ref[at(j), :] = weighted * mult
        return (
            states[TILE - 1 : TILE],
            sum_d + fold(d_dp),
            sum_o + fold(d_ip),
            sum_p - fold((0.25 + rate) * d_log),
        )

    s_in = sin_ref[0:1, :]

    def long_step(i, carry):
        j = 1 + i
        states = st_ref[at(j), :] + pr_ref[at(j), :] * s_in
        total = tot_ref[at(j), :] + rch_ref[at(j), :] * c_in
        return gate_step(j, states, total, 1.0, carry)

    def short_step(i, carry):
        j = 1 + ltiles + i
        return gate_step(j, st_ref[at(j), :], tot_ref[at(j), :], jnp.where(i == 0, 0.0, 1.0), carry)

    carry = lax.fori_loop(0, ltiles, long_step, (s_in, zero8, zero8, zero8))
    carry = lax.fori_loop(
        0, tiles - 1 - ltiles, short_step, (jnp.zeros((1, width), F32),) + carry[1:]
    )
    _, sum_d, sum_o, sum_p = carry
    point(1)

    low, dlow, olow = cl_ref[...], dl_ref[...], ol_ref[...]
    half = width // 2
    for which, grads in ((0, dlow), (1, olow)):
        product = dot_tn(low, grads).astype(BF16)
        gg_ref[which, 0] = product[:half, :half]
        gg_ref[which, 1] = product[half:, half:]
    dc_ref[...] += dot_nt(dlow, wd_ref[0]) + dot_nt(olow, wo_ref[0])

    point(2)

    def conv_step(j, carry):
        sum_c, sum_i, sums = carry
        live = jnp.where(j == 1 + ltiles, 0.0, 1.0)
        cur = dc_ref[at(j), :]
        up = jnp.where((j == ltiles) | (j == tiles - 1), 0.0, 1.0)
        later = dc_ref[at(jnp.minimum(j + 1, tiles - 1)), :] * up
        _, moved = conv_tile(in_ref, pc_ref, jnp.maximum(j, 1), live)
        d_in = pc_ref[CW : CW + 1, :] * cur
        for k in range(1, 4):
            d_in = d_in + pc_ref[CW + k : CW + k + 1, :] * shift_up(cur, later, k)
        d_in = d_in * jnp.where(j == 0, first_ref[0, 0], 1.0)
        il_ref[at(j), :] = d_in.astype(BF16)
        return (
            sum_c + fold(cur),
            sum_i + fold(d_in),
            tuple(s + fold(cur * m) for s, m in zip(sums, moved)),
        )

    sum_c, sum_i, sums = lax.fori_loop(0, tiles, conv_step, (zero8, zero8, (zero8,) * 4))
    parts = [sum_i, *sums, sum_c, sum_d, sum_o, sum_p * pc_ref[S8 : S8 + 1, :], bias_ref[...]]
    rows = [jnp.sum(p, axis=0, keepdims=True) for p in parts]
    small_ref[...] = jnp.concatenate(rows + [jnp.zeros((16 - len(rows), width), F32)], axis=0)

    point(3)
    nm = nm_ref[...]
    dwi_ref[...] = dot_tn(il_ref[...], nm).astype(BF16).reshape(dwi_ref.shape)
    dwg_ref[...] = dot_tn(gl_ref[...], nm).astype(BF16).reshape(dwg_ref.shape)
    point(4)
    part = dot_nn(gl_ref[...], flat(wg_ref[...])) + dot_nn(il_ref[...], flat(wi_ref[...]))

    @pl.when(step == 0)
    def _():
        acc[...] = part

    @pl.when(step > 0)
    def _():
        acc[...] += part

    @pl.when(step == groups - 1)
    def _():
        residual.wait()

        def norm_back(j):
            v = x_ref[at(j), :].astype(F32)
            dn = acc[at(j), :]
            s = lax.rsqrt(jnp.mean(v * v, axis=1, keepdims=True) + EPSILON)
            e = dn * gain_ref[...]
            inner = jnp.mean(e * v, axis=1, keepdims=True)
            return s * e - v * (s * s * s * inner), fold(dn * (v * s))

        halo, total = norm_back(0)
        halo_ref[...] = halo

        def one(i, total):
            d, part = norm_back(1 + i)
            dx_ref[at(i), :] = dx_ref[at(i), :] + d
            return total + part

        gain_grad_ref[...] = lax.fori_loop(0, tiles - 1, one, total)

    point(5)


class Exchange:
    def __init__(self, mine, theirs, ssem, rsem):
        self.mine, self.theirs, self.ssem, self.rsem = mine, theirs, ssem, rsem
        self.count = lax.axis_size("seq")
        self.place = lax.axis_index("seq")

    def peer(self, k):
        return (lax.rem(self.place + k, self.count), lax.axis_index("row"))

    def go(self, g, act):
        for k in range(1, self.count):
            act(
                remote(
                    self.mine.at[g],
                    self.theirs.at[g, self.place],
                    self.ssem.at[g, k - 1],
                    self.rsem.at[g, k - 1],
                    self.peer(k),
                )
            )

    def start(self, g):
        self.go(g, lambda d: d.start())

    def entering(self, g, reverse):
        self.go(g, lambda d: d.wait_recv())
        state = jnp.zeros((1, self.mine.shape[-1]), F32)
        for hop in range(self.count - 1):
            source = self.count - 1 - hop if reverse else hop
            ahead = source > self.place if reverse else source < self.place
            reach = self.theirs[g, source, 0:1, :]
            drive = self.theirs[g, source, 1:2, :]
            state = jnp.where(ahead, reach * state + drive, state)
        return state

    def drain(self, groups):
        for g in range(groups):
            self.go(g, lambda d: d.wait_send())


def exchange_scratch(groups, width, count):
    links = pltpu.SemaphoreType.DMA((groups, count - 1))
    return [
        pltpu.VMEM((groups, 8, width), F32),
        pltpu.VMEM((groups, count, 8, width), F32),
        links, links,
    ]


def meet_all(exchange, zcount):
    place, row = exchange.place, lax.axis_index("row")
    everyone = [exchange.peer(k) for k in range(1, exchange.count)]
    everyone += [(place, lax.rem(row + k, zcount)) for k in range(1, zcount)]
    barrier = pltpu.get_barrier_semaphore()
    for peer in everyone:
        pl.semaphore_signal(barrier, inc=1, device_id=peer, device_id_type=pl.DeviceIdType.MESH)
    pl.semaphore_wait(barrier, len(everyone))


def tail_kernel(ltiles, tiles, groups, links, *refs):
    (
        first_ref, x_ref, gain_ref, nm_ref, dres_hbm, rlow_ref, w_ref, wg_ref, wi_ref, wd_ref,
        wo_ref, pc_ref, mixl_ref, mixs_ref, gp_ref, in_ref, dp_ref, ip_ref, st_ref, pr_ref, sin_ref,
    ) = refs[:21]
    refs = refs[21:]
    step = pl.program_id(0)
    group = lax.rem(step, groups)
    back_point, last_point, scatter = no_point, no_point, None
    if links is not None:
        zcount, chunks, lags, plan = links
        halved = (refs[-9], None, *refs[-8:-5])
        scatter = Scatter(
            zcount, [refs[0]], refs[9:12], [None, None, None, halved], refs[-5:], chunks, lags
        )
        refs = refs[1:9] + refs[12:-9]
        back_point = in_turn(scatter, step, plan[:groups])
        last_point = in_turn(scatter, step, plan[groups:], groups)
    dx_ref, halo_ref, gain_grad_ref, dwo_ref, dwg_ref, dwi_ref, gg_ref, small_ref = refs[:8]
    (
        acc, dc_ref, cl_ref, dl_ref, ol_ref, il_ref, gls, tots, rchs, bias_ref, dsem, *swap
    ) = refs[8:]
    exchange = Exchange(*swap)
    gl_ref, tot_ref, rch_ref = gls.at[group], tots.at[group], rchs.at[group]
    residual = pltpu.make_async_copy(dres_hbm, dx_ref, dsem)
    width = gp_ref.shape[1]

    @pl.when(step == 0)
    def _():
        meet_all(exchange, 1 if scatter is None else zcount)

    @pl.when(step < groups)
    def _():
        back_part(
            ltiles, tiles, back_point, rlow_ref, w_ref, mixl_ref, mixs_ref, gp_ref, st_ref, pr_ref,
            sin_ref, dp_ref, pc_ref, dwo_ref, gl_ref, tot_ref, rch_ref, exchange.mine.at[group],
            bias_ref.at[group], acc.at[0 : rlow_ref.shape[0], 0:width],
        )
        for g in range(groups):

            @pl.when(step == g)
            def _(g=g):
                exchange.theirs[g, exchange.place] = jnp.zeros(exchange.theirs.shape[2:], F32)
                exchange.start(g)

    @pl.when(step >= groups)
    def _():
        last_part(
            ltiles, tiles, groups, last_point, exchange, residual, first_ref, x_ref, gain_ref, nm_ref,
            wg_ref, wi_ref, wd_ref, wo_ref, pc_ref, in_ref, dp_ref, ip_ref, st_ref, pr_ref, sin_ref,
            tot_ref, rch_ref, gl_ref, bias_ref.at[group], dx_ref, halo_ref, gain_grad_ref, dwg_ref,
            dwi_ref, gg_ref, small_ref, acc, dc_ref, cl_ref, dl_ref, ol_ref, il_ref,
        )

    @pl.when(step == pl.num_programs(0) - 1)
    def _():
        exchange.drain(groups)
        if scatter is not None:
            scatter.drain()


def shape_of(shape, dtype):
    return jax.ShapeDtypeStruct(shape, dtype)


def whole(shape):
    return pl.BlockSpec(shape, lambda g: (0,) * len(shape), pipeline_mode=pl.Buffered(1))


def kept(shape):
    return pl.BlockSpec(shape, lambda g: (0,) * len(shape))


def columns(rows, width):
    return pl.BlockSpec((rows, width), lambda g: (0, g))


def params(limit, **more):
    return pltpu.CompilerParams(
        dimension_semantics=("arbitrary",), vmem_limit_bytes=int(limit * MIB), **more
    )


def pair_blocks(weight):
    blocks, width, _ = weight.shape
    pairs = weight.reshape(blocks // 2, 2, width, width)
    zero = jnp.zeros_like(pairs[:, 0])
    top = jnp.concatenate([pairs[:, 0], zero], axis=2)
    low = jnp.concatenate([zero, pairs[:, 1]], axis=2)
    return jnp.concatenate([top, low], axis=1)


def to_slots(parts, count):
    rows = parts[0].shape[0]
    depth = parts[0].shape[1]
    got = lax.all_gather(jnp.concatenate(parts, axis=0), ("seq", "row"), axis=0, tiled=False)
    if count != SLOTS:
        got = got.reshape(count, len(parts), rows, depth).transpose(1, 0, 2, 3)
        got = got.reshape(len(parts), SLOTS, rows * count // SLOTS, depth).transpose(1, 0, 2, 3)
    return got.reshape(SLOTS, -1, depth)


def scatter_slots(grads, number, count):
    slots, rows, depth = grads.shape
    if count != SLOTS:
        grads = grads.reshape(slots, number, rows // number, depth).transpose(1, 0, 2, 3)
        grads = grads.reshape(number, count, -1, depth).transpose(1, 0, 2, 3)
    flat_grads = grads.reshape(slots * rows, depth)
    own = lax.psum_scatter(flat_grads, ("seq", "row"), scatter_dimension=0, tiled=True)
    own = own.astype(F32).reshape(number, -1, depth)
    return [own[i] for i in range(number)]


def entering(ends, reverse):
    count = lax.axis_size("seq")
    place = lax.axis_index("seq")
    got = lax.all_gather(ends, "seq")
    state = jnp.zeros_like(ends[0])
    for hop in range(count - 1):
        source = count - 1 - hop if reverse else hop
        ahead = source > place if reverse else source < place
        state = jnp.where(ahead, got[source, 0] * state + got[source, 1], state)
    return jnp.broadcast_to(state[None], (8, state.shape[0]))


def hop(value, axis, steps):
    count = lax.axis_size(axis)
    first, last = (max(0, -steps), min(count, count - steps))
    return lax.ppermute(value, axis, [(source, source + steps) for source in range(first, last)])


def shards(
    long_tokens,
    short_tokens,
    long_length,
    long_cotangent,
    short_cotangent,
    first_gain,
    gate_weight,
    gate_bias,
    input_weight,
    input_bias,
    conv_weight,
    conv_bias,
    decay_gate_weight,
    decay_gate_bias,
    input_gate_weight,
    input_gate_bias,
    decay_param,
    out_weight,
    second_gain,
    mlp_gate_weight,
    mlp_up_weight,
    mlp_down_weight,
):
    count = lax.axis_size("seq") * lax.axis_size("row")
    lrows, srows, depth = long_tokens.shape[1], short_tokens.shape[1], long_tokens.shape[2]
    chans = gate_bias.shape[0]
    units = mlp_gate_weight.shape[1] * count
    tokens = lrows + srows
    total = HALO + tokens
    ltiles, tiles = lrows // TILE, total // TILE
    cshare, ushare = chans // SLOTS, units // SLOTS
    groups = 4
    width = chans // groups
    per = SLOTS // groups

    long_x = long_tokens.reshape(lrows, depth)
    halo_x = hop(long_x[lrows - HALO :], "seq", 1)
    pair_own = [gate_weight.T, input_weight.T]
    mlp_own = [mlp_gate_weight.T, mlp_up_weight.T, mlp_down_weight]
    zcount = lax.axis_size("row")
    fast = lax.axis_size("seq") == 8 and count == SLOTS
    hbm = pl.BlockSpec(memory_space=pl.ANY)
    if fast:
        (pairw,) = gather_call([jnp.concatenate(pair_own, axis=0)], zcount)
        hshare = mlp_own[0].shape[0] // 2
        mlp_first, mlp_second = [
            jnp.concatenate([w[h * hshare : (h + 1) * hshare] for w in mlp_own]) for h in range(2)
        ]
        front_own = [out_weight, mlp_first]
        front_chunks = row_chunks(front_own, 16)
        lags = (2, 2, 3, 2)
        plan = spread_out(len(front_chunks) + sum(lags) + 1, 2, 4, 4)
        front_links = (zcount, front_chunks, lags, plan, len(front_own))
        front_extra = dict(
            specs=[hbm] * 2,
            shapes=[gathered(w, zcount) for w in front_own],
            scratch=gather_sems(len(front_chunks), zcount),
            params=dict(collective_id=2, has_side_effects=True),
        )
    else:
        pairw = to_slots(pair_own, count)
        outw = to_slots([out_weight], count)
        mlpw = to_slots(mlp_own, count).reshape(GRID + (3, 2, -1, depth))
        w_first, w_second = [mlpw[..., h, :, :].reshape(GRID + (-1, depth)) for h in range(2)]
        front_own, front_links = [], None
        front_extra = dict(specs=[], shapes=[], scratch=[], params={})
    pairw = pairw.reshape(SLOTS, -1, depth)
    x = jnp.concatenate([halo_x, long_x, short_tokens.reshape(srows, depth)], axis=0)
    place = lax.axis_index("seq")
    first = jnp.where(place > 0, 1.0, 0.0).astype(F32).reshape(1, 1)
    positions = place * lrows + jnp.arange(lrows, dtype=jnp.int32)
    keep = positions[:, None] < long_length[0]
    masked = jnp.where(keep, long_cotangent.reshape(lrows, depth), jnp.zeros((), BF16))
    cot = jnp.concatenate([masked, short_cotangent.reshape(srows, depth)], axis=0)
    chan = jnp.concatenate(
        [
            jnp.stack([gate_bias, input_bias]),
            conv_weight,
            jnp.stack(
                [
                    conv_bias,
                    decay_gate_bias,
                    input_gate_bias,
                    8.0 * jax.nn.softplus(decay_param),
                    8.0 * jax.nn.sigmoid(decay_param),
                ]
            ),
            jnp.zeros((5, chans), F32),
        ],
        axis=0,
    )
    pair_d = pair_blocks(decay_gate_weight)
    pair_o = pair_blocks(input_gate_weight)
    gain1 = first_gain[None]
    gain2 = second_gain[None]
    scalar = pl.BlockSpec(memory_space=pltpu.SMEM)

    def mix_part(which):
        return pl.BlockSpec((per, cshare, depth), lambda g: (g, which, 0))

    pair_spec = pl.BlockSpec((1, width, width), lambda g: (g, 0, 0))
    col = columns(total, width)
    col_long = columns(HALO + lrows, width)
    pc_spec = columns(16, width)
    col8 = columns(8, width)

    wide = shape_of((total, chans), F32)
    narrow = shape_of((HALO + lrows, chans), F32)
    gp, inner, dp, ip, states, reach, mix_s, ends, normed, *wide_w = pl.pallas_call(
        functools.partial(front_kernel, ltiles, tiles, front_links),
        grid=(groups,),
        in_specs=[
            scalar, whole((total, depth)), whole((1, depth)), mix_part(0), mix_part(1),
            pair_spec, pair_spec, pc_spec, *front_extra["specs"],
        ],
        out_specs=[
            col, col, col, col, col, col_long, columns(srows, width), col8,
            kept((total, depth)), *front_extra["specs"],
        ],
        out_shape=[
            wide, wide, wide, wide, wide, narrow, shape_of((srows, chans), BF16),
            shape_of((8, chans), F32), shape_of((total, depth), BF16), *front_extra["shapes"],
        ],
        scratch_shapes=[
            pltpu.VMEM((total, width), F32), pltpu.VMEM((total, width), BF16),
            *front_extra["scratch"],
        ],
        compiler_params=params(48, **front_extra["params"]),
        name="front",
    )(first, x, gain1, pairw, pairw, pair_d, pair_o, chan, *front_own)
    if fast:
        outw, w_first = wide_w
        outw = outw.reshape(SLOTS, -1, depth)

    s_in = entering(ends[0:2], False)

    steps = 4
    hid = units // steps
    block = GRID[1:] + (3 * ushare // 2, depth)
    wbuf = pltpu.VMEM((2,) + block, BF16)
    dwbuf = pltpu.VMEM(block, BF16)
    one_dma = pltpu.SemaphoreType.DMA
    if fast:
        chunks = row_chunks([mlp_second], 16)
        waves = len(chunks) + sum(lags) + 1
        plan = spread_out(waves, 3, 3, 8)
        mlp_links = (zcount, chunks, lags, plan)
        w_last, more_specs, more_shapes = mlp_second, [hbm], [gathered(mlp_second, zcount)]
        half_block = (block[0],) + block[2:]
        more_scratch = [
            pltpu.VMEM(half_block, BF16), one_dma((2,)), pltpu.SemaphoreType.REGULAR,
            *gather_sems(len(chunks), zcount),
        ]
        dw_shape = (2, 2) + half_block
        more_params = dict(collective_id=3, has_side_effects=True)
    else:
        mlp_links, w_last, more_specs, more_shapes, more_scratch = None, w_second, [], [], []
        dw_shape, more_params = (2, 2) + block, {}
    out, d_res, rlow, mix_l, gain2_grad, dmlp, *_ = pl.pallas_call(
        functools.partial(mlp_kernel, ltiles, tokens // TILE, mlp_links),
        grid=(steps,),
        in_specs=[
            whole((total, depth)), whole((tokens, depth)), whole((HALO + lrows, chans)),
            whole((HALO + lrows, chans)), whole((HALO + lrows, chans)), whole((8, chans)),
            whole((srows, chans)), whole((SLOTS, cshare, depth)), whole((1, depth)), hbm, hbm,
        ],
        out_specs=[
            whole((tokens, depth)), whole((tokens, depth)), whole((tokens, depth)),
            whole((lrows, chans)), whole((8, depth)), hbm, *more_specs,
        ],
        out_shape=[
            shape_of((tokens, depth), BF16), shape_of((tokens, depth), F32),
            shape_of((tokens, depth), BF16), shape_of((lrows, chans), BF16),
            shape_of((8, depth), F32), shape_of(dw_shape, BF16), *more_shapes,
        ],
        scratch_shapes=[
            pltpu.VMEM((tokens, depth), BF16), pltpu.VMEM((tokens, depth), F32),
            pltpu.VMEM((tokens, depth), F32), pltpu.VMEM((tokens, hid), F32),
            pltpu.VMEM((tokens, hid), F32), pltpu.VMEM((tokens, hid), F32),
            pltpu.VMEM((tokens, hid), BF16), pltpu.VMEM((tokens, hid), BF16),
            pltpu.VMEM((tokens, hid), BF16), wbuf, dwbuf, one_dma((2,)), one_dma, *more_scratch,
        ],
        compiler_params=params(62, **more_params),
        name="mlp",
    )(x, cot, states, reach, gp, s_in, mix_s, outw, gain2, w_first, w_last)

    slot_shape = shape_of((SLOTS, cshare, depth), BF16)
    blocks, bwidth = decay_gate_weight.shape[0:2]

    def early(g):
        return jnp.minimum(g, groups - 1)

    def late(g):
        return jnp.maximum(g - groups, 0)

    def both_times(g):
        return lax.rem(g, groups)

    def slot_at(when, which=0):
        return pl.BlockSpec((per, cshare, depth), lambda g: (when(g), which, 0))

    def pair_at(when):
        return pl.BlockSpec((1, width, width), lambda g: (when(g), 0, 0))

    def cols_at(nrows, when):
        return pl.BlockSpec((nrows, width), lambda g: (0, when(g)))

    tail_links, tail_in, tail_specs, tail_shapes, tail_scratch, tail_params = None, [], [], [], [], {}
    if fast:
        size = 16
        tail_chunks = []
        for h in range(2):
            for start in range(0, 3 * ushare // 2, size):
                k, offset = divmod(start, ushare // 2)
                tail_chunks.append(
                    (HALVED, len(tail_chunks) % TAIL_SLOTS, 0, h, (start, size), k, h * (ushare // 2) + offset)
                )
        tail_lags = (1, 2, 2, 2)
        marks = [[5.0 * g + t for t in (0.0, 1.5, 4.0)] for g in range(groups)]
        marks += [
            [5.0 * groups + 12.5 * g + t for t in (0.0, 5.0, 6.0, 9.0, 10.5, 12.5)] for g in range(groups)
        ]
        plan = paced(len(tail_chunks) + sum(tail_lags) + 1, 3, marks)
        tail_links = (zcount, tail_chunks, tail_lags, plan)
        tail_in, tail_specs = [dmlp], [hbm]
        tail_shapes = [shape_of((ushare, depth), F32)] * 3
        lone = five(TAIL_SLOTS, (size, depth), BF16, zcount)
        links = one_dma((len(tail_chunks), zcount + 2))
        tail_scratch = [lone[0], *lone[2:], one_dma((len(tail_chunks),)), links, links, links, links]
    d_x, d_halo, gain1_grad, d_out, d_gate, d_input, d_gates, small, *mlp_grads = pl.pallas_call(
        functools.partial(tail_kernel, ltiles, tiles, groups, tail_links),
        grid=(2 * groups,),
        in_specs=[
            scalar, whole((total, depth)), whole((1, depth)), whole((total, depth)), hbm,
            whole((tokens, depth)), slot_at(early), slot_at(late, 0), slot_at(late, 1),
            pair_at(late), pair_at(late), cols_at(16, both_times), cols_at(lrows, early),
            cols_at(srows, early), cols_at(total, early), cols_at(total, late),
            cols_at(total, both_times), cols_at(total, late), cols_at(total, both_times),
            cols_at(HALO + lrows, both_times), cols_at(8, both_times), *tail_specs,
        ],
        out_specs=[
            whole((tokens, depth)), whole((HALO, depth)), whole((8, depth)), slot_at(early),
            slot_at(late), slot_at(late),
            pl.BlockSpec((2, 2, bwidth, bwidth), lambda g: (0, late(g), 0, 0)), cols_at(16, late),
            *[whole(t.shape) for t in tail_shapes],
        ],
        out_shape=[
            shape_of((tokens, depth), F32), shape_of((HALO, depth), F32), shape_of((8, depth), F32),
            slot_shape, slot_shape, slot_shape, shape_of((2, blocks, bwidth, bwidth), BF16),
            shape_of((16, chans), F32), *tail_shapes,
        ],
        scratch_shapes=[
            pltpu.VMEM((total, depth), F32), pltpu.VMEM((total, width), F32),
            pltpu.VMEM((total, width), BF16), pltpu.VMEM((total, width), BF16),
            pltpu.VMEM((total, width), BF16), pltpu.VMEM((total, width), BF16),
            pltpu.VMEM((groups, total, width), BF16), pltpu.VMEM((groups, total, width), F32),
            pltpu.VMEM((groups, HALO + lrows, width), F32), pltpu.VMEM((groups, 8, width), F32),
            one_dma, *exchange_scratch(groups, width, lax.axis_size("seq")), *tail_scratch,
        ],
        compiler_params=params(63, collective_id=4, has_side_effects=True),
        name="tail",
    )(
        first, x, gain1, normed, d_res, rlow, outw, pairw, pairw, pair_d, pair_o, chan, mix_l, mix_s,
        gp, inner, dp, ip, states, reach, s_in, *tail_in,
    )

    ahead = hop(d_halo, "seq", -1)
    long_grad = d_x[:lrows].at[lrows - HALO :].add(ahead)
    short_grad = d_x[lrows:]

    lanes = 2048
    gains = jnp.stack([jnp.sum(gain1_grad, axis=0), jnp.sum(gain2_grad, axis=0)])
    small = jnp.concatenate(
        [
            jnp.pad(small[0:10], ((0, 0), (0, lanes - chans))),
            jnp.pad(gains, ((0, 0), (0, lanes - depth))),
            jnp.zeros((4, lanes), F32),
        ],
        axis=0,
    )
    if fast:
        mains = [d_gate, d_input, d_out]
        tiled = small.reshape(2, 8, lanes // 128, 128).transpose(0, 2, 1, 3)
        shares = scatter_call(
            mains, d_gates.reshape(SLOTS, -1, bwidth), tiled.reshape(SLOTS, 8, 128), zcount
        )
        g_gate, g_input, g_out, gate_sums, sums = shares
        g_mgate, g_mup, g_down = mlp_grads
        gate_sums = gate_sums.reshape(d_gates.shape)
        sums = sums.reshape(2, lanes // 128, 8, 128).transpose(0, 2, 1, 3).reshape(16, lanes)
    else:
        dmlp = dmlp.reshape(2, SLOTS, 3, -1, depth).transpose(1, 2, 0, 3, 4)
        g_mgate, g_mup, g_down = scatter_slots(dmlp.reshape(SLOTS, -1, depth), 3, count)
        dmix = jnp.concatenate([d_gate, d_input, d_out], axis=1)
        g_gate, g_input, g_out = scatter_slots(dmix, 3, count)
        gate_sums, sums = lax.psum((d_gates.astype(F32), small), ("seq", "row"))
    gate_sums = gate_sums.astype(F32)
    rows = sums[0:10, :chans]
    return (
        out[:lrows].reshape(long_tokens.shape),
        out[lrows:].reshape(short_tokens.shape),
        long_grad.reshape(long_tokens.shape),
        short_grad.reshape(short_tokens.shape),
        sums[10, :depth],
        g_gate.T,
        rows[9],
        g_input.T,
        rows[0],
        rows[1:5],
        rows[5],
        gate_sums[0],
        rows[6],
        gate_sums[1],
        rows[7],
        rows[8],
        g_out,
        sums[11, :depth],
        g_mgate.T,
        g_mup.T,
        g_down,
    )


def solution(mesh):
    both = ("seq", "row")
    long_spec = P("row", "seq", None)
    short_spec = P(both, None, None)
    cols = P(None, both)
    rows = P(both, None)
    return jax.shard_map(
        shards,
        mesh=mesh,
        in_specs=(
            long_spec, short_spec, P("row"), long_spec, short_spec, P(), cols, P(), cols, P(),
            P(), P(), P(), P(), P(), P(), P(), rows, P(), cols, cols, rows,
        ),
        out_specs=(
            long_spec, short_spec, long_spec, short_spec, P(), cols, P(), cols, P(), P(), P(),
            P(), P(), P(), P(), P(), rows, P(), cols, cols, rows,
        ),
        check_vma=False,
    )
```

```python
import functools

import jax
import jax.numpy as jnp
from jax import lax
from jax.experimental import pallas as pl
from jax.experimental.pallas import tpu as pltpu
from jax.sharding import PartitionSpec as P

EPSILON = 1e-06
F32 = jnp.float32
BF16 = jnp.bfloat16
GRID = (2, 2, 2, 4)
SLOTS = 32
TILE = 16
HALO = 16
MIB = 1024 * 1024
TAIL_SLOTS = 10
CORE_SLOTS = 5
GELU_A = 0.7978845608028654
GELU_B = 0.044715


def dot_nn(a, b):
    return lax.dot_general(a, b, (((1,), (0,)), ((), ())), preferred_element_type=F32)


def dot_nt(a, b):
    return lax.dot_general(a, b, (((1,), (1,)), ((), ())), preferred_element_type=F32)


def dot_tn(a, b):
    return lax.dot_general(a, b, (((0,), (0,)), ((), ())), preferred_element_type=F32)


def sigmoid(v):
    return 0.5 * jnp.tanh(0.5 * v) + 0.5


def gelu(v):
    t = jnp.tanh(v * (GELU_A + (GELU_A * GELU_B) * (v * v)))
    h = 0.5 * v
    return h + h * t


def gelu_pair(v):
    w = v * v
    t = jnp.tanh(v * (GELU_A + (GELU_A * GELU_B) * w))
    h = 0.5 * v
    slope = 0.5 + 0.5 * t + (h - h * (t * t)) * (GELU_A + (3.0 * GELU_A * GELU_B) * w)
    return h + h * t, slope


def row_iota(shape):
    return lax.broadcasted_iota(jnp.int32, shape, 0)


def at(j):
    return pl.ds(pl.multiple_of(j * TILE, TILE), TILE)


def scan_tile(a, b, reverse):
    rows = row_iota(a.shape)
    step = 1
    while step < TILE:
        if reverse:
            keep, shift = rows < TILE - step, TILE - step
        else:
            keep, shift = rows >= step, step
        b = jnp.where(keep, a * pltpu.roll(b, shift, 0) + b, b)
        a = jnp.where(keep, a * pltpu.roll(a, shift, 0), a)
        step *= 2
    return a, b


def shift_down(cur, prev, k):
    if k == 0:
        return cur
    rows = row_iota(cur.shape)
    return jnp.where(rows < k, pltpu.roll(prev, k, 0), pltpu.roll(cur, k, 0))


def shift_up(cur, later, k):
    if k == 0:
        return cur
    rows = row_iota(cur.shape)
    return jnp.where(
        rows >= TILE - k, pltpu.roll(later, TILE - k, 0), pltpu.roll(cur, TILE - k, 0)
    )


def fold(v):
    return v[0:8] + v[8:16]


def flat(block):
    return block.reshape(-1, block.shape[-1])


def gates(dp, ip, c8):
    rate = sigmoid(dp)
    opening = sigmoid(ip)
    log_decay = -c8 * (0.25 + rate)
    decay = jnp.exp(log_decay)
    square = -jnp.tanh(log_decay) * (1.0 + decay * decay)
    return rate, opening, decay, square


GB, IB, CW, CB, DB, OB, C8, S8 = 0, 1, 2, 6, 7, 8, 9, 10


def conv_tile(in_ref, pc_ref, j, live):
    cur = in_ref[at(j), :]
    prev = in_ref[at(j - 1), :] * live
    out = pc_ref[CB : CB + 1, :] + pc_ref[CW : CW + 1, :] * cur
    moved = [cur]
    for k in range(1, 4):
        m = shift_down(cur, prev, k)
        moved.append(m)
        out = out + pc_ref[CW + k : CW + k + 1, :] * m
    return out, moved


def place_of():
    s = lax.axis_index("seq")
    return s // 4, (s // 2) % 2, s % 2, lax.axis_index("row")


def device_at(y, x, c, z):
    return ((y * 2 + x) * 2 + c, z)


class Peers:
    def __init__(self, zcount):
        y, x, c, z = self.place = place_of()
        self.far = [(z + k) % zcount for k in range(1, zcount)]
        self.along = [device_at(y, x, c, q) for q in self.far]
        self.near = ((y + c) % 2, (x + 1 - c) % 2)
        self.first = device_at(*self.near, c, z)
        self.second = device_at((y + 1 - c) % 2, (x + c) % 2, c, z)
        self.other = device_at(y, x, 1 - c, z)

    def meet(self):
        everyone = [*self.along, self.first, self.second, self.other]
        barrier = pltpu.get_barrier_semaphore()
        for peer in everyone:
            pl.semaphore_signal(
                barrier, inc=1, device_id=peer, device_id_type=pl.DeviceIdType.MESH
            )
        pl.semaphore_wait(barrier, len(everyone))


def remote(source, target, send, recv, device):
    return pltpu.make_async_remote_copy(
        src_ref=source,
        dst_ref=target,
        send_sem=send,
        recv_sem=recv,
        device_id=device,
        device_id_type=pl.DeviceIdType.MESH,
    )


class Spread:
    def __init__(self, peers, own, full, send, recv):
        self.peers, self.own, self.full, self.send, self.recv = peers, own, full, send, recv

    def go(self, stage, act):
        y, x, c, z = self.peers.place
        p, full = self.peers, self.full
        if stage == 0:
            for k, device in enumerate(p.along):
                act(remote(self.own, full(y, x, c, z), self.send(k), self.recv(k), device))
            return
        k = len(p.along) + stage - 1
        if stage == 2:

            @pl.when(c == 0)
            def _():
                part = full(y, slice(None), c, slice(None))
                act(remote(part, part, self.send(k), self.recv(k), p.second))

            @pl.when(c == 1)
            def _():
                part = full(slice(None), x, c, slice(None))
                act(remote(part, part, self.send(k), self.recv(k), p.second))

            return
        if stage == 1:
            part, device = full(y, x, c, slice(None)), p.first
        else:
            part, device = full(slice(None), slice(None), c, slice(None)), p.other
        act(remote(part, part, self.send(k), self.recv(k), device))

    def start(self, stage):
        self.go(stage, lambda d: d.start())

    def arrive(self, stage):
        self.go(stage, lambda d: d.wait_recv())

    def drain(self):
        for stage in range(4):
            self.go(stage, lambda d: d.wait_send())


def wave_of(t, count, lags):
    for stage in range(len(lags), -1, -1):
        piece = t - sum(lags[:stage])
        if 0 <= piece < count:
            yield piece, stage


class Gather:
    def __init__(self, zcount, ins, outs, sems, chunks, lags):
        self.csem, self.ssem, self.rsem = sems
        self.peers = Peers(zcount)
        self.lags = lags
        y, x, c, z = self.peers.place
        self.spreads, self.copies = [], []
        for i, (which, start, size) in enumerate(chunks):
            rows = pl.ds(start, size)
            own = ins[which].at[rows]

            def full(a, b, d, e, ref=outs[which], rows=rows):
                return ref.at[a, b, d, e, rows]

            def send(k, i=i):
                return self.ssem.at[i, k]

            def recv(k, i=i):
                return self.rsem.at[i, k]

            self.spreads.append(Spread(self.peers, own, full, send, recv))
            self.copies.append(pltpu.make_async_copy(own, full(y, x, c, z), self.csem.at[i]))
        self.waves = len(chunks) + sum(lags) + 1

    def wave(self, t):
        for i, stage in wave_of(t, len(self.spreads), self.lags):
            if stage == 0:
                self.copies[i].start()
            elif stage == 1:
                self.copies[i].wait()
            if stage > 0:
                self.spreads[i].arrive(stage - 1)
            if stage < 4:
                self.spreads[i].start(stage)

    def drain(self):
        for spread in self.spreads:
            spread.drain()


def in_turn(weave, step, plan, first=0):
    def point(k):
        for s, points in enumerate(plan, first):
            if k < len(points) and points[k]:

                @pl.when(step == s)
                def _(todo=points[k]):
                    for t in todo:
                        weave.wave(t)

    return point


def spread_out(waves, ahead, steps, points):
    todo = list(range(waves))
    plan = []
    for s in range(steps):
        row = []
        for k in range(points):
            take = ahead if s == 0 and k == 0 else 1
            if s == steps - 1 and k == points - 1:
                take = len(todo)
            row.append(todo[:take])
            todo = todo[take:]
        plan.append(row)
    return plan


def paced(waves, ahead, marks):
    last = marks[-1][-1]
    plan = [[[] for _ in row] for row in marks]
    spots = [(t, s, k) for s, row in enumerate(marks) for k, t in enumerate(row)]
    for w in range(waves):
        due = last * max(0, w - ahead) / max(1, waves - ahead)
        _, s, k = next(spot for spot in spots if spot[0] >= due)
        plan[s][k].append(w)
    return plan


def row_chunks(parts, size):
    return [
        (which, start, size)
        for which, part in enumerate(parts)
        for start in range(0, part.shape[0], size)
    ]


def gather_sems(count, zcount):
    links = pltpu.SemaphoreType.DMA((count, zcount + 2))
    return [pltpu.SemaphoreType.DMA((count,)), links, links]


def gathered(part, zcount):
    return jax.ShapeDtypeStruct((2, 2, 2, zcount) + part.shape, part.dtype)


def gather_kernel(zcount, chunks, lags, number, *refs):
    gather = Gather(zcount, refs[:number], refs[number : 2 * number], refs[2 * number :], chunks, lags)
    gather.peers.meet()
    for t in range(gather.waves):
        gather.wave(t)
    gather.drain()


def gather_call(parts, zcount):
    chunks = row_chunks(parts, 16)
    hbm = pl.BlockSpec(memory_space=pl.ANY)
    return pl.pallas_call(
        functools.partial(gather_kernel, zcount, chunks, (2, 2, 3, 2), len(parts)),
        out_shape=[gathered(p, zcount) for p in parts],
        in_specs=[hbm] * len(parts),
        out_specs=[hbm] * len(parts),
        scratch_shapes=gather_sems(len(chunks), zcount),
        compiler_params=pltpu.CompilerParams(collective_id=0, has_side_effects=True),
        name="gather",
    )(*parts)


CORE, GATES, SUMS, HALVED = 0, 1, 2, 3


class Scatter:
    def __init__(self, zcount, ins, outs, buffers, sems, chunks, lags):
        self.peers = Peers(zcount)
        self.zcount, self.chunks, self.lags = zcount, chunks, lags
        self.ins, self.outs, self.buffers = ins, outs, buffers
        self.csem, self.ssem, self.rsem = sems[:3]
        self.pieces = [Piece(self, i, sems[3:], *chunk) for i, chunk in enumerate(chunks)]
        self.waves = len(chunks) + sum(lags) + 1

    def wave(self, t):
        for i, stage in wave_of(t, len(self.pieces), self.lags):
            if stage <= 4 or self.pieces[i].spread is not None:
                self.pieces[i].step(stage)

    def drain(self):
        for piece in self.pieces:
            piece.drain()


def slot_of_core(i, slots):
    return i % slots


def add_into(into, i, part, j):
    into[i] = (into[i].astype(F32) + part[j].astype(F32)).astype(into.dtype)


class Piece:
    def __init__(self, owner, i, sems, kind, slot, which, source, span, target, place):
        self.o, self.i, self.kind, self.slot = owner, i, kind, slot
        self.a, self.r0, self.r1, self.r2, self.r3 = owner.buffers[kind]
        self.from_core = 0 if self.r0 is None else slot_of_core(i, self.r0.shape[0])
        self.source, self.lead, self.rows = owner.ins[which], source, pl.ds(*span)
        self.target, self.place = owner.outs[target], place
        self.spread, self.drained = None, False
        if kind in (GATES, SUMS):
            y, x, c, z = owner.peers.place

            def full(*at_place):
                return self.target.at[at_place]

            def send(k):
                return sems[0].at[i, k]

            def recv(k):
                return sems[1].at[i, k]

            self.spread = Spread(owner.peers, full(y, x, c, z), full, send, recv)

    def local(self):
        c = self.o.peers.place[2]
        if self.kind == HALVED:
            mine = self.source.at[self.lead, :, :, :, self.rows]
        else:
            mine = self.source.at[:, :, c, :, self.rows]
        return pltpu.make_async_copy(mine, self.a.at[self.slot], self.o.csem.at[self.i])

    def send(self, stage, act):
        s, peers = self.slot, self.o.peers
        y, x, c, z = peers.place

        def go(source, target, k, device):
            act(remote(source, target, self.o.ssem.at[self.i, k], self.o.rsem.at[self.i, k], device))

        if stage == 0:
            if self.kind != HALVED:
                theirs = self.source.at[:, :, 1 - c, :, self.rows]
                go(theirs, self.r0.at[self.from_core], 0, peers.other)
        elif stage == 1:

            @pl.when(c == 0)
            def _():
                go(self.a.at[s, 1 - y], self.r1.at[s], 1, peers.second)

            @pl.when(c == 1)
            def _():
                go(self.a.at[s, :, 1 - x], self.r1.at[s], 1, peers.second)

        elif stage == 2:
            go(self.a.at[(s, *peers.near)], self.r2.at[s], 2, peers.first)
        else:
            for k, device in enumerate(peers.along):
                go(self.a.at[s, y, x, peers.far[k]], self.r3.at[s, k], 3 + k, device)

    def step(self, stage):
        s, zcount = self.slot, self.o.zcount
        y, x, c, z = self.o.peers.place
        if stage == 0:
            for earlier in self.o.pieces[: self.i]:
                if earlier.a is self.a and earlier.slot == s:
                    earlier.drain()
            self.local().start()
        elif stage <= 4:
            self.send(stage - 1, lambda d: d.wait_recv())
        else:
            self.spread.arrive(stage - 5)
        if stage == 1:
            self.local().wait()
            if self.kind != HALVED:

                @pl.loop(0, 4 * zcount)
                def _(q):
                    i = (q // (2 * zcount), (q // zcount) % 2, q % zcount)
                    add_into(self.a, (s, *i), self.r0, (self.from_core, *i))

        elif stage == 2:

            @pl.loop(0, 2 * zcount)
            def _(q):
                h = q // zcount
                i = (s, y * (1 - c) + h * c, h * (1 - c) + x * c, q % zcount)
                add_into(self.a, i, self.r1, (s, h, q % zcount))

        elif stage == 3:

            @pl.loop(0, zcount)
            def _(q):
                add_into(self.a, (s, y, x, q), self.r2, (s, q))

        elif stage == 4:
            total = self.a[s, y, x, z].astype(F32)
            for k in range(zcount - 1):
                total = total + self.r3[s, k].astype(F32)
            if self.spread is None:
                self.target[self.place : self.place + total.shape[0]] = total
            else:
                self.target[y, x, c, z] = total.astype(self.target.dtype)
        if stage < 4:
            self.send(stage, lambda d: d.start())
        elif stage < 8 and self.spread is not None:
            self.spread.start(stage - 4)

    def drain(self):
        if self.drained:
            return
        self.drained = True
        for stage in range(4):
            self.send(stage, lambda d: d.wait_send())
        if self.spread is not None:
            self.spread.drain()


def five(number, shape, dtype, zcount):
    lead = [(2, 2, zcount), (2, 2, zcount), (2, zcount), (zcount,), (zcount - 1,)]
    return [pltpu.VMEM((number, *d, *shape), dtype) for d in lead]


def no_point(k):
    pass


def front_kernel(ltiles, tiles, links, *refs):
    (
        first_ref, x_ref, gain_ref, wg_ref, wi_ref, wd_ref, wo_ref, pc_ref
    ) = refs[:8]
    refs = refs[8:]
    point, gather = no_point, None
    step = pl.program_id(0)
    if links is not None:
        zcount, chunks, lags, plan, number = links
        gather = Gather(
            zcount, refs[:number], refs[number + 9 : 2 * number + 9], refs[2 * number + 11 :], chunks, lags
        )
        refs = refs[number : number + 9] + refs[2 * number + 9 : 2 * number + 11]
        point = in_turn(gather, step, plan)
    gp_ref, in_ref, dp_ref, ip_ref, st_ref, pr_ref, mix_ref, end_ref, nm_ref, cv_ref, cl_ref = refs

    @pl.when(step == 0)
    def _():
        if gather is not None:
            gather.peers.meet()

    point(0)

    @pl.when(step == 0)
    def _():
        @pl.loop(0, tiles)
        def _(j):
            v = x_ref[at(j), :].astype(F32)
            s = lax.rsqrt(jnp.mean(v * v, axis=1, keepdims=True) + EPSILON)
            nm_ref[at(j), :] = (v * s * gain_ref[...]).astype(BF16)

    nm = nm_ref[...]
    gp_ref[...] = dot_nt(nm, flat(wg_ref[...])) + pc_ref[GB : GB + 1, :]
    in_ref[...] = dot_nt(nm, flat(wi_ref[...])) + pc_ref[IB : IB + 1, :]
    point(1)
    in_ref[0:HALO, :] = in_ref[0:HALO, :] * first_ref[0, 0]
    cl_ref[0:HALO, :] = jnp.zeros((HALO, cl_ref.shape[1]), BF16)

    @pl.loop(1, tiles)
    def _(j):
        live = jnp.where(j == 1 + ltiles, 0.0, 1.0)
        out, _ = conv_tile(in_ref, pc_ref, j, live)
        cv_ref[at(j), :] = out
        cl_ref[at(j), :] = out.astype(BF16)

    point(2)
    low = cl_ref[...]
    dp_ref[...] = dot_nn(low, wd_ref[0]) + pc_ref[DB : DB + 1, :]
    ip_ref[...] = dot_nn(low, wo_ref[0]) + pc_ref[OB : OB + 1, :]

    def scanned(j):
        _, opening, a, square = gates(dp_ref[at(j), :], ip_ref[at(j), :], pc_ref[C8 : C8 + 1, :])
        b = (square * lax.rsqrt(square)) * opening * cv_ref[at(j), :]
        return scan_tile(a, b, False)

    width = gp_ref.shape[1]

    def long_step(i, carry):
        state, reach = carry
        a, b = scanned(1 + i)
        s = b + a * state
        r = a * reach
        st_ref[at(1 + i), :] = s
        pr_ref[at(1 + i), :] = r
        return s[TILE - 1 : TILE], r[TILE - 1 : TILE]

    state, reach = lax.fori_loop(
        0, ltiles, long_step, (jnp.zeros((1, width), F32), jnp.ones((1, width), F32))
    )
    end_ref[...] = jnp.concatenate([reach, state, jnp.zeros((6, width), F32)], axis=0)

    def short_step(i, state):
        j = 1 + ltiles + i
        a, b = scanned(j)
        s = b + a * state
        st_ref[at(j), :] = s
        mix_ref[at(i), :] = (s * gelu(gp_ref[at(j), :])).astype(BF16)
        return s[TILE - 1 : TILE]

    lax.fori_loop(0, tiles - 1 - ltiles, short_step, jnp.zeros((1, width), F32))
    point(3)
    if gather is not None:

        @pl.when(step == pl.num_programs(0) - 1)
        def _():
            gather.drain()


def mlp_kernel(ltiles, tiles, links, *refs):
    (
        x_ref, cot_ref, st_ref, pr_ref, gp_ref, sin_ref, mixs_ref, wo_ref, gain_ref, w1_ref, w2_ref
    ) = refs[:11]
    refs = refs[11:]
    point, gather = no_point, None
    step = pl.program_id(0)
    last = pl.num_programs(0) - 1
    out_ref, dres_ref, rlow_ref, mixl_ref, gain_grad_ref, dw_hbm = refs[:6]
    refs = refs[6:]
    if links is not None:
        zcount, chunks, lags, plan = links
        own_ref, w2_ref = w2_ref, refs[0]
        gather = Gather(zcount, [own_ref], [w2_ref], refs[-3:], chunks, lags)
        got_ref, sems, credit = refs[-6], refs[-5], refs[-4]
        refs = refs[1:-6]
        point = in_turn(gather, step, plan)
    (
        n2_ref, acc_o, acc_n, g_ref, u_ref, d_ref, h_ref, dg_ref, du_ref, wbuf, dwbuf, wsem, dsem
    ) = refs
    lrows = ltiles * TILE
    half = g_ref.shape[1] // 2
    share = wbuf.shape[-2] // 3
    steps = 2 * GRID[0]

    def load(s):
        source = w1_ref if s < steps // 2 else w2_ref
        return pltpu.make_async_copy(
            source.at[s % (steps // 2)], wbuf.at[s % 2], wsem.at[s % 2]
        )

    def each(todo, first=0):
        for s in range(first, steps):

            @pl.when(step == s)
            def _(s=s):
                todo(s)

    if gather is not None:
        y, x, c, z = gather.peers.place

    def store(s):
        h, q = s // (steps // 2), s % (steps // 2)
        mine = dwbuf if gather is None else dwbuf.at[:, c]
        return pltpu.make_async_copy(mine, dw_hbm.at[h, q], dsem)

    def swap():
        return remote(
            dwbuf.at[:, 1 - c], got_ref, sems.at[0], sems.at[1], gather.peers.other
        )

    def settle(s):
        if gather is not None:
            swap().wait_recv()

            @pl.loop(0, got_ref.shape[0] * got_ref.shape[1])
            def _(k):
                i, j = k // got_ref.shape[1], k % got_ref.shape[1]
                both = dwbuf[i, c, j].astype(F32) + got_ref[i, j].astype(F32)
                dwbuf[i, c, j] = both.astype(BF16)

            if s < steps - 1:
                pl.semaphore_signal(
                    credit,
                    inc=1,
                    device_id=gather.peers.other,
                    device_id_type=pl.DeviceIdType.MESH,
                )
        store(s).start()

    def clear(s):
        store(s).wait()
        if gather is not None:
            swap().wait_send()

    @pl.when(step == 0)
    def _():
        load(0).start()
        load(1).start()
        if gather is not None:
            gather.peers.meet()

    point(0)

    @pl.when(step == 0)
    def _():
        s_in = sin_ref[0:1, :]

        @pl.loop(0, ltiles)
        def _(i):
            s = st_ref[at(1 + i), :] + pr_ref[at(1 + i), :] * s_in
            mixl_ref[at(i), :] = (s * gelu(gp_ref[at(1 + i), :])).astype(BF16)

        wo = flat(wo_ref[...])
        dres_ref[0:lrows, :] = dot_nn(mixl_ref[...], wo)
        dres_ref[lrows:, :] = dot_nn(mixs_ref[...], wo)

        @pl.loop(0, tiles)
        def _(i):
            r = dres_ref[at(i), :] + x_ref[at(1 + i), :].astype(F32)
            dres_ref[at(i), :] = r
            acc_o[at(i), :] = r
            s = lax.rsqrt(jnp.mean(r * r, axis=1, keepdims=True) + EPSILON)
            n2_ref[at(i), :] = (r * s * gain_ref[...]).astype(BF16)

        acc_n[...] = jnp.zeros_like(acc_n)

    point(1)

    @pl.when(step == steps // 2)
    def _():
        load(steps // 2).start()
        load(steps // 2 + 1).start()

    each(lambda s: load(s).wait())
    slot = lax.rem(step, 2)
    n2 = n2_ref[...]
    wg = flat(wbuf[slot, ..., 0:share, :])
    wu = flat(wbuf[slot, ..., share : 2 * share, :])
    wd = flat(wbuf[slot, ..., 2 * share :, :])
    g_ref[...] = dot_nt(n2, wg)
    u_ref[...] = dot_nt(n2, wu)
    point(2)
    d_ref[...] = dot_nt(cot_ref[...], wd)
    each(lambda s: settle(s - 1), 1)
    point(3)

    @pl.loop(0, tiles)
    def _(i):
        for k in range(2):
            cols = slice(k * half, (k + 1) * half)
            ge, slope = gelu_pair(g_ref[at(i), cols])
            u = u_ref[at(i), cols]
            d = d_ref[at(i), cols]
            h_ref[at(i), cols] = (ge * u).astype(BF16)
            dg_ref[at(i), cols] = (d * u * slope).astype(BF16)
            du_ref[at(i), cols] = (d * ge).astype(BF16)

    point(4)
    acc_o[...] += dot_nn(h_ref[...], wd)
    acc_n[...] += dot_nn(dg_ref[...], wg) + dot_nn(du_ref[...], wu)
    point(5)
    each(lambda s: clear(s - 1), 1)
    lead = dwbuf.shape[:-2]
    rest = (share, dwbuf.shape[-1])
    for k, (left, right) in enumerate(((dg_ref, n2_ref), (du_ref, n2_ref), (h_ref, cot_ref))):
        grad = dot_tn(left[...], right[...]).astype(BF16)
        dwbuf[..., k * share : (k + 1) * share, :] = grad.reshape(lead + rest)
        if k < 2:
            point(6 + k)

    if gather is not None:
        @pl.when(step > 0)
        def _():
            pl.semaphore_wait(credit, 1)

        swap().start()

    @pl.when(step == last)
    def _():
        def one(i, total):
            r = dres_ref[at(i), :]
            out_ref[at(i), :] = acc_o[at(i), :].astype(BF16)
            dn = acc_n[at(i), :]
            s = lax.rsqrt(jnp.mean(r * r, axis=1, keepdims=True) + EPSILON)
            e = dn * gain_ref[...]
            inner = jnp.mean(e * r, axis=1, keepdims=True)
            dr = cot_ref[at(i), :].astype(F32) + s * e - r * (s * s * s * inner)
            dres_ref[at(i), :] = dr
            rlow_ref[at(i), :] = dr.astype(BF16)
            return total + fold(dn * (r * s))

        gain_grad_ref[...] = lax.fori_loop(0, tiles, one, jnp.zeros(gain_grad_ref.shape, F32))
        settle(steps - 1)
        clear(steps - 1)
        if gather is not None:
            gather.drain()


def back_part(
    ltiles, tiles, point, rlow_ref, wo_ref, mixl_ref, mixs_ref, gp_ref, st_ref, pr_ref, sin_ref,
    dp_ref, pc_ref, dwo_ref, gl_ref, tot_ref, rch_ref, end_ref, bias_ref, dm_ref, free,
):
    point(0)
    lrows = ltiles * TILE
    width = gp_ref.shape[1]
    rlow = rlow_ref[...]
    dm_ref[...] = dot_nt(rlow, flat(wo_ref[...]))
    free()
    grad = dot_tn(mixl_ref[...], rlow_ref[0:lrows, :]) + dot_tn(mixs_ref[...], rlow_ref[lrows:, :])
    dwo_ref[...] = grad.astype(BF16).reshape(dwo_ref.shape)
    point(1)
    gl_ref[0:HALO, :] = jnp.zeros((HALO, width), BF16)
    last = row_iota((TILE, width)) == TILE - 1

    def local(j, states):
        dm = dm_ref[at(j - 1), :]
        ge, slope = gelu_pair(gp_ref[at(j), :])
        dgate = dm * states * slope
        gl_ref[at(j), :] = dgate.astype(BF16)
        ds = dm * ge
        rate = sigmoid(dp_ref[at(j), :])
        decay = jnp.exp(-pc_ref[C8 : C8 + 1, :] * (0.25 + rate))
        a, b = scan_tile(decay, decay * ds, True)
        return a, b, ds, fold(dgate)

    def short_step(i, carry):
        c, bias = carry
        j = tiles - 1 - i
        a, b, ds, part = local(j, st_ref[at(j), :])
        cs = b + a * c
        tot_ref[at(j), :] = ds + jnp.where(last, c, pltpu.roll(cs, TILE - 1, 0))
        return cs[0:1], bias + part

    _, bias = lax.fori_loop(
        0,
        tiles - 1 - ltiles,
        short_step,
        (jnp.zeros((1, width), F32), jnp.zeros((8, width), F32)),
    )
    point(2)
    s_in = sin_ref[0:1, :]

    def long_step(i, carry):
        c, reach, bias = carry
        j = ltiles - i
        a, b, ds, part = local(j, st_ref[at(j), :] + pr_ref[at(j), :] * s_in)
        cs = b + a * c
        rs = a * reach
        tot_ref[at(j), :] = ds + jnp.where(last, c, pltpu.roll(cs, TILE - 1, 0))
        rch_ref[at(j), :] = jnp.where(last, reach, pltpu.roll(rs, TILE - 1, 0))
        return cs[0:1], rs[0:1], bias + part

    c, reach, bias = lax.fori_loop(
        0, ltiles, long_step, (jnp.zeros((1, width), F32), jnp.ones((1, width), F32), bias)
    )
    end_ref[...] = jnp.concatenate([reach, c, jnp.zeros((6, width), F32)], axis=0)
    bias_ref[...] = bias


def last_part(
    ltiles, tiles, groups, point, exchange, residual, first_ref, x_ref, gain_ref, nm_ref,
    wg_ref, wi_ref, wd_ref, wo_ref, pc_ref, in_ref, dp_ref, ip_ref, st_ref, pr_ref, sin_ref,
    tot_ref, rch_ref, gl_ref, bias_ref, dx_ref, halo_ref, gain_grad_ref, dwg_ref, dwi_ref,
    gg_ref, small_ref, acc, dc_ref, cl_ref, dl_ref, ol_ref, il_ref, gain2_ref, free, keep,
):
    width = in_ref.shape[1]
    step = pl.program_id(0) - groups
    point(0)
    for g in range(groups):

        @pl.when(step == g)
        def _(g=g):
            dc_ref[0:1, :] = exchange.entering(g, True)

    c_in = dc_ref[0:1, :]

    @pl.when(step == groups - 1)
    def _():
        residual.start()

    zero8 = jnp.zeros((8, width), F32)
    cl_ref[0:HALO, :] = jnp.zeros((HALO, width), BF16)
    dl_ref[0:HALO, :] = jnp.zeros((HALO, width), BF16)
    ol_ref[0:HALO, :] = jnp.zeros((HALO, width), BF16)
    dc_ref[0:HALO, :] = jnp.zeros((HALO, width), F32)

    def gate_step(j, states, total, live, carry):
        before, sum_d, sum_o, sum_p = carry
        rows = row_iota((TILE, width))
        prior = jnp.where(rows == 0, before, pltpu.roll(states, 1, 0))
        conv, _ = conv_tile(in_ref, pc_ref, j, live)
        rate, opening, decay, square = gates(
            dp_ref[at(j), :], ip_ref[at(j), :], pc_ref[C8 : C8 + 1, :]
        )
        inv = lax.rsqrt(square)
        mult = square * inv
        weighted = total * opening
        d_open = total * mult * conv
        d_log = decay * (total * prior - (weighted * conv) * (decay * inv))
        d_rate = -pc_ref[C8 : C8 + 1, :] * d_log
        d_dp = d_rate * (rate - rate * rate)
        d_ip = d_open * (opening - opening * opening)
        cl_ref[at(j), :] = conv.astype(BF16)
        dl_ref[at(j), :] = d_dp.astype(BF16)
        ol_ref[at(j), :] = d_ip.astype(BF16)
        dc_ref[at(j), :] = weighted * mult
        return (
            states[TILE - 1 : TILE],
            sum_d + fold(d_dp),
            sum_o + fold(d_ip),
            sum_p - fold((0.25 + rate) * d_log),
        )

    s_in = sin_ref[0:1, :]

    def long_step(i, carry):
        j = 1 + i
        states = st_ref[at(j), :] + pr_ref[at(j), :] * s_in
        total = tot_ref[at(j), :] + rch_ref[at(j), :] * c_in
        return gate_step(j, states, total, 1.0, carry)

    def short_step(i, carry):
        j = 1 + ltiles + i
        return gate_step(j, st_ref[at(j), :], tot_ref[at(j), :], jnp.where(i == 0, 0.0, 1.0), carry)

    carry = lax.fori_loop(0, ltiles, long_step, (s_in, zero8, zero8, zero8))
    carry = lax.fori_loop(
        0, tiles - 1 - ltiles, short_step, (jnp.zeros((1, width), F32),) + carry[1:]
    )
    _, sum_d, sum_o, sum_p = carry
    point(1)

    low, dlow, olow = cl_ref[...], dl_ref[...], ol_ref[...]
    half = width // 2
    for which, grads in ((0, dlow), (1, olow)):
        product = dot_tn(low, grads).astype(BF16)
        shape = (2, half // 2, half)
        place = (which, step // 2, lax.rem(step, 2))
        gg_ref[(*place, slice(0, 2))] = product[:half, :half].reshape(shape)
        gg_ref[(*place, slice(2, 4))] = product[half:, half:].reshape(shape)
    dc_ref[...] += dot_nt(dlow, wd_ref[0]) + dot_nt(olow, wo_ref[0])

    point(2)

    def conv_step(j, carry):
        sum_c, sum_i, sums = carry
        live = jnp.where(j == 1 + ltiles, 0.0, 1.0)
        cur = dc_ref[at(j), :]
        up = jnp.where((j == ltiles) | (j == tiles - 1), 0.0, 1.0)
        later = dc_ref[at(jnp.minimum(j + 1, tiles - 1)), :] * up
        _, moved = conv_tile(in_ref, pc_ref, jnp.maximum(j, 1), live)
        d_in = pc_ref[CW : CW + 1, :] * cur
        for k in range(1, 4):
            d_in = d_in + pc_ref[CW + k : CW + k + 1, :] * shift_up(cur, later, k)
        d_in = d_in * jnp.where(j == 0, first_ref[0, 0], 1.0)
        il_ref[at(j), :] = d_in.astype(BF16)
        return (
            sum_c + fold(cur),
            sum_i + fold(d_in),
            tuple(s + fold(cur * m) for s, m in zip(sums, moved)),
        )

    sum_c, sum_i, sums = lax.fori_loop(0, tiles, conv_step, (zero8, zero8, (zero8,) * 4))
    parts = [sum_i, *sums, sum_c, sum_d, sum_o, sum_p * pc_ref[S8 : S8 + 1, :], bias_ref[...]]
    rows = [jnp.sum(p, axis=0, keepdims=True) for p in parts]
    block = jnp.concatenate(rows + [jnp.zeros((16 - len(rows), width), F32)], axis=0)
    for i in range(width // 128):
        at_block = step * (width // 128) + i
        x, c, z = at_block // 8, lax.rem(at_block // 4, 2), lax.rem(at_block, 4)
        for h in range(2):
            small_ref[h, x, c, z] = block[8 * h : 8 * h + 8, 128 * i : 128 * i + 128]

    point(3)
    free()
    nm = nm_ref[...]
    dwi_ref[...] = dot_tn(il_ref[...], nm).astype(BF16).reshape(dwi_ref.shape)
    dwg_ref[...] = dot_tn(gl_ref[...], nm).astype(BF16).reshape(dwg_ref.shape)
    keep()
    point(4)
    part = dot_nn(gl_ref[...], flat(wg_ref[...])) + dot_nn(il_ref[...], flat(wi_ref[...]))

    @pl.when(step == 0)
    def _():
        acc[...] = part

    @pl.when(step > 0)
    def _():
        acc[...] += part

    @pl.when(step == groups - 1)
    def _():
        residual.wait()

        def norm_back(j):
            v = x_ref[at(j), :].astype(F32)
            dn = acc[at(j), :]
            s = lax.rsqrt(jnp.mean(v * v, axis=1, keepdims=True) + EPSILON)
            e = dn * gain_ref[...]
            inner = jnp.mean(e * v, axis=1, keepdims=True)
            return s * e - v * (s * s * s * inner), fold(dn * (v * s))

        halo, total = norm_back(0)
        halo_ref[...] = halo

        def one(i, total):
            d, part = norm_back(1 + i)
            dx_ref[at(i), :] = dx_ref[at(i), :] + d
            return total + part

        gain_grad_ref[...] = lax.fori_loop(0, tiles - 1, one, total)
        zero = jnp.zeros((8, 128), F32)
        for h in range(2):
            for z in range(4):
                small_ref[h, 1, 1, z] = zero
        for z, ref in enumerate((gain_grad_ref, gain2_ref)):
            total = jnp.sum(ref[...], axis=0, keepdims=True)
            for i in range(8):
                small_ref[0, 1, 1, z, i : i + 1, :] = total[:, 128 * i : 128 * i + 128]

    point(5)


class Exchange:
    def __init__(self, mine, theirs, ssem, rsem):
        self.mine, self.theirs, self.ssem, self.rsem = mine, theirs, ssem, rsem
        self.count = lax.axis_size("seq")
        self.place = lax.axis_index("seq")

    def peer(self, k):
        return (lax.rem(self.place + k, self.count), lax.axis_index("row"))

    def go(self, g, act):
        for k in range(1, self.count):
            act(
                remote(
                    self.mine.at[g],
                    self.theirs.at[g, self.place],
                    self.ssem.at[g, k - 1],
                    self.rsem.at[g, k - 1],
                    self.peer(k),
                )
            )

    def start(self, g):
        self.go(g, lambda d: d.start())

    def entering(self, g, reverse):
        self.go(g, lambda d: d.wait_recv())
        state = jnp.zeros((1, self.mine.shape[-1]), F32)
        for hop in range(self.count - 1):
            source = self.count - 1 - hop if reverse else hop
            ahead = source > self.place if reverse else source < self.place
            reach = self.theirs[g, source, 0:1, :]
            drive = self.theirs[g, source, 1:2, :]
            state = jnp.where(ahead, reach * state + drive, state)
        return state

    def drain(self, groups):
        for g in range(groups):
            self.go(g, lambda d: d.wait_send())


def exchange_scratch(groups, width, count):
    links = pltpu.SemaphoreType.DMA((groups, count - 1))
    return [
        pltpu.VMEM((groups, 8, width), F32),
        pltpu.VMEM((groups, count, 8, width), F32),
        links, links,
    ]


def meet_all(exchange, zcount):
    place, row = exchange.place, lax.axis_index("row")
    everyone = [exchange.peer(k) for k in range(1, exchange.count)]
    everyone += [(place, lax.rem(row + k, zcount)) for k in range(1, zcount)]
    barrier = pltpu.get_barrier_semaphore()
    for peer in everyone:
        pl.semaphore_signal(barrier, inc=1, device_id=peer, device_id_type=pl.DeviceIdType.MESH)
    pl.semaphore_wait(barrier, len(everyone))


def tail_kernel(ltiles, tiles, groups, links, *refs):
    (
        first_ref, x_ref, gain_ref, nm_ref, dres_hbm, rlow_ref, w_ref, wg_ref, wi_ref, wd_ref,
        wo_ref, pc_ref, mixl_ref, mixs_ref, gp_ref, in_ref, dp_ref, ip_ref, st_ref, pr_ref, sin_ref,
    ) = refs[:21]
    gain2_ref = refs[21]
    refs = refs[22:]
    step = pl.program_id(0)
    group = lax.rem(step, groups)
    back_point, last_point, scatter = no_point, no_point, None
    nscratch = 19
    if links is not None:
        zcount, chunks, lags, plan = links
        halved_ref, refs = refs[0], refs[1:]
        outs, shares = refs[:8], refs[8:14]
        scratch, pool = refs[14 : 14 + nscratch], refs[14 + nscratch :]
    else:
        outs, scratch = refs[:8], refs[8:]
    dx_ref, halo_ref, gain_grad_ref, dwo_hbm, dwg_hbm, dwi_hbm, gates_hbm, sums_hbm = outs
    (
        acc, dc_ref, cl_ref, dl_ref, ol_ref, il_ref, gls, tots, rchs, bias_ref, wst, gsrc, ssrc,
        dsem, wsem, *swap
    ) = scratch
    gates_full, sums_full = gsrc, ssrc
    if links is not None:
        *pool, gates_full, sums_full = pool
        main, gate_pool, sum_pool = pool[0:5], pool[5:10], pool[10:15]
        scatter = Scatter(
            zcount,
            [halved_ref, dwo_hbm, dwg_hbm, dwi_hbm, gsrc, ssrc],
            [*shares, gates_full, sums_full],
            [main, gate_pool, sum_pool, main],
            pool[15:],
            chunks,
            lags,
        )
        back_point = in_turn(scatter, step, plan[:groups])
        last_point = in_turn(scatter, step, plan[groups:], groups)

    def stash(g, k, target):
        return pltpu.make_async_copy(wst.at[k], target.at[g // 2, g % 2], wsem.at[k])

    def stashed(first, what):
        for g in range(groups):

            @pl.when(step == first + g)
            def _(g=g):
                what(g)

    exchange = Exchange(*swap)
    gl_ref, tot_ref, rch_ref = gls.at[group], tots.at[group], rchs.at[group]
    residual = pltpu.make_async_copy(dres_hbm, dx_ref, dsem)
    width = gp_ref.shape[1]

    @pl.when(step == 0)
    def _():
        meet_all(exchange, 1 if scatter is None else zcount)

    @pl.when(step < groups)
    def _():
        back_part(
            ltiles, tiles, back_point, rlow_ref, w_ref, mixl_ref, mixs_ref, gp_ref, st_ref, pr_ref,
            sin_ref, dp_ref, pc_ref, wst.at[0], gl_ref, tot_ref, rch_ref, exchange.mine.at[group],
            bias_ref.at[group], acc.at[0 : rlow_ref.shape[0], 0:width],
            lambda: stashed(0, lambda g: stash(g - 1, 0, dwo_hbm).wait() if g > 0 else None),
        )
        stashed(0, lambda g: stash(g, 0, dwo_hbm).start())
        for g in range(groups):

            @pl.when(step == g)
            def _(g=g):
                exchange.theirs[g, exchange.place] = jnp.zeros(exchange.theirs.shape[2:], F32)
                exchange.start(g)

    @pl.when(step >= groups)
    def _():
        @pl.when(step == groups)
        def _():
            stash(groups - 1, 0, dwo_hbm).wait()

        def before(g):
            if g > 0:
                stash(g - 1, 1, dwg_hbm).wait()
                stash(g - 1, 2, dwi_hbm).wait()

        def after(g):
            stash(g, 1, dwg_hbm).start()
            stash(g, 2, dwi_hbm).start()
            if g == groups - 1:
                stash(g, 1, dwg_hbm).wait()
                stash(g, 2, dwi_hbm).wait()

        last_part(
            ltiles, tiles, groups, last_point, exchange, residual, first_ref, x_ref, gain_ref, nm_ref,
            wg_ref, wi_ref, wd_ref, wo_ref, pc_ref, in_ref, dp_ref, ip_ref, st_ref, pr_ref, sin_ref,
            tot_ref, rch_ref, gl_ref, bias_ref.at[group], dx_ref, halo_ref, gain_grad_ref,
            wst.at[1], wst.at[2], gsrc, ssrc, acc, dc_ref, cl_ref, dl_ref, ol_ref, il_ref, gain2_ref,
            lambda: stashed(groups, before), lambda: stashed(groups, after),
        )

    @pl.when(step == pl.num_programs(0) - 1)
    def _():
        exchange.drain(groups)
        if scatter is not None:
            scatter.drain()
        final = [
            pltpu.make_async_copy(gates_full, gates_hbm, wsem.at[0]),
            pltpu.make_async_copy(sums_full, sums_hbm, wsem.at[1]),
        ]
        for copy in final:
            copy.start()
        for copy in final:
            copy.wait()


def shape_of(shape, dtype):
    return jax.ShapeDtypeStruct(shape, dtype)


def whole(shape):
    return pl.BlockSpec(shape, lambda g: (0,) * len(shape), pipeline_mode=pl.Buffered(1))


def kept(shape):
    return pl.BlockSpec(shape, lambda g: (0,) * len(shape))


def columns(rows, width):
    return pl.BlockSpec((rows, width), lambda g: (0, g))


def params(limit, **more):
    return pltpu.CompilerParams(
        dimension_semantics=("arbitrary",), vmem_limit_bytes=int(limit * MIB), **more
    )


def pair_blocks(weight):
    blocks, width, _ = weight.shape
    pairs = weight.reshape(blocks // 2, 2, width, width)
    zero = jnp.zeros_like(pairs[:, 0])
    top = jnp.concatenate([pairs[:, 0], zero], axis=2)
    low = jnp.concatenate([zero, pairs[:, 1]], axis=2)
    return jnp.concatenate([top, low], axis=1)


def to_slots(parts, count):
    rows = parts[0].shape[0]
    depth = parts[0].shape[1]
    got = lax.all_gather(jnp.concatenate(parts, axis=0), ("seq", "row"), axis=0, tiled=False)
    if count != SLOTS:
        got = got.reshape(count, len(parts), rows, depth).transpose(1, 0, 2, 3)
        got = got.reshape(len(parts), SLOTS, rows * count // SLOTS, depth).transpose(1, 0, 2, 3)
    return got.reshape(SLOTS, -1, depth)


def scatter_slots(grads, number, count):
    slots, rows, depth = grads.shape
    if count != SLOTS:
        grads = grads.reshape(slots, number, rows // number, depth).transpose(1, 0, 2, 3)
        grads = grads.reshape(number, count, -1, depth).transpose(1, 0, 2, 3)
    flat_grads = grads.reshape(slots * rows, depth)
    own = lax.psum_scatter(flat_grads, ("seq", "row"), scatter_dimension=0, tiled=True)
    own = own.astype(F32).reshape(number, -1, depth)
    return [own[i] for i in range(number)]


def entering(ends, reverse):
    count = lax.axis_size("seq")
    place = lax.axis_index("seq")
    got = lax.all_gather(ends, "seq")
    state = jnp.zeros_like(ends[0])
    for hop in range(count - 1):
        source = count - 1 - hop if reverse else hop
        ahead = source > place if reverse else source < place
        state = jnp.where(ahead, got[source, 0] * state + got[source, 1], state)
    return jnp.broadcast_to(state[None], (8, state.shape[0]))


def hop(value, axis, steps):
    count = lax.axis_size(axis)
    first, last = (max(0, -steps), min(count, count - steps))
    return lax.ppermute(value, axis, [(source, source + steps) for source in range(first, last)])


def shards(
    long_tokens,
    short_tokens,
    long_length,
    long_cotangent,
    short_cotangent,
    first_gain,
    gate_weight,
    gate_bias,
    input_weight,
    input_bias,
    conv_weight,
    conv_bias,
    decay_gate_weight,
    decay_gate_bias,
    input_gate_weight,
    input_gate_bias,
    decay_param,
    out_weight,
    second_gain,
    mlp_gate_weight,
    mlp_up_weight,
    mlp_down_weight,
):
    count = lax.axis_size("seq") * lax.axis_size("row")
    lrows, srows, depth = long_tokens.shape[1], short_tokens.shape[1], long_tokens.shape[2]
    chans = gate_bias.shape[0]
    units = mlp_gate_weight.shape[1] * count
    tokens = lrows + srows
    total = HALO + tokens
    ltiles, tiles = lrows // TILE, total // TILE
    cshare, ushare = chans // SLOTS, units // SLOTS
    groups = 4
    width = chans // groups
    per = SLOTS // groups

    long_x = long_tokens.reshape(lrows, depth)
    halo_x = hop(long_x[lrows - HALO :], "seq", 1)
    pair_own = [gate_weight.T, input_weight.T]
    mlp_own = [mlp_gate_weight.T, mlp_up_weight.T, mlp_down_weight]
    zcount = lax.axis_size("row")
    fast = lax.axis_size("seq") == 8 and count == SLOTS
    hbm = pl.BlockSpec(memory_space=pl.ANY)
    if fast:
        (pairw,) = gather_call([jnp.concatenate(pair_own, axis=0)], zcount)
        hshare = mlp_own[0].shape[0] // 2
        mlp_first, mlp_second = [
            jnp.concatenate([w[h * hshare : (h + 1) * hshare] for w in mlp_own]) for h in range(2)
        ]
        front_own = [out_weight, mlp_first]
        front_chunks = row_chunks(front_own, 16)
        lags = (2, 2, 3, 2)
        plan = spread_out(len(front_chunks) + sum(lags) + 1, 2, 4, 4)
        front_links = (zcount, front_chunks, lags, plan, len(front_own))
        front_extra = dict(
            specs=[hbm] * 2,
            shapes=[gathered(w, zcount) for w in front_own],
            scratch=gather_sems(len(front_chunks), zcount),
            params=dict(collective_id=2, has_side_effects=True),
        )
    else:
        pairw = to_slots(pair_own, count)
        outw = to_slots([out_weight], count)
        mlpw = to_slots(mlp_own, count).reshape(GRID + (3, 2, -1, depth))
        w_first, w_second = [mlpw[..., h, :, :].reshape(GRID + (-1, depth)) for h in range(2)]
        front_own, front_links = [], None
        front_extra = dict(specs=[], shapes=[], scratch=[], params={})
    pairw = pairw.reshape(SLOTS, -1, depth)
    x = jnp.concatenate([halo_x, long_x, short_tokens.reshape(srows, depth)], axis=0)
    place = lax.axis_index("seq")
    first = jnp.where(place > 0, 1.0, 0.0).astype(F32).reshape(1, 1)
    positions = place * lrows + jnp.arange(lrows, dtype=jnp.int32)
    keep = positions[:, None] < long_length[0]
    masked = jnp.where(keep, long_cotangent.reshape(lrows, depth), jnp.zeros((), BF16))
    cot = jnp.concatenate([masked, short_cotangent.reshape(srows, depth)], axis=0)
    chan = jnp.concatenate(
        [
            jnp.stack([gate_bias, input_bias]),
            conv_weight,
            jnp.stack(
                [
                    conv_bias,
                    decay_gate_bias,
                    input_gate_bias,
                    8.0 * jax.nn.softplus(decay_param),
                    8.0 * jax.nn.sigmoid(decay_param),
                ]
            ),
            jnp.zeros((5, chans), F32),
        ],
        axis=0,
    )
    pair_d = pair_blocks(decay_gate_weight)
    pair_o = pair_blocks(input_gate_weight)
    gain1 = first_gain[None]
    gain2 = second_gain[None]
    scalar = pl.BlockSpec(memory_space=pltpu.SMEM)

    def mix_part(which):
        return pl.BlockSpec((per, cshare, depth), lambda g: (g, which, 0))

    pair_spec = pl.BlockSpec((1, width, width), lambda g: (g, 0, 0))
    col = columns(total, width)
    col_long = columns(HALO + lrows, width)
    pc_spec = columns(16, width)
    col8 = columns(8, width)

    wide = shape_of((total, chans), F32)
    narrow = shape_of((HALO + lrows, chans), F32)
    gp, inner, dp, ip, states, reach, mix_s, ends, normed, *wide_w = pl.pallas_call(
        functools.partial(front_kernel, ltiles, tiles, front_links),
        grid=(groups,),
        in_specs=[
            scalar, whole((total, depth)), whole((1, depth)), mix_part(0), mix_part(1),
            pair_spec, pair_spec, pc_spec, *front_extra["specs"],
        ],
        out_specs=[
            col, col, col, col, col, col_long, columns(srows, width), col8,
            kept((total, depth)), *front_extra["specs"],
        ],
        out_shape=[
            wide, wide, wide, wide, wide, narrow, shape_of((srows, chans), BF16),
            shape_of((8, chans), F32), shape_of((total, depth), BF16), *front_extra["shapes"],
        ],
        scratch_shapes=[
            pltpu.VMEM((total, width), F32), pltpu.VMEM((total, width), BF16),
            *front_extra["scratch"],
        ],
        compiler_params=params(48, **front_extra["params"]),
        name="front",
    )(first, x, gain1, pairw, pairw, pair_d, pair_o, chan, *front_own)
    if fast:
        outw, w_first = wide_w
        outw = outw.reshape(SLOTS, -1, depth)

    s_in = entering(ends[0:2], False)

    steps = 4
    hid = units // steps
    block = GRID[1:] + (3 * ushare // 2, depth)
    wbuf = pltpu.VMEM((2,) + block, BF16)
    dwbuf = pltpu.VMEM(block, BF16)
    one_dma = pltpu.SemaphoreType.DMA
    if fast:
        chunks = row_chunks([mlp_second], 16)
        waves = len(chunks) + sum(lags) + 1
        plan = spread_out(waves, 3, 3, 8)
        mlp_links = (zcount, chunks, lags, plan)
        w_last, more_specs, more_shapes = mlp_second, [hbm], [gathered(mlp_second, zcount)]
        half_block = (block[0],) + block[2:]
        more_scratch = [
            pltpu.VMEM(half_block, BF16), one_dma((2,)), pltpu.SemaphoreType.REGULAR,
            *gather_sems(len(chunks), zcount),
        ]
        dw_shape = (2, 2) + half_block
        more_params = dict(collective_id=3, has_side_effects=True)
    else:
        mlp_links, w_last, more_specs, more_shapes, more_scratch = None, w_second, [], [], []
        dw_shape, more_params = (2, 2) + block, {}
    out, d_res, rlow, mix_l, gain2_grad, dmlp, *_ = pl.pallas_call(
        functools.partial(mlp_kernel, ltiles, tokens // TILE, mlp_links),
        grid=(steps,),
        in_specs=[
            whole((total, depth)), whole((tokens, depth)), whole((HALO + lrows, chans)),
            whole((HALO + lrows, chans)), whole((HALO + lrows, chans)), whole((8, chans)),
            whole((srows, chans)), whole((SLOTS, cshare, depth)), whole((1, depth)), hbm, hbm,
        ],
        out_specs=[
            whole((tokens, depth)), whole((tokens, depth)), whole((tokens, depth)),
            whole((lrows, chans)), whole((8, depth)), hbm, *more_specs,
        ],
        out_shape=[
            shape_of((tokens, depth), BF16), shape_of((tokens, depth), F32),
            shape_of((tokens, depth), BF16), shape_of((lrows, chans), BF16),
            shape_of((8, depth), F32), shape_of(dw_shape, BF16), *more_shapes,
        ],
        scratch_shapes=[
            pltpu.VMEM((tokens, depth), BF16), pltpu.VMEM((tokens, depth), F32),
            pltpu.VMEM((tokens, depth), F32), pltpu.VMEM((tokens, hid), F32),
            pltpu.VMEM((tokens, hid), F32), pltpu.VMEM((tokens, hid), F32),
            pltpu.VMEM((tokens, hid), BF16), pltpu.VMEM((tokens, hid), BF16),
            pltpu.VMEM((tokens, hid), BF16), wbuf, dwbuf, one_dma((2,)), one_dma, *more_scratch,
        ],
        compiler_params=params(62, **more_params),
        name="mlp",
    )(x, cot, states, reach, gp, s_in, mix_s, outw, gain2, w_first, w_last)

    slot_shape = shape_of((SLOTS, cshare, depth), BF16)
    blocks, bwidth = decay_gate_weight.shape[0:2]

    def early(g):
        return jnp.minimum(g, groups - 1)

    def late(g):
        return jnp.maximum(g - groups, 0)

    def both_times(g):
        return lax.rem(g, groups)

    def slot_at(when, which=0):
        return pl.BlockSpec((per, cshare, depth), lambda g: (when(g), which, 0))

    def pair_at(when):
        return pl.BlockSpec((1, width, width), lambda g: (when(g), 0, 0))

    def cols_at(nrows, when):
        return pl.BlockSpec((nrows, width), lambda g: (0, when(g)))

    gate_shape, sum_shape = GRID + (bwidth // 2, bwidth), GRID + (8, 128)
    grads_shape = shape_of(GRID + (cshare, depth), BF16)
    tail_links, tail_in, tail_specs, tail_shapes, tail_scratch = None, [], [], [], []
    if fast:
        size, hshare = 16, ushare // 2
        tail_chunks = []
        number = 0
        for h in range(2):
            for start in range(0, 3 * hshare, size):
                k, offset = divmod(start, hshare)
                tail_chunks.append(
                    (HALVED, number % TAIL_SLOTS, 0, h, (start, size), k, h * hshare + offset)
                )
                number += 1
        for which in (1, 2, 3):
            if which == 2:
                tail_chunks.append((SUMS, 0, 5, None, (0, 8), 7, 0))
                tail_chunks.append((GATES, 0, 4, None, (0, bwidth // 2), 6, 0))
                during = len(tail_chunks) - 2
            for start in range(0, cshare, size):
                tail_chunks.append(
                    (CORE, number % TAIL_SLOTS, which, None, (start, size), 2 + which, start)
                )
                number += 1
        tail_lags = (1, 2, 2, 2, 1, 1, 1, 1)
        marks = [[5.0 * g + t for t in (0.0, 1.5, 4.0)] for g in range(groups)]
        marks += [
            [5.0 * groups + 12.5 * g + t for t in (0.0, 5.0, 6.0, 9.0, 10.5, 12.5)] for g in range(groups)
        ]
        plan = paced(during, 3, marks)
        plan[-1][-1] += range(during, len(tail_chunks) + sum(tail_lags) + 1)
        tail_links = (zcount, tail_chunks, tail_lags, plan)
        tail_in, tail_specs = [dmlp], [whole((ushare, depth))] * 3 + [whole((cshare, depth))] * 3
        tail_shapes = [shape_of((ushare, depth), F32)] * 3 + [shape_of((cshare, depth), F32)] * 3
        lone = five(TAIL_SLOTS, (size, depth), BF16, zcount)
        lone[1] = five(CORE_SLOTS, (size, depth), BF16, zcount)[1]
        n = len(tail_chunks)
        links = one_dma((n, zcount + 2))
        tail_scratch = [
            *lone,
            *five(1, gate_shape[4:], BF16, zcount),
            *five(1, sum_shape[4:], F32, zcount),
            one_dma((n,)), links, links, links, links,
            pltpu.VMEM(gate_shape, BF16), pltpu.VMEM(sum_shape, F32),
        ]
    d_x, d_halo, _, d_out, d_gate, d_input, gate_sums, sums, *shares = pl.pallas_call(
        functools.partial(tail_kernel, ltiles, tiles, groups, tail_links),
        grid=(2 * groups,),
        in_specs=[
            scalar, whole((total, depth)), whole((1, depth)), whole((total, depth)), hbm,
            whole((tokens, depth)), slot_at(early), slot_at(late, 0), slot_at(late, 1),
            pair_at(late), pair_at(late), cols_at(16, both_times), cols_at(lrows, early),
            cols_at(srows, early), cols_at(total, early), cols_at(total, late),
            cols_at(total, both_times), cols_at(total, late), cols_at(total, both_times),
            cols_at(HALO + lrows, both_times), cols_at(8, both_times), whole((8, depth)),
            *[hbm for _ in tail_in],
        ],
        out_specs=[
            whole((tokens, depth)), whole((HALO, depth)), whole((8, depth)), hbm, hbm, hbm, hbm, hbm,
            *tail_specs,
        ],
        out_shape=[
            shape_of((tokens, depth), F32), shape_of((HALO, depth), F32), shape_of((8, depth), F32),
            grads_shape, grads_shape, grads_shape, shape_of(gate_shape, BF16),
            shape_of(sum_shape, F32), *tail_shapes,
        ],
        scratch_shapes=[
            pltpu.VMEM((total, depth), F32), pltpu.VMEM((total, width), F32),
            pltpu.VMEM((total, width), BF16), pltpu.VMEM((total, width), BF16),
            pltpu.VMEM((total, width), BF16), pltpu.VMEM((total, width), BF16),
            pltpu.VMEM((groups, total, width), BF16), pltpu.VMEM((groups, total, width), F32),
            pltpu.VMEM((groups, HALO + lrows, width), F32), pltpu.VMEM((groups, 8, width), F32),
            pltpu.VMEM((3,) + GRID[2:] + (cshare, depth), BF16), pltpu.VMEM(gate_shape, BF16),
            pltpu.VMEM(sum_shape, F32), one_dma, one_dma((3,)),
            *exchange_scratch(groups, width, lax.axis_size("seq")), *tail_scratch,
        ],
        compiler_params=params(63, collective_id=4, has_side_effects=True),
        name="tail",
    )(
        first, x, gain1, normed, d_res, rlow, outw, pairw, pairw, pair_d, pair_o, chan, mix_l, mix_s,
        gp, inner, dp, ip, states, reach, s_in, gain2_grad, *tail_in,
    )

    ahead = hop(d_halo, "seq", -1)
    long_grad = d_x[:lrows].at[lrows - HALO :].add(ahead)
    short_grad = d_x[lrows:]

    if fast:
        g_mgate, g_mup, g_down, g_out, g_gate, g_input = shares
    else:
        dmlp = dmlp.reshape(2, SLOTS, 3, -1, depth).transpose(1, 2, 0, 3, 4)
        g_mgate, g_mup, g_down = scatter_slots(dmlp.reshape(SLOTS, -1, depth), 3, count)
        dmix = jnp.concatenate([d_gate, d_input, d_out], axis=4).reshape(SLOTS, -1, depth)
        g_gate, g_input, g_out = scatter_slots(dmix, 3, count)
        gate_sums, sums = lax.psum((gate_sums.astype(F32), sums), ("seq", "row"))
    gate_sums = gate_sums.reshape(2, blocks, bwidth, bwidth).astype(F32)
    sums = sums.reshape(2, 16, 8, 128)
    gain_sums = sums[0, 12:14].reshape(2, depth)
    rows = sums.transpose(0, 2, 1, 3).reshape(16, 2048)[0:10, :chans]
    return (
        out[:lrows].reshape(long_tokens.shape),
        out[lrows:].reshape(short_tokens.shape),
        long_grad.reshape(long_tokens.shape),
        short_grad.reshape(short_tokens.shape),
        gain_sums[0],
        g_gate.T,
        rows[9],
        g_input.T,
        rows[0],
        rows[1:5],
        rows[5],
        gate_sums[0],
        rows[6],
        gate_sums[1],
        rows[7],
        rows[8],
        g_out,
        gain_sums[1],
        g_mgate.T,
        g_mup.T,
        g_down,
    )


def solution(mesh):
    both = ("seq", "row")
    long_spec = P("row", "seq", None)
    short_spec = P(both, None, None)
    cols = P(None, both)
    rows = P(both, None)
    return jax.shard_map(
        shards,
        mesh=mesh,
        in_specs=(
            long_spec, short_spec, P("row"), long_spec, short_spec, P(), cols, P(), cols, P(),
            P(), P(), P(), P(), P(), P(), P(), rows, P(), cols, cols, rows,
        ),
        out_specs=(
            long_spec, short_spec, long_spec, short_spec, P(), cols, P(), cols, P(), P(), P(),
            P(), P(), P(), P(), P(), rows, P(), cols, cols, rows,
        ),
        check_vma=False,
    )
```

```python
import functools

import jax
import jax.numpy as jnp
from jax import lax
from jax.experimental import pallas as pl
from jax.experimental.pallas import tpu as pltpu
from jax.sharding import PartitionSpec as P

EPSILON = 1e-06
F32 = jnp.float32
BF16 = jnp.bfloat16
GRID = (2, 2, 2, 4)
SLOTS = 32
TILE = 16
HALO = 16
MIB = 1024 * 1024
TAIL_SLOTS = 10
CORE_SLOTS = 5
GELU_A = 0.7978845608028654
GELU_B = 0.044715


def dot_nn(a, b):
    return lax.dot_general(a, b, (((1,), (0,)), ((), ())), preferred_element_type=F32)


def dot_nt(a, b):
    return lax.dot_general(a, b, (((1,), (1,)), ((), ())), preferred_element_type=F32)


def dot_tn(a, b):
    return lax.dot_general(a, b, (((0,), (0,)), ((), ())), preferred_element_type=F32)


def sigmoid(v):
    return 0.5 * jnp.tanh(0.5 * v) + 0.5


def gelu(v):
    t = jnp.tanh(v * (GELU_A + (GELU_A * GELU_B) * (v * v)))
    h = 0.5 * v
    return h + h * t


def gelu_pair(v):
    w = v * v
    t = jnp.tanh(v * (GELU_A + (GELU_A * GELU_B) * w))
    h = 0.5 * v
    slope = 0.5 + 0.5 * t + (h - h * (t * t)) * (GELU_A + (3.0 * GELU_A * GELU_B) * w)
    return h + h * t, slope


def row_iota(shape):
    return lax.broadcasted_iota(jnp.int32, shape, 0)


def at(j):
    return pl.ds(pl.multiple_of(j * TILE, TILE), TILE)


def scan_tile(a, b, reverse):
    rows = row_iota(a.shape)
    step = 1
    while step < TILE:
        if reverse:
            keep, shift = rows < TILE - step, TILE - step
        else:
            keep, shift = rows >= step, step
        b = jnp.where(keep, a * pltpu.roll(b, shift, 0) + b, b)
        a = jnp.where(keep, a * pltpu.roll(a, shift, 0), a)
        step *= 2
    return a, b


def shift_down(cur, prev, k):
    if k == 0:
        return cur
    rows = row_iota(cur.shape)
    return jnp.where(rows < k, pltpu.roll(prev, k, 0), pltpu.roll(cur, k, 0))


def shift_up(cur, later, k):
    if k == 0:
        return cur
    rows = row_iota(cur.shape)
    return jnp.where(
        rows >= TILE - k, pltpu.roll(later, TILE - k, 0), pltpu.roll(cur, TILE - k, 0)
    )


def fold(v):
    return v[0:8] + v[8:16]


def flat(block):
    return block.reshape(-1, block.shape[-1])


def gates(dp, ip, c8):
    rate = sigmoid(dp)
    opening = sigmoid(ip)
    log_decay = -c8 * (0.25 + rate)
    decay = jnp.exp(log_decay)
    square = -jnp.tanh(log_decay) * (1.0 + decay * decay)
    return rate, opening, decay, square


GB, IB, CW, CB, DB, OB, C8, S8 = 0, 1, 2, 6, 7, 8, 9, 10


def conv_tile(in_ref, pc_ref, j, live):
    cur = in_ref[at(j), :]
    prev = in_ref[at(j - 1), :] * live
    out = pc_ref[CB : CB + 1, :] + pc_ref[CW : CW + 1, :] * cur
    moved = [cur]
    for k in range(1, 4):
        m = shift_down(cur, prev, k)
        moved.append(m)
        out = out + pc_ref[CW + k : CW + k + 1, :] * m
    return out, moved


def place_of():
    s = lax.axis_index("seq")
    return s // 4, (s // 2) % 2, s % 2, lax.axis_index("row")


def device_at(y, x, c, z):
    return ((y * 2 + x) * 2 + c, z)


class Peers:
    def __init__(self, zcount):
        y, x, c, z = self.place = place_of()
        self.far = [(z + k) % zcount for k in range(1, zcount)]
        self.along = [device_at(y, x, c, q) for q in self.far]
        self.near = ((y + c) % 2, (x + 1 - c) % 2)
        self.first = device_at(*self.near, c, z)
        self.second = device_at((y + 1 - c) % 2, (x + c) % 2, c, z)
        self.other = device_at(y, x, 1 - c, z)

    def meet(self):
        everyone = [*self.along, self.first, self.second, self.other]
        barrier = pltpu.get_barrier_semaphore()
        for peer in everyone:
            pl.semaphore_signal(
                barrier, inc=1, device_id=peer, device_id_type=pl.DeviceIdType.MESH
            )
        pl.semaphore_wait(barrier, len(everyone))


def remote(source, target, send, recv, device):
    return pltpu.make_async_remote_copy(
        src_ref=source,
        dst_ref=target,
        send_sem=send,
        recv_sem=recv,
        device_id=device,
        device_id_type=pl.DeviceIdType.MESH,
    )


class Spread:
    def __init__(self, peers, own, full, send, recv):
        self.peers, self.own, self.full, self.send, self.recv = peers, own, full, send, recv

    def go(self, stage, act):
        y, x, c, z = self.peers.place
        p, full = self.peers, self.full
        if stage == 0:
            for k, device in enumerate(p.along):
                act(remote(self.own, full(y, x, c, z), self.send(k), self.recv(k), device))
            return
        k = len(p.along) + stage - 1
        if stage == 2:

            @pl.when(c == 0)
            def _():
                part = full(y, slice(None), c, slice(None))
                act(remote(part, part, self.send(k), self.recv(k), p.second))

            @pl.when(c == 1)
            def _():
                part = full(slice(None), x, c, slice(None))
                act(remote(part, part, self.send(k), self.recv(k), p.second))

            return
        if stage == 1:
            part, device = full(y, x, c, slice(None)), p.first
        else:
            part, device = full(slice(None), slice(None), c, slice(None)), p.other
        act(remote(part, part, self.send(k), self.recv(k), device))

    def start(self, stage):
        self.go(stage, lambda d: d.start())

    def arrive(self, stage):
        self.go(stage, lambda d: d.wait_recv())

    def drain(self):
        for stage in range(4):
            self.go(stage, lambda d: d.wait_send())


def wave_of(t, count, lags):
    for stage in range(len(lags), -1, -1):
        piece = t - sum(lags[:stage])
        if 0 <= piece < count:
            yield piece, stage


class Gather:
    def __init__(self, zcount, ins, outs, sems, chunks, lags):
        self.csem, self.ssem, self.rsem = sems
        self.peers = Peers(zcount)
        self.lags = lags
        y, x, c, z = self.peers.place
        self.spreads, self.copies = [], []
        for i, (which, start, size, target, offset) in enumerate(chunks):
            own = ins[which].at[pl.ds(start, size)]
            rows = pl.ds(offset, size)

            def full(a, b, d, e, ref=outs[target], rows=rows):
                return ref.at[a, b, d, e, rows]

            def send(k, i=i):
                return self.ssem.at[i, k]

            def recv(k, i=i):
                return self.rsem.at[i, k]

            self.spreads.append(Spread(self.peers, own, full, send, recv))
            self.copies.append(pltpu.make_async_copy(own, full(y, x, c, z), self.csem.at[i]))
        self.waves = len(chunks) + sum(lags) + 1

    def wave(self, t):
        for i, stage in wave_of(t, len(self.spreads), self.lags):
            if stage == 0:
                self.copies[i].start()
            elif stage == 1:
                self.copies[i].wait()
            if stage > 0:
                self.spreads[i].arrive(stage - 1)
            if stage < 4:
                self.spreads[i].start(stage)

    def drain(self):
        for spread in self.spreads:
            spread.drain()


def in_turn(weave, step, plan, first=0):
    def point(k):
        for s, points in enumerate(plan, first):
            if k < len(points) and points[k]:

                @pl.when(step == s)
                def _(todo=points[k]):
                    for t in todo:
                        weave.wave(t)

    return point


def spread_out(waves, ahead, steps, points):
    todo = list(range(waves))
    plan = []
    for s in range(steps):
        row = []
        for k in range(points):
            take = ahead if s == 0 and k == 0 else 1
            if s == steps - 1 and k == points - 1:
                take = len(todo)
            row.append(todo[:take])
            todo = todo[take:]
        plan.append(row)
    return plan


def paced(waves, ahead, marks):
    last = marks[-1][-1]
    plan = [[[] for _ in row] for row in marks]
    spots = [(t, s, k) for s, row in enumerate(marks) for k, t in enumerate(row)]
    for w in range(waves):
        due = last * max(0, w - ahead) / max(1, waves - ahead)
        _, s, k = next(spot for spot in spots if spot[0] >= due)
        plan[s][k].append(w)
    return plan


def row_chunks(parts, size):
    return [
        (which, start + i, size, target, offset + i)
        for which, start, count, target, offset in parts
        for i in range(0, count, size)
    ]


def gather_sems(count, zcount):
    links = pltpu.SemaphoreType.DMA((count, zcount + 2))
    return [pltpu.SemaphoreType.DMA((count,)), links, links]


CORE, GATES, SUMS, HALVED = 0, 1, 2, 3


class Scatter:
    def __init__(self, zcount, ins, outs, buffers, sems, chunks, lags):
        self.peers = Peers(zcount)
        self.zcount, self.chunks, self.lags = zcount, chunks, lags
        self.ins, self.outs, self.buffers = ins, outs, buffers
        self.csem, self.ssem, self.rsem = sems[:3]
        self.pieces = [Piece(self, i, sems[3:], *chunk) for i, chunk in enumerate(chunks)]
        self.waves = len(chunks) + sum(lags) + 1

    def wave(self, t):
        for i, stage in wave_of(t, len(self.pieces), self.lags):
            if stage <= 4 or self.pieces[i].spread is not None:
                self.pieces[i].step(stage)

    def drain(self):
        for piece in self.pieces:
            piece.drain()


def slot_of_core(i, slots):
    return i % slots


def add_into(into, i, part, j):
    into[i] = (into[i].astype(F32) + part[j].astype(F32)).astype(into.dtype)


class Piece:
    def __init__(self, owner, i, sems, kind, slot, which, source, span, target, place):
        self.o, self.i, self.kind, self.slot = owner, i, kind, slot
        self.a, self.r0, self.r1, self.r2, self.r3 = owner.buffers[kind]
        self.from_core = 0 if self.r0 is None else slot_of_core(i, self.r0.shape[0])
        self.source, self.lead, self.rows = owner.ins[which], source, pl.ds(*span)
        self.target, self.place = owner.outs[target], place
        self.spread, self.drained = None, False
        if kind in (GATES, SUMS):
            y, x, c, z = owner.peers.place

            def full(*at_place):
                return self.target.at[at_place]

            def send(k):
                return sems[0].at[i, k]

            def recv(k):
                return sems[1].at[i, k]

            self.spread = Spread(owner.peers, full(y, x, c, z), full, send, recv)

    def local(self):
        c = self.o.peers.place[2]
        if self.kind == HALVED:
            mine = self.source.at[self.lead, :, :, :, self.rows]
        else:
            mine = self.source.at[:, :, c, :, self.rows]
        return pltpu.make_async_copy(mine, self.a.at[self.slot], self.o.csem.at[self.i])

    def send(self, stage, act):
        s, peers = self.slot, self.o.peers
        y, x, c, z = peers.place

        def go(source, target, k, device):
            act(remote(source, target, self.o.ssem.at[self.i, k], self.o.rsem.at[self.i, k], device))

        if stage == 0:
            if self.kind != HALVED:
                theirs = self.source.at[:, :, 1 - c, :, self.rows]
                go(theirs, self.r0.at[self.from_core], 0, peers.other)
        elif stage == 1:

            @pl.when(c == 0)
            def _():
                go(self.a.at[s, 1 - y], self.r1.at[s], 1, peers.second)

            @pl.when(c == 1)
            def _():
                go(self.a.at[s, :, 1 - x], self.r1.at[s], 1, peers.second)

        elif stage == 2:
            go(self.a.at[(s, *peers.near)], self.r2.at[s], 2, peers.first)
        else:
            for k, device in enumerate(peers.along):
                go(self.a.at[s, y, x, peers.far[k]], self.r3.at[s, k], 3 + k, device)

    def step(self, stage):
        s, zcount = self.slot, self.o.zcount
        y, x, c, z = self.o.peers.place
        if stage == 0:
            for earlier in self.o.pieces[: self.i]:
                if earlier.a is self.a and earlier.slot == s:
                    earlier.drain()
            self.local().start()
        elif stage <= 4:
            self.send(stage - 1, lambda d: d.wait_recv())
        else:
            self.spread.arrive(stage - 5)
        if stage == 1:
            self.local().wait()
            if self.kind != HALVED:

                @pl.loop(0, 4 * zcount)
                def _(q):
                    i = (q // (2 * zcount), (q // zcount) % 2, q % zcount)
                    add_into(self.a, (s, *i), self.r0, (self.from_core, *i))

        elif stage == 2:

            @pl.loop(0, 2 * zcount)
            def _(q):
                h = q // zcount
                i = (s, y * (1 - c) + h * c, h * (1 - c) + x * c, q % zcount)
                add_into(self.a, i, self.r1, (s, h, q % zcount))

        elif stage == 3:

            @pl.loop(0, zcount)
            def _(q):
                add_into(self.a, (s, y, x, q), self.r2, (s, q))

        elif stage == 4:
            total = self.a[s, y, x, z].astype(F32)
            for k in range(zcount - 1):
                total = total + self.r3[s, k].astype(F32)
            if self.spread is None:
                self.target[self.place : self.place + total.shape[0]] = total
            else:
                self.target[y, x, c, z] = total.astype(self.target.dtype)
        if stage < 4:
            self.send(stage, lambda d: d.start())
        elif stage < 8 and self.spread is not None:
            self.spread.start(stage - 4)

    def drain(self):
        if self.drained:
            return
        self.drained = True
        for stage in range(4):
            self.send(stage, lambda d: d.wait_send())
        if self.spread is not None:
            self.spread.drain()


def five(number, shape, dtype, zcount):
    lead = [(2, 2, zcount), (2, 2, zcount), (2, zcount), (zcount,), (zcount - 1,)]
    return [pltpu.VMEM((number, *d, *shape), dtype) for d in lead]


def no_point(k):
    pass


class Exchange:
    def __init__(self, mine, theirs, ssem, rsem):
        self.mine, self.theirs, self.ssem, self.rsem = mine, theirs, ssem, rsem
        self.count = lax.axis_size("seq")
        self.place = lax.axis_index("seq")

    def peer(self, k):
        return (lax.rem(self.place + k, self.count), lax.axis_index("row"))

    def go(self, g, act):
        for k in range(1, self.count):
            act(
                remote(
                    self.mine.at[g],
                    self.theirs.at[g, self.place],
                    self.ssem.at[g, k - 1],
                    self.rsem.at[g, k - 1],
                    self.peer(k),
                )
            )

    def start(self, g):
        self.go(g, lambda d: d.start())

    def entering(self, g, reverse):
        self.go(g, lambda d: d.wait_recv())
        state = jnp.zeros((1, self.mine.shape[-1]), F32)
        for hop in range(self.count - 1):
            source = self.count - 1 - hop if reverse else hop
            ahead = source > self.place if reverse else source < self.place
            reach = self.theirs[g, source, 0:1, :]
            drive = self.theirs[g, source, 1:2, :]
            state = jnp.where(ahead, reach * state + drive, state)
        return state

    def drain(self, groups):
        for g in range(groups):
            self.go(g, lambda d: d.wait_send())


def exchange_scratch(groups, width, count):
    links = pltpu.SemaphoreType.DMA((groups, count - 1))
    return [
        pltpu.VMEM((groups, 8, width), F32),
        pltpu.VMEM((groups, count, 8, width), F32),
        links, links,
    ]


def meet_all(exchange, zcount):
    place, row = exchange.place, lax.axis_index("row")
    everyone = [exchange.peer(k) for k in range(1, exchange.count)]
    everyone += [(place, lax.rem(row + k, zcount)) for k in range(1, zcount)]
    barrier = pltpu.get_barrier_semaphore()
    for peer in everyone:
        pl.semaphore_signal(barrier, inc=1, device_id=peer, device_id_type=pl.DeviceIdType.MESH)
    pl.semaphore_wait(barrier, len(everyone))


def pair_up(pair, blocks):
    half = blocks.shape[1]
    pair[...] = jnp.zeros_like(pair)
    pair[0:half, 0:half] = blocks[0]
    pair[half:, half:] = blocks[1]


def front_kernel(ltiles, tiles, groups, links, *refs):
    (
        long_ref, short_ref, lcot_ref, scot_ref, length_ref, gain_ref, *channel_refs
    ) = refs[:14]
    wd_ref, wo_ref = refs[14:16]
    refs = refs[16:]
    step = pl.program_id(0)
    point, gather = no_point, None
    zcount = 1
    if links is None:
        pairw, refs = refs[0], refs[1:]
    else:
        zcount, chunks, lags, ready, plan = links
        owns, made = refs[:6], refs[18:21]
        pairw = made[0]
        gather = Gather(zcount, owns, made, refs[-3:], chunks, lags)
        refs = refs[6:18] + refs[21:-3]
        point = in_turn(gather, step, plan)
    gp, inn, dp, ip, st, pr, mix, sin_ref, nm_ref, x_ref, cot_ref, pc_ref = refs[:12]
    cv_ref, cl_ref, wbuf, pairs, halo, isem, wsem, hsem, *swap = refs[12:]
    exchange = Exchange(*swap)
    lrows = ltiles * TILE
    place = exchange.place

    def load(g):
        return pltpu.make_async_copy(pairw.at[g // 2, g % 2], wbuf.at[g % 2], wsem.at[g % 2])

    @pl.when(step == 0)
    def _():
        srows = short_ref.shape[0]
        copies = [
            pltpu.make_async_copy(source, target, isem.at[k])
            for k, (source, target) in enumerate(
                [
                    (long_ref, x_ref.at[pl.ds(HALO, lrows)]),
                    (short_ref, x_ref.at[pl.ds(HALO + lrows, srows)]),
                    (lcot_ref, cot_ref.at[pl.ds(0, lrows)]),
                    (scot_ref, cot_ref.at[pl.ds(lrows, srows)]),
                ]
            )
        ]
        for copy in copies:
            copy.start()
        meet_all(exchange, zcount)
        ahead = remote(
            long_ref.at[pl.ds(lrows - HALO, HALO)], halo, hsem.at[0], hsem.at[1], exchange.peer(1)
        )
        ahead.start()
        todo = [] if gather is None else list(range(ready))

        def some(count):
            for t in todo[:count]:
                gather.wave(t)
            del todo[:count]

        some(4)
        for copy in copies:
            copy.wait()

        @pl.loop(0, ltiles)
        def _(i):
            rows = row_iota((TILE, 1)) + (place * lrows + i * TILE)
            keep = jnp.where(rows < length_ref[0], 1.0, 0.0)
            cot_ref[at(i), :] = (cot_ref[at(i), :].astype(F32) * keep).astype(BF16)

        some(1)
        ahead.wait_recv()
        x_ref[0:HALO, :] = halo[...]

        def norm(j):
            v = x_ref[at(j), :].astype(F32)
            s = lax.rsqrt(jnp.mean(v * v, axis=1, keepdims=True) + EPSILON)
            nm_ref[at(j), :] = (v * s * gain_ref[...]).astype(BF16)

        pl.loop(0, tiles // 2)(norm)
        some(1)
        pl.loop(tiles // 2, tiles)(norm)
        some(len(todo))
        ahead.wait_send()
        load(0).start()
        load(1).start()

    @pl.when(step > 0)
    def _():
        for g in range(groups):

            @pl.when(step == g + 1)
            def _(g=g):
                load(g).wait()

        for k, ref in zip((GB, IB, CW, CB, DB, OB, C8, S8), channel_refs):
            pc_ref[k : k + ref.shape[0], :] = ref[...]
        pc_ref[S8 + 1 :, :] = jnp.zeros((15 - S8, pc_ref.shape[1]), F32)
        pair_up(pairs.at[0], wd_ref)
        pair_up(pairs.at[1], wo_ref)
        slot = lax.rem(step - 1, 2)
        share = wbuf.shape[-2] // 2
        front_part(
            ltiles, tiles, point, place, nm_ref, wbuf.at[slot, :, :, 0:share],
            wbuf.at[slot, :, :, share : 2 * share], pairs, pc_ref, gp, inn, dp, ip, st, pr, mix,
            exchange.mine.at[step - 1], cv_ref, cl_ref,
        )
        for g in range(groups):

            @pl.when(step == g + 1)
            def _(g=g):
                if g + 2 < groups:
                    load(g + 2).start()
                exchange.theirs[g, place] = jnp.zeros(exchange.theirs.shape[2:], F32)
                exchange.start(g)

        point(3)

    @pl.when(step == groups)
    def _():
        width = gp.shape[1]
        for g in range(groups):
            state = exchange.entering(g, False)
            sin_ref[:, g * width : (g + 1) * width] = jnp.broadcast_to(state, (8, width))
        exchange.drain(groups)
        if gather is not None:
            gather.drain()


def front_part(
    ltiles, tiles, point, place, nm_ref, wg_ref, wi_ref, pairs, pc_ref, gp_ref, in_ref, dp_ref,
    ip_ref, st_ref, pr_ref, mix_ref, end_ref, cv_ref, cl_ref,
):
    point(0)
    nm = nm_ref[...]
    gp_ref[...] = dot_nt(nm, flat(wg_ref[...])) + pc_ref[GB : GB + 1, :]
    in_ref[...] = dot_nt(nm, flat(wi_ref[...])) + pc_ref[IB : IB + 1, :]
    point(1)
    in_ref[0:HALO, :] = in_ref[0:HALO, :] * jnp.where(place > 0, 1.0, 0.0)
    cl_ref[0:HALO, :] = jnp.zeros((HALO, cl_ref.shape[1]), BF16)

    @pl.loop(1, tiles)
    def _(j):
        live = jnp.where(j == 1 + ltiles, 0.0, 1.0)
        out, _ = conv_tile(in_ref, pc_ref, j, live)
        cv_ref[at(j), :] = out
        cl_ref[at(j), :] = out.astype(BF16)

    point(2)
    low = cl_ref[...]
    dp_ref[...] = dot_nn(low, pairs[0]) + pc_ref[DB : DB + 1, :]
    ip_ref[...] = dot_nn(low, pairs[1]) + pc_ref[OB : OB + 1, :]

    def scanned(j):
        _, opening, a, square = gates(dp_ref[at(j), :], ip_ref[at(j), :], pc_ref[C8 : C8 + 1, :])
        b = (square * lax.rsqrt(square)) * opening * cv_ref[at(j), :]
        return scan_tile(a, b, False)

    width = gp_ref.shape[1]

    def long_step(i, carry):
        state, reach = carry
        a, b = scanned(1 + i)
        s = b + a * state
        r = a * reach
        st_ref[at(1 + i), :] = s
        pr_ref[at(1 + i), :] = r
        return s[TILE - 1 : TILE], r[TILE - 1 : TILE]

    state, reach = lax.fori_loop(
        0, ltiles, long_step, (jnp.zeros((1, width), F32), jnp.ones((1, width), F32))
    )
    end_ref[...] = jnp.concatenate([reach, state, jnp.zeros((6, width), F32)], axis=0)

    def short_step(i, state):
        j = 1 + ltiles + i
        a, b = scanned(j)
        s = b + a * state
        st_ref[at(j), :] = s
        mix_ref[at(i), :] = (s * gelu(gp_ref[at(j), :])).astype(BF16)
        return s[TILE - 1 : TILE]

    lax.fori_loop(0, tiles - 1 - ltiles, short_step, jnp.zeros((1, width), F32))


def mlp_kernel(ltiles, tiles, links, *refs):
    (
        x_ref, cot_ref, st_ref, pr_ref, gp_ref, sin_ref, mixs_ref, wo_ref, gain_ref, w1_ref, w2_ref
    ) = refs[:11]
    refs = refs[11:]
    point, gather = no_point, None
    step = pl.program_id(0)
    last = pl.num_programs(0) - 1
    if links is not None:
        zcount, chunks, lags, plan = links
        owns = [w2_ref, *refs[:2]]
        refs = refs[2:]
    outl_ref, outs_ref, dres_ref, rlow_ref, mixl_ref, gain_grad_ref, dw_hbm = refs[:7]
    refs = refs[7:]
    if links is not None:
        w2_ref = refs[0]
        gather = Gather(zcount, owns, [w2_ref], refs[-3:], chunks, lags)
        got_ref, sems, credit = refs[-6], refs[-5], refs[-4]
        refs = refs[1:-6]
        point = in_turn(gather, step, plan)
    (
        n2_ref, acc_o, acc_n, g_ref, u_ref, d_ref, h_ref, dg_ref, du_ref, wbuf, dwbuf, wsem, dsem
    ) = refs
    lrows = ltiles * TILE
    half = g_ref.shape[1] // 2
    share = wbuf.shape[-2] // 3
    steps = 2 * GRID[0]

    def load(s):
        source = w1_ref if s < steps // 2 else w2_ref
        return pltpu.make_async_copy(
            source.at[s % (steps // 2)], wbuf.at[s % 2], wsem.at[s % 2]
        )

    def each(todo, first=0):
        for s in range(first, steps):

            @pl.when(step == s)
            def _(s=s):
                todo(s)

    if gather is not None:
        y, x, c, z = gather.peers.place

    def store(s):
        h, q = s // (steps // 2), s % (steps // 2)
        mine = dwbuf if gather is None else dwbuf.at[:, c]
        return pltpu.make_async_copy(mine, dw_hbm.at[h, q], dsem)

    def swap():
        return remote(
            dwbuf.at[:, 1 - c], got_ref, sems.at[0], sems.at[1], gather.peers.other
        )

    def settle(s):
        if gather is not None:
            swap().wait_recv()

            @pl.loop(0, got_ref.shape[0] * got_ref.shape[1])
            def _(k):
                i, j = k // got_ref.shape[1], k % got_ref.shape[1]
                both = dwbuf[i, c, j].astype(F32) + got_ref[i, j].astype(F32)
                dwbuf[i, c, j] = both.astype(BF16)

            if s < steps - 1:
                pl.semaphore_signal(
                    credit,
                    inc=1,
                    device_id=gather.peers.other,
                    device_id_type=pl.DeviceIdType.MESH,
                )
        store(s).start()

    def clear(s):
        store(s).wait()
        if gather is not None:
            swap().wait_send()

    @pl.when(step == 0)
    def _():
        load(0).start()
        load(1).start()
        if gather is not None:
            gather.peers.meet()

    point(0)

    @pl.when(step == 0)
    def _():
        s_in = sin_ref[0:1, :]

        @pl.loop(0, ltiles)
        def _(i):
            s = st_ref[at(1 + i), :] + pr_ref[at(1 + i), :] * s_in
            mixl_ref[at(i), :] = (s * gelu(gp_ref[at(1 + i), :])).astype(BF16)

        wo = flat(wo_ref[...])
        dres_ref[0:lrows, :] = dot_nn(mixl_ref[...], wo)
        dres_ref[lrows:, :] = dot_nn(mixs_ref[...], wo)

        @pl.loop(0, tiles)
        def _(i):
            r = dres_ref[at(i), :] + x_ref[at(1 + i), :].astype(F32)
            dres_ref[at(i), :] = r
            acc_o[at(i), :] = r
            s = lax.rsqrt(jnp.mean(r * r, axis=1, keepdims=True) + EPSILON)
            n2_ref[at(i), :] = (r * s * gain_ref[...]).astype(BF16)

        acc_n[...] = jnp.zeros_like(acc_n)

    point(1)

    @pl.when(step == steps // 2)
    def _():
        load(steps // 2).start()
        load(steps // 2 + 1).start()

    each(lambda s: load(s).wait())
    slot = lax.rem(step, 2)
    n2 = n2_ref[...]
    wg = flat(wbuf[slot, ..., 0:share, :])
    wu = flat(wbuf[slot, ..., share : 2 * share, :])
    wd = flat(wbuf[slot, ..., 2 * share :, :])
    g_ref[...] = dot_nt(n2, wg)
    u_ref[...] = dot_nt(n2, wu)
    point(2)
    d_ref[...] = dot_nt(cot_ref[...], wd)
    each(lambda s: settle(s - 1), 1)
    point(3)

    @pl.loop(0, tiles)
    def _(i):
        for k in range(2):
            cols = slice(k * half, (k + 1) * half)
            ge, slope = gelu_pair(g_ref[at(i), cols])
            u = u_ref[at(i), cols]
            d = d_ref[at(i), cols]
            h_ref[at(i), cols] = (ge * u).astype(BF16)
            dg_ref[at(i), cols] = (d * u * slope).astype(BF16)
            du_ref[at(i), cols] = (d * ge).astype(BF16)

    point(4)
    acc_o[...] += dot_nn(h_ref[...], wd)
    acc_n[...] += dot_nn(dg_ref[...], wg) + dot_nn(du_ref[...], wu)
    point(5)
    each(lambda s: clear(s - 1), 1)
    lead = dwbuf.shape[:-2]
    rest = (share, dwbuf.shape[-1])
    for k, (left, right) in enumerate(((dg_ref, n2_ref), (du_ref, n2_ref), (h_ref, cot_ref))):
        grad = dot_tn(left[...], right[...]).astype(BF16)
        dwbuf[..., k * share : (k + 1) * share, :] = grad.reshape(lead + rest)
        if k < 2:
            point(6 + k)

    if gather is not None:
        @pl.when(step > 0)
        def _():
            pl.semaphore_wait(credit, 1)

        swap().start()

    @pl.when(step == last)
    def _():
        def one(i, total):
            r = dres_ref[at(i), :]
            dn = acc_n[at(i), :]
            s = lax.rsqrt(jnp.mean(r * r, axis=1, keepdims=True) + EPSILON)
            e = dn * gain_ref[...]
            inner = jnp.mean(e * r, axis=1, keepdims=True)
            dr = cot_ref[at(i), :].astype(F32) + s * e - r * (s * s * s * inner)
            dres_ref[at(i), :] = dr
            rlow_ref[at(i), :] = dr.astype(BF16)
            return total + fold(dn * (r * s))

        gain_grad_ref[...] = lax.fori_loop(0, tiles, one, jnp.zeros(gain_grad_ref.shape, F32))
        outl_ref[...] = acc_o[0:lrows, :].astype(BF16)
        outs_ref[...] = acc_o[lrows:, :].astype(BF16)
        settle(steps - 1)
        clear(steps - 1)
        if gather is not None:
            gather.drain()


def back_part(
    ltiles, tiles, point, rlow_ref, wo_ref, mixl_ref, mixs_ref, gp_ref, st_ref, pr_ref, sin_ref,
    dp_ref, pc_ref, dwo_ref, gl_ref, tot_ref, rch_ref, end_ref, bias_ref, dm_ref, free,
):
    point(0)
    lrows = ltiles * TILE
    width = gp_ref.shape[1]
    rlow = rlow_ref[...]
    dm_ref[...] = dot_nt(rlow, flat(wo_ref[...]))
    free()
    grad = dot_tn(mixl_ref[...], rlow_ref[0:lrows, :]) + dot_tn(mixs_ref[...], rlow_ref[lrows:, :])
    dwo_ref[...] = grad.astype(BF16).reshape(dwo_ref.shape)
    point(1)
    gl_ref[0:HALO, :] = jnp.zeros((HALO, width), BF16)
    last = row_iota((TILE, width)) == TILE - 1

    def local(j, states):
        dm = dm_ref[at(j - 1), :]
        ge, slope = gelu_pair(gp_ref[at(j), :])
        dgate = dm * states * slope
        gl_ref[at(j), :] = dgate.astype(BF16)
        ds = dm * ge
        rate = sigmoid(dp_ref[at(j), :])
        decay = jnp.exp(-pc_ref[C8 : C8 + 1, :] * (0.25 + rate))
        a, b = scan_tile(decay, decay * ds, True)
        return a, b, ds, fold(dgate)

    def short_step(i, carry):
        c, bias = carry
        j = tiles - 1 - i
        a, b, ds, part = local(j, st_ref[at(j), :])
        cs = b + a * c
        tot_ref[at(j), :] = ds + jnp.where(last, c, pltpu.roll(cs, TILE - 1, 0))
        return cs[0:1], bias + part

    _, bias = lax.fori_loop(
        0,
        tiles - 1 - ltiles,
        short_step,
        (jnp.zeros((1, width), F32), jnp.zeros((8, width), F32)),
    )
    point(2)
    s_in = sin_ref[0:1, :]

    def long_step(i, carry):
        c, reach, bias = carry
        j = ltiles - i
        a, b, ds, part = local(j, st_ref[at(j), :] + pr_ref[at(j), :] * s_in)
        cs = b + a * c
        rs = a * reach
        tot_ref[at(j), :] = ds + jnp.where(last, c, pltpu.roll(cs, TILE - 1, 0))
        rch_ref[at(j), :] = jnp.where(last, reach, pltpu.roll(rs, TILE - 1, 0))
        return cs[0:1], rs[0:1], bias + part

    c, reach, bias = lax.fori_loop(
        0, ltiles, long_step, (jnp.zeros((1, width), F32), jnp.ones((1, width), F32), bias)
    )
    end_ref[...] = jnp.concatenate([reach, c, jnp.zeros((6, width), F32)], axis=0)
    bias_ref[...] = bias


def last_part(
    ltiles, tiles, groups, point, exchange, residual, x_ref, gain_ref, nm_ref, wg_ref, wi_ref,
    wd_ref, wo_ref, pc_ref, in_ref, dp_ref, ip_ref, st_ref, pr_ref, sin_ref, tot_ref, rch_ref,
    gl_ref, bias_ref, dxl_ref, dxs_ref, halo_ref, behind, pairs, gain_grad_ref, dwg_ref, dwi_ref,
    gg_ref, small_ref, acc, dc_ref, cl_ref, dl_ref, ol_ref, il_ref, gain2_ref, free, keep,
):
    width = in_ref.shape[1]
    step = pl.program_id(0) - groups
    point(0)
    for g in range(groups):

        @pl.when(step == g)
        def _(g=g):
            dc_ref[0:1, :] = exchange.entering(g, True)

    c_in = dc_ref[0:1, :]

    @pl.when(step == groups - 1)
    def _():
        for copy in residual:
            copy.start()

    first = jnp.where(exchange.place > 0, 1.0, 0.0)
    pair_up(pairs.at[0], wd_ref)
    pair_up(pairs.at[1], wo_ref)
    zero8 = jnp.zeros((8, width), F32)
    cl_ref[0:HALO, :] = jnp.zeros((HALO, width), BF16)
    dl_ref[0:HALO, :] = jnp.zeros((HALO, width), BF16)
    ol_ref[0:HALO, :] = jnp.zeros((HALO, width), BF16)
    dc_ref[0:HALO, :] = jnp.zeros((HALO, width), F32)

    def gate_step(j, states, total, live, carry):
        before, sum_d, sum_o, sum_p = carry
        rows = row_iota((TILE, width))
        prior = jnp.where(rows == 0, before, pltpu.roll(states, 1, 0))
        conv, _ = conv_tile(in_ref, pc_ref, j, live)
        rate, opening, decay, square = gates(
            dp_ref[at(j), :], ip_ref[at(j), :], pc_ref[C8 : C8 + 1, :]
        )
        inv = lax.rsqrt(square)
        mult = square * inv
        weighted = total * opening
        d_open = total * mult * conv
        d_log = decay * (total * prior - (weighted * conv) * (decay * inv))
        d_rate = -pc_ref[C8 : C8 + 1, :] * d_log
        d_dp = d_rate * (rate - rate * rate)
        d_ip = d_open * (opening - opening * opening)
        cl_ref[at(j), :] = conv.astype(BF16)
        dl_ref[at(j), :] = d_dp.astype(BF16)
        ol_ref[at(j), :] = d_ip.astype(BF16)
        dc_ref[at(j), :] = weighted * mult
        return (
            states[TILE - 1 : TILE],
            sum_d + fold(d_dp),
            sum_o + fold(d_ip),
            sum_p - fold((0.25 + rate) * d_log),
        )

    s_in = sin_ref[0:1, :]

    def long_step(i, carry):
        j = 1 + i
        states = st_ref[at(j), :] + pr_ref[at(j), :] * s_in
        total = tot_ref[at(j), :] + rch_ref[at(j), :] * c_in
        return gate_step(j, states, total, 1.0, carry)

    def short_step(i, carry):
        j = 1 + ltiles + i
        return gate_step(j, st_ref[at(j), :], tot_ref[at(j), :], jnp.where(i == 0, 0.0, 1.0), carry)

    carry = lax.fori_loop(0, ltiles, long_step, (s_in, zero8, zero8, zero8))
    carry = lax.fori_loop(
        0, tiles - 1 - ltiles, short_step, (jnp.zeros((1, width), F32),) + carry[1:]
    )
    _, sum_d, sum_o, sum_p = carry
    point(1)

    low, dlow, olow = cl_ref[...], dl_ref[...], ol_ref[...]
    half = width // 2
    for which, grads in ((0, dlow), (1, olow)):
        product = dot_tn(low, grads).astype(BF16)
        shape = (2, half // 2, half)
        place = (which, step // 2, lax.rem(step, 2))
        gg_ref[(*place, slice(0, 2))] = product[:half, :half].reshape(shape)
        gg_ref[(*place, slice(2, 4))] = product[half:, half:].reshape(shape)
    dc_ref[...] += dot_nt(dlow, pairs[0]) + dot_nt(olow, pairs[1])

    point(2)

    def conv_step(j, carry):
        sum_c, sum_i, sums = carry
        live = jnp.where(j == 1 + ltiles, 0.0, 1.0)
        cur = dc_ref[at(j), :]
        up = jnp.where((j == ltiles) | (j == tiles - 1), 0.0, 1.0)
        later = dc_ref[at(jnp.minimum(j + 1, tiles - 1)), :] * up
        _, moved = conv_tile(in_ref, pc_ref, jnp.maximum(j, 1), live)
        d_in = pc_ref[CW : CW + 1, :] * cur
        for k in range(1, 4):
            d_in = d_in + pc_ref[CW + k : CW + k + 1, :] * shift_up(cur, later, k)
        d_in = d_in * jnp.where(j == 0, first, 1.0)
        il_ref[at(j), :] = d_in.astype(BF16)
        return (
            sum_c + fold(cur),
            sum_i + fold(d_in),
            tuple(s + fold(cur * m) for s, m in zip(sums, moved)),
        )

    sum_c, sum_i, sums = lax.fori_loop(0, tiles, conv_step, (zero8, zero8, (zero8,) * 4))
    parts = [sum_i, *sums, sum_c, sum_d, sum_o, sum_p * pc_ref[S8 : S8 + 1, :], bias_ref[...]]
    rows = [jnp.sum(p, axis=0, keepdims=True) for p in parts]
    block = jnp.concatenate(rows + [jnp.zeros((16 - len(rows), width), F32)], axis=0)
    for i in range(width // 128):
        at_block = step * (width // 128) + i
        x, c, z = at_block // 8, lax.rem(at_block // 4, 2), lax.rem(at_block, 4)
        for h in range(2):
            small_ref[h, x, c, z] = block[8 * h : 8 * h + 8, 128 * i : 128 * i + 128]

    point(3)
    free()
    nm = nm_ref[...]
    dwi_ref[...] = dot_tn(il_ref[...], nm).astype(BF16).reshape(dwi_ref.shape)
    dwg_ref[...] = dot_tn(gl_ref[...], nm).astype(BF16).reshape(dwg_ref.shape)
    keep()
    point(4)
    part = dot_nn(gl_ref[...], flat(wg_ref[...])) + dot_nn(il_ref[...], flat(wi_ref[...]))

    @pl.when(step == 0)
    def _():
        acc[...] = part

    @pl.when(step > 0)
    def _():
        acc[...] += part

    @pl.when(step == groups - 1)
    def _():
        for copy in residual:
            copy.wait()

        def norm_back(j):
            v = x_ref[at(j), :].astype(F32)
            dn = acc[at(j), :]
            s = lax.rsqrt(jnp.mean(v * v, axis=1, keepdims=True) + EPSILON)
            e = dn * gain_ref[...]
            inner = jnp.mean(e * v, axis=1, keepdims=True)
            return s * e - v * (s * s * s * inner), fold(dn * (v * s))

        halo, total = norm_back(0)
        halo_ref[...] = halo
        behind.start()
        done = 1
        for ref in (dxl_ref, dxs_ref):

            def one(i, total, ref=ref, done=done):
                d, part = norm_back(done + i)
                ref[at(i), :] = ref[at(i), :] + d
                return total + part

            total = lax.fori_loop(0, ref.shape[0] // TILE, one, total)
            done += ref.shape[0] // TILE
        gain_grad_ref[...] = total
        zero = jnp.zeros((8, 128), F32)
        for h in range(2):
            for z in range(4):
                small_ref[h, 1, 1, z] = zero
        for z, ref in enumerate((gain_grad_ref, gain2_ref)):
            total = jnp.sum(ref[...], axis=0, keepdims=True)
            for i in range(8):
                small_ref[0, 1, 1, z, i : i + 1, :] = total[:, 128 * i : 128 * i + 128]

    point(5)


def tail_kernel(ltiles, tiles, groups, links, *refs):
    (
        x_ref, gain_ref, nm_ref, dres_hbm, rlow_ref, w_ref, wg_ref, wi_ref, wd_ref, wo_ref, pc_ref,
        mixl_ref, mixs_ref, gp_ref, in_ref, dp_ref, ip_ref, st_ref, pr_ref, sin_ref, gain2_ref,
    ) = refs[:21]
    refs = refs[21:]
    step = pl.program_id(0)
    group = lax.rem(step, groups)
    back_point, last_point, scatter = no_point, no_point, None
    nscratch = 23
    if links is not None:
        zcount, chunks, lags, plan = links
        halved_ref, refs = refs[0], refs[1:]
        outs, shares = refs[:8], refs[8:14]
        scratch, pool = refs[14 : 14 + nscratch], refs[14 + nscratch :]
    else:
        outs, scratch = refs[:8], refs[8:]
    dxl_ref, dxs_ref, gain_grad_ref, dwo_hbm, dwg_hbm, dwi_hbm, gates_hbm, sums_hbm = outs
    (
        acc, dc_ref, cl_ref, dl_ref, ol_ref, il_ref, gls, tots, rchs, bias_ref, wst, gsrc, ssrc,
        pairs, halo_out, halo_in, hsem, dsem, wsem, *swap
    ) = scratch
    gates_full, sums_full = gsrc, ssrc
    if links is not None:
        *pool, gates_full, sums_full = pool
        main, gate_pool, sum_pool = pool[0:5], pool[5:10], pool[10:15]
        scatter = Scatter(
            zcount,
            [halved_ref, dwo_hbm, dwg_hbm, dwi_hbm, gsrc, ssrc],
            [*shares, gates_full, sums_full],
            [main, gate_pool, sum_pool, main],
            pool[15:],
            chunks,
            lags,
        )
        back_point = in_turn(scatter, step, plan[:groups])
        last_point = in_turn(scatter, step, plan[groups:], groups)

    def stash(g, k, target):
        return pltpu.make_async_copy(wst.at[k], target.at[g // 2, g % 2], wsem.at[k])

    def stashed(first, what):
        for g in range(groups):

            @pl.when(step == first + g)
            def _(g=g):
                what(g)

    exchange = Exchange(*swap)
    gl_ref, tot_ref, rch_ref = gls.at[group], tots.at[group], rchs.at[group]
    lrows = ltiles * TILE
    residual = [
        pltpu.make_async_copy(dres_hbm.at[pl.ds(0, lrows)], dxl_ref, dsem.at[0]),
        pltpu.make_async_copy(
            dres_hbm.at[pl.ds(lrows, dxs_ref.shape[0])], dxs_ref, dsem.at[1]
        ),
    ]
    behind = remote(
        halo_out, halo_in, hsem.at[0], hsem.at[1], exchange.peer(exchange.count - 1)
    )
    width = gp_ref.shape[1]

    @pl.when(step == 0)
    def _():
        meet_all(exchange, 1 if scatter is None else zcount)

    @pl.when(step < groups)
    def _():
        back_part(
            ltiles, tiles, back_point, rlow_ref, w_ref, mixl_ref, mixs_ref, gp_ref, st_ref, pr_ref,
            sin_ref, dp_ref, pc_ref, wst.at[0], gl_ref, tot_ref, rch_ref, exchange.mine.at[group],
            bias_ref.at[group], acc.at[0 : rlow_ref.shape[0], 0:width],
            lambda: stashed(0, lambda g: stash(g - 1, 0, dwo_hbm).wait() if g > 0 else None),
        )
        stashed(0, lambda g: stash(g, 0, dwo_hbm).start())
        for g in range(groups):

            @pl.when(step == g)
            def _(g=g):
                exchange.theirs[g, exchange.place] = jnp.zeros(exchange.theirs.shape[2:], F32)
                exchange.start(g)

    @pl.when(step >= groups)
    def _():
        @pl.when(step == groups)
        def _():
            stash(groups - 1, 0, dwo_hbm).wait()

        def before(g):
            if g > 0:
                stash(g - 1, 1, dwg_hbm).wait()
                stash(g - 1, 2, dwi_hbm).wait()

        def after(g):
            stash(g, 1, dwg_hbm).start()
            stash(g, 2, dwi_hbm).start()
            if g == groups - 1:
                stash(g, 1, dwg_hbm).wait()
                stash(g, 2, dwi_hbm).wait()

        last_part(
            ltiles, tiles, groups, last_point, exchange, residual, x_ref, gain_ref, nm_ref,
            wg_ref, wi_ref, wd_ref, wo_ref, pc_ref, in_ref, dp_ref, ip_ref, st_ref, pr_ref, sin_ref,
            tot_ref, rch_ref, gl_ref, bias_ref.at[group], dxl_ref, dxs_ref, halo_out, behind, pairs,
            gain_grad_ref, wst.at[1], wst.at[2], gsrc, ssrc, acc, dc_ref, cl_ref, dl_ref, ol_ref, il_ref, gain2_ref,
            lambda: stashed(groups, before), lambda: stashed(groups, after),
        )

    @pl.when(step == pl.num_programs(0) - 1)
    def _():
        exchange.drain(groups)
        behind.wait()
        rows = slice(lrows - HALO, lrows)
        dxl_ref[rows, :] = dxl_ref[rows, :] + halo_in[...]
        if scatter is not None:
            scatter.drain()
        final = [
            pltpu.make_async_copy(gates_full, gates_hbm, wsem.at[0]),
            pltpu.make_async_copy(sums_full, sums_hbm, wsem.at[1]),
        ]
        for copy in final:
            copy.start()
        for copy in final:
            copy.wait()


def shape_of(shape, dtype):
    return jax.ShapeDtypeStruct(shape, dtype)


def whole(shape):
    return pl.BlockSpec(shape, lambda g: (0,) * len(shape), pipeline_mode=pl.Buffered(1))


def params(limit, **more):
    return pltpu.CompilerParams(
        dimension_semantics=("arbitrary",), vmem_limit_bytes=int(limit * MIB), **more
    )


def to_slots(parts, count):
    rows = parts[0].shape[0]
    depth = parts[0].shape[1]
    got = lax.all_gather(jnp.concatenate(parts, axis=0), ("seq", "row"), axis=0, tiled=False)
    if count != SLOTS:
        got = got.reshape(count, len(parts), rows, depth).transpose(1, 0, 2, 3)
        got = got.reshape(len(parts), SLOTS, rows * count // SLOTS, depth).transpose(1, 0, 2, 3)
    return got.reshape(SLOTS, -1, depth)


def scatter_slots(grads, number, count):
    slots, rows, depth = grads.shape
    if count != SLOTS:
        grads = grads.reshape(slots, number, rows // number, depth).transpose(1, 0, 2, 3)
        grads = grads.reshape(number, count, -1, depth).transpose(1, 0, 2, 3)
    flat_grads = grads.reshape(slots * rows, depth)
    own = lax.psum_scatter(flat_grads, ("seq", "row"), scatter_dimension=0, tiled=True)
    own = own.astype(F32).reshape(number, -1, depth)
    return [own[i] for i in range(number)]


def shards(
    long_tokens,
    short_tokens,
    long_length,
    long_cotangent,
    short_cotangent,
    first_gain,
    gate_weight,
    gate_bias,
    input_weight,
    input_bias,
    conv_weight,
    conv_bias,
    decay_gate_weight,
    decay_gate_bias,
    input_gate_weight,
    input_gate_bias,
    decay_param,
    out_weight,
    second_gain,
    mlp_gate_weight,
    mlp_up_weight,
    mlp_down_weight,
):
    count = lax.axis_size("seq") * lax.axis_size("row")
    lrows, srows, depth = long_tokens.shape[1], short_tokens.shape[1], long_tokens.shape[2]
    chans = gate_bias.shape[0]
    units = mlp_gate_weight.shape[1] * count
    tokens = lrows + srows
    total = HALO + tokens
    ltiles, tiles = lrows // TILE, total // TILE
    cshare, ushare = chans // SLOTS, units // SLOTS
    groups = 4
    width = chans // groups
    per = SLOTS // groups

    zcount = lax.axis_size("row")
    seqs = lax.axis_size("seq")
    fast = seqs == 8 and count == SLOTS
    hbm = pl.BlockSpec(memory_space=pl.ANY)
    one_dma = pltpu.SemaphoreType.DMA
    hshare = ushare // 2
    blocks, bwidth = decay_gate_weight.shape[0:2]
    mlp_own = [mlp_gate_weight.T, mlp_up_weight.T, mlp_down_weight]
    channel = [
        gate_bias, input_bias, conv_weight, conv_bias, decay_gate_bias, input_gate_bias,
        8.0 * jax.nn.softplus(decay_param), 8.0 * jax.nn.sigmoid(decay_param),
    ]
    channel = [c.reshape(-1, chans) for c in channel]
    gain1 = first_gain[None]
    gain2 = second_gain[None]

    def early(g):
        return jnp.minimum(g, groups - 1)

    def after_one(g):
        return jnp.maximum(g - 1, 0)

    def late(g):
        return jnp.maximum(g - groups, 0)

    def both_times(g):
        return lax.rem(g, groups)

    def slot_at(when, which=0):
        return pl.BlockSpec((per, cshare, depth), lambda g: (when(g), which, 0))

    def blocks_at(when):
        return pl.BlockSpec((2, bwidth, bwidth), lambda g: (when(g), 0, 0))

    def cols_at(nrows, when):
        return pl.BlockSpec((nrows, width), lambda g: (0, when(g)))

    lags = (2, 2, 3, 2)
    if fast:
        front_own = [gate_weight.T, input_weight.T, out_weight, *mlp_own]
        parts = [(0, 0, cshare, 0, 0), (1, 0, cshare, 0, cshare)]
        ready = len(row_chunks(parts, 16)) + sum(lags)
        parts += [(2, 0, cshare, 1, 0)]
        parts += [(3 + k, 0, hshare, 2, k * hshare) for k in range(3)]
        chunks = row_chunks(parts, 16)
        plan = [[]] + spread_out(len(chunks) + sum(lags) + 1 - ready, 1, groups, 4)
        plan = [[[ready + t for t in p] for p in row] for row in plan]
        front_links = (zcount, chunks, lags, ready, plan)
        front_shapes = [
            shape_of(GRID + (n, depth), BF16) for n in (2 * cshare, cshare, 3 * hshare)
        ]
        front_scratch = gather_sems(len(chunks), zcount)
    else:
        pairw = to_slots([gate_weight.T, input_weight.T], count)
        outw = to_slots([out_weight], count)
        mlpw = to_slots(mlp_own, count).reshape(GRID + (3, 2, -1, depth))
        w_first, w_second = [mlpw[..., h, :, :].reshape(GRID + (-1, depth)) for h in range(2)]
        front_own = [pairw.reshape(GRID + (-1, depth))]
        front_links, front_shapes, front_scratch = None, [], []

    col = cols_at(total, after_one)
    wide = shape_of((total, chans), F32)
    narrow = shape_of((HALO + lrows, chans), F32)
    gp, inner, dp, ip, states, reach, mix_s, s_in, normed, x, cot, chan, *made = pl.pallas_call(
        functools.partial(front_kernel, ltiles, tiles, groups, front_links),
        grid=(1 + groups,),
        in_specs=[
            hbm, hbm, hbm, hbm, pl.BlockSpec(memory_space=pltpu.SMEM), whole((1, depth)),
            *[cols_at(c.shape[0], after_one) for c in channel], blocks_at(after_one),
            blocks_at(after_one), *[hbm for _ in front_own],
        ],
        out_specs=[
            col, col, col, col, col, cols_at(HALO + lrows, after_one), cols_at(srows, after_one),
            whole((8, chans)), whole((total, depth)), whole((total, depth)),
            whole((tokens, depth)), cols_at(16, after_one), *[hbm for _ in front_shapes],
        ],
        out_shape=[
            wide, wide, wide, wide, wide, narrow, shape_of((srows, chans), BF16),
            shape_of((8, chans), F32), shape_of((total, depth), BF16),
            shape_of((total, depth), BF16), shape_of((tokens, depth), BF16),
            shape_of((16, chans), F32), *front_shapes,
        ],
        scratch_shapes=[
            pltpu.VMEM((total, width), F32), pltpu.VMEM((total, width), BF16),
            pltpu.VMEM((2,) + GRID[2:] + (2 * cshare, depth), BF16),
            pltpu.VMEM((2, width, width), BF16), pltpu.VMEM((HALO, depth), BF16),
            one_dma((4,)), one_dma((2,)), one_dma((2,)), *exchange_scratch(groups, width, seqs),
            *front_scratch,
        ],
        compiler_params=params(56, collective_id=0, has_side_effects=True),
        name="front",
    )(
        long_tokens.reshape(lrows, depth), short_tokens.reshape(srows, depth),
        long_cotangent.reshape(lrows, depth), short_cotangent.reshape(srows, depth), long_length,
        gain1, *channel, decay_gate_weight, input_gate_weight, *front_own,
    )
    if fast:
        pairw, outw, w_first = made
    outw = outw.reshape(SLOTS, -1, depth)
    pairw = pairw.reshape(SLOTS, -1, depth)

    steps = 4
    hid = units // steps
    block = GRID[1:] + (3 * ushare // 2, depth)
    wbuf = pltpu.VMEM((2,) + block, BF16)
    dwbuf = pltpu.VMEM(block, BF16)
    if fast:
        chunks = row_chunks([(k, hshare, hshare, 0, k * hshare) for k in range(3)], 16)
        waves = len(chunks) + sum(lags) + 1
        plan = spread_out(waves, 3, 3, 8)
        mlp_links = (zcount, chunks, lags, plan)
        w_last, more_specs, more_shapes = mlp_own, [hbm], [shape_of(w_first.shape, BF16)]
        half_block = (block[0],) + block[2:]
        more_scratch = [
            pltpu.VMEM(half_block, BF16), one_dma((2,)), pltpu.SemaphoreType.REGULAR,
            *gather_sems(len(chunks), zcount),
        ]
        dw_shape = (2, 2) + half_block
        more_params = dict(collective_id=3, has_side_effects=True)
    else:
        mlp_links, w_last, more_specs, more_shapes, more_scratch = None, [w_second], [], [], []
        dw_shape, more_params = (2, 2) + block, {}
    out_l, out_s, d_res, rlow, mix_l, gain2_grad, dmlp, *_ = pl.pallas_call(
        functools.partial(mlp_kernel, ltiles, tokens // TILE, mlp_links),
        grid=(steps,),
        in_specs=[
            whole((total, depth)), whole((tokens, depth)), whole((HALO + lrows, chans)),
            whole((HALO + lrows, chans)), whole((HALO + lrows, chans)), whole((8, chans)),
            whole((srows, chans)), whole((SLOTS, cshare, depth)), whole((1, depth)), hbm,
            *[hbm for _ in w_last],
        ],
        out_specs=[
            whole((lrows, depth)), whole((srows, depth)), whole((tokens, depth)), whole((tokens, depth)),
            whole((lrows, chans)), whole((8, depth)), hbm, *more_specs,
        ],
        out_shape=[
            shape_of((lrows, depth), BF16), shape_of((srows, depth), BF16),
            shape_of((tokens, depth), F32), shape_of((tokens, depth), BF16),
            shape_of((lrows, chans), BF16),
            shape_of((8, depth), F32), shape_of(dw_shape, BF16), *more_shapes,
        ],
        scratch_shapes=[
            pltpu.VMEM((tokens, depth), BF16), pltpu.VMEM((tokens, depth), F32),
            pltpu.VMEM((tokens, depth), F32), pltpu.VMEM((tokens, hid), F32),
            pltpu.VMEM((tokens, hid), F32), pltpu.VMEM((tokens, hid), F32),
            pltpu.VMEM((tokens, hid), BF16), pltpu.VMEM((tokens, hid), BF16),
            pltpu.VMEM((tokens, hid), BF16), wbuf, dwbuf, one_dma((2,)), one_dma, *more_scratch,
        ],
        compiler_params=params(62, **more_params),
        name="mlp",
    )(x, cot, states, reach, gp, s_in, mix_s, outw, gain2, w_first, *w_last)

    gate_shape, sum_shape = GRID + (bwidth // 2, bwidth), GRID + (8, 128)
    grads_shape = shape_of(GRID + (cshare, depth), BF16)
    tail_links, tail_in, tail_specs, tail_shapes, tail_scratch = None, [], [], [], []
    if fast:
        size = 16
        tail_chunks = []
        number = 0
        for h in range(2):
            for start in range(0, 3 * hshare, size):
                k, offset = divmod(start, hshare)
                tail_chunks.append(
                    (HALVED, number % TAIL_SLOTS, 0, h, (start, size), k, h * hshare + offset)
                )
                number += 1
        for which in (1, 2, 3):
            if which == 2:
                tail_chunks.append((SUMS, 0, 5, None, (0, 8), 7, 0))
                tail_chunks.append((GATES, 0, 4, None, (0, bwidth // 2), 6, 0))
                during = len(tail_chunks) - 2
            for start in range(0, cshare, size):
                tail_chunks.append(
                    (CORE, number % TAIL_SLOTS, which, None, (start, size), 2 + which, start)
                )
                number += 1
        tail_lags = (1, 2, 2, 2, 1, 1, 1, 1)
        marks = [[5.0 * g + t for t in (0.0, 1.5, 4.0)] for g in range(groups)]
        marks += [
            [5.0 * groups + 12.5 * g + t for t in (0.0, 5.0, 6.0, 9.0, 10.5, 12.5)] for g in range(groups)
        ]
        plan = paced(during, 3, marks)
        plan[-1][-1] += range(during, len(tail_chunks) + sum(tail_lags) + 1)
        tail_links = (zcount, tail_chunks, tail_lags, plan)
        tail_in, tail_specs = [dmlp], [whole((ushare, depth))] * 3 + [whole((cshare, depth))] * 3
        tail_shapes = [shape_of((ushare, depth), F32)] * 3 + [shape_of((cshare, depth), F32)] * 3
        lone = five(TAIL_SLOTS, (size, depth), BF16, zcount)
        lone[1] = five(CORE_SLOTS, (size, depth), BF16, zcount)[1]
        n = len(tail_chunks)
        links = one_dma((n, zcount + 2))
        tail_scratch = [
            *lone,
            *five(1, gate_shape[4:], BF16, zcount),
            *five(1, sum_shape[4:], F32, zcount),
            one_dma((n,)), links, links, links, links,
            pltpu.VMEM(gate_shape, BF16), pltpu.VMEM(sum_shape, F32),
        ]
    dx_l, dx_s, _, d_out, d_gate, d_input, gate_sums, sums, *shares = pl.pallas_call(
        functools.partial(tail_kernel, ltiles, tiles, groups, tail_links),
        grid=(2 * groups,),
        in_specs=[
            whole((total, depth)), whole((1, depth)), whole((total, depth)), hbm,
            whole((tokens, depth)), slot_at(early), slot_at(late, 0), slot_at(late, 1),
            blocks_at(late), blocks_at(late), cols_at(16, both_times), cols_at(lrows, early),
            cols_at(srows, early), cols_at(total, early), cols_at(total, late),
            cols_at(total, both_times), cols_at(total, late), cols_at(total, both_times),
            cols_at(HALO + lrows, both_times), cols_at(8, both_times), whole((8, depth)),
            *[hbm for _ in tail_in],
        ],
        out_specs=[
            whole((lrows, depth)), whole((srows, depth)), whole((8, depth)), hbm, hbm, hbm, hbm, hbm,
            *tail_specs,
        ],
        out_shape=[
            shape_of((lrows, depth), F32), shape_of((srows, depth), F32), shape_of((8, depth), F32),
            grads_shape, grads_shape, grads_shape, shape_of(gate_shape, BF16),
            shape_of(sum_shape, F32), *tail_shapes,
        ],
        scratch_shapes=[
            pltpu.VMEM((total, depth), F32), pltpu.VMEM((total, width), F32),
            pltpu.VMEM((total, width), BF16), pltpu.VMEM((total, width), BF16),
            pltpu.VMEM((total, width), BF16), pltpu.VMEM((total, width), BF16),
            pltpu.VMEM((groups, total, width), BF16), pltpu.VMEM((groups, total, width), F32),
            pltpu.VMEM((groups, HALO + lrows, width), F32), pltpu.VMEM((groups, 8, width), F32),
            pltpu.VMEM((3,) + GRID[2:] + (cshare, depth), BF16), pltpu.VMEM(gate_shape, BF16),
            pltpu.VMEM(sum_shape, F32), pltpu.VMEM((2, width, width), BF16),
            pltpu.VMEM((HALO, depth), F32), pltpu.VMEM((HALO, depth), F32), one_dma((2,)),
            one_dma((2,)), one_dma((3,)), *exchange_scratch(groups, width, seqs), *tail_scratch,
        ],
        compiler_params=params(63, collective_id=4, has_side_effects=True),
        name="tail",
    )(
        x, gain1, normed, d_res, rlow, outw, pairw, pairw, decay_gate_weight, input_gate_weight, chan,
        mix_l, mix_s, gp, inner, dp, ip, states, reach, s_in, gain2_grad, *tail_in,
    )

    if fast:
        g_mgate, g_mup, g_down, g_out, g_gate, g_input = shares
    else:
        dmlp = dmlp.reshape(2, SLOTS, 3, -1, depth).transpose(1, 2, 0, 3, 4)
        g_mgate, g_mup, g_down = scatter_slots(dmlp.reshape(SLOTS, -1, depth), 3, count)
        dmix = jnp.concatenate([d_gate, d_input, d_out], axis=4).reshape(SLOTS, -1, depth)
        g_gate, g_input, g_out = scatter_slots(dmix, 3, count)
        gate_sums, sums = lax.psum((gate_sums.astype(F32), sums), ("seq", "row"))
    gate_sums = gate_sums.reshape(2, blocks, bwidth, bwidth).astype(F32)
    sums = sums.reshape(2, 16, 8, 128)
    gain_sums = sums[0, 12:14].reshape(2, depth)
    rows = sums.transpose(0, 2, 1, 3).reshape(16, 2048)[0:10, :chans]
    return (
        out_l.reshape(long_tokens.shape),
        out_s.reshape(short_tokens.shape),
        dx_l.reshape(long_tokens.shape),
        dx_s.reshape(short_tokens.shape),
        gain_sums[0],
        g_gate.T,
        rows[9],
        g_input.T,
        rows[0],
        rows[1:5],
        rows[5],
        gate_sums[0],
        rows[6],
        gate_sums[1],
        rows[7],
        rows[8],
        g_out,
        gain_sums[1],
        g_mgate.T,
        g_mup.T,
        g_down,
    )


def solution(mesh):
    both = ("seq", "row")
    long_spec = P("row", "seq", None)
    short_spec = P(both, None, None)
    cols = P(None, both)
    rows = P(both, None)
    return jax.shard_map(
        shards,
        mesh=mesh,
        in_specs=(
            long_spec, short_spec, P("row"), long_spec, short_spec, P(), cols, P(), cols, P(),
            P(), P(), P(), P(), P(), P(), P(), rows, P(), cols, cols, rows,
        ),
        out_specs=(
            long_spec, short_spec, long_spec, short_spec, P(), cols, P(), cols, P(), P(), P(),
            P(), P(), P(), P(), P(), rows, P(), cols, cols, rows,
        ),
        check_vma=False,
    )
```

```python
import functools

import jax
import jax.numpy as jnp
from jax import lax
from jax.experimental import pallas as pl
from jax.experimental.pallas import tpu as pltpu
from jax.sharding import PartitionSpec as P

EPSILON = 1e-06
F32 = jnp.float32
BF16 = jnp.bfloat16
GRID = (2, 2, 2, 4)
SLOTS = 32
TILE = 16
HALO = 16
MIB = 1024 * 1024
MLP_AHEAD = 1
EARLY_PARTS = 2
EARLY_GAP = 3
FRONT_PARTS = 3
TAIL_SLOTS = 10
CORE_SLOTS = 5
GELU_A = 0.7978845608028654
GELU_B = 0.044715


def dot_nn(a, b):
    return lax.dot_general(a, b, (((1,), (0,)), ((), ())), preferred_element_type=F32)


def dot_nt(a, b):
    return lax.dot_general(a, b, (((1,), (1,)), ((), ())), preferred_element_type=F32)


def dot_tn(a, b):
    return lax.dot_general(a, b, (((0,), (0,)), ((), ())), preferred_element_type=F32)


def sigmoid(v):
    return 0.5 * jnp.tanh(0.5 * v) + 0.5


def gelu(v):
    t = jnp.tanh(v * (GELU_A + (GELU_A * GELU_B) * (v * v)))
    h = 0.5 * v
    return h + h * t


def gelu_pair(v):
    w = v * v
    t = jnp.tanh(v * (GELU_A + (GELU_A * GELU_B) * w))
    h = 0.5 * v
    slope = 0.5 + 0.5 * t + (h - h * (t * t)) * (GELU_A + (3.0 * GELU_A * GELU_B) * w)
    return h + h * t, slope


def row_iota(shape):
    return lax.broadcasted_iota(jnp.int32, shape, 0)


def at(j):
    return pl.ds(pl.multiple_of(j * TILE, TILE), TILE)


def scan_tile(a, b, reverse):
    rows = row_iota(a.shape)
    step = 1
    while step < TILE:
        if reverse:
            keep, shift = rows < TILE - step, TILE - step
        else:
            keep, shift = rows >= step, step
        b = jnp.where(keep, a * pltpu.roll(b, shift, 0) + b, b)
        a = jnp.where(keep, a * pltpu.roll(a, shift, 0), a)
        step *= 2
    return a, b


def shift_down(cur, prev, k):
    if k == 0:
        return cur
    rows = row_iota(cur.shape)
    return jnp.where(rows < k, pltpu.roll(prev, k, 0), pltpu.roll(cur, k, 0))


def shift_up(cur, later, k):
    if k == 0:
        return cur
    rows = row_iota(cur.shape)
    return jnp.where(
        rows >= TILE - k, pltpu.roll(later, TILE - k, 0), pltpu.roll(cur, TILE - k, 0)
    )


def fold(v):
    return v[0:8] + v[8:16]


def flat(block):
    return block.reshape(-1, block.shape[-1])


def gates(dp, ip, c8):
    rate = sigmoid(dp)
    opening = sigmoid(ip)
    log_decay = -c8 * (0.25 + rate)
    decay = jnp.exp(log_decay)
    square = -jnp.tanh(log_decay) * (1.0 + decay * decay)
    return rate, opening, decay, square


GB, IB, CW, CB, DB, OB, C8, S8 = 0, 1, 2, 6, 7, 8, 9, 10


def conv_tile(in_ref, pc_ref, j, live):
    cur = in_ref[at(j), :]
    prev = in_ref[at(j - 1), :] * live
    out = pc_ref[CB : CB + 1, :] + pc_ref[CW : CW + 1, :] * cur
    moved = [cur]
    for k in range(1, 4):
        m = shift_down(cur, prev, k)
        moved.append(m)
        out = out + pc_ref[CW + k : CW + k + 1, :] * m
    return out, moved


def place_of():
    s = lax.axis_index("seq")
    return s // 4, (s // 2) % 2, s % 2, lax.axis_index("row")


def device_at(y, x, c, z):
    return ((y * 2 + x) * 2 + c, z)


class Peers:
    def __init__(self, zcount):
        y, x, c, z = self.place = place_of()
        self.far = [(z + k) % zcount for k in range(1, zcount)]
        self.along = [device_at(y, x, c, q) for q in self.far]
        self.near = ((y + c) % 2, (x + 1 - c) % 2)
        self.first = device_at(*self.near, c, z)
        self.second = device_at((y + 1 - c) % 2, (x + c) % 2, c, z)
        self.other = device_at(y, x, 1 - c, z)

    def meet(self):
        everyone = [*self.along, self.first, self.second, self.other]
        barrier = pltpu.get_barrier_semaphore()
        for peer in everyone:
            pl.semaphore_signal(
                barrier, inc=1, device_id=peer, device_id_type=pl.DeviceIdType.MESH
            )
        pl.semaphore_wait(barrier, len(everyone))


def remote(source, target, send, recv, device):
    return pltpu.make_async_remote_copy(
        src_ref=source,
        dst_ref=target,
        send_sem=send,
        recv_sem=recv,
        device_id=device,
        device_id_type=pl.DeviceIdType.MESH,
    )


class Spread:
    def __init__(self, peers, own, full, send, recv):
        self.peers, self.own, self.full, self.send, self.recv = peers, own, full, send, recv

    def go(self, stage, act):
        y, x, c, z = self.peers.place
        p, full = self.peers, self.full
        if stage == 0:
            for k, device in enumerate(p.along):
                act(remote(self.own, full(y, x, c, z), self.send(k), self.recv(k), device))
            return
        k = len(p.along) + stage - 1
        if stage == 2:

            @pl.when(c == 0)
            def _():
                part = full(y, slice(None), c, slice(None))
                act(remote(part, part, self.send(k), self.recv(k), p.second))

            @pl.when(c == 1)
            def _():
                part = full(slice(None), x, c, slice(None))
                act(remote(part, part, self.send(k), self.recv(k), p.second))

            return
        if stage == 1:
            part, device = full(y, x, c, slice(None)), p.first
        else:
            part, device = full(slice(None), slice(None), c, slice(None)), p.other
        act(remote(part, part, self.send(k), self.recv(k), device))

    def start(self, stage):
        self.go(stage, lambda d: d.start())

    def arrive(self, stage):
        self.go(stage, lambda d: d.wait_recv())

    def drain(self):
        for stage in range(4):
            self.go(stage, lambda d: d.wait_send())


def wave_of(t, count, lags):
    for stage in range(len(lags), -1, -1):
        piece = t - sum(lags[:stage])
        if 0 <= piece < count:
            yield piece, stage


class Gather:
    def __init__(self, zcount, ins, outs, sems, chunks, lags):
        self.csem, self.ssem, self.rsem = sems
        self.peers = Peers(zcount)
        self.lags = lags
        y, x, c, z = self.peers.place
        self.spreads, self.copies = [], []
        for i, (which, start, size, target, offset) in enumerate(chunks):
            own = ins[which].at[pl.ds(start, size)]
            rows = pl.ds(offset, size)

            def full(a, b, d, e, ref=outs[target], rows=rows):
                return ref.at[a, b, d, e, rows]

            def send(k, i=i):
                return self.ssem.at[i, k]

            def recv(k, i=i):
                return self.rsem.at[i, k]

            self.spreads.append(Spread(self.peers, own, full, send, recv))
            self.copies.append(pltpu.make_async_copy(own, full(y, x, c, z), self.csem.at[i]))
        self.waves = len(chunks) + sum(lags) + 1

    def wave(self, t):
        for i, stage in wave_of(t, len(self.spreads), self.lags):
            if stage == 0:
                self.copies[i].start()
            elif stage == 1:
                self.copies[i].wait()
            if stage > 0:
                self.spreads[i].arrive(stage - 1)
            if stage < 4:
                self.spreads[i].start(stage)

    def drain(self):
        for spread in self.spreads:
            spread.drain()


def in_turn(weave, step, plan, first=0):
    def point(k):
        for s, points in enumerate(plan, first):
            if k < len(points) and points[k]:

                @pl.when(step == s)
                def _(todo=points[k]):
                    for t in todo:
                        weave.wave(t)

    return point


def spread_out(waves, ahead, steps, points):
    todo = list(range(waves))
    plan = []
    for s in range(steps):
        row = []
        for k in range(points):
            take = ahead if s == 0 and k == 0 else 1
            if s == steps - 1 and k == points - 1:
                take = len(todo)
            row.append(todo[:take])
            todo = todo[take:]
        plan.append(row)
    return plan


def paced(waves, ahead, marks):
    last = marks[-1][-1]
    plan = [[[] for _ in row] for row in marks]
    spots = [(t, s, k) for s, row in enumerate(marks) for k, t in enumerate(row)]
    for w in range(waves):
        due = last * max(0, w - ahead) / max(1, waves - ahead)
        _, s, k = next(spot for spot in spots if spot[0] >= due)
        plan[s][k].append(w)
    return plan


def row_chunks(parts, size):
    return [
        (which, start + i, size, target, offset + i)
        for which, start, count, target, offset in parts
        for i in range(0, count, size)
    ]


def gather_sems(count, zcount):
    links = pltpu.SemaphoreType.DMA((count, zcount + 2))
    return [pltpu.SemaphoreType.DMA((count,)), links, links]


CORE, GATES, SUMS, HALVED = 0, 1, 2, 3


class Scatter:
    def __init__(self, zcount, ins, outs, buffers, sems, chunks, lags):
        self.peers = Peers(zcount)
        self.zcount, self.chunks, self.lags = zcount, chunks, lags
        self.ins, self.outs, self.buffers = ins, outs, buffers
        self.csem, self.ssem, self.rsem = sems[:3]
        self.pieces = [Piece(self, i, sems[3:], *chunk) for i, chunk in enumerate(chunks)]
        self.waves = len(chunks) + sum(lags) + 1

    def wave(self, t):
        for i, stage in wave_of(t, len(self.pieces), self.lags):
            if stage <= 4 or self.pieces[i].spread is not None:
                self.pieces[i].step(stage)

    def drain(self):
        for piece in self.pieces:
            piece.drain()


def slot_of_core(i, slots):
    return i % slots


def add_into(into, i, part, j):
    into[i] = (into[i].astype(F32) + part[j].astype(F32)).astype(into.dtype)


class Piece:
    def __init__(self, owner, i, sems, kind, slot, which, source, span, target, place):
        self.o, self.i, self.kind, self.slot = owner, i, kind, slot
        self.a, self.r0, self.r1, self.r2, self.r3 = owner.buffers[kind]
        self.from_core = 0 if self.r0 is None else slot_of_core(i, self.r0.shape[0])
        self.source, self.lead, self.rows = owner.ins[which], source, pl.ds(*span)
        self.target, self.place = owner.outs[target], place
        self.spread, self.drained = None, False
        if kind in (GATES, SUMS):
            y, x, c, z = owner.peers.place

            def full(*at_place):
                return self.target.at[at_place]

            def send(k):
                return sems[0].at[i, k]

            def recv(k):
                return sems[1].at[i, k]

            self.spread = Spread(owner.peers, full(y, x, c, z), full, send, recv)

    def local(self):
        c = self.o.peers.place[2]
        if self.kind == HALVED:
            mine = self.source.at[self.lead]
        else:
            mine = self.source.at[:, :, c, :, self.rows]
        return pltpu.make_async_copy(mine, self.a.at[self.slot], self.o.csem.at[self.i])

    def send(self, stage, act):
        s, peers = self.slot, self.o.peers
        y, x, c, z = peers.place

        def go(source, target, k, device):
            act(remote(source, target, self.o.ssem.at[self.i, k], self.o.rsem.at[self.i, k], device))

        if stage == 0:
            if self.kind != HALVED:
                theirs = self.source.at[:, :, 1 - c, :, self.rows]
                go(theirs, self.r0.at[self.from_core], 0, peers.other)
        elif stage == 1:

            @pl.when(c == 0)
            def _():
                go(self.a.at[s, 1 - y], self.r1.at[s], 1, peers.second)

            @pl.when(c == 1)
            def _():
                go(self.a.at[s, :, 1 - x], self.r1.at[s], 1, peers.second)

        elif stage == 2:
            go(self.a.at[(s, *peers.near)], self.r2.at[s], 2, peers.first)
        else:
            for k, device in enumerate(peers.along):
                go(self.a.at[s, y, x, peers.far[k]], self.r3.at[s, k], 3 + k, device)

    def step(self, stage):
        s, zcount = self.slot, self.o.zcount
        y, x, c, z = self.o.peers.place
        if stage == 0:
            for earlier in self.o.pieces[: self.i]:
                if earlier.a is self.a and earlier.slot == s:
                    earlier.drain()
            self.local().start()
        elif stage <= 4:
            self.send(stage - 1, lambda d: d.wait_recv())
        else:
            self.spread.arrive(stage - 5)
        if stage == 1:
            self.local().wait()
            if self.kind != HALVED:

                @pl.loop(0, 4 * zcount)
                def _(q):
                    i = (q // (2 * zcount), (q // zcount) % 2, q % zcount)
                    add_into(self.a, (s, *i), self.r0, (self.from_core, *i))

        elif stage == 2:

            @pl.loop(0, 2 * zcount)
            def _(q):
                h = q // zcount
                i = (s, y * (1 - c) + h * c, h * (1 - c) + x * c, q % zcount)
                add_into(self.a, i, self.r1, (s, h, q % zcount))

        elif stage == 3:

            @pl.loop(0, zcount)
            def _(q):
                add_into(self.a, (s, y, x, q), self.r2, (s, q))

        elif stage == 4:
            total = self.a[s, y, x, z].astype(F32)
            for k in range(zcount - 1):
                total = total + self.r3[s, k].astype(F32)
            if self.spread is None:
                self.target[self.place : self.place + total.shape[0]] = total
            else:
                self.target[y, x, c, z] = total.astype(self.target.dtype)
        if stage < 4:
            self.send(stage, lambda d: d.start())
        elif stage < 8 and self.spread is not None:
            self.spread.start(stage - 4)

    def drain(self):
        if self.drained:
            return
        self.drained = True
        for stage in range(4):
            self.send(stage, lambda d: d.wait_send())
        if self.spread is not None:
            self.spread.drain()


def five(number, shape, dtype, zcount):
    lead = [(2, 2, zcount), (2, 2, zcount), (2, zcount), (zcount,), (zcount - 1,)]
    return [pltpu.VMEM((number, *d, *shape), dtype) for d in lead]


def halved_scratch(count, slots, depth, zcount):
    lone = five(slots, (16, depth), BF16, zcount)
    links = pltpu.SemaphoreType.DMA((count, zcount + 2))
    return [lone[0], *lone[2:], pltpu.SemaphoreType.DMA((count,)), links, links, links, links]


def no_point(k):
    pass


class Exchange:
    def __init__(self, mine, theirs, ssem, rsem):
        self.mine, self.theirs, self.ssem, self.rsem = mine, theirs, ssem, rsem
        self.count = lax.axis_size("seq")
        self.place = lax.axis_index("seq")

    def peer(self, k):
        return (lax.rem(self.place + k, self.count), lax.axis_index("row"))

    def go(self, g, act):
        for k in range(1, self.count):
            act(
                remote(
                    self.mine.at[g],
                    self.theirs.at[g, self.place],
                    self.ssem.at[g, k - 1],
                    self.rsem.at[g, k - 1],
                    self.peer(k),
                )
            )

    def start(self, g):
        self.go(g, lambda d: d.start())

    def entering(self, g, reverse):
        self.go(g, lambda d: d.wait_recv())
        state = jnp.zeros((1, self.mine.shape[-1]), F32)
        for hop in range(self.count - 1):
            source = self.count - 1 - hop if reverse else hop
            ahead = source > self.place if reverse else source < self.place
            reach = self.theirs[g, source, 0:1, :]
            drive = self.theirs[g, source, 1:2, :]
            state = jnp.where(ahead, reach * state + drive, state)
        return state

    def drain(self, groups):
        for g in range(groups):
            self.go(g, lambda d: d.wait_send())


def exchange_scratch(groups, width, count):
    links = pltpu.SemaphoreType.DMA((groups, count - 1))
    return [
        pltpu.VMEM((groups, 8, width), F32),
        pltpu.VMEM((groups, count, 8, width), F32),
        links, links,
    ]


def meet_all(exchange, zcount):
    place, row = exchange.place, lax.axis_index("row")
    everyone = [exchange.peer(k) for k in range(1, exchange.count)]
    everyone += [(place, lax.rem(row + k, zcount)) for k in range(1, zcount)]
    barrier = pltpu.get_barrier_semaphore()
    for peer in everyone:
        pl.semaphore_signal(barrier, inc=1, device_id=peer, device_id_type=pl.DeviceIdType.MESH)
    pl.semaphore_wait(barrier, len(everyone))


def pair_up(pair, blocks):
    half = blocks.shape[1]
    pair[...] = jnp.zeros_like(pair)
    pair[0:half, 0:half] = blocks[0]
    pair[half:, half:] = blocks[1]


def front_kernel(ltiles, tiles, groups, links, *refs):
    (
        long_ref, short_ref, lcot_ref, scot_ref, length_ref, gain_ref, *channel_refs
    ) = refs[:14]
    wd_ref, wo_ref = refs[14:16]
    refs = refs[16:]
    step = pl.program_id(0)
    point, gather = no_point, None
    zcount = 1
    if links is None:
        pairw, refs = refs[0], refs[1:]
    else:
        zcount, chunks, lags, ready, plan = links
        owns, made = refs[:6], refs[18:21]
        pairw = made[0]
        gather = Gather(zcount, owns, made, refs[-3:], chunks, lags)
        refs = refs[6:18] + refs[21:-3]
        point = in_turn(gather, step, plan)
    gp, inn, dp, ip, st, pr, mix, sin_ref, nm_ref, x_ref, cot_ref, pc_ref = refs[:12]
    cv_ref, cl_ref, wbuf, pairs, halo, isem, wsem, hsem, *swap = refs[12:]
    exchange = Exchange(*swap)
    lrows = ltiles * TILE
    place = exchange.place

    def load(g):
        return pltpu.make_async_copy(pairw.at[g // 2, g % 2], wbuf.at[g % 2], wsem.at[g % 2])

    @pl.when(step == 0)
    def _():
        srows = short_ref.shape[0]
        copies = [
            pltpu.make_async_copy(source, target, isem.at[k])
            for k, (source, target) in enumerate(
                [
                    (long_ref, x_ref.at[pl.ds(HALO, lrows)]),
                    (short_ref, x_ref.at[pl.ds(HALO + lrows, srows)]),
                    (lcot_ref, cot_ref.at[pl.ds(0, lrows)]),
                    (scot_ref, cot_ref.at[pl.ds(lrows, srows)]),
                ]
            )
        ]
        for copy in copies:
            copy.start()
        meet_all(exchange, zcount)
        ahead = remote(
            long_ref.at[pl.ds(lrows - HALO, HALO)], halo, hsem.at[0], hsem.at[1], exchange.peer(1)
        )
        ahead.start()
        todo = [] if gather is None else list(range(ready))

        def some(count):
            for t in todo[:count]:
                gather.wave(t)
            del todo[:count]

        some(4)
        for copy in copies:
            copy.wait()

        @pl.loop(0, ltiles)
        def _(i):
            rows = row_iota((TILE, 1)) + (place * lrows + i * TILE)
            keep = jnp.where(rows < length_ref[0], 1.0, 0.0)
            cot_ref[at(i), :] = (cot_ref[at(i), :].astype(F32) * keep).astype(BF16)

        some(1)
        ahead.wait_recv()
        x_ref[0:HALO, :] = halo[...]

        def norm(j):
            v = x_ref[at(j), :].astype(F32)
            s = lax.rsqrt(jnp.mean(v * v, axis=1, keepdims=True) + EPSILON)
            nm_ref[at(j), :] = (v * s * gain_ref[...]).astype(BF16)

        pl.loop(0, tiles // 2)(norm)
        some(1)
        pl.loop(tiles // 2, tiles)(norm)
        some(len(todo))
        ahead.wait_send()
        load(0).start()
        load(1).start()

    @pl.when(step > 0)
    def _():
        for g in range(groups):

            @pl.when(step == g + 1)
            def _(g=g):
                load(g).wait()

        for k, ref in zip((GB, IB, CW, CB, DB, OB, C8, S8), channel_refs):
            pc_ref[k : k + ref.shape[0], :] = ref[...]
        pc_ref[S8 + 1 :, :] = jnp.zeros((15 - S8, pc_ref.shape[1]), F32)
        pair_up(pairs.at[0], wd_ref)
        pair_up(pairs.at[1], wo_ref)
        slot = lax.rem(step - 1, 2)
        share = wbuf.shape[-2] // 2
        front_part(
            ltiles, tiles, point, place, nm_ref, wbuf.at[slot, :, :, 0:share],
            wbuf.at[slot, :, :, share : 2 * share], pairs, pc_ref, gp, inn, dp, ip, st, pr, mix,
            exchange.mine.at[step - 1], cv_ref, cl_ref,
        )
        for g in range(groups):

            @pl.when(step == g + 1)
            def _(g=g):
                if g + 2 < groups:
                    load(g + 2).start()
                exchange.theirs[g, place] = jnp.zeros(exchange.theirs.shape[2:], F32)
                exchange.start(g)

        point(3)

    @pl.when(step == groups)
    def _():
        width = gp.shape[1]
        for g in range(groups):
            state = exchange.entering(g, False)
            sin_ref[:, g * width : (g + 1) * width] = jnp.broadcast_to(state, (8, width))
        exchange.drain(groups)
        if gather is not None:
            gather.drain()


def front_part(
    ltiles, tiles, point, place, nm_ref, wg_ref, wi_ref, pairs, pc_ref, gp_ref, in_ref, dp_ref,
    ip_ref, st_ref, pr_ref, mix_ref, end_ref, cv_ref, cl_ref,
):
    point(0)
    nm = nm_ref[...]
    gp_ref[...] = dot_nt(nm, flat(wg_ref[...])) + pc_ref[GB : GB + 1, :]
    in_ref[...] = dot_nt(nm, flat(wi_ref[...])) + pc_ref[IB : IB + 1, :]
    point(1)
    in_ref[0:HALO, :] = in_ref[0:HALO, :] * jnp.where(place > 0, 1.0, 0.0)
    cl_ref[0:HALO, :] = jnp.zeros((HALO, cl_ref.shape[1]), BF16)

    @pl.loop(1, tiles)
    def _(j):
        live = jnp.where(j == 1 + ltiles, 0.0, 1.0)
        out, _ = conv_tile(in_ref, pc_ref, j, live)
        cv_ref[at(j), :] = out
        cl_ref[at(j), :] = out.astype(BF16)

    point(2)
    low = cl_ref[...]
    dp_ref[...] = dot_nn(low, pairs[0]) + pc_ref[DB : DB + 1, :]
    ip_ref[...] = dot_nn(low, pairs[1]) + pc_ref[OB : OB + 1, :]

    def scanned(j):
        _, opening, a, square = gates(dp_ref[at(j), :], ip_ref[at(j), :], pc_ref[C8 : C8 + 1, :])
        b = (square * lax.rsqrt(square)) * opening * cv_ref[at(j), :]
        return scan_tile(a, b, False)

    width = gp_ref.shape[1]

    def long_step(i, carry):
        state, reach = carry
        a, b = scanned(1 + i)
        s = b + a * state
        r = a * reach
        st_ref[at(1 + i), :] = s
        pr_ref[at(1 + i), :] = r
        return s[TILE - 1 : TILE], r[TILE - 1 : TILE]

    state, reach = lax.fori_loop(
        0, ltiles, long_step, (jnp.zeros((1, width), F32), jnp.ones((1, width), F32))
    )
    end_ref[...] = jnp.concatenate([reach, state, jnp.zeros((6, width), F32)], axis=0)

    def short_step(i, state):
        j = 1 + ltiles + i
        a, b = scanned(j)
        s = b + a * state
        st_ref[at(j), :] = s
        mix_ref[at(i), :] = (s * gelu(gp_ref[at(j), :])).astype(BF16)
        return s[TILE - 1 : TILE]

    lax.fori_loop(0, tiles - 1 - ltiles, short_step, jnp.zeros((1, width), F32))


def mlp_kernel(ltiles, tiles, links, *refs):
    (
        x_ref, cot_ref, st_ref, pr_ref, gp_ref, sin_ref, mixs_ref, wo_ref, gain_ref, w1_ref, w2_ref
    ) = refs[:11]
    refs = refs[11:]
    point, gather = no_point, None
    step = pl.program_id(0)
    last = pl.num_programs(0) - 1
    if links is not None:
        zcount, chunks, lags, plan, sum_chunks, sum_lags, sum_plan = links
        owns = [w2_ref, *refs[:2]]
        refs = refs[2:]
    outl_ref, outs_ref, dres_ref, rlow_ref, mixl_ref, gain_grad_ref, dw_hbm = refs[:7]
    refs = refs[7:]
    if links is not None:
        w2_ref, early_ref = refs[:2]
        halved = (refs[-9], None, *refs[-8:-5])
        buffers = [None, None, None, halved]
        scatter = Scatter(zcount, [dw_hbm], [early_ref], buffers, refs[-5:], sum_chunks, sum_lags)
        refs = refs[2:-9]
        gather = Gather(zcount, owns, [w2_ref], refs[-3:], chunks, lags)
        got_ref, sems, credit = refs[-6], refs[-5], refs[-4]
        refs = refs[:-6]
        gather_point = in_turn(gather, step, plan)
        scatter_point = in_turn(scatter, step, sum_plan)

        def point(k):
            gather_point(k)
            scatter_point(k)

    (
        n2_ref, acc_o, acc_n, gu_ref, d_ref, h_ref, dgu_ref, wbuf, dwbuf, wsem, dsem
    ) = refs
    lrows = ltiles * TILE
    hid = h_ref.shape[1]
    half = hid // 2
    share = wbuf.shape[-2]
    rows = 3 * share
    ready = w1_ref.shape[-2] // rows
    steps = ready + w2_ref.shape[-2] // rows

    def load(s):
        source, part = (w1_ref, s) if s < ready else (w2_ref, s - ready)
        return [
            pltpu.make_async_copy(
                source.at[:, :, :, :, pl.ds(part * rows + k * share, share)],
                wbuf.at[s % 2, k],
                wsem.at[s % 2, k],
            )
            for k in range(3)
        ]

    def start_load(s):
        for copy in load(s):
            copy.start()

    def wait_load(s):
        for copy in load(s):
            copy.wait()

    def load_next(s):
        if s + 1 < steps and s + 1 >= min(2, ready):
            start_load(s + 1)

    def each(todo, first=0):
        for s in range(first, steps):

            @pl.when(step == s)
            def _(s=s):
                todo(s)

    if gather is not None:
        y, x, c, z = gather.peers.place

    def store(s):
        mine = dwbuf if gather is None else dwbuf.at[:, :, :, c]
        return pltpu.make_async_copy(mine, dw_hbm.at[s], dsem)

    def swap():
        return remote(
            dwbuf.at[:, :, :, 1 - c], got_ref, sems.at[0], sems.at[1], gather.peers.other
        )

    def settle(s):
        if gather is not None:
            swap().wait_recv()

            @pl.loop(0, SLOTS // 2)
            def _(k):
                i, j, m = k // (2 * GRID[3]), (k // GRID[3]) % 2, k % GRID[3]
                for n in range(3):
                    both = dwbuf[n, i, j, c, m].astype(F32) + got_ref[n, i, j, m].astype(F32)
                    dwbuf[n, i, j, c, m] = both.astype(BF16)

            if s < steps - 1:
                pl.semaphore_signal(
                    credit,
                    inc=1,
                    device_id=gather.peers.other,
                    device_id_type=pl.DeviceIdType.MESH,
                )
        store(s).start()

    def clear(s):
        store(s).wait()
        if gather is not None:
            swap().wait_send()

    @pl.when(step == 0)
    def _():
        for s in range(min(2, ready)):
            start_load(s)
        if gather is not None:
            gather.peers.meet()

    point(0)

    @pl.when(step == 0)
    def _():
        s_in = sin_ref[0:1, :]

        @pl.loop(0, ltiles)
        def _(i):
            s = st_ref[at(1 + i), :] + pr_ref[at(1 + i), :] * s_in
            mixl_ref[at(i), :] = (s * gelu(gp_ref[at(1 + i), :])).astype(BF16)

        wo = flat(wo_ref[...])
        dres_ref[0:lrows, :] = dot_nn(mixl_ref[...], wo)
        dres_ref[lrows:, :] = dot_nn(mixs_ref[...], wo)

        @pl.loop(0, tiles)
        def _(i):
            r = dres_ref[at(i), :] + x_ref[at(1 + i), :].astype(F32)
            dres_ref[at(i), :] = r
            acc_o[at(i), :] = r
            s = lax.rsqrt(jnp.mean(r * r, axis=1, keepdims=True) + EPSILON)
            n2_ref[at(i), :] = (r * s * gain_ref[...]).astype(BF16)

        acc_n[...] = jnp.zeros_like(acc_n)

    point(1)

    each(wait_load)
    slot = lax.rem(step, 2)

    def gate_up():
        return flat(wbuf[slot, 0:2])

    def down():
        return flat(wbuf[slot, 2])

    gu_ref[...] = dot_nt(n2_ref[...], gate_up())
    point(2)
    d_ref[...] = dot_nt(cot_ref[...], down())
    each(lambda s: settle(s - 1), 1)
    point(3)

    @pl.loop(0, tiles)
    def _(i):
        for k in range(2):
            cols = slice(k * half, (k + 1) * half)
            more = slice(hid + k * half, hid + (k + 1) * half)
            ge, slope = gelu_pair(gu_ref[at(i), cols])
            u = gu_ref[at(i), more]
            d = d_ref[at(i), cols]
            h_ref[at(i), cols] = (ge * u).astype(BF16)
            dgu_ref[at(i), cols] = (d * u * slope).astype(BF16)
            dgu_ref[at(i), more] = (d * ge).astype(BF16)

    point(4)
    acc_o[...] += dot_nn(h_ref[...], down())
    point(5)
    acc_n[...] += dot_nn(dgu_ref[...], gate_up())
    point(6)
    each(lambda s: clear(s - 1), 1)
    dwbuf[2] = dot_tn(h_ref[...], cot_ref[...]).astype(BF16).reshape(dwbuf.shape[1:])
    point(7)
    each(load_next)
    grad = dot_tn(dgu_ref[...], n2_ref[...]).astype(BF16)
    dwbuf[0:2] = grad.reshape((2,) + dwbuf.shape[1:])

    if gather is not None:
        @pl.when(step > 0)
        def _():
            pl.semaphore_wait(credit, 1)

        swap().start()

    @pl.when(step == last)
    def _():
        def one(i, total):
            r = dres_ref[at(i), :]
            dn = acc_n[at(i), :]
            s = lax.rsqrt(jnp.mean(r * r, axis=1, keepdims=True) + EPSILON)
            e = dn * gain_ref[...]
            inner = jnp.mean(e * r, axis=1, keepdims=True)
            dr = cot_ref[at(i), :].astype(F32) + s * e - r * (s * s * s * inner)
            dres_ref[at(i), :] = dr
            rlow_ref[at(i), :] = dr.astype(BF16)
            return total + fold(dn * (r * s))

        gain_grad_ref[...] = lax.fori_loop(0, tiles, one, jnp.zeros(gain_grad_ref.shape, F32))
        outl_ref[...] = acc_o[0:lrows, :].astype(BF16)
        outs_ref[...] = acc_o[lrows:, :].astype(BF16)
        settle(steps - 1)
        clear(steps - 1)

    point(8)
    if gather is not None:

        @pl.when(step == last)
        def _():
            gather.drain()
            scatter.drain()


def back_part(
    ltiles, tiles, point, rlow_ref, wo_ref, mixl_ref, mixs_ref, gp_ref, st_ref, pr_ref, sin_ref,
    dp_ref, pc_ref, dwo_ref, gl_ref, tot_ref, rch_ref, end_ref, bias_ref, dm_ref, free,
):
    point(0)
    lrows = ltiles * TILE
    width = gp_ref.shape[1]
    rlow = rlow_ref[...]
    dm_ref[...] = dot_nt(rlow, flat(wo_ref[...]))
    free()
    grad = dot_tn(mixl_ref[...], rlow_ref[0:lrows, :]) + dot_tn(mixs_ref[...], rlow_ref[lrows:, :])
    dwo_ref[...] = grad.astype(BF16).reshape(dwo_ref.shape)
    point(1)
    gl_ref[0:HALO, :] = jnp.zeros((HALO, width), BF16)
    last = row_iota((TILE, width)) == TILE - 1

    def local(j, states):
        dm = dm_ref[at(j - 1), :]
        ge, slope = gelu_pair(gp_ref[at(j), :])
        dgate = dm * states * slope
        gl_ref[at(j), :] = dgate.astype(BF16)
        ds = dm * ge
        rate = sigmoid(dp_ref[at(j), :])
        decay = jnp.exp(-pc_ref[C8 : C8 + 1, :] * (0.25 + rate))
        a, b = scan_tile(decay, decay * ds, True)
        return a, b, ds, fold(dgate)

    def short_step(i, carry):
        c, bias = carry
        j = tiles - 1 - i
        a, b, ds, part = local(j, st_ref[at(j), :])
        cs = b + a * c
        tot_ref[at(j), :] = ds + jnp.where(last, c, pltpu.roll(cs, TILE - 1, 0))
        return cs[0:1], bias + part

    _, bias = lax.fori_loop(
        0,
        tiles - 1 - ltiles,
        short_step,
        (jnp.zeros((1, width), F32), jnp.zeros((8, width), F32)),
    )
    point(2)
    s_in = sin_ref[0:1, :]

    def long_step(i, carry):
        c, reach, bias = carry
        j = ltiles - i
        a, b, ds, part = local(j, st_ref[at(j), :] + pr_ref[at(j), :] * s_in)
        cs = b + a * c
        rs = a * reach
        tot_ref[at(j), :] = ds + jnp.where(last, c, pltpu.roll(cs, TILE - 1, 0))
        rch_ref[at(j), :] = jnp.where(last, reach, pltpu.roll(rs, TILE - 1, 0))
        return cs[0:1], rs[0:1], bias + part

    c, reach, bias = lax.fori_loop(
        0, ltiles, long_step, (jnp.zeros((1, width), F32), jnp.ones((1, width), F32), bias)
    )
    end_ref[...] = jnp.concatenate([reach, c, jnp.zeros((6, width), F32)], axis=0)
    bias_ref[...] = bias


def last_part(
    ltiles, tiles, groups, point, exchange, residual, x_ref, gain_ref, nm_ref, wg_ref, wi_ref,
    wd_ref, wo_ref, pc_ref, in_ref, dp_ref, ip_ref, st_ref, pr_ref, sin_ref, tot_ref, rch_ref,
    gl_ref, bias_ref, dxl_ref, dxs_ref, halo_ref, behind, pairs, gain_grad_ref, dwg_ref, dwi_ref,
    gg_ref, small_ref, acc, dc_ref, cl_ref, dl_ref, ol_ref, il_ref, gain2_ref, free, keep,
):
    width = in_ref.shape[1]
    step = pl.program_id(0) - groups
    point(0)
    for g in range(groups):

        @pl.when(step == g)
        def _(g=g):
            dc_ref[0:1, :] = exchange.entering(g, True)

    c_in = dc_ref[0:1, :]

    @pl.when(step == groups - 1)
    def _():
        for copy in residual:
            copy.start()

    first = jnp.where(exchange.place > 0, 1.0, 0.0)
    pair_up(pairs.at[0], wd_ref)
    pair_up(pairs.at[1], wo_ref)
    zero8 = jnp.zeros((8, width), F32)
    cl_ref[0:HALO, :] = jnp.zeros((HALO, width), BF16)
    dl_ref[0:HALO, :] = jnp.zeros((HALO, width), BF16)
    ol_ref[0:HALO, :] = jnp.zeros((HALO, width), BF16)
    dc_ref[0:HALO, :] = jnp.zeros((HALO, width), F32)

    def gate_step(j, states, total, live, carry):
        before, sum_d, sum_o, sum_p = carry
        rows = row_iota((TILE, width))
        prior = jnp.where(rows == 0, before, pltpu.roll(states, 1, 0))
        conv, _ = conv_tile(in_ref, pc_ref, j, live)
        rate, opening, decay, square = gates(
            dp_ref[at(j), :], ip_ref[at(j), :], pc_ref[C8 : C8 + 1, :]
        )
        inv = lax.rsqrt(square)
        mult = square * inv
        weighted = total * opening
        d_open = total * mult * conv
        d_log = decay * (total * prior - (weighted * conv) * (decay * inv))
        d_rate = -pc_ref[C8 : C8 + 1, :] * d_log
        d_dp = d_rate * (rate - rate * rate)
        d_ip = d_open * (opening - opening * opening)
        cl_ref[at(j), :] = conv.astype(BF16)
        dl_ref[at(j), :] = d_dp.astype(BF16)
        ol_ref[at(j), :] = d_ip.astype(BF16)
        dc_ref[at(j), :] = weighted * mult
        return (
            states[TILE - 1 : TILE],
            sum_d + fold(d_dp),
            sum_o + fold(d_ip),
            sum_p - fold((0.25 + rate) * d_log),
        )

    s_in = sin_ref[0:1, :]

    def long_step(i, carry):
        j = 1 + i
        states = st_ref[at(j), :] + pr_ref[at(j), :] * s_in
        total = tot_ref[at(j), :] + rch_ref[at(j), :] * c_in
        return gate_step(j, states, total, 1.0, carry)

    def short_step(i, carry):
        j = 1 + ltiles + i
        return gate_step(j, st_ref[at(j), :], tot_ref[at(j), :], jnp.where(i == 0, 0.0, 1.0), carry)

    carry = lax.fori_loop(0, ltiles, long_step, (s_in, zero8, zero8, zero8))
    carry = lax.fori_loop(
        0, tiles - 1 - ltiles, short_step, (jnp.zeros((1, width), F32),) + carry[1:]
    )
    _, sum_d, sum_o, sum_p = carry
    point(1)

    low, dlow, olow = cl_ref[...], dl_ref[...], ol_ref[...]
    half = width // 2
    for which, grads in ((0, dlow), (1, olow)):
        product = dot_tn(low, grads).astype(BF16)
        shape = (2, half // 2, half)
        place = (which, step // 2, lax.rem(step, 2))
        gg_ref[(*place, slice(0, 2))] = product[:half, :half].reshape(shape)
        gg_ref[(*place, slice(2, 4))] = product[half:, half:].reshape(shape)
    dc_ref[...] += dot_nt(dlow, pairs[0]) + dot_nt(olow, pairs[1])

    point(2)

    def conv_step(j, carry):
        sum_c, sum_i, sums = carry
        live = jnp.where(j == 1 + ltiles, 0.0, 1.0)
        cur = dc_ref[at(j), :]
        up = jnp.where((j == ltiles) | (j == tiles - 1), 0.0, 1.0)
        later = dc_ref[at(jnp.minimum(j + 1, tiles - 1)), :] * up
        _, moved = conv_tile(in_ref, pc_ref, jnp.maximum(j, 1), live)
        d_in = pc_ref[CW : CW + 1, :] * cur
        for k in range(1, 4):
            d_in = d_in + pc_ref[CW + k : CW + k + 1, :] * shift_up(cur, later, k)
        d_in = d_in * jnp.where(j == 0, first, 1.0)
        il_ref[at(j), :] = d_in.astype(BF16)
        return (
            sum_c + fold(cur),
            sum_i + fold(d_in),
            tuple(s + fold(cur * m) for s, m in zip(sums, moved)),
        )

    sum_c, sum_i, sums = lax.fori_loop(0, tiles, conv_step, (zero8, zero8, (zero8,) * 4))
    parts = [sum_i, *sums, sum_c, sum_d, sum_o, sum_p * pc_ref[S8 : S8 + 1, :], bias_ref[...]]
    rows = [jnp.sum(p, axis=0, keepdims=True) for p in parts]
    block = jnp.concatenate(rows + [jnp.zeros((16 - len(rows), width), F32)], axis=0)
    for i in range(width // 128):
        at_block = step * (width // 128) + i
        x, c, z = at_block // 8, lax.rem(at_block // 4, 2), lax.rem(at_block, 4)
        for h in range(2):
            small_ref[h, x, c, z] = block[8 * h : 8 * h + 8, 128 * i : 128 * i + 128]

    point(3)
    free()
    nm = nm_ref[...]
    dwi_ref[...] = dot_tn(il_ref[...], nm).astype(BF16).reshape(dwi_ref.shape)
    dwg_ref[...] = dot_tn(gl_ref[...], nm).astype(BF16).reshape(dwg_ref.shape)
    keep()
    point(4)
    part = dot_nn(gl_ref[...], flat(wg_ref[...])) + dot_nn(il_ref[...], flat(wi_ref[...]))

    @pl.when(step == 0)
    def _():
        acc[...] = part

    @pl.when(step > 0)
    def _():
        acc[...] += part

    @pl.when(step == groups - 1)
    def _():
        for copy in residual:
            copy.wait()

        def norm_back(j):
            v = x_ref[at(j), :].astype(F32)
            dn = acc[at(j), :]
            s = lax.rsqrt(jnp.mean(v * v, axis=1, keepdims=True) + EPSILON)
            e = dn * gain_ref[...]
            inner = jnp.mean(e * v, axis=1, keepdims=True)
            return s * e - v * (s * s * s * inner), fold(dn * (v * s))

        halo, total = norm_back(0)
        halo_ref[...] = halo
        behind.start()
        done = 1
        for ref in (dxl_ref, dxs_ref):

            def one(i, total, ref=ref, done=done):
                d, part = norm_back(done + i)
                ref[at(i), :] = ref[at(i), :] + d
                return total + part

            total = lax.fori_loop(0, ref.shape[0] // TILE, one, total)
            done += ref.shape[0] // TILE
        gain_grad_ref[...] = total
        zero = jnp.zeros((8, 128), F32)
        for h in range(2):
            for z in range(4):
                small_ref[h, 1, 1, z] = zero
        for z, ref in enumerate((gain_grad_ref, gain2_ref)):
            total = jnp.sum(ref[...], axis=0, keepdims=True)
            for i in range(8):
                small_ref[0, 1, 1, z, i : i + 1, :] = total[:, 128 * i : 128 * i + 128]

    point(5)


def tail_kernel(ltiles, tiles, groups, links, *refs):
    (
        x_ref, gain_ref, nm_ref, dres_hbm, rlow_ref, w_ref, wg_ref, wi_ref, wd_ref, wo_ref, pc_ref,
        mixl_ref, mixs_ref, gp_ref, in_ref, dp_ref, ip_ref, st_ref, pr_ref, sin_ref, gain2_ref,
    ) = refs[:21]
    refs = refs[21:]
    step = pl.program_id(0)
    group = lax.rem(step, groups)
    back_point, last_point, scatter = no_point, no_point, None
    nscratch = 23
    if links is not None:
        zcount, chunks, lags, plan = links
        halved_ref, early_ref, refs = refs[0], refs[1], refs[2:]
        outs, shares = refs[:8], refs[8:14]
        scratch, pool = refs[14 : 14 + nscratch], refs[14 + nscratch :]
    else:
        outs, scratch = refs[:8], refs[8:]
    dxl_ref, dxs_ref, gain_grad_ref, dwo_hbm, dwg_hbm, dwi_hbm, gates_hbm, sums_hbm = outs
    (
        acc, dc_ref, cl_ref, dl_ref, ol_ref, il_ref, gls, tots, rchs, bias_ref, wst, gsrc, ssrc,
        pairs, halo_out, halo_in, hsem, dsem, wsem, *swap
    ) = scratch
    gates_full, sums_full = gsrc, ssrc
    if links is not None:
        *pool, gates_full, sums_full = pool
        main, gate_pool, sum_pool = pool[0:5], pool[5:10], pool[10:15]
        scatter = Scatter(
            zcount,
            [halved_ref, dwo_hbm, dwg_hbm, dwi_hbm, gsrc, ssrc],
            [*shares, gates_full, sums_full],
            [main, gate_pool, sum_pool, main],
            pool[15:],
            chunks,
            lags,
        )
        back_point = in_turn(scatter, step, plan[:groups])
        last_point = in_turn(scatter, step, plan[groups:], groups)

        @pl.when(step == 0)
        def _():
            rows = early_ref.shape[0] // 3
            for k in range(3):
                shares[k][0:rows, :] = early_ref[k * rows : (k + 1) * rows, :]

    def stash(g, k, target):
        return pltpu.make_async_copy(wst.at[k], target.at[g // 2, g % 2], wsem.at[k])

    def stashed(first, what):
        for g in range(groups):

            @pl.when(step == first + g)
            def _(g=g):
                what(g)

    exchange = Exchange(*swap)
    gl_ref, tot_ref, rch_ref = gls.at[group], tots.at[group], rchs.at[group]
    lrows = ltiles * TILE
    residual = [
        pltpu.make_async_copy(dres_hbm.at[pl.ds(0, lrows)], dxl_ref, dsem.at[0]),
        pltpu.make_async_copy(
            dres_hbm.at[pl.ds(lrows, dxs_ref.shape[0])], dxs_ref, dsem.at[1]
        ),
    ]
    behind = remote(
        halo_out, halo_in, hsem.at[0], hsem.at[1], exchange.peer(exchange.count - 1)
    )
    width = gp_ref.shape[1]

    @pl.when(step == 0)
    def _():
        meet_all(exchange, 1 if scatter is None else zcount)

    @pl.when(step < groups)
    def _():
        back_part(
            ltiles, tiles, back_point, rlow_ref, w_ref, mixl_ref, mixs_ref, gp_ref, st_ref, pr_ref,
            sin_ref, dp_ref, pc_ref, wst.at[0], gl_ref, tot_ref, rch_ref, exchange.mine.at[group],
            bias_ref.at[group], acc.at[0 : rlow_ref.shape[0], 0:width],
            lambda: stashed(0, lambda g: stash(g - 1, 0, dwo_hbm).wait() if g > 0 else None),
        )
        stashed(0, lambda g: stash(g, 0, dwo_hbm).start())
        for g in range(groups):

            @pl.when(step == g)
            def _(g=g):
                exchange.theirs[g, exchange.place] = jnp.zeros(exchange.theirs.shape[2:], F32)
                exchange.start(g)

    @pl.when(step >= groups)
    def _():
        @pl.when(step == groups)
        def _():
            stash(groups - 1, 0, dwo_hbm).wait()

        def before(g):
            if g > 0:
                stash(g - 1, 1, dwg_hbm).wait()
                stash(g - 1, 2, dwi_hbm).wait()

        def after(g):
            stash(g, 1, dwg_hbm).start()
            stash(g, 2, dwi_hbm).start()
            if g == groups - 1:
                stash(g, 1, dwg_hbm).wait()
                stash(g, 2, dwi_hbm).wait()

        last_part(
            ltiles, tiles, groups, last_point, exchange, residual, x_ref, gain_ref, nm_ref,
            wg_ref, wi_ref, wd_ref, wo_ref, pc_ref, in_ref, dp_ref, ip_ref, st_ref, pr_ref, sin_ref,
            tot_ref, rch_ref, gl_ref, bias_ref.at[group], dxl_ref, dxs_ref, halo_out, behind, pairs,
            gain_grad_ref, wst.at[1], wst.at[2], gsrc, ssrc, acc, dc_ref, cl_ref, dl_ref, ol_ref, il_ref, gain2_ref,
            lambda: stashed(groups, before), lambda: stashed(groups, after),
        )

    @pl.when(step == pl.num_programs(0) - 1)
    def _():
        exchange.drain(groups)
        behind.wait()
        rows = slice(lrows - HALO, lrows)
        dxl_ref[rows, :] = dxl_ref[rows, :] + halo_in[...]
        if scatter is not None:
            scatter.drain()
        final = [
            pltpu.make_async_copy(gates_full, gates_hbm, wsem.at[0]),
            pltpu.make_async_copy(sums_full, sums_hbm, wsem.at[1]),
        ]
        for copy in final:
            copy.start()
        for copy in final:
            copy.wait()


def shape_of(shape, dtype):
    return jax.ShapeDtypeStruct(shape, dtype)


def whole(shape):
    return pl.BlockSpec(shape, lambda g: (0,) * len(shape), pipeline_mode=pl.Buffered(1))


def params(limit, **more):
    return pltpu.CompilerParams(
        dimension_semantics=("arbitrary",), vmem_limit_bytes=int(limit * MIB), **more
    )


def to_slots(parts, count):
    rows = parts[0].shape[0]
    depth = parts[0].shape[1]
    got = lax.all_gather(jnp.concatenate(parts, axis=0), ("seq", "row"), axis=0, tiled=False)
    if count != SLOTS:
        got = got.reshape(count, len(parts), rows, depth).transpose(1, 0, 2, 3)
        got = got.reshape(len(parts), SLOTS, rows * count // SLOTS, depth).transpose(1, 0, 2, 3)
    return got.reshape(SLOTS, -1, depth)


def scatter_slots(grads, number, count):
    slots, rows, depth = grads.shape
    if count != SLOTS:
        grads = grads.reshape(slots, number, rows // number, depth).transpose(1, 0, 2, 3)
        grads = grads.reshape(number, count, -1, depth).transpose(1, 0, 2, 3)
    flat_grads = grads.reshape(slots * rows, depth)
    own = lax.psum_scatter(flat_grads, ("seq", "row"), scatter_dimension=0, tiled=True)
    own = own.astype(F32).reshape(number, -1, depth)
    return [own[i] for i in range(number)]


def shards(
    long_tokens,
    short_tokens,
    long_length,
    long_cotangent,
    short_cotangent,
    first_gain,
    gate_weight,
    gate_bias,
    input_weight,
    input_bias,
    conv_weight,
    conv_bias,
    decay_gate_weight,
    decay_gate_bias,
    input_gate_weight,
    input_gate_bias,
    decay_param,
    out_weight,
    second_gain,
    mlp_gate_weight,
    mlp_up_weight,
    mlp_down_weight,
):
    count = lax.axis_size("seq") * lax.axis_size("row")
    lrows, srows, depth = long_tokens.shape[1], short_tokens.shape[1], long_tokens.shape[2]
    chans = gate_bias.shape[0]
    units = mlp_gate_weight.shape[1] * count
    tokens = lrows + srows
    total = HALO + tokens
    ltiles, tiles = lrows // TILE, total // TILE
    cshare, ushare = chans // SLOTS, units // SLOTS
    groups = 4
    width = chans // groups
    per = SLOTS // groups

    zcount = lax.axis_size("row")
    seqs = lax.axis_size("seq")
    fast = seqs == 8 and count == SLOTS
    hbm = pl.BlockSpec(memory_space=pl.ANY)
    one_dma = pltpu.SemaphoreType.DMA
    steps = ushare // 16
    ready_parts = max(1, min(steps - 1, FRONT_PARTS))
    blocks, bwidth = decay_gate_weight.shape[0:2]
    mlp_own = [mlp_gate_weight.T, mlp_up_weight.T, mlp_down_weight]
    channel = [
        gate_bias, input_bias, conv_weight, conv_bias, decay_gate_bias, input_gate_bias,
        8.0 * jax.nn.softplus(decay_param), 8.0 * jax.nn.sigmoid(decay_param),
    ]
    channel = [c.reshape(-1, chans) for c in channel]
    gain1 = first_gain[None]
    gain2 = second_gain[None]

    def early(g):
        return jnp.minimum(g, groups - 1)

    def after_one(g):
        return jnp.maximum(g - 1, 0)

    def late(g):
        return jnp.maximum(g - groups, 0)

    def both_times(g):
        return lax.rem(g, groups)

    def slot_at(when, which=0):
        return pl.BlockSpec((per, cshare, depth), lambda g: (when(g), which, 0))

    def blocks_at(when):
        return pl.BlockSpec((2, bwidth, bwidth), lambda g: (when(g), 0, 0))

    def cols_at(nrows, when):
        return pl.BlockSpec((nrows, width), lambda g: (0, when(g)))

    lags = (2, 2, 3, 2)
    if fast:
        front_own = [gate_weight.T, input_weight.T, out_weight, *mlp_own]
        parts = [(0, 0, cshare, 0, 0), (1, 0, cshare, 0, cshare)]
        ready = len(row_chunks(parts, 16)) + sum(lags)
        parts += [(2, 0, cshare, 1, 0)]
        parts += [
            (3 + k, 16 * p, 16, 2, 48 * p + 16 * k) for p in range(ready_parts) for k in range(3)
        ]
        chunks = row_chunks(parts, 16)
        plan = [[]] + spread_out(len(chunks) + sum(lags) + 1 - ready, 1, groups, 4)
        plan = [[[ready + t for t in p] for p in row] for row in plan]
        front_links = (zcount, chunks, lags, ready, plan)
        front_shapes = [
            shape_of(GRID + (n, depth), BF16) for n in (2 * cshare, cshare, 48 * ready_parts)
        ]
        front_scratch = gather_sems(len(chunks), zcount)
    else:
        pairw = to_slots([gate_weight.T, input_weight.T], count)
        outw = to_slots([out_weight], count)
        mlpw = to_slots(mlp_own, count).reshape(GRID + (3, steps, 16, depth))
        mlpw = jnp.swapaxes(mlpw, 4, 5).reshape(GRID + (48 * steps, depth))
        w_first, w_second = jnp.split(mlpw, [48 * ready_parts], axis=4)
        front_own = [pairw.reshape(GRID + (-1, depth))]
        front_links, front_shapes, front_scratch = None, [], []

    col = cols_at(total, after_one)
    wide = shape_of((total, chans), F32)
    narrow = shape_of((HALO + lrows, chans), F32)
    gp, inner, dp, ip, states, reach, mix_s, s_in, normed, x, cot, chan, *made = pl.pallas_call(
        functools.partial(front_kernel, ltiles, tiles, groups, front_links),
        grid=(1 + groups,),
        in_specs=[
            hbm, hbm, hbm, hbm, pl.BlockSpec(memory_space=pltpu.SMEM), whole((1, depth)),
            *[cols_at(c.shape[0], after_one) for c in channel], blocks_at(after_one),
            blocks_at(after_one), *[hbm for _ in front_own],
        ],
        out_specs=[
            col, col, col, col, col, cols_at(HALO + lrows, after_one), cols_at(srows, after_one),
            whole((8, chans)), whole((total, depth)), whole((total, depth)),
            whole((tokens, depth)), cols_at(16, after_one), *[hbm for _ in front_shapes],
        ],
        out_shape=[
            wide, wide, wide, wide, wide, narrow, shape_of((srows, chans), BF16),
            shape_of((8, chans), F32), shape_of((total, depth), BF16),
            shape_of((total, depth), BF16), shape_of((tokens, depth), BF16),
            shape_of((16, chans), F32), *front_shapes,
        ],
        scratch_shapes=[
            pltpu.VMEM((total, width), F32), pltpu.VMEM((total, width), BF16),
            pltpu.VMEM((2,) + GRID[2:] + (2 * cshare, depth), BF16),
            pltpu.VMEM((2, width, width), BF16), pltpu.VMEM((HALO, depth), BF16),
            one_dma((4,)), one_dma((2,)), one_dma((2,)), *exchange_scratch(groups, width, seqs),
            *front_scratch,
        ],
        compiler_params=params(56, collective_id=0, has_side_effects=True),
        name="front",
    )(
        long_tokens.reshape(lrows, depth), short_tokens.reshape(srows, depth),
        long_cotangent.reshape(lrows, depth), short_cotangent.reshape(srows, depth), long_length,
        gain1, *channel, decay_gate_weight, input_gate_weight, *front_own,
    )
    if fast:
        pairw, outw, w_first = made
    outw = outw.reshape(SLOTS, -1, depth)
    pairw = pairw.reshape(SLOTS, -1, depth)

    hid = units // steps
    block = (3,) + GRID + (16, depth)
    wbuf = pltpu.VMEM((2,) + block, BF16)
    dwbuf = pltpu.VMEM(block, BF16)
    if fast:
        chunks = [
            (k, 16 * (ready_parts + p), 16, 0, 48 * p + 16 * k)
            for p in range(steps - ready_parts)
            for k in range(3)
        ]
        plan = [[[] for _ in range(8)] for _ in range(steps)]
        todo = list(range(len(chunks) + sum(lags)))
        for s in range(ready_parts - 1, steps - 1):
            due = 3 * (s - ready_parts + 1) + 3 + sum(lags)
            now, todo = [t for t in todo if t < due], [t for t in todo if t >= due]
            first = 0 if s == ready_parts - 1 else s
            spots = [(q, k) for q in range(first, s + 1) for k in range(8)]
            for n, t in enumerate(now):
                lead = min(MLP_AHEAD, len(now) - 1) if first == 0 else 0
                share = max(0, n - lead) / max(1, len(now) - lead)
                q, k = spots[int(share * len(spots))]
                plan[q][k].append(t)
        soon = [(p, k) for p in range(EARLY_PARTS) for k in range(3)]
        early_chunks = [
            (HALVED, n, 0, (p, k), (0, 16), 0, 16 * (k * EARLY_PARTS + p))
            for n, (p, k) in enumerate(soon)
        ]
        early_lags = (1, 2, 2, 2)
        early_plan = [[[] for _ in range(9)] for _ in range(steps)]
        spot = 0
        for t in range(len(soon) + sum(early_lags)):
            after = 8 * (t // 3 + 1) + 7 if t < len(soon) else 0
            spot = max(after, spot + EARLY_GAP)
            q, k = divmod(min(spot, 8 * steps), 8)
            q, k = (q, k) if q < steps else (steps - 1, 8)
            early_plan[q][k].append(t)
        mlp_links = (zcount, chunks, lags, plan, early_chunks, early_lags, early_plan)
        w_last, more_specs = mlp_own, [hbm, whole((16 * len(soon), depth))]
        more_shapes = [
            shape_of(GRID + (48 * (steps - ready_parts), depth), BF16),
            shape_of((16 * len(soon), depth), F32),
        ]
        half_block = block[:3] + block[4:]
        more_scratch = [
            pltpu.VMEM(half_block, BF16), one_dma((2,)), pltpu.SemaphoreType.REGULAR,
            *gather_sems(len(chunks), zcount), *halved_scratch(len(soon), len(soon), depth, zcount),
        ]
        dw_shape = (steps,) + half_block
        more_params = dict(collective_id=3, has_side_effects=True)
    else:
        mlp_links, w_last, more_specs, more_shapes, more_scratch = None, [w_second], [], [], []
        dw_shape, more_params = (steps,) + block, {}
    out_l, out_s, d_res, rlow, mix_l, gain2_grad, dmlp, *more_out = pl.pallas_call(
        functools.partial(mlp_kernel, ltiles, tokens // TILE, mlp_links),
        grid=(steps,),
        in_specs=[
            whole((total, depth)), whole((tokens, depth)), whole((HALO + lrows, chans)),
            whole((HALO + lrows, chans)), whole((HALO + lrows, chans)), whole((8, chans)),
            whole((srows, chans)), whole((SLOTS, cshare, depth)), whole((1, depth)), hbm,
            *[hbm for _ in w_last],
        ],
        out_specs=[
            whole((lrows, depth)), whole((srows, depth)), whole((tokens, depth)), whole((tokens, depth)),
            whole((lrows, chans)), whole((8, depth)), hbm, *more_specs,
        ],
        out_shape=[
            shape_of((lrows, depth), BF16), shape_of((srows, depth), BF16),
            shape_of((tokens, depth), F32), shape_of((tokens, depth), BF16),
            shape_of((lrows, chans), BF16),
            shape_of((8, depth), F32), shape_of(dw_shape, BF16), *more_shapes,
        ],
        scratch_shapes=[
            pltpu.VMEM((tokens, depth), BF16), pltpu.VMEM((tokens, depth), F32),
            pltpu.VMEM((tokens, depth), F32), pltpu.VMEM((tokens, 2 * hid), F32),
            pltpu.VMEM((tokens, hid), F32), pltpu.VMEM((tokens, hid), BF16),
            pltpu.VMEM((tokens, 2 * hid), BF16), wbuf, dwbuf, one_dma((2, 3)), one_dma, *more_scratch,
        ],
        compiler_params=params(62, **more_params),
        name="mlp",
    )(x, cot, states, reach, gp, s_in, mix_s, outw, gain2, w_first, *w_last)

    gate_shape, sum_shape = GRID + (bwidth // 2, bwidth), GRID + (8, 128)
    grads_shape = shape_of(GRID + (cshare, depth), BF16)
    tail_links, tail_in, tail_specs, tail_shapes, tail_scratch = None, [], [], [], []
    if fast:
        size = 16
        tail_chunks = []
        number = 0
        for p in range(EARLY_PARTS, steps):
            for k in range(3):
                tail_chunks.append(
                    (HALVED, number % TAIL_SLOTS, 0, (p, k), (0, size), k, 16 * p)
                )
                number += 1
        for which in (1, 2, 3):
            if which == 2:
                tail_chunks.append((SUMS, 0, 5, None, (0, 8), 7, 0))
                tail_chunks.append((GATES, 0, 4, None, (0, bwidth // 2), 6, 0))
                during = len(tail_chunks) - 2
            for start in range(0, cshare, size):
                tail_chunks.append(
                    (CORE, number % TAIL_SLOTS, which, None, (start, size), 2 + which, start)
                )
                number += 1
        tail_lags = (1, 2, 2, 2, 1, 1, 1, 1)
        marks = [[5.0 * g + t for t in (0.0, 1.5, 4.0)] for g in range(groups)]
        marks += [
            [5.0 * groups + 12.5 * g + t for t in (0.0, 5.0, 6.0, 9.0, 10.5, 12.5)] for g in range(groups)
        ]
        plan = paced(during, 3, marks)
        plan[-1][-1] += range(during, len(tail_chunks) + sum(tail_lags) + 1)
        tail_links = (zcount, tail_chunks, tail_lags, plan)
        early_sums = more_out[1]
        tail_in, tail_specs = [dmlp, early_sums], [whole((ushare, depth))] * 3 + [whole((cshare, depth))] * 3
        tail_shapes = [shape_of((ushare, depth), F32)] * 3 + [shape_of((cshare, depth), F32)] * 3
        lone = five(TAIL_SLOTS, (size, depth), BF16, zcount)
        lone[1] = five(CORE_SLOTS, (size, depth), BF16, zcount)[1]
        n = len(tail_chunks)
        links = one_dma((n, zcount + 2))
        tail_scratch = [
            *lone,
            *five(1, gate_shape[4:], BF16, zcount),
            *five(1, sum_shape[4:], F32, zcount),
            one_dma((n,)), links, links, links, links,
            pltpu.VMEM(gate_shape, BF16), pltpu.VMEM(sum_shape, F32),
        ]
    dx_l, dx_s, _, d_out, d_gate, d_input, gate_sums, sums, *shares = pl.pallas_call(
        functools.partial(tail_kernel, ltiles, tiles, groups, tail_links),
        grid=(2 * groups,),
        in_specs=[
            whole((total, depth)), whole((1, depth)), whole((total, depth)), hbm,
            whole((tokens, depth)), slot_at(early), slot_at(late, 0), slot_at(late, 1),
            blocks_at(late), blocks_at(late), cols_at(16, both_times), cols_at(lrows, early),
            cols_at(srows, early), cols_at(total, early), cols_at(total, late),
            cols_at(total, both_times), cols_at(total, late), cols_at(total, both_times),
            cols_at(HALO + lrows, both_times), cols_at(8, both_times), whole((8, depth)),
            *([hbm, whole(early_sums.shape)] if fast else []),
        ],
        out_specs=[
            whole((lrows, depth)), whole((srows, depth)), whole((8, depth)), hbm, hbm, hbm, hbm, hbm,
            *tail_specs,
        ],
        out_shape=[
            shape_of((lrows, depth), F32), shape_of((srows, depth), F32), shape_of((8, depth), F32),
            grads_shape, grads_shape, grads_shape, shape_of(gate_shape, BF16),
            shape_of(sum_shape, F32), *tail_shapes,
        ],
        scratch_shapes=[
            pltpu.VMEM((total, depth), F32), pltpu.VMEM((total, width), F32),
            pltpu.VMEM((total, width), BF16), pltpu.VMEM((total, width), BF16),
            pltpu.VMEM((total, width), BF16), pltpu.VMEM((total, width), BF16),
            pltpu.VMEM((groups, total, width), BF16), pltpu.VMEM((groups, total, width), F32),
            pltpu.VMEM((groups, HALO + lrows, width), F32), pltpu.VMEM((groups, 8, width), F32),
            pltpu.VMEM((3,) + GRID[2:] + (cshare, depth), BF16), pltpu.VMEM(gate_shape, BF16),
            pltpu.VMEM(sum_shape, F32), pltpu.VMEM((2, width, width), BF16),
            pltpu.VMEM((HALO, depth), F32), pltpu.VMEM((HALO, depth), F32), one_dma((2,)),
            one_dma((2,)), one_dma((3,)), *exchange_scratch(groups, width, seqs), *tail_scratch,
        ],
        compiler_params=params(63, collective_id=4, has_side_effects=True),
        name="tail",
    )(
        x, gain1, normed, d_res, rlow, outw, pairw, pairw, decay_gate_weight, input_gate_weight, chan,
        mix_l, mix_s, gp, inner, dp, ip, states, reach, s_in, gain2_grad, *tail_in,
    )

    if fast:
        g_mgate, g_mup, g_down, g_out, g_gate, g_input = shares
    else:
        dmlp = dmlp.reshape(steps, 3, SLOTS, -1, depth).transpose(2, 1, 0, 3, 4)
        g_mgate, g_mup, g_down = scatter_slots(dmlp.reshape(SLOTS, -1, depth), 3, count)
        dmix = jnp.concatenate([d_gate, d_input, d_out], axis=4).reshape(SLOTS, -1, depth)
        g_gate, g_input, g_out = scatter_slots(dmix, 3, count)
        gate_sums, sums = lax.psum((gate_sums.astype(F32), sums), ("seq", "row"))
    gate_sums = gate_sums.reshape(2, blocks, bwidth, bwidth).astype(F32)
    sums = sums.reshape(2, 16, 8, 128)
    gain_sums = sums[0, 12:14].reshape(2, depth)
    rows = sums.transpose(0, 2, 1, 3).reshape(16, 2048)[0:10, :chans]
    return (
        out_l.reshape(long_tokens.shape),
        out_s.reshape(short_tokens.shape),
        dx_l.reshape(long_tokens.shape),
        dx_s.reshape(short_tokens.shape),
        gain_sums[0],
        g_gate.T,
        rows[9],
        g_input.T,
        rows[0],
        rows[1:5],
        rows[5],
        gate_sums[0],
        rows[6],
        gate_sums[1],
        rows[7],
        rows[8],
        g_out,
        gain_sums[1],
        g_mgate.T,
        g_mup.T,
        g_down,
    )


def solution(mesh):
    both = ("seq", "row")
    long_spec = P("row", "seq", None)
    short_spec = P(both, None, None)
    cols = P(None, both)
    rows = P(both, None)
    return jax.shard_map(
        shards,
        mesh=mesh,
        in_specs=(
            long_spec, short_spec, P("row"), long_spec, short_spec, P(), cols, P(), cols, P(),
            P(), P(), P(), P(), P(), P(), P(), rows, P(), cols, cols, rows,
        ),
        out_specs=(
            long_spec, short_spec, long_spec, short_spec, P(), cols, P(), cols, P(), P(), P(),
            P(), P(), P(), P(), P(), rows, P(), cols, cols, rows,
        ),
        check_vma=False,
    )
```

```python
import functools

import jax
import jax.numpy as jnp
from jax import lax
from jax.experimental import pallas as pl
from jax.experimental.pallas import tpu as pltpu
from jax.sharding import PartitionSpec as P

EPSILON = 1e-06
F32 = jnp.float32
BF16 = jnp.bfloat16
GRID = (2, 2, 2, 4)
SLOTS = 32
TILE = 16
HALO = 16
MIB = 1024 * 1024
MLP_AHEAD = 1
EARLY_PARTS = 2
EARLY_GAP = 3
FRONT_PARTS = 3
TAIL_SLOTS = 11
CORE_SLOTS = 5
GELU_A = 0.7978845608028654
GELU_B = 0.044715


def dot_nn(a, b):
    return lax.dot_general(a, b, (((1,), (0,)), ((), ())), preferred_element_type=F32)


def dot_nt(a, b):
    return lax.dot_general(a, b, (((1,), (1,)), ((), ())), preferred_element_type=F32)


def dot_tn(a, b):
    return lax.dot_general(a, b, (((0,), (0,)), ((), ())), preferred_element_type=F32)


def sigmoid(v):
    return 0.5 * jnp.tanh(0.5 * v) + 0.5


def gelu(v):
    t = jnp.tanh(v * (GELU_A + (GELU_A * GELU_B) * (v * v)))
    h = 0.5 * v
    return h + h * t


def gelu_pair(v):
    w = v * v
    t = jnp.tanh(v * (GELU_A + (GELU_A * GELU_B) * w))
    h = 0.5 * v
    slope = 0.5 + 0.5 * t + (h - h * (t * t)) * (GELU_A + (3.0 * GELU_A * GELU_B) * w)
    return h + h * t, slope


def row_iota(shape):
    return lax.broadcasted_iota(jnp.int32, shape, 0)


def at(j):
    return pl.ds(pl.multiple_of(j * TILE, TILE), TILE)


def scan_tile(a, b, reverse):
    rows = row_iota(a.shape)
    step = 1
    while step < TILE:
        if reverse:
            keep, shift = rows < TILE - step, TILE - step
        else:
            keep, shift = rows >= step, step
        b = jnp.where(keep, a * pltpu.roll(b, shift, 0) + b, b)
        a = jnp.where(keep, a * pltpu.roll(a, shift, 0), a)
        step *= 2
    return a, b


def shift_down(cur, prev, k):
    if k == 0:
        return cur
    rows = row_iota(cur.shape)
    return jnp.where(rows < k, pltpu.roll(prev, k, 0), pltpu.roll(cur, k, 0))


def shift_up(cur, later, k):
    if k == 0:
        return cur
    rows = row_iota(cur.shape)
    return jnp.where(
        rows >= TILE - k, pltpu.roll(later, TILE - k, 0), pltpu.roll(cur, TILE - k, 0)
    )


def fold(v):
    return v[0:8] + v[8:16]


def flat(block):
    return block.reshape(-1, block.shape[-1])


def gates(dp, ip, c8):
    rate = sigmoid(dp)
    opening = sigmoid(ip)
    log_decay = -c8 * (0.25 + rate)
    decay = jnp.exp(log_decay)
    square = -jnp.tanh(log_decay) * (1.0 + decay * decay)
    return rate, opening, decay, square


GB, IB, CW, CB, DB, OB, C8, S8 = 0, 1, 2, 6, 7, 8, 9, 10


def conv_tile(in_ref, pc_ref, j, live):
    cur = in_ref[at(j), :]
    prev = in_ref[at(j - 1), :] * live
    out = pc_ref[CB : CB + 1, :] + pc_ref[CW : CW + 1, :] * cur
    moved = [cur]
    for k in range(1, 4):
        m = shift_down(cur, prev, k)
        moved.append(m)
        out = out + pc_ref[CW + k : CW + k + 1, :] * m
    return out, moved


def place_of():
    s = lax.axis_index("seq")
    return s // 4, (s // 2) % 2, s % 2, lax.axis_index("row")


def device_at(y, x, c, z):
    return ((y * 2 + x) * 2 + c, z)


class Peers:
    def __init__(self, zcount):
        y, x, c, z = self.place = place_of()
        self.far = [(z + k) % zcount for k in range(1, zcount)]
        self.along = [device_at(y, x, c, q) for q in self.far]
        self.near = ((y + c) % 2, (x + 1 - c) % 2)
        self.first = device_at(*self.near, c, z)
        self.second = device_at((y + 1 - c) % 2, (x + c) % 2, c, z)
        self.other = device_at(y, x, 1 - c, z)

    def meet(self):
        everyone = [*self.along, self.first, self.second, self.other]
        barrier = pltpu.get_barrier_semaphore()
        for peer in everyone:
            pl.semaphore_signal(
                barrier, inc=1, device_id=peer, device_id_type=pl.DeviceIdType.MESH
            )
        pl.semaphore_wait(barrier, len(everyone))


def remote(source, target, send, recv, device):
    return pltpu.make_async_remote_copy(
        src_ref=source,
        dst_ref=target,
        send_sem=send,
        recv_sem=recv,
        device_id=device,
        device_id_type=pl.DeviceIdType.MESH,
    )


class Spread:
    def __init__(self, peers, own, full, send, recv):
        self.peers, self.own, self.full, self.send, self.recv = peers, own, full, send, recv

    def go(self, stage, act):
        y, x, c, z = self.peers.place
        p, full = self.peers, self.full
        if stage == 0:
            for k, device in enumerate(p.along):
                act(remote(self.own, full(y, x, c, z), self.send(k), self.recv(k), device))
            return
        k = len(p.along) + stage - 1
        if stage == 2:

            @pl.when(c == 0)
            def _():
                part = full(y, slice(None), c, slice(None))
                act(remote(part, part, self.send(k), self.recv(k), p.second))

            @pl.when(c == 1)
            def _():
                part = full(slice(None), x, c, slice(None))
                act(remote(part, part, self.send(k), self.recv(k), p.second))

            return
        if stage == 1:
            part, device = full(y, x, c, slice(None)), p.first
        else:
            part, device = full(slice(None), slice(None), c, slice(None)), p.other
        act(remote(part, part, self.send(k), self.recv(k), device))

    def start(self, stage):
        self.go(stage, lambda d: d.start())

    def arrive(self, stage):
        self.go(stage, lambda d: d.wait_recv())

    def drain(self):
        for stage in range(4):
            self.go(stage, lambda d: d.wait_send())


def wave_of(t, count, lags):
    for stage in range(len(lags), -1, -1):
        piece = t - sum(lags[:stage])
        if 0 <= piece < count:
            yield piece, stage


class Gather:
    def __init__(self, zcount, ins, outs, sems, chunks, lags):
        self.csem, self.ssem, self.rsem = sems
        self.peers = Peers(zcount)
        self.lags = lags
        y, x, c, z = self.peers.place
        self.spreads, self.copies = [], []
        for i, (which, start, size, target, offset) in enumerate(chunks):
            own = ins[which].at[pl.ds(start, size)]
            rows = pl.ds(offset, size)

            def full(a, b, d, e, ref=outs[target], rows=rows):
                return ref.at[a, b, d, e, rows]

            def send(k, i=i):
                return self.ssem.at[i, k]

            def recv(k, i=i):
                return self.rsem.at[i, k]

            self.spreads.append(Spread(self.peers, own, full, send, recv))
            self.copies.append(pltpu.make_async_copy(own, full(y, x, c, z), self.csem.at[i]))
        self.waves = len(chunks) + sum(lags) + 1

    def wave(self, t):
        for i, stage in wave_of(t, len(self.spreads), self.lags):
            if stage == 0:
                self.copies[i].start()
            elif stage == 1:
                self.copies[i].wait()
            if stage > 0:
                self.spreads[i].arrive(stage - 1)
            if stage < 4:
                self.spreads[i].start(stage)

    def drain(self):
        for spread in self.spreads:
            spread.drain()


def in_turn(weave, step, plan, first=0):
    def point(k):
        for s, points in enumerate(plan, first):
            if k < len(points) and points[k]:

                @pl.when(step == s)
                def _(todo=points[k]):
                    for t in todo:
                        weave.wave(t)

    return point


def spread_out(waves, ahead, steps, points):
    todo = list(range(waves))
    plan = []
    for s in range(steps):
        row = []
        for k in range(points):
            take = ahead if s == 0 and k == 0 else 1
            if s == steps - 1 and k == points - 1:
                take = len(todo)
            row.append(todo[:take])
            todo = todo[take:]
        plan.append(row)
    return plan


def paced(waves, ahead, marks):
    last = marks[-1][-1]
    plan = [[[] for _ in row] for row in marks]
    spots = [(t, s, k) for s, row in enumerate(marks) for k, t in enumerate(row)]
    for w in range(waves):
        due = last * max(0, w - ahead) / max(1, waves - ahead)
        _, s, k = next(spot for spot in spots if spot[0] >= due)
        plan[s][k].append(w)
    return plan


def row_chunks(parts, size):
    return [
        (which, start + i, size, target, offset + i)
        for which, start, count, target, offset in parts
        for i in range(0, count, size)
    ]


def gather_sems(count, zcount):
    links = pltpu.SemaphoreType.DMA((count, zcount + 2))
    return [pltpu.SemaphoreType.DMA((count,)), links, links]


CORE, GATES, SUMS, HALVED = 0, 1, 2, 3


class Scatter:
    def __init__(self, zcount, ins, outs, buffers, sems, chunks, lags):
        self.peers = Peers(zcount)
        self.zcount, self.chunks, self.lags = zcount, chunks, lags
        self.ins, self.outs, self.buffers = ins, outs, buffers
        self.csem, self.ssem, self.rsem = sems[:3]
        self.pieces = [Piece(self, i, sems[3:], *chunk) for i, chunk in enumerate(chunks)]
        self.waves = len(chunks) + sum(lags) + 1

    def wave(self, t):
        for i, stage in wave_of(t, len(self.pieces), self.lags):
            if stage <= 4 or self.pieces[i].spread is not None:
                self.pieces[i].step(stage)

    def drain(self):
        for piece in self.pieces:
            piece.drain()


def slot_of_core(i, slots):
    return i % slots


def add_into(into, i, part, j):
    into[i] = (into[i].astype(F32) + part[j].astype(F32)).astype(into.dtype)


class Piece:
    def __init__(self, owner, i, sems, kind, slot, which, source, span, target, place):
        self.o, self.i, self.kind, self.slot = owner, i, kind, slot
        self.a, self.r0, self.r1, self.r2, self.r3 = owner.buffers[kind]
        self.from_core = 0 if self.r0 is None else slot_of_core(i, self.r0.shape[0])
        self.source, self.lead, self.rows = owner.ins[which], source, pl.ds(*span)
        self.target, self.place = owner.outs[target], place
        self.spread, self.drained = None, False
        if kind in (GATES, SUMS):
            y, x, c, z = owner.peers.place

            def full(*at_place):
                return self.target.at[at_place]

            def send(k):
                return sems[0].at[i, k]

            def recv(k):
                return sems[1].at[i, k]

            self.spread = Spread(owner.peers, full(y, x, c, z), full, send, recv)

    def local(self):
        c = self.o.peers.place[2]
        if self.kind == HALVED:
            mine = self.source.at[self.lead]
        else:
            mine = self.source.at[:, :, c, :, self.rows]
        return pltpu.make_async_copy(mine, self.a.at[self.slot], self.o.csem.at[self.i])

    def send(self, stage, act):
        s, peers = self.slot, self.o.peers
        y, x, c, z = peers.place

        def go(source, target, k, device):
            act(remote(source, target, self.o.ssem.at[self.i, k], self.o.rsem.at[self.i, k], device))

        if stage == 0:
            if self.kind != HALVED:
                theirs = self.source.at[:, :, 1 - c, :, self.rows]
                go(theirs, self.r0.at[self.from_core], 0, peers.other)
        elif stage == 1:

            @pl.when(c == 0)
            def _():
                go(self.a.at[s, 1 - y], self.r1.at[s], 1, peers.second)

            @pl.when(c == 1)
            def _():
                go(self.a.at[s, :, 1 - x], self.r1.at[s], 1, peers.second)

        elif stage == 2:
            go(self.a.at[(s, *peers.near)], self.r2.at[s], 2, peers.first)
        else:
            for k, device in enumerate(peers.along):
                go(self.a.at[s, y, x, peers.far[k]], self.r3.at[s, k], 3 + k, device)

    def step(self, stage):
        s, zcount = self.slot, self.o.zcount
        y, x, c, z = self.o.peers.place
        if stage == 0:
            for earlier in self.o.pieces[: self.i]:
                if earlier.a is self.a and earlier.slot == s:
                    earlier.drain()
            self.local().start()
        elif stage <= 4:
            self.send(stage - 1, lambda d: d.wait_recv())
        else:
            self.spread.arrive(stage - 5)
        if stage == 1:
            self.local().wait()
            if self.kind != HALVED:

                @pl.loop(0, 4 * zcount)
                def _(q):
                    i = (q // (2 * zcount), (q // zcount) % 2, q % zcount)
                    add_into(self.a, (s, *i), self.r0, (self.from_core, *i))

        elif stage == 2:

            @pl.loop(0, 2 * zcount)
            def _(q):
                h = q // zcount
                i = (s, y * (1 - c) + h * c, h * (1 - c) + x * c, q % zcount)
                add_into(self.a, i, self.r1, (s, h, q % zcount))

        elif stage == 3:

            @pl.loop(0, zcount)
            def _(q):
                add_into(self.a, (s, y, x, q), self.r2, (s, q))

        elif stage == 4:
            total = self.a[s, y, x, z].astype(F32)
            for k in range(zcount - 1):
                total = total + self.r3[s, k].astype(F32)
            if self.spread is None:
                self.target[self.place : self.place + total.shape[0]] = total
            else:
                self.target[y, x, c, z] = total.astype(self.target.dtype)
        if stage < 4:
            self.send(stage, lambda d: d.start())
        elif stage < 8 and self.spread is not None:
            self.spread.start(stage - 4)

    def drain(self):
        if self.drained:
            return
        self.drained = True
        for stage in range(4):
            self.send(stage, lambda d: d.wait_send())
        if self.spread is not None:
            self.spread.drain()


def five(number, shape, dtype, zcount):
    lead = [(2, 2, zcount), (2, 2, zcount), (2, zcount), (zcount,), (zcount - 1,)]
    return [pltpu.VMEM((number, *d, *shape), dtype) for d in lead]


def halved_scratch(count, slots, depth, zcount):
    lone = five(slots, (16, depth), BF16, zcount)
    links = pltpu.SemaphoreType.DMA((count, zcount + 2))
    return [lone[0], *lone[2:], pltpu.SemaphoreType.DMA((count,)), links, links, links, links]


def no_point(k):
    pass


class Exchange:
    def __init__(self, mine, theirs, ssem, rsem):
        self.mine, self.theirs, self.ssem, self.rsem = mine, theirs, ssem, rsem
        self.count = lax.axis_size("seq")
        self.place = lax.axis_index("seq")

    def peer(self, k):
        return (lax.rem(self.place + k, self.count), lax.axis_index("row"))

    def go(self, g, act):
        for k in range(1, self.count):
            act(
                remote(
                    self.mine.at[g],
                    self.theirs.at[g, self.place],
                    self.ssem.at[g, k - 1],
                    self.rsem.at[g, k - 1],
                    self.peer(k),
                )
            )

    def start(self, g):
        self.go(g, lambda d: d.start())

    def entering(self, g, reverse):
        self.go(g, lambda d: d.wait_recv())
        state = jnp.zeros((1, self.mine.shape[-1]), F32)
        for hop in range(self.count - 1):
            source = self.count - 1 - hop if reverse else hop
            ahead = source > self.place if reverse else source < self.place
            reach = self.theirs[g, source, 0:1, :]
            drive = self.theirs[g, source, 1:2, :]
            state = jnp.where(ahead, reach * state + drive, state)
        return state

    def drain(self, groups):
        for g in range(groups):
            self.go(g, lambda d: d.wait_send())


def exchange_scratch(groups, width, count):
    links = pltpu.SemaphoreType.DMA((groups, count - 1))
    return [
        pltpu.VMEM((groups, 8, width), F32),
        pltpu.VMEM((groups, count, 8, width), F32),
        links, links,
    ]


def meet_all(exchange, zcount):
    place, row = exchange.place, lax.axis_index("row")
    everyone = [exchange.peer(k) for k in range(1, exchange.count)]
    everyone += [(place, lax.rem(row + k, zcount)) for k in range(1, zcount)]
    barrier = pltpu.get_barrier_semaphore()
    for peer in everyone:
        pl.semaphore_signal(barrier, inc=1, device_id=peer, device_id_type=pl.DeviceIdType.MESH)
    pl.semaphore_wait(barrier, len(everyone))


def pair_up(pair, blocks):
    half = blocks.shape[1]
    pair[...] = jnp.zeros_like(pair)
    pair[0:half, 0:half] = blocks[0]
    pair[half:, half:] = blocks[1]


def front_kernel(ltiles, tiles, groups, links, *refs):
    (
        long_ref, short_ref, lcot_ref, scot_ref, length_ref, gain_ref, *channel_refs
    ) = refs[:14]
    wd_ref, wo_ref = refs[14:16]
    refs = refs[16:]
    step = pl.program_id(0)
    point, gather = no_point, None
    zcount = 1
    if links is None:
        pairw, refs = refs[0], refs[1:]
    else:
        zcount, chunks, lags, ready, plan = links
        owns, made = refs[:6], refs[18:21]
        pairw = made[0]
        gather = Gather(zcount, owns, made, refs[-3:], chunks, lags)
        refs = refs[6:18] + refs[21:-3]
        point = in_turn(gather, step, plan)
    gp, inn, dp, ip, st, pr, mix, sin_ref, nm_ref, x_ref, cot_ref, pc_ref = refs[:12]
    cv_ref, cl_ref, wbuf, pairs, halo, all_pc, isem, wsem, hsem, *swap = refs[12:]
    exchange = Exchange(*swap)
    lrows = ltiles * TILE
    place = exchange.place

    def load(g):
        return pltpu.make_async_copy(pairw.at[g // 2, g % 2], wbuf.at[g % 2], wsem.at[g % 2])

    @pl.when(step == 0)
    def _():
        srows = short_ref.shape[0]
        copies = [
            pltpu.make_async_copy(source, target, isem.at[k])
            for k, (source, target) in enumerate(
                [
                    (long_ref, x_ref.at[pl.ds(HALO, lrows)]),
                    (short_ref, x_ref.at[pl.ds(HALO + lrows, srows)]),
                    (lcot_ref, cot_ref.at[pl.ds(0, lrows)]),
                    (scot_ref, cot_ref.at[pl.ds(lrows, srows)]),
                ]
            )
        ]
        for copy in copies:
            copy.start()
        meet_all(exchange, zcount)
        ahead = remote(
            long_ref.at[pl.ds(lrows - HALO, HALO)], halo, hsem.at[0], hsem.at[1], exchange.peer(1)
        )
        ahead.start()
        row = 0
        for ref in channel_refs:
            value = ref[...] if len(ref.shape) == 2 else ref[...].reshape(1, ref.shape[0])
            all_pc[row : row + value.shape[0], :] = value
            row += value.shape[0]
        all_pc[row:, :] = jnp.zeros((16 - row, all_pc.shape[1]), F32)
        todo = [] if gather is None else list(range(ready))

        def some(count):
            for t in todo[:count]:
                gather.wave(t)
            del todo[:count]

        some(4)
        for copy in copies:
            copy.wait()

        @pl.loop(0, ltiles)
        def _(i):
            rows = row_iota((TILE, 1)) + (place * lrows + i * TILE)
            keep = jnp.where(rows < length_ref[0], 1.0, 0.0)
            cot_ref[at(i), :] = (cot_ref[at(i), :].astype(F32) * keep).astype(BF16)

        some(1)
        ahead.wait_recv()
        x_ref[0:HALO, :] = halo[...]

        def norm(j):
            v = x_ref[at(j), :].astype(F32)
            s = lax.rsqrt(jnp.mean(v * v, axis=1, keepdims=True) + EPSILON)
            nm_ref[at(j), :] = (v * s * gain_ref[...]).astype(BF16)

        pl.loop(0, tiles // 2)(norm)
        some(1)
        pl.loop(tiles // 2, tiles)(norm)
        some(len(todo))
        ahead.wait_send()
        load(0).start()
        load(1).start()

    @pl.when(step > 0)
    def _():
        for g in range(groups):

            @pl.when(step == g + 1)
            def _(g=g):
                load(g).wait()
                width = pc_ref.shape[1]
                pc_ref[...] = all_pc[:, g * width : (g + 1) * width]

        pair_up(pairs.at[0], wd_ref)
        pair_up(pairs.at[1], wo_ref)
        slot = lax.rem(step - 1, 2)
        share = wbuf.shape[-2] // 2
        front_part(
            ltiles, tiles, point, place, nm_ref, wbuf.at[slot, :, :, 0:share],
            wbuf.at[slot, :, :, share : 2 * share], pairs, pc_ref, gp, inn, dp, ip, st, pr, mix,
            exchange.mine.at[step - 1], cv_ref, cl_ref,
        )
        for g in range(groups):

            @pl.when(step == g + 1)
            def _(g=g):
                if g + 2 < groups:
                    load(g + 2).start()
                exchange.theirs[g, place] = jnp.zeros(exchange.theirs.shape[2:], F32)
                exchange.start(g)

        point(3)

    @pl.when(step == groups)
    def _():
        width = gp.shape[1]
        for g in range(groups):
            state = exchange.entering(g, False)
            sin_ref[:, g * width : (g + 1) * width] = jnp.broadcast_to(state, (8, width))
        exchange.drain(groups)
        if gather is not None:
            gather.drain()


def front_part(
    ltiles, tiles, point, place, nm_ref, wg_ref, wi_ref, pairs, pc_ref, gp_ref, in_ref, dp_ref,
    ip_ref, st_ref, pr_ref, mix_ref, end_ref, cv_ref, cl_ref,
):
    point(0)
    nm = nm_ref[...]
    gp_ref[...] = dot_nt(nm, flat(wg_ref[...])) + pc_ref[GB : GB + 1, :]
    in_ref[...] = dot_nt(nm, flat(wi_ref[...])) + pc_ref[IB : IB + 1, :]
    point(1)
    in_ref[0:HALO, :] = in_ref[0:HALO, :] * jnp.where(place > 0, 1.0, 0.0)
    cl_ref[0:HALO, :] = jnp.zeros((HALO, cl_ref.shape[1]), BF16)

    @pl.loop(1, tiles)
    def _(j):
        live = jnp.where(j == 1 + ltiles, 0.0, 1.0)
        out, _ = conv_tile(in_ref, pc_ref, j, live)
        cv_ref[at(j), :] = out
        cl_ref[at(j), :] = out.astype(BF16)

    point(2)
    low = cl_ref[...]
    dp_ref[...] = dot_nn(low, pairs[0]) + pc_ref[DB : DB + 1, :]
    ip_ref[...] = dot_nn(low, pairs[1]) + pc_ref[OB : OB + 1, :]

    def scanned(j):
        _, opening, a, square = gates(dp_ref[at(j), :], ip_ref[at(j), :], pc_ref[C8 : C8 + 1, :])
        b = (square * lax.rsqrt(square)) * opening * cv_ref[at(j), :]
        return scan_tile(a, b, False)

    width = gp_ref.shape[1]

    def long_step(i, carry):
        state, reach = carry
        a, b = scanned(1 + i)
        s = b + a * state
        r = a * reach
        st_ref[at(1 + i), :] = s
        pr_ref[at(1 + i), :] = r
        return s[TILE - 1 : TILE], r[TILE - 1 : TILE]

    state, reach = lax.fori_loop(
        0, ltiles, long_step, (jnp.zeros((1, width), F32), jnp.ones((1, width), F32))
    )
    end_ref[...] = jnp.concatenate([reach, state, jnp.zeros((6, width), F32)], axis=0)

    def short_step(i, state):
        j = 1 + ltiles + i
        a, b = scanned(j)
        s = b + a * state
        st_ref[at(j), :] = s
        mix_ref[at(i), :] = (s * gelu(gp_ref[at(j), :])).astype(BF16)
        return s[TILE - 1 : TILE]

    lax.fori_loop(0, tiles - 1 - ltiles, short_step, jnp.zeros((1, width), F32))


def mlp_kernel(ltiles, tiles, links, *refs):
    (
        x_ref, cot_ref, st_ref, pr_ref, gp_ref, sin_ref, mixs_ref, wo_ref, gain_ref, w1_ref, w2_ref
    ) = refs[:11]
    refs = refs[11:]
    point, gather = no_point, None
    step = pl.program_id(0)
    last = pl.num_programs(0) - 1
    if links is not None:
        zcount, chunks, lags, plan, sum_chunks, sum_lags, sum_plan = links
        owns = [w2_ref, *refs[:2]]
        refs = refs[2:]
    outl_ref, outs_ref, dres_ref, rlow_ref, mixl_ref, gain_grad_ref, dw_hbm = refs[:7]
    refs = refs[7:]
    if links is not None:
        w2_ref, early_ref = refs[:2]
        halved = (refs[-9], None, *refs[-8:-5])
        buffers = [None, None, None, halved]
        scatter = Scatter(zcount, [dw_hbm], [early_ref], buffers, refs[-5:], sum_chunks, sum_lags)
        refs = refs[2:-9]
        gather = Gather(zcount, owns, [w2_ref], refs[-3:], chunks, lags)
        got_ref, sems, credit = refs[-6], refs[-5], refs[-4]
        refs = refs[:-6]
        gather_point = in_turn(gather, step, plan)
        scatter_point = in_turn(scatter, step, sum_plan)

        def point(k):
            gather_point(k)
            scatter_point(k)

    (
        n2_ref, acc_o, acc_n, gu_ref, d_ref, h_ref, dgu_ref, wbuf, dwbuf, wsem, dsem
    ) = refs
    lrows = ltiles * TILE
    hid = h_ref.shape[1]
    half = hid // 2
    share = wbuf.shape[-2]
    rows = 3 * share
    ready = w1_ref.shape[-2] // rows
    steps = ready + w2_ref.shape[-2] // rows

    def load(s):
        source, part = (w1_ref, s) if s < ready else (w2_ref, s - ready)
        return [
            pltpu.make_async_copy(
                source.at[:, :, :, :, pl.ds(part * rows + k * share, share)],
                wbuf.at[s % 2, k],
                wsem.at[s % 2, k],
            )
            for k in range(3)
        ]

    def start_load(s):
        for copy in load(s):
            copy.start()

    def wait_load(s):
        for copy in load(s):
            copy.wait()

    def load_next(s):
        if s + 1 < steps and s + 1 >= min(2, ready):
            start_load(s + 1)

    def each(todo, first=0):
        for s in range(first, steps):

            @pl.when(step == s)
            def _(s=s):
                todo(s)

    if gather is not None:
        y, x, c, z = gather.peers.place

    def store(s):
        mine = dwbuf if gather is None else dwbuf.at[:, :, :, c]
        return pltpu.make_async_copy(mine, dw_hbm.at[s], dsem)

    def swap():
        return remote(
            dwbuf.at[:, :, :, 1 - c], got_ref, sems.at[0], sems.at[1], gather.peers.other
        )

    def settle(s):
        if gather is not None:
            swap().wait_recv()

            @pl.loop(0, SLOTS // 2)
            def _(k):
                i, j, m = k // (2 * GRID[3]), (k // GRID[3]) % 2, k % GRID[3]
                for n in range(3):
                    both = dwbuf[n, i, j, c, m].astype(F32) + got_ref[n, i, j, m].astype(F32)
                    dwbuf[n, i, j, c, m] = both.astype(BF16)

            if s < steps - 1:
                pl.semaphore_signal(
                    credit,
                    inc=1,
                    device_id=gather.peers.other,
                    device_id_type=pl.DeviceIdType.MESH,
                )
        store(s).start()

    def clear(s):
        store(s).wait()
        if gather is not None:
            swap().wait_send()

    @pl.when(step == 0)
    def _():
        for s in range(min(2, ready)):
            start_load(s)
        if gather is not None:
            gather.peers.meet()

    point(0)

    @pl.when(step == 0)
    def _():
        s_in = sin_ref[0:1, :]

        @pl.loop(0, ltiles)
        def _(i):
            s = st_ref[at(1 + i), :] + pr_ref[at(1 + i), :] * s_in
            mixl_ref[at(i), :] = (s * gelu(gp_ref[at(1 + i), :])).astype(BF16)

        wo = flat(wo_ref[...])
        dres_ref[0:lrows, :] = dot_nn(mixl_ref[...], wo)
        dres_ref[lrows:, :] = dot_nn(mixs_ref[...], wo)

        @pl.loop(0, tiles)
        def _(i):
            r = dres_ref[at(i), :] + x_ref[at(1 + i), :].astype(F32)
            dres_ref[at(i), :] = r
            acc_o[at(i), :] = r
            s = lax.rsqrt(jnp.mean(r * r, axis=1, keepdims=True) + EPSILON)
            n2_ref[at(i), :] = (r * s * gain_ref[...]).astype(BF16)

        acc_n[...] = jnp.zeros_like(acc_n)

    point(1)

    each(wait_load)
    slot = lax.rem(step, 2)

    def gate_up():
        return flat(wbuf[slot, 0:2])

    def down():
        return flat(wbuf[slot, 2])

    gu_ref[...] = dot_nt(n2_ref[...], gate_up())
    point(2)
    d_ref[...] = dot_nt(cot_ref[...], down())
    each(lambda s: settle(s - 1), 1)
    point(3)

    @pl.loop(0, tiles)
    def _(i):
        for k in range(2):
            cols = slice(k * half, (k + 1) * half)
            more = slice(hid + k * half, hid + (k + 1) * half)
            ge, slope = gelu_pair(gu_ref[at(i), cols])
            u = gu_ref[at(i), more]
            d = d_ref[at(i), cols]
            h_ref[at(i), cols] = (ge * u).astype(BF16)
            dgu_ref[at(i), cols] = (d * u * slope).astype(BF16)
            dgu_ref[at(i), more] = (d * ge).astype(BF16)

    point(4)
    acc_o[...] += dot_nn(h_ref[...], down())
    point(5)
    acc_n[...] += dot_nn(dgu_ref[...], gate_up())
    point(6)
    each(lambda s: clear(s - 1), 1)
    dwbuf[2] = dot_tn(h_ref[...], cot_ref[...]).astype(BF16).reshape(dwbuf.shape[1:])
    point(7)
    each(load_next)
    grad = dot_tn(dgu_ref[...], n2_ref[...]).astype(BF16)
    dwbuf[0:2] = grad.reshape((2,) + dwbuf.shape[1:])

    if gather is not None:
        @pl.when(step > 0)
        def _():
            pl.semaphore_wait(credit, 1)

        swap().start()

    @pl.when(step == last)
    def _():
        def one(i, total):
            r = dres_ref[at(i), :]
            dn = acc_n[at(i), :]
            s = lax.rsqrt(jnp.mean(r * r, axis=1, keepdims=True) + EPSILON)
            e = dn * gain_ref[...]
            inner = jnp.mean(e * r, axis=1, keepdims=True)
            dr = cot_ref[at(i), :].astype(F32) + s * e - r * (s * s * s * inner)
            dres_ref[at(i), :] = dr
            rlow_ref[at(i), :] = dr.astype(BF16)
            return total + fold(dn * (r * s))

        gain_grad_ref[...] = lax.fori_loop(0, tiles, one, jnp.zeros(gain_grad_ref.shape, F32))
        outl_ref[...] = acc_o[0:lrows, :].astype(BF16)
        outs_ref[...] = acc_o[lrows:, :].astype(BF16)
        settle(steps - 1)
        clear(steps - 1)

    point(8)
    if gather is not None:

        @pl.when(step == last)
        def _():
            gather.drain()
            scatter.drain()


def back_part(
    ltiles, tiles, point, rlow_ref, wo_ref, mixl_ref, mixs_ref, gp_ref, st_ref, pr_ref, sin_ref,
    dp_ref, pc_ref, dwo_ref, gl_ref, tot_ref, rch_ref, end_ref, bias_ref, dm_ref, free,
):
    point(0)
    lrows = ltiles * TILE
    width = gp_ref.shape[1]
    rlow = rlow_ref[...]
    dm_ref[...] = dot_nt(rlow, flat(wo_ref[...]))
    free()
    grad = dot_tn(mixl_ref[...], rlow_ref[0:lrows, :]) + dot_tn(mixs_ref[...], rlow_ref[lrows:, :])
    dwo_ref[...] = grad.astype(BF16).reshape(dwo_ref.shape)
    point(1)
    gl_ref[0:HALO, :] = jnp.zeros((HALO, width), BF16)
    last = row_iota((TILE, width)) == TILE - 1

    def local(j, states):
        dm = dm_ref[at(j - 1), :]
        ge, slope = gelu_pair(gp_ref[at(j), :])
        dgate = dm * states * slope
        gl_ref[at(j), :] = dgate.astype(BF16)
        ds = dm * ge
        rate = sigmoid(dp_ref[at(j), :])
        decay = jnp.exp(-pc_ref[C8 : C8 + 1, :] * (0.25 + rate))
        a, b = scan_tile(decay, decay * ds, True)
        return a, b, ds, fold(dgate)

    def short_step(i, carry):
        c, bias = carry
        j = tiles - 1 - i
        a, b, ds, part = local(j, st_ref[at(j), :])
        cs = b + a * c
        tot_ref[at(j), :] = ds + jnp.where(last, c, pltpu.roll(cs, TILE - 1, 0))
        return cs[0:1], bias + part

    _, bias = lax.fori_loop(
        0,
        tiles - 1 - ltiles,
        short_step,
        (jnp.zeros((1, width), F32), jnp.zeros((8, width), F32)),
    )
    point(2)
    s_in = sin_ref[0:1, :]

    def long_step(i, carry):
        c, reach, bias = carry
        j = ltiles - i
        a, b, ds, part = local(j, st_ref[at(j), :] + pr_ref[at(j), :] * s_in)
        cs = b + a * c
        rs = a * reach
        tot_ref[at(j), :] = ds + jnp.where(last, c, pltpu.roll(cs, TILE - 1, 0))
        rch_ref[at(j), :] = jnp.where(last, reach, pltpu.roll(rs, TILE - 1, 0))
        return cs[0:1], rs[0:1], bias + part

    c, reach, bias = lax.fori_loop(
        0, ltiles, long_step, (jnp.zeros((1, width), F32), jnp.ones((1, width), F32), bias)
    )
    end_ref[...] = jnp.concatenate([reach, c, jnp.zeros((6, width), F32)], axis=0)
    bias_ref[...] = bias


def last_part(
    ltiles, tiles, groups, point, exchange, residual, x_ref, gain_ref, nm_ref, wg_ref, wi_ref,
    wd_ref, wo_ref, pc_ref, in_ref, dp_ref, ip_ref, st_ref, pr_ref, sin_ref, tot_ref, rch_ref,
    gl_ref, bias_ref, dxl_ref, dxs_ref, halo_ref, behind, pairs, gain_grad_ref, dwg_ref, dwi_ref,
    gg_ref, small_ref, acc, dc_ref, cl_ref, dl_ref, ol_ref, il_ref, gain2_ref, free, keep,
):
    width = in_ref.shape[1]
    step = pl.program_id(0) - groups
    point(0)
    for g in range(groups):

        @pl.when(step == g)
        def _(g=g):
            dc_ref[0:1, :] = exchange.entering(g, True)

    c_in = dc_ref[0:1, :]

    @pl.when(step == groups - 1)
    def _():
        for copy in residual:
            copy.start()

    first = jnp.where(exchange.place > 0, 1.0, 0.0)
    pair_up(pairs.at[0], wd_ref)
    pair_up(pairs.at[1], wo_ref)
    zero8 = jnp.zeros((8, width), F32)
    cl_ref[0:HALO, :] = jnp.zeros((HALO, width), BF16)
    dl_ref[0:HALO, :] = jnp.zeros((HALO, width), BF16)
    ol_ref[0:HALO, :] = jnp.zeros((HALO, width), BF16)
    dc_ref[0:HALO, :] = jnp.zeros((HALO, width), F32)

    def gate_step(j, states, total, live, carry):
        before, sum_d, sum_o, sum_p = carry
        rows = row_iota((TILE, width))
        prior = jnp.where(rows == 0, before, pltpu.roll(states, 1, 0))
        conv, _ = conv_tile(in_ref, pc_ref, j, live)
        rate, opening, decay, square = gates(
            dp_ref[at(j), :], ip_ref[at(j), :], pc_ref[C8 : C8 + 1, :]
        )
        inv = lax.rsqrt(square)
        mult = square * inv
        weighted = total * opening
        d_open = total * mult * conv
        d_log = decay * (total * prior - (weighted * conv) * (decay * inv))
        d_rate = -pc_ref[C8 : C8 + 1, :] * d_log
        d_dp = d_rate * (rate - rate * rate)
        d_ip = d_open * (opening - opening * opening)
        cl_ref[at(j), :] = conv.astype(BF16)
        dl_ref[at(j), :] = d_dp.astype(BF16)
        ol_ref[at(j), :] = d_ip.astype(BF16)
        dc_ref[at(j), :] = weighted * mult
        return (
            states[TILE - 1 : TILE],
            sum_d + fold(d_dp),
            sum_o + fold(d_ip),
            sum_p - fold((0.25 + rate) * d_log),
        )

    s_in = sin_ref[0:1, :]

    def long_step(i, carry):
        j = 1 + i
        states = st_ref[at(j), :] + pr_ref[at(j), :] * s_in
        total = tot_ref[at(j), :] + rch_ref[at(j), :] * c_in
        return gate_step(j, states, total, 1.0, carry)

    def short_step(i, carry):
        j = 1 + ltiles + i
        return gate_step(j, st_ref[at(j), :], tot_ref[at(j), :], jnp.where(i == 0, 0.0, 1.0), carry)

    carry = lax.fori_loop(0, ltiles, long_step, (s_in, zero8, zero8, zero8))
    carry = lax.fori_loop(
        0, tiles - 1 - ltiles, short_step, (jnp.zeros((1, width), F32),) + carry[1:]
    )
    _, sum_d, sum_o, sum_p = carry
    point(1)

    low, dlow, olow = cl_ref[...], dl_ref[...], ol_ref[...]
    half = width // 2
    for which, grads in ((0, dlow), (1, olow)):
        product = dot_tn(low, grads).astype(BF16)
        shape = (2, half // 2, half)
        place = (which, step // 2, lax.rem(step, 2))
        gg_ref[(*place, slice(0, 2))] = product[:half, :half].reshape(shape)
        gg_ref[(*place, slice(2, 4))] = product[half:, half:].reshape(shape)
    dc_ref[...] += dot_nt(dlow, pairs[0]) + dot_nt(olow, pairs[1])

    point(2)

    def conv_step(j, carry):
        sum_c, sum_i, sums = carry
        live = jnp.where(j == 1 + ltiles, 0.0, 1.0)
        cur = dc_ref[at(j), :]
        up = jnp.where((j == ltiles) | (j == tiles - 1), 0.0, 1.0)
        later = dc_ref[at(jnp.minimum(j + 1, tiles - 1)), :] * up
        _, moved = conv_tile(in_ref, pc_ref, jnp.maximum(j, 1), live)
        d_in = pc_ref[CW : CW + 1, :] * cur
        for k in range(1, 4):
            d_in = d_in + pc_ref[CW + k : CW + k + 1, :] * shift_up(cur, later, k)
        d_in = d_in * jnp.where(j == 0, first, 1.0)
        il_ref[at(j), :] = d_in.astype(BF16)
        return (
            sum_c + fold(cur),
            sum_i + fold(d_in),
            tuple(s + fold(cur * m) for s, m in zip(sums, moved)),
        )

    sum_c, sum_i, sums = lax.fori_loop(0, tiles, conv_step, (zero8, zero8, (zero8,) * 4))
    parts = [sum_i, *sums, sum_c, sum_d, sum_o, sum_p * pc_ref[S8 : S8 + 1, :], bias_ref[...]]
    rows = [jnp.sum(p, axis=0, keepdims=True) for p in parts]
    block = jnp.concatenate(rows + [jnp.zeros((16 - len(rows), width), F32)], axis=0)
    for i in range(width // 128):
        at_block = step * (width // 128) + i
        x, c, z = at_block // 8, lax.rem(at_block // 4, 2), lax.rem(at_block, 4)
        for h in range(2):
            small_ref[h, x, c, z] = block[8 * h : 8 * h + 8, 128 * i : 128 * i + 128]

    point(3)
    free()
    nm = nm_ref[...]
    dwi_ref[...] = dot_tn(il_ref[...], nm).astype(BF16).reshape(dwi_ref.shape)
    dwg_ref[...] = dot_tn(gl_ref[...], nm).astype(BF16).reshape(dwg_ref.shape)
    keep()
    point(4)
    part = dot_nn(gl_ref[...], flat(wg_ref[...])) + dot_nn(il_ref[...], flat(wi_ref[...]))

    @pl.when(step == 0)
    def _():
        acc[...] = part

    @pl.when(step > 0)
    def _():
        acc[...] += part

    @pl.when(step == groups - 1)
    def _():
        for copy in residual:
            copy.wait()

        def norm_back(j):
            v = x_ref[at(j), :].astype(F32)
            dn = acc[at(j), :]
            s = lax.rsqrt(jnp.mean(v * v, axis=1, keepdims=True) + EPSILON)
            e = dn * gain_ref[...]
            inner = jnp.mean(e * v, axis=1, keepdims=True)
            return s * e - v * (s * s * s * inner), fold(dn * (v * s))

        halo, total = norm_back(0)
        halo_ref[...] = halo
        behind.start()
        done = 1
        for ref in (dxl_ref, dxs_ref):

            def one(i, total, ref=ref, done=done):
                d, part = norm_back(done + i)
                ref[at(i), :] = ref[at(i), :] + d
                return total + part

            total = lax.fori_loop(0, ref.shape[0] // TILE, one, total)
            done += ref.shape[0] // TILE
        gain_grad_ref[...] = total
        zero = jnp.zeros((8, 128), F32)
        for h in range(2):
            for z in range(4):
                small_ref[h, 1, 1, z] = zero
        for z, ref in enumerate((gain_grad_ref, gain2_ref)):
            total = jnp.sum(ref[...], axis=0, keepdims=True)
            for i in range(8):
                small_ref[0, 1, 1, z, i : i + 1, :] = total[:, 128 * i : 128 * i + 128]

    point(5)


def tail_kernel(ltiles, tiles, groups, links, *refs):
    (
        x_ref, gain_ref, nm_ref, dres_hbm, rlow_ref, w_ref, wg_ref, wi_ref, wd_ref, wo_ref, pc_ref,
        mixl_ref, mixs_ref, gp_ref, in_ref, dp_ref, ip_ref, st_ref, pr_ref, sin_ref, gain2_ref,
    ) = refs[:21]
    refs = refs[21:]
    step = pl.program_id(0)
    group = lax.rem(step, groups)
    back_point, last_point, scatter = no_point, no_point, None
    nscratch = 23
    if links is not None:
        zcount, chunks, lags, plan = links
        halved_ref, early_ref, refs = refs[0], refs[1], refs[2:]
        outs, shares = refs[:8], refs[8:14]
        scratch, pool = refs[14 : 14 + nscratch], refs[14 + nscratch :]
    else:
        outs, scratch = refs[:8], refs[8:]
    dxl_ref, dxs_ref, gain_grad_ref, dwo_hbm, dwg_hbm, dwi_hbm, gates_hbm, sums_hbm = outs
    (
        acc, dc_ref, cl_ref, dl_ref, ol_ref, il_ref, gls, tots, rchs, bias_ref, wst, gsrc, ssrc,
        pairs, halo_out, halo_in, hsem, dsem, wsem, *swap
    ) = scratch
    gates_full, sums_full = gsrc, ssrc
    if links is not None:
        *pool, gates_full, sums_full = pool
        main, gate_pool, sum_pool = pool[0:5], pool[5:10], pool[10:15]
        scatter = Scatter(
            zcount,
            [halved_ref, dwo_hbm, dwg_hbm, dwi_hbm, gsrc, ssrc],
            [*shares, gates_full, sums_full],
            [main, gate_pool, sum_pool, main],
            pool[15:],
            chunks,
            lags,
        )
        back_point = in_turn(scatter, step, plan[:groups])
        last_point = in_turn(scatter, step, plan[groups:], groups)

        @pl.when(step == 0)
        def _():
            rows = early_ref.shape[0] // 3
            for k in range(3):
                shares[k][0:rows, :] = early_ref[k * rows : (k + 1) * rows, :]

    def stash(g, k, target):
        return pltpu.make_async_copy(wst.at[k], target.at[g // 2, g % 2], wsem.at[k])

    def stashed(first, what):
        for g in range(groups):

            @pl.when(step == first + g)
            def _(g=g):
                what(g)

    exchange = Exchange(*swap)
    gl_ref, tot_ref, rch_ref = gls.at[group], tots.at[group], rchs.at[group]
    lrows = ltiles * TILE
    residual = [
        pltpu.make_async_copy(dres_hbm.at[pl.ds(0, lrows)], dxl_ref, dsem.at[0]),
        pltpu.make_async_copy(
            dres_hbm.at[pl.ds(lrows, dxs_ref.shape[0])], dxs_ref, dsem.at[1]
        ),
    ]
    behind = remote(
        halo_out, halo_in, hsem.at[0], hsem.at[1], exchange.peer(exchange.count - 1)
    )
    width = gp_ref.shape[1]

    @pl.when(step == 0)
    def _():
        meet_all(exchange, 1 if scatter is None else zcount)

    @pl.when(step < groups)
    def _():
        back_part(
            ltiles, tiles, back_point, rlow_ref, w_ref, mixl_ref, mixs_ref, gp_ref, st_ref, pr_ref,
            sin_ref, dp_ref, pc_ref, wst.at[0], gl_ref, tot_ref, rch_ref, exchange.mine.at[group],
            bias_ref.at[group], acc.at[0 : rlow_ref.shape[0], 0:width],
            lambda: stashed(0, lambda g: stash(g - 1, 0, dwo_hbm).wait() if g > 0 else None),
        )
        stashed(0, lambda g: stash(g, 0, dwo_hbm).start())
        for g in range(groups):

            @pl.when(step == g)
            def _(g=g):
                exchange.theirs[g, exchange.place] = jnp.zeros(exchange.theirs.shape[2:], F32)
                exchange.start(g)

    @pl.when(step >= groups)
    def _():
        @pl.when(step == groups)
        def _():
            stash(groups - 1, 0, dwo_hbm).wait()

        def before(g):
            if g > 0:
                stash(g - 1, 1, dwg_hbm).wait()
                stash(g - 1, 2, dwi_hbm).wait()

        def after(g):
            stash(g, 1, dwg_hbm).start()
            stash(g, 2, dwi_hbm).start()
            if g == groups - 1:
                stash(g, 1, dwg_hbm).wait()
                stash(g, 2, dwi_hbm).wait()

        last_part(
            ltiles, tiles, groups, last_point, exchange, residual, x_ref, gain_ref, nm_ref,
            wg_ref, wi_ref, wd_ref, wo_ref, pc_ref, in_ref, dp_ref, ip_ref, st_ref, pr_ref, sin_ref,
            tot_ref, rch_ref, gl_ref, bias_ref.at[group], dxl_ref, dxs_ref, halo_out, behind, pairs,
            gain_grad_ref, wst.at[1], wst.at[2], gsrc, ssrc, acc, dc_ref, cl_ref, dl_ref, ol_ref, il_ref, gain2_ref,
            lambda: stashed(groups, before), lambda: stashed(groups, after),
        )

    @pl.when(step == pl.num_programs(0) - 1)
    def _():
        exchange.drain(groups)
        behind.wait()
        rows = slice(lrows - HALO, lrows)
        dxl_ref[rows, :] = dxl_ref[rows, :] + halo_in[...]
        if scatter is not None:
            scatter.drain()
        final = [
            pltpu.make_async_copy(gates_full, gates_hbm, wsem.at[0]),
            pltpu.make_async_copy(sums_full, sums_hbm, wsem.at[1]),
        ]
        for copy in final:
            copy.start()
        for copy in final:
            copy.wait()


def finish_kernel(number, *refs):
    ins, (gates_ref, sums_ref) = refs[:number], refs[number : number + 2]
    outs = refs[number + 2 : 2 * number + 2]
    gd_ref, go_ref, gain1_ref, gain2_ref, conv_ref, *rows = refs[2 * number + 2 : -number - 3]
    *held, table, sem_in, sem_out = refs[-number - 3 :]
    copies = []
    for k, (a, h, b) in enumerate(zip(ins, held, outs)):
        copies.append(
            (
                pltpu.make_async_copy(a, h, sem_in.at[k]),
                pltpu.make_async_copy(h, b, sem_out.at[k]),
            )
        )
        copies[-1][0].start()
    for come, go in copies:
        come.wait()
        go.start()
    gd_ref[...] = gates_ref[0].astype(F32)
    go_ref[...] = gates_ref[1].astype(F32)
    for h in range(2):
        for k in range(16):
            table[8 * h : 8 * h + 8, 128 * k : 128 * k + 128] = sums_ref[h, k]
    chans = conv_ref.shape[1]
    conv_ref[...] = table[1:5, 0:chans]
    for r, ref in zip((0, 5, 6, 7, 8, 9), rows):
        ref[...] = table[r : r + 1, 0:chans].reshape(chans)
    for k, ref in enumerate((gain1_ref, gain2_ref)):
        for i in range(8):
            table[0:1, 128 * i : 128 * i + 128] = sums_ref[0, 12 + k, i : i + 1, :]
        ref[...] = table[0:1, 0:1024].reshape(1024)
    for _, go in copies:
        go.wait()


def shape_of(shape, dtype):
    return jax.ShapeDtypeStruct(shape, dtype)


def whole(shape):
    return pl.BlockSpec(shape, lambda g: (0,) * len(shape), pipeline_mode=pl.Buffered(1))


def params(limit, **more):
    return pltpu.CompilerParams(
        dimension_semantics=("arbitrary",), vmem_limit_bytes=int(limit * MIB), **more
    )


def to_slots(parts, count):
    rows = parts[0].shape[0]
    depth = parts[0].shape[1]
    got = lax.all_gather(jnp.concatenate(parts, axis=0), ("seq", "row"), axis=0, tiled=False)
    if count != SLOTS:
        got = got.reshape(count, len(parts), rows, depth).transpose(1, 0, 2, 3)
        got = got.reshape(len(parts), SLOTS, rows * count // SLOTS, depth).transpose(1, 0, 2, 3)
    return got.reshape(SLOTS, -1, depth)


def scatter_slots(grads, number, count):
    slots, rows, depth = grads.shape
    if count != SLOTS:
        grads = grads.reshape(slots, number, rows // number, depth).transpose(1, 0, 2, 3)
        grads = grads.reshape(number, count, -1, depth).transpose(1, 0, 2, 3)
    flat_grads = grads.reshape(slots * rows, depth)
    own = lax.psum_scatter(flat_grads, ("seq", "row"), scatter_dimension=0, tiled=True)
    own = own.astype(F32).reshape(number, -1, depth)
    return [own[i] for i in range(number)]


def shards(
    long_tokens,
    short_tokens,
    long_length,
    long_cotangent,
    short_cotangent,
    first_gain,
    gate_weight,
    gate_bias,
    input_weight,
    input_bias,
    conv_weight,
    conv_bias,
    decay_gate_weight,
    decay_gate_bias,
    input_gate_weight,
    input_gate_bias,
    decay_param,
    out_weight,
    second_gain,
    mlp_gate_weight,
    mlp_up_weight,
    mlp_down_weight,
):
    count = lax.axis_size("seq") * lax.axis_size("row")
    lrows, srows, depth = long_tokens.shape[1], short_tokens.shape[1], long_tokens.shape[2]
    chans = gate_bias.shape[0]
    units = mlp_gate_weight.shape[1] * count
    tokens = lrows + srows
    total = HALO + tokens
    ltiles, tiles = lrows // TILE, total // TILE
    cshare, ushare = chans // SLOTS, units // SLOTS
    groups = 4
    width = chans // groups
    per = SLOTS // groups

    zcount = lax.axis_size("row")
    seqs = lax.axis_size("seq")
    fast = seqs == 8 and count == SLOTS
    hbm = pl.BlockSpec(memory_space=pl.ANY)
    one_dma = pltpu.SemaphoreType.DMA
    steps = ushare // 16
    ready_parts = max(1, min(steps - 1, FRONT_PARTS))
    blocks, bwidth = decay_gate_weight.shape[0:2]
    mlp_own = [mlp_gate_weight.T, mlp_up_weight.T, mlp_down_weight]
    channel = [
        gate_bias, input_bias, conv_weight, conv_bias, decay_gate_bias, input_gate_bias,
        8.0 * jax.nn.softplus(decay_param), 8.0 * jax.nn.sigmoid(decay_param),
    ]
    gain1 = first_gain[None]
    gain2 = second_gain[None]

    def early(g):
        return jnp.minimum(g, groups - 1)

    def after_one(g):
        return jnp.maximum(g - 1, 0)

    def late(g):
        return jnp.maximum(g - groups, 0)

    def both_times(g):
        return lax.rem(g, groups)

    def slot_at(when, which=0):
        return pl.BlockSpec((per, cshare, depth), lambda g: (when(g), which, 0))

    def blocks_at(when):
        return pl.BlockSpec((2, bwidth, bwidth), lambda g: (when(g), 0, 0))

    def cols_at(nrows, when):
        return pl.BlockSpec((nrows, width), lambda g: (0, when(g)))

    lags = (2, 2, 3, 2)
    if fast:
        front_own = [gate_weight.T, input_weight.T, out_weight, *mlp_own]
        parts = [(0, 0, cshare, 0, 0), (1, 0, cshare, 0, cshare)]
        ready = len(row_chunks(parts, 16)) + sum(lags)
        parts += [(2, 0, cshare, 1, 0)]
        parts += [
            (3 + k, 16 * p, 16, 2, 48 * p + 16 * k) for p in range(ready_parts) for k in range(3)
        ]
        chunks = row_chunks(parts, 16)
        plan = [[]] + spread_out(len(chunks) + sum(lags) + 1 - ready, 1, groups, 4)
        plan = [[[ready + t for t in p] for p in row] for row in plan]
        front_links = (zcount, chunks, lags, ready, plan)
        front_shapes = [
            shape_of(GRID + (n, depth), BF16) for n in (2 * cshare, cshare, 48 * ready_parts)
        ]
        front_scratch = gather_sems(len(chunks), zcount)
    else:
        pairw = to_slots([gate_weight.T, input_weight.T], count)
        outw = to_slots([out_weight], count)
        mlpw = to_slots(mlp_own, count).reshape(GRID + (3, steps, 16, depth))
        mlpw = jnp.swapaxes(mlpw, 4, 5).reshape(GRID + (48 * steps, depth))
        w_first, w_second = jnp.split(mlpw, [48 * ready_parts], axis=4)
        front_own = [pairw.reshape(GRID + (-1, depth))]
        front_links, front_shapes, front_scratch = None, [], []

    col = cols_at(total, after_one)
    wide = shape_of((total, chans), F32)
    narrow = shape_of((HALO + lrows, chans), F32)
    gp, inner, dp, ip, states, reach, mix_s, s_in, normed, x, cot, chan, *made = pl.pallas_call(
        functools.partial(front_kernel, ltiles, tiles, groups, front_links),
        grid=(1 + groups,),
        in_specs=[
            hbm, hbm, hbm, hbm, pl.BlockSpec(memory_space=pltpu.SMEM), whole((1, depth)),
            *[whole(c.shape) for c in channel], blocks_at(after_one),
            blocks_at(after_one), *[whole(w.shape) if fast else hbm for w in front_own],
        ],
        out_specs=[
            col, col, col, col, col, cols_at(HALO + lrows, after_one), cols_at(srows, after_one),
            whole((8, chans)), whole((total, depth)), whole((total, depth)),
            whole((tokens, depth)), cols_at(16, after_one), *[hbm for _ in front_shapes],
        ],
        out_shape=[
            wide, wide, wide, wide, wide, narrow, shape_of((srows, chans), BF16),
            shape_of((8, chans), F32), shape_of((total, depth), BF16),
            shape_of((total, depth), BF16), shape_of((tokens, depth), BF16),
            shape_of((16, chans), F32), *front_shapes,
        ],
        scratch_shapes=[
            pltpu.VMEM((total, width), F32), pltpu.VMEM((total, width), BF16),
            pltpu.VMEM((2,) + GRID[2:] + (2 * cshare, depth), BF16),
            pltpu.VMEM((2, width, width), BF16), pltpu.VMEM((HALO, depth), BF16),
            pltpu.VMEM((16, chans), F32), one_dma((4,)), one_dma((2,)), one_dma((2,)), *exchange_scratch(groups, width, seqs),
            *front_scratch,
        ],
        compiler_params=params(56, collective_id=0, has_side_effects=True),
        name="front",
    )(
        long_tokens.reshape(lrows, depth), short_tokens.reshape(srows, depth),
        long_cotangent.reshape(lrows, depth), short_cotangent.reshape(srows, depth), long_length,
        gain1, *channel, decay_gate_weight, input_gate_weight, *front_own,
    )
    if fast:
        pairw, outw, w_first = made
    outw = outw.reshape(SLOTS, -1, depth)
    pairw = pairw.reshape(SLOTS, -1, depth)

    hid = units // steps
    block = (3,) + GRID + (16, depth)
    wbuf = pltpu.VMEM((2,) + block, BF16)
    dwbuf = pltpu.VMEM(block, BF16)
    if fast:
        chunks = [
            (k, 16 * (ready_parts + p), 16, 0, 48 * p + 16 * k)
            for p in range(steps - ready_parts)
            for k in range(3)
        ]
        plan = [[[] for _ in range(8)] for _ in range(steps)]
        todo = list(range(len(chunks) + sum(lags)))
        for s in range(ready_parts - 1, steps - 1):
            due = 3 * (s - ready_parts + 1) + 3 + sum(lags)
            now, todo = [t for t in todo if t < due], [t for t in todo if t >= due]
            first = 0 if s == ready_parts - 1 else s
            spots = [(q, k) for q in range(first, s + 1) for k in range(8)]
            for n, t in enumerate(now):
                lead = min(MLP_AHEAD, len(now) - 1) if first == 0 else 0
                share = max(0, n - lead) / max(1, len(now) - lead)
                q, k = spots[int(share * len(spots))]
                plan[q][k].append(t)
        soon = [(p, k) for p in range(EARLY_PARTS) for k in range(3)]
        early_chunks = [
            (HALVED, n, 0, (p, k), (0, 16), 0, 16 * (k * EARLY_PARTS + p))
            for n, (p, k) in enumerate(soon)
        ]
        early_lags = (1, 2, 2, 2)
        early_plan = [[[] for _ in range(9)] for _ in range(steps)]
        spot = 0
        for t in range(len(soon) + sum(early_lags)):
            after = 8 * (t // 3 + 1) + 7 if t < len(soon) else 0
            spot = max(after, spot + EARLY_GAP)
            q, k = divmod(min(spot, 8 * steps), 8)
            q, k = (q, k) if q < steps else (steps - 1, 8)
            early_plan[q][k].append(t)
        mlp_links = (zcount, chunks, lags, plan, early_chunks, early_lags, early_plan)
        w_last, more_specs = mlp_own, [hbm, whole((16 * len(soon), depth))]
        more_shapes = [
            shape_of(GRID + (48 * (steps - ready_parts), depth), BF16),
            shape_of((16 * len(soon), depth), F32),
        ]
        half_block = block[:3] + block[4:]
        more_scratch = [
            pltpu.VMEM(half_block, BF16), one_dma((2,)), pltpu.SemaphoreType.REGULAR,
            *gather_sems(len(chunks), zcount), *halved_scratch(len(soon), len(soon), depth, zcount),
        ]
        dw_shape = (steps,) + half_block
        more_params = dict(collective_id=3, has_side_effects=True)
    else:
        mlp_links, w_last, more_specs, more_shapes, more_scratch = None, [w_second], [], [], []
        dw_shape, more_params = (steps,) + block, {}
    out_l, out_s, d_res, rlow, mix_l, gain2_grad, dmlp, *more_out = pl.pallas_call(
        functools.partial(mlp_kernel, ltiles, tokens // TILE, mlp_links),
        grid=(steps,),
        in_specs=[
            whole((total, depth)), whole((tokens, depth)), whole((HALO + lrows, chans)),
            whole((HALO + lrows, chans)), whole((HALO + lrows, chans)), whole((8, chans)),
            whole((srows, chans)), whole((SLOTS, cshare, depth)), whole((1, depth)), hbm,
            *[whole(w.shape) if fast else hbm for w in w_last],
        ],
        out_specs=[
            whole((lrows, depth)), whole((srows, depth)), whole((tokens, depth)), whole((tokens, depth)),
            whole((lrows, chans)), whole((8, depth)), hbm, *more_specs,
        ],
        out_shape=[
            shape_of((lrows, depth), BF16), shape_of((srows, depth), BF16),
            shape_of((tokens, depth), F32), shape_of((tokens, depth), BF16),
            shape_of((lrows, chans), BF16),
            shape_of((8, depth), F32), shape_of(dw_shape, BF16), *more_shapes,
        ],
        scratch_shapes=[
            pltpu.VMEM((tokens, depth), BF16), pltpu.VMEM((tokens, depth), F32),
            pltpu.VMEM((tokens, depth), F32), pltpu.VMEM((tokens, 2 * hid), F32),
            pltpu.VMEM((tokens, hid), F32), pltpu.VMEM((tokens, hid), BF16),
            pltpu.VMEM((tokens, 2 * hid), BF16), wbuf, dwbuf, one_dma((2, 3)), one_dma, *more_scratch,
        ],
        compiler_params=params(62, **more_params),
        name="mlp",
    )(x, cot, states, reach, gp, s_in, mix_s, outw, gain2, w_first, *w_last)

    gate_shape, sum_shape = GRID + (bwidth // 2, bwidth), GRID + (8, 128)
    grads_shape = shape_of(GRID + (cshare, depth), BF16)
    tail_links, tail_in, tail_specs, tail_shapes, tail_scratch = None, [], [], [], []
    if fast:
        size = 16
        tail_chunks = []
        number = 0
        for p in range(EARLY_PARTS, steps):
            for k in range(3):
                tail_chunks.append(
                    (HALVED, number % TAIL_SLOTS, 0, (p, k), (0, size), k, 16 * p)
                )
                number += 1
        for which in (1, 2, 3):
            if which == 2:
                tail_chunks.append((SUMS, 0, 5, None, (0, 8), 7, 0))
                tail_chunks.append((GATES, 0, 4, None, (0, bwidth // 2), 6, 0))
                during = len(tail_chunks) - 2
            for start in range(0, cshare, size):
                tail_chunks.append(
                    (CORE, number % TAIL_SLOTS, which, None, (start, size), 2 + which, start)
                )
                number += 1
        tail_lags = (1, 3, 3, 3, 1, 1, 1, 1)
        marks = [[5.0 * g + t for t in (0.0, 1.5, 4.0)] for g in range(groups)]
        marks += [
            [5.0 * groups + 12.5 * g + t for t in (0.0, 5.0, 6.0, 9.0, 10.5, 12.5)] for g in range(groups)
        ]
        plan = paced(during, 3, marks)
        plan[-1][-1] += range(during, len(tail_chunks) + sum(tail_lags) + 1)
        tail_links = (zcount, tail_chunks, tail_lags, plan)
        early_sums = more_out[1]
        tail_in, tail_specs = [dmlp, early_sums], [whole((ushare, depth))] * 3 + [whole((cshare, depth))] * 3
        tail_shapes = [shape_of((ushare, depth), F32)] * 3 + [shape_of((cshare, depth), F32)] * 3
        lone = five(TAIL_SLOTS, (size, depth), BF16, zcount)
        lone[1] = five(CORE_SLOTS, (size, depth), BF16, zcount)[1]
        n = len(tail_chunks)
        links = one_dma((n, zcount + 2))
        tail_scratch = [
            *lone,
            *five(1, gate_shape[4:], BF16, zcount),
            *five(1, sum_shape[4:], F32, zcount),
            one_dma((n,)), links, links, links, links,
            pltpu.VMEM(gate_shape, BF16), pltpu.VMEM(sum_shape, F32),
        ]
    dx_l, dx_s, _, d_out, d_gate, d_input, gate_sums, sums, *shares = pl.pallas_call(
        functools.partial(tail_kernel, ltiles, tiles, groups, tail_links),
        grid=(2 * groups,),
        in_specs=[
            whole((total, depth)), whole((1, depth)), whole((total, depth)), hbm,
            whole((tokens, depth)), slot_at(early), slot_at(late, 0), slot_at(late, 1),
            blocks_at(late), blocks_at(late), cols_at(16, both_times), cols_at(lrows, early),
            cols_at(srows, early), cols_at(total, early), cols_at(total, late),
            cols_at(total, both_times), cols_at(total, late), cols_at(total, both_times),
            cols_at(HALO + lrows, both_times), cols_at(8, both_times), whole((8, depth)),
            *([hbm, whole(early_sums.shape)] if fast else []),
        ],
        out_specs=[
            whole((lrows, depth)), whole((srows, depth)), whole((8, depth)), hbm, hbm, hbm, hbm, hbm,
            *tail_specs,
        ],
        out_shape=[
            shape_of((lrows, depth), F32), shape_of((srows, depth), F32), shape_of((8, depth), F32),
            grads_shape, grads_shape, grads_shape, shape_of(gate_shape, BF16),
            shape_of(sum_shape, F32), *tail_shapes,
        ],
        scratch_shapes=[
            pltpu.VMEM((total, depth), F32), pltpu.VMEM((total, width), F32),
            pltpu.VMEM((total, width), BF16), pltpu.VMEM((total, width), BF16),
            pltpu.VMEM((total, width), BF16), pltpu.VMEM((total, width), BF16),
            pltpu.VMEM((groups, total, width), BF16), pltpu.VMEM((groups, total, width), F32),
            pltpu.VMEM((groups, HALO + lrows, width), F32), pltpu.VMEM((groups, 8, width), F32),
            pltpu.VMEM((3,) + GRID[2:] + (cshare, depth), BF16), pltpu.VMEM(gate_shape, BF16),
            pltpu.VMEM(sum_shape, F32), pltpu.VMEM((2, width, width), BF16),
            pltpu.VMEM((HALO, depth), F32), pltpu.VMEM((HALO, depth), F32), one_dma((2,)),
            one_dma((2,)), one_dma((3,)), *exchange_scratch(groups, width, seqs), *tail_scratch,
        ],
        compiler_params=params(63, collective_id=4, has_side_effects=True),
        name="tail",
    )(
        x, gain1, normed, d_res, rlow, outw, pairw, pairw, decay_gate_weight, input_gate_weight, chan,
        mix_l, mix_s, gp, inner, dp, ip, states, reach, s_in, gain2_grad, *tail_in,
    )

    if fast:
        g_mgate, g_mup, g_down, g_out, g_gate, g_input = shares
    else:
        dmlp = dmlp.reshape(steps, 3, SLOTS, -1, depth).transpose(2, 1, 0, 3, 4)
        g_mgate, g_mup, g_down = scatter_slots(dmlp.reshape(SLOTS, -1, depth), 3, count)
        dmix = jnp.concatenate([d_gate, d_input, d_out], axis=4).reshape(SLOTS, -1, depth)
        g_gate, g_input, g_out = scatter_slots(dmix, 3, count)
        gate_sums, sums = lax.psum((gate_sums.astype(F32), sums), ("seq", "row"))
    large = [out_l, out_s, dx_l, dx_s, g_gate, g_input, g_out, g_mgate, g_mup, g_down]
    vector = shape_of((chans,), F32)
    gate_grad = shape_of((blocks, bwidth, bwidth), F32)
    gain_grad = shape_of((depth,), F32)
    vmem = pl.BlockSpec(memory_space=pltpu.VMEM)
    (
        out_l, out_s, dx_l, dx_s, g_gate, g_input, g_out, g_mgate, g_mup, g_down, decay_grad,
        open_grad, gain1_grad, gain2_grad, conv_grad, input_bias_grad, conv_bias_grad,
        decay_bias_grad, open_bias_grad, param_grad, gate_bias_grad,
    ) = pl.pallas_call(
        functools.partial(finish_kernel, len(large)),
        in_specs=[hbm] * len(large) + [vmem, vmem],
        out_specs=[hbm] * len(large) + [vmem] * 11,
        out_shape=[shape_of(a.shape, a.dtype) for a in large]
        + [gate_grad, gate_grad, gain_grad, gain_grad, shape_of(conv_weight.shape, F32)]
        + [vector] * 6,
        scratch_shapes=[
            *[pltpu.VMEM(a.shape, a.dtype) for a in large], pltpu.VMEM((16, 2048), F32),
            one_dma((len(large),)), one_dma((len(large),)),
        ],
        compiler_params=pltpu.CompilerParams(vmem_limit_bytes=62 * MIB),
        name="finish",
    )(*large, gate_sums.reshape(2, blocks, bwidth, bwidth), sums.reshape(2, 16, 8, 128))
    return (
        out_l.reshape(long_tokens.shape),
        out_s.reshape(short_tokens.shape),
        dx_l.reshape(long_tokens.shape),
        dx_s.reshape(short_tokens.shape),
        gain1_grad,
        g_gate.T,
        gate_bias_grad,
        g_input.T,
        input_bias_grad,
        conv_grad,
        conv_bias_grad,
        decay_grad,
        decay_bias_grad,
        open_grad,
        open_bias_grad,
        param_grad,
        g_out,
        gain2_grad,
        g_mgate.T,
        g_mup.T,
        g_down,
    )


def solution(mesh):
    both = ("seq", "row")
    long_spec = P("row", "seq", None)
    short_spec = P(both, None, None)
    cols = P(None, both)
    rows = P(both, None)
    return jax.shard_map(
        shards,
        mesh=mesh,
        in_specs=(
            long_spec, short_spec, P("row"), long_spec, short_spec, P(), cols, P(), cols, P(),
            P(), P(), P(), P(), P(), P(), P(), rows, P(), cols, cols, rows,
        ),
        out_specs=(
            long_spec, short_spec, long_spec, short_spec, P(), cols, P(), cols, P(), P(), P(),
            P(), P(), P(), P(), P(), rows, P(), cols, cols, rows,
        ),
        check_vma=False,
    )
```

```python
import functools

import jax
import jax.numpy as jnp
from jax import lax
from jax.experimental import pallas as pl
from jax.experimental.pallas import tpu as pltpu
from jax.sharding import PartitionSpec as P

EPSILON = 1e-06
F32 = jnp.float32
BF16 = jnp.bfloat16
GRID = (2, 2, 2, 4)
SLOTS = 32
TILE = 16
HALO = 16
MIB = 1024 * 1024
MLP_AHEAD = 1
EARLY_PARTS = 2
EARLY_GAP = 3
FRONT_LEFT = 9
FRONT_DELAY = 3
FRONT_PARTS = 3
TAIL_SLOTS = 11
CORE_SLOTS = 5
GELU_A = 0.7978845608028654
GELU_B = 0.044715


def dot_nn(a, b):
    return lax.dot_general(a, b, (((1,), (0,)), ((), ())), preferred_element_type=F32)


def dot_nt(a, b):
    return lax.dot_general(a, b, (((1,), (1,)), ((), ())), preferred_element_type=F32)


def dot_tn(a, b):
    return lax.dot_general(a, b, (((0,), (0,)), ((), ())), preferred_element_type=F32)


def sigmoid(v):
    return 0.5 * jnp.tanh(0.5 * v) + 0.5


def gelu(v):
    t = jnp.tanh(v * (GELU_A + (GELU_A * GELU_B) * (v * v)))
    h = 0.5 * v
    return h + h * t


def gelu_pair(v):
    w = v * v
    t = jnp.tanh(v * (GELU_A + (GELU_A * GELU_B) * w))
    h = 0.5 * v
    slope = 0.5 + 0.5 * t + (h - h * (t * t)) * (GELU_A + (3.0 * GELU_A * GELU_B) * w)
    return h + h * t, slope


def row_iota(shape):
    return lax.broadcasted_iota(jnp.int32, shape, 0)


def at(j):
    return pl.ds(pl.multiple_of(j * TILE, TILE), TILE)


def scan_tile(a, b, reverse):
    rows = row_iota(a.shape)
    step = 1
    while step < TILE:
        if reverse:
            keep, shift = rows < TILE - step, TILE - step
        else:
            keep, shift = rows >= step, step
        b = jnp.where(keep, a * pltpu.roll(b, shift, 0) + b, b)
        a = jnp.where(keep, a * pltpu.roll(a, shift, 0), a)
        step *= 2
    return a, b


def shift_down(cur, prev, k):
    if k == 0:
        return cur
    rows = row_iota(cur.shape)
    return jnp.where(rows < k, pltpu.roll(prev, k, 0), pltpu.roll(cur, k, 0))


def shift_up(cur, later, k):
    if k == 0:
        return cur
    rows = row_iota(cur.shape)
    return jnp.where(
        rows >= TILE - k, pltpu.roll(later, TILE - k, 0), pltpu.roll(cur, TILE - k, 0)
    )


def fold(v):
    return v[0:8] + v[8:16]


def flat(block):
    return block.reshape(-1, block.shape[-1])


def gates(dp, ip, c8):
    rate = sigmoid(dp)
    opening = sigmoid(ip)
    log_decay = -c8 * (0.25 + rate)
    decay = jnp.exp(log_decay)
    square = -jnp.tanh(log_decay) * (1.0 + decay * decay)
    return rate, opening, decay, square


GB, IB, CW, CB, DB, OB, C8, S8 = 0, 1, 2, 6, 7, 8, 9, 10


def conv_tile(in_ref, pc_ref, j, live):
    cur = in_ref[at(j), :]
    prev = in_ref[at(j - 1), :] * live
    out = pc_ref[CB : CB + 1, :] + pc_ref[CW : CW + 1, :] * cur
    moved = [cur]
    for k in range(1, 4):
        m = shift_down(cur, prev, k)
        moved.append(m)
        out = out + pc_ref[CW + k : CW + k + 1, :] * m
    return out, moved


def place_of():
    s = lax.axis_index("seq")
    return s // 4, (s // 2) % 2, s % 2, lax.axis_index("row")


def device_at(y, x, c, z):
    return ((y * 2 + x) * 2 + c, z)


class Peers:
    def __init__(self, zcount):
        y, x, c, z = self.place = place_of()
        self.far = [(z + k) % zcount for k in range(1, zcount)]
        self.along = [device_at(y, x, c, q) for q in self.far]
        self.near = ((y + c) % 2, (x + 1 - c) % 2)
        self.first = device_at(*self.near, c, z)
        self.second = device_at((y + 1 - c) % 2, (x + c) % 2, c, z)
        self.other = device_at(y, x, 1 - c, z)

    def meet(self):
        everyone = [*self.along, self.first, self.second, self.other]
        barrier = pltpu.get_barrier_semaphore()
        for peer in everyone:
            pl.semaphore_signal(
                barrier, inc=1, device_id=peer, device_id_type=pl.DeviceIdType.MESH
            )
        pl.semaphore_wait(barrier, len(everyone))


def remote(source, target, send, recv, device):
    return pltpu.make_async_remote_copy(
        src_ref=source,
        dst_ref=target,
        send_sem=send,
        recv_sem=recv,
        device_id=device,
        device_id_type=pl.DeviceIdType.MESH,
    )


class Spread:
    def __init__(self, peers, own, full, send, recv):
        self.peers, self.own, self.full, self.send, self.recv = peers, own, full, send, recv

    def go(self, stage, act):
        y, x, c, z = self.peers.place
        p, full = self.peers, self.full
        if stage == 0:
            for k, device in enumerate(p.along):
                act(remote(self.own, full(y, x, c, z), self.send(k), self.recv(k), device))
            return
        k = len(p.along) + stage - 1
        if stage == 2:

            @pl.when(c == 0)
            def _():
                part = full(y, slice(None), c, slice(None))
                act(remote(part, part, self.send(k), self.recv(k), p.second))

            @pl.when(c == 1)
            def _():
                part = full(slice(None), x, c, slice(None))
                act(remote(part, part, self.send(k), self.recv(k), p.second))

            return
        if stage == 1:
            part, device = full(y, x, c, slice(None)), p.first
        else:
            part, device = full(slice(None), slice(None), c, slice(None)), p.other
        act(remote(part, part, self.send(k), self.recv(k), device))

    def start(self, stage):
        self.go(stage, lambda d: d.start())

    def arrive(self, stage):
        self.go(stage, lambda d: d.wait_recv())

    def drain(self):
        for stage in range(4):
            self.go(stage, lambda d: d.wait_send())


def wave_of(t, count, lags, urgent=None, delay=0):
    urgent = count if urgent is None else urgent
    for stage in range(len(lags), -1, -1):
        piece = t - sum(lags[:stage])
        if 0 <= piece < urgent:
            yield piece, stage
        elif urgent <= piece - delay < count:
            yield piece - delay, stage


class Gather:
    def __init__(self, zcount, ins, outs, sems, chunks, lags, urgent=None, delay=0):
        self.order = (len(chunks), lags, urgent, delay)
        self.csem, self.ssem, self.rsem = sems
        self.peers = Peers(zcount)
        y, x, c, z = self.peers.place
        self.spreads, self.copies = [], []
        for i, (which, start, size, target, offset) in enumerate(chunks):
            own = ins[which].at[pl.ds(start, size)]
            rows = pl.ds(offset, size)

            def full(a, b, d, e, ref=outs[target], rows=rows):
                return ref.at[a, b, d, e, rows]

            def send(k, i=i):
                return self.ssem.at[i, k]

            def recv(k, i=i):
                return self.rsem.at[i, k]

            self.spreads.append(Spread(self.peers, own, full, send, recv))
            self.copies.append(pltpu.make_async_copy(own, full(y, x, c, z), self.csem.at[i]))

    def wave(self, t):
        for i, stage in wave_of(t, *self.order):
            if stage == 0:
                self.copies[i].start()
            elif stage == 1:
                self.copies[i].wait()
            if stage > 0:
                self.spreads[i].arrive(stage - 1)
            if stage < 4:
                self.spreads[i].start(stage)

    def drain(self):
        for spread in self.spreads:
            spread.drain()


def in_turn(weave, step, plan, first=0):
    def point(k):
        for s, points in enumerate(plan, first):
            if k < len(points) and points[k]:

                @pl.when(step == s)
                def _(todo=points[k]):
                    for t in todo:
                        weave.wave(t)

    return point


def spread_out(waves, ahead, steps, points):
    todo = list(range(waves))
    plan = []
    for s in range(steps):
        row = []
        for k in range(points):
            take = ahead if s == 0 and k == 0 else 1
            if s == steps - 1 and k == points - 1:
                take = len(todo)
            row.append(todo[:take])
            todo = todo[take:]
        plan.append(row)
    return plan


def paced(waves, ahead, marks):
    last = marks[-1][-1]
    plan = [[[] for _ in row] for row in marks]
    spots = [(t, s, k) for s, row in enumerate(marks) for k, t in enumerate(row)]
    for w in range(waves):
        due = last * max(0, w - ahead) / max(1, waves - ahead)
        _, s, k = next(spot for spot in spots if spot[0] >= due)
        plan[s][k].append(w)
    return plan


def row_chunks(parts, size):
    return [
        (which, start + i, size, target, offset + i)
        for which, start, count, target, offset in parts
        for i in range(0, count, size)
    ]


def gather_sems(count, zcount):
    links = pltpu.SemaphoreType.DMA((count, zcount + 2))
    return [pltpu.SemaphoreType.DMA((count,)), links, links]


CORE, GATES, SUMS, HALVED = 0, 1, 2, 3


class Scatter:
    def __init__(self, zcount, ins, outs, buffers, sems, chunks, lags):
        self.peers = Peers(zcount)
        self.zcount, self.chunks, self.lags = zcount, chunks, lags
        self.ins, self.outs, self.buffers = ins, outs, buffers
        self.csem, self.ssem, self.rsem = sems[:3]
        self.pieces = [Piece(self, i, sems[3:], *chunk) for i, chunk in enumerate(chunks)]
        self.waves = len(chunks) + sum(lags) + 1

    def wave(self, t):
        for i, stage in wave_of(t, len(self.pieces), self.lags):
            if stage <= 4 or self.pieces[i].spread is not None:
                self.pieces[i].step(stage)

    def drain(self):
        for piece in self.pieces:
            piece.drain()


def slot_of_core(i, slots):
    return i % slots


def add_into(into, i, part, j):
    into[i] = (into[i].astype(F32) + part[j].astype(F32)).astype(into.dtype)


class Piece:
    def __init__(self, owner, i, sems, kind, slot, which, source, span, target, place):
        self.o, self.i, self.kind, self.slot = owner, i, kind, slot
        self.a, self.r0, self.r1, self.r2, self.r3 = owner.buffers[kind]
        self.from_core = 0 if self.r0 is None else slot_of_core(i, self.r0.shape[0])
        self.source, self.lead, self.rows = owner.ins[which], source, pl.ds(*span)
        self.target, self.place = owner.outs[target], place
        self.spread, self.drained = None, False
        if kind in (GATES, SUMS):
            y, x, c, z = owner.peers.place

            def full(*at_place):
                return self.target.at[at_place]

            def send(k):
                return sems[0].at[i, k]

            def recv(k):
                return sems[1].at[i, k]

            self.spread = Spread(owner.peers, full(y, x, c, z), full, send, recv)

    def local(self):
        c = self.o.peers.place[2]
        if self.kind == HALVED:
            mine = self.source.at[self.lead]
        else:
            mine = self.source.at[:, :, c, :, self.rows]
        return pltpu.make_async_copy(mine, self.a.at[self.slot], self.o.csem.at[self.i])

    def send(self, stage, act):
        s, peers = self.slot, self.o.peers
        y, x, c, z = peers.place

        def go(source, target, k, device):
            act(remote(source, target, self.o.ssem.at[self.i, k], self.o.rsem.at[self.i, k], device))

        if stage == 0:
            if self.kind != HALVED:
                theirs = self.source.at[:, :, 1 - c, :, self.rows]
                go(theirs, self.r0.at[self.from_core], 0, peers.other)
        elif stage == 1:

            @pl.when(c == 0)
            def _():
                go(self.a.at[s, 1 - y], self.r1.at[s], 1, peers.second)

            @pl.when(c == 1)
            def _():
                go(self.a.at[s, :, 1 - x], self.r1.at[s], 1, peers.second)

        elif stage == 2:
            go(self.a.at[(s, *peers.near)], self.r2.at[s], 2, peers.first)
        else:
            for k, device in enumerate(peers.along):
                go(self.a.at[s, y, x, peers.far[k]], self.r3.at[s, k], 3 + k, device)

    def step(self, stage):
        s, zcount = self.slot, self.o.zcount
        y, x, c, z = self.o.peers.place
        if stage == 0:
            for earlier in self.o.pieces[: self.i]:
                if earlier.a is self.a and earlier.slot == s:
                    earlier.drain()
            self.local().start()
        elif stage <= 4:
            self.send(stage - 1, lambda d: d.wait_recv())
        else:
            self.spread.arrive(stage - 5)
        if stage == 1:
            self.local().wait()
            if self.kind != HALVED:

                @pl.loop(0, 4 * zcount)
                def _(q):
                    i = (q // (2 * zcount), (q // zcount) % 2, q % zcount)
                    add_into(self.a, (s, *i), self.r0, (self.from_core, *i))

        elif stage == 2:

            @pl.loop(0, 2 * zcount)
            def _(q):
                h = q // zcount
                i = (s, y * (1 - c) + h * c, h * (1 - c) + x * c, q % zcount)
                add_into(self.a, i, self.r1, (s, h, q % zcount))

        elif stage == 3:

            @pl.loop(0, zcount)
            def _(q):
                add_into(self.a, (s, y, x, q), self.r2, (s, q))

        elif stage == 4:
            total = self.a[s, y, x, z].astype(F32)
            for k in range(zcount - 1):
                total = total + self.r3[s, k].astype(F32)
            if self.spread is None:
                self.target[self.place : self.place + total.shape[0]] = total
            else:
                self.target[y, x, c, z] = total.astype(self.target.dtype)
        if stage < 4:
            self.send(stage, lambda d: d.start())
        elif stage < 8 and self.spread is not None:
            self.spread.start(stage - 4)

    def drain(self):
        if self.drained:
            return
        self.drained = True
        for stage in range(4):
            self.send(stage, lambda d: d.wait_send())
        if self.spread is not None:
            self.spread.drain()


def five(number, shape, dtype, zcount):
    lead = [(2, 2, zcount), (2, 2, zcount), (2, zcount), (zcount,), (zcount - 1,)]
    return [pltpu.VMEM((number, *d, *shape), dtype) for d in lead]


def halved_scratch(count, slots, depth, zcount):
    lone = five(slots, (16, depth), BF16, zcount)
    links = pltpu.SemaphoreType.DMA((count, zcount + 2))
    return [lone[0], *lone[2:], pltpu.SemaphoreType.DMA((count,)), links, links, links, links]


def no_point(k):
    pass


class Exchange:
    def __init__(self, mine, theirs, ssem, rsem):
        self.mine, self.theirs, self.ssem, self.rsem = mine, theirs, ssem, rsem
        self.count = lax.axis_size("seq")
        self.place = lax.axis_index("seq")

    def peer(self, k):
        return (lax.rem(self.place + k, self.count), lax.axis_index("row"))

    def go(self, g, act):
        for k in range(1, self.count):
            act(
                remote(
                    self.mine.at[g],
                    self.theirs.at[g, self.place],
                    self.ssem.at[g, k - 1],
                    self.rsem.at[g, k - 1],
                    self.peer(k),
                )
            )

    def start(self, g):
        self.go(g, lambda d: d.start())

    def entering(self, g, reverse):
        self.go(g, lambda d: d.wait_recv())
        state = jnp.zeros((1, self.mine.shape[-1]), F32)
        for hop in range(self.count - 1):
            source = self.count - 1 - hop if reverse else hop
            ahead = source > self.place if reverse else source < self.place
            reach = self.theirs[g, source, 0:1, :]
            drive = self.theirs[g, source, 1:2, :]
            state = jnp.where(ahead, reach * state + drive, state)
        return state

    def drain(self, groups):
        for g in range(groups):
            self.go(g, lambda d: d.wait_send())


def exchange_scratch(groups, width, count):
    links = pltpu.SemaphoreType.DMA((groups, count - 1))
    return [
        pltpu.VMEM((groups, 8, width), F32),
        pltpu.VMEM((groups, count, 8, width), F32),
        links, links,
    ]


def meet_all(exchange, zcount):
    place, row = exchange.place, lax.axis_index("row")
    everyone = [exchange.peer(k) for k in range(1, exchange.count)]
    everyone += [(place, lax.rem(row + k, zcount)) for k in range(1, zcount)]
    barrier = pltpu.get_barrier_semaphore()
    for peer in everyone:
        pl.semaphore_signal(barrier, inc=1, device_id=peer, device_id_type=pl.DeviceIdType.MESH)
    pl.semaphore_wait(barrier, len(everyone))


def pair_up(pair, blocks):
    half = blocks.shape[1]
    pair[...] = jnp.zeros_like(pair)
    pair[0:half, 0:half] = blocks[0]
    pair[half:, half:] = blocks[1]


def front_kernel(ltiles, tiles, groups, links, *refs):
    (
        long_ref, short_ref, lcot_ref, scot_ref, length_ref, gain_ref, *channel_refs
    ) = refs[:14]
    wd_ref, wo_ref, gain2_ref = refs[14:17]
    refs = refs[17:]
    step = pl.program_id(0)
    point, gather = no_point, None
    zcount = 1
    if links is None:
        pairw, outw, refs = refs[0], refs[1], refs[2:]
    else:
        zcount, chunks, lags, urgent, ready, plan = links
        owns, made = refs[:6], refs[21:24]
        pairw, outw = made[:2]
        gather = Gather(zcount, owns, made, refs[-3:], chunks, lags, urgent, FRONT_DELAY)
        refs = refs[6:21] + refs[24:-3]
        point = in_turn(gather, step, plan)
    gp, inn, dp, ip, st, pr, mix, sin_ref, nm_ref, x_ref, cot_ref, pc_ref = refs[:12]
    resid_ref, n2_ref, mixl_ref = refs[12:15]
    (
        cv_ref, cl_ref, wbuf, pairs, halo, all_pc, mixes, longs, wobuf, isem, wsem, hsem, osem, *swap
    ) = refs[15:]
    exchange = Exchange(*swap)
    lrows = ltiles * TILE
    place = exchange.place

    def load(g):
        return pltpu.make_async_copy(pairw.at[g // 2, g % 2], wbuf.at[g % 2], wsem.at[g % 2])

    @pl.when(step == 0)
    def _():
        srows = short_ref.shape[0]
        copies = [
            pltpu.make_async_copy(source, target, isem.at[k])
            for k, (source, target) in enumerate(
                [
                    (long_ref, x_ref.at[pl.ds(HALO, lrows)]),
                    (short_ref, x_ref.at[pl.ds(HALO + lrows, srows)]),
                    (lcot_ref, cot_ref.at[pl.ds(0, lrows)]),
                    (scot_ref, cot_ref.at[pl.ds(lrows, srows)]),
                ]
            )
        ]
        for copy in copies:
            copy.start()
        meet_all(exchange, zcount)
        ahead = remote(
            long_ref.at[pl.ds(lrows - HALO, HALO)], halo, hsem.at[0], hsem.at[1], exchange.peer(1)
        )
        ahead.start()
        row = 0
        for ref in channel_refs:
            value = ref[...] if len(ref.shape) == 2 else ref[...].reshape(1, ref.shape[0])
            all_pc[row : row + value.shape[0], :] = value
            row += value.shape[0]
        all_pc[row:, :] = jnp.zeros((16 - row, all_pc.shape[1]), F32)
        todo = [] if gather is None else list(range(ready))

        def some(count):
            for t in todo[:count]:
                gather.wave(t)
            del todo[:count]

        some(4)
        for copy in copies:
            copy.wait()

        @pl.loop(0, ltiles)
        def _(i):
            rows = row_iota((TILE, 1)) + (place * lrows + i * TILE)
            keep = jnp.where(rows < length_ref[0], 1.0, 0.0)
            cot_ref[at(i), :] = (cot_ref[at(i), :].astype(F32) * keep).astype(BF16)

        some(1)
        ahead.wait_recv()
        x_ref[0:HALO, :] = halo[...]

        def norm(j):
            v = x_ref[at(j), :].astype(F32)
            s = lax.rsqrt(jnp.mean(v * v, axis=1, keepdims=True) + EPSILON)
            nm_ref[at(j), :] = (v * s * gain_ref[...]).astype(BF16)

        pl.loop(0, tiles // 2)(norm)
        some(1)
        pl.loop(tiles // 2, tiles)(norm)
        some(len(todo))
        ahead.wait_send()
        load(0).start()
        load(1).start()

    @pl.when(step > 0)
    def _():
        for g in range(groups):

            @pl.when(step == g + 1)
            def _(g=g):
                load(g).wait()
                width = pc_ref.shape[1]
                pc_ref[...] = all_pc[:, g * width : (g + 1) * width]

        pair_up(pairs.at[0], wd_ref)
        pair_up(pairs.at[1], wo_ref)
        slot = lax.rem(step - 1, 2)
        share = wbuf.shape[-2] // 2
        front_part(
            ltiles, tiles, point, place, nm_ref, wbuf.at[slot, :, :, 0:share],
            wbuf.at[slot, :, :, share : 2 * share], pairs, pc_ref, gp, inn, dp, ip, st, pr, mix,
            exchange.mine.at[step - 1], cv_ref, cl_ref,
        )
        for g in range(groups):

            @pl.when(step == g + 1)
            def _(g=g):
                if g + 2 < groups:
                    load(g + 2).start()
                exchange.theirs[g, place] = jnp.zeros(exchange.theirs.shape[2:], F32)
                exchange.start(g)

        point(3)

    @pl.when(step > 0)
    def _():
        g = step - 1
        mixes[g] = mix[...]
        for k, ref in enumerate((st, pr, gp)):
            longs[k, g] = ref[HALO : HALO + lrows, :]

    whole_out = pltpu.make_async_copy(outw, wobuf, osem)

    @pl.when(step == groups)
    def _():
        whole_out.start()
        width = gp.shape[1]
        for g in range(groups):
            cols = slice(g * width, (g + 1) * width)
            state = exchange.entering(g, False)
            sin_ref[:, cols] = jnp.broadcast_to(state, (8, width))
            states = longs[0, g] + longs[1, g] * state
            mixl_ref[:, cols] = (states * gelu(longs[2, g])).astype(BF16)
        whole_out.wait()

    point(4)

    @pl.when(step == groups)
    def _():
        width = gp.shape[1]
        for g in range(groups):
            part = flat(wobuf[g // 2, g % 2])
            top = dot_nn(mixl_ref[:, g * width : (g + 1) * width], part)
            low = dot_nn(mixes[g], part)
            if g == 0:
                resid_ref[0:lrows, :] = top
                resid_ref[lrows:, :] = low
            else:
                resid_ref[0:lrows, :] += top
                resid_ref[lrows:, :] += low

    point(5)

    @pl.when(step == groups)
    def _():
        @pl.loop(0, tiles - 1)
        def _(i):
            r = resid_ref[at(i), :] + x_ref[at(1 + i), :].astype(F32)
            resid_ref[at(i), :] = r
            s = lax.rsqrt(jnp.mean(r * r, axis=1, keepdims=True) + EPSILON)
            n2_ref[at(i), :] = (r * s * gain2_ref[...]).astype(BF16)

    point(6)

    @pl.when(step == groups)
    def _():
        exchange.drain(groups)
        if gather is not None:
            gather.drain()


def front_part(
    ltiles, tiles, point, place, nm_ref, wg_ref, wi_ref, pairs, pc_ref, gp_ref, in_ref, dp_ref,
    ip_ref, st_ref, pr_ref, mix_ref, end_ref, cv_ref, cl_ref,
):
    point(0)
    nm = nm_ref[...]
    gp_ref[...] = dot_nt(nm, flat(wg_ref[...])) + pc_ref[GB : GB + 1, :]
    in_ref[...] = dot_nt(nm, flat(wi_ref[...])) + pc_ref[IB : IB + 1, :]
    point(1)
    in_ref[0:HALO, :] = in_ref[0:HALO, :] * jnp.where(place > 0, 1.0, 0.0)
    cl_ref[0:HALO, :] = jnp.zeros((HALO, cl_ref.shape[1]), BF16)

    @pl.loop(1, tiles)
    def _(j):
        live = jnp.where(j == 1 + ltiles, 0.0, 1.0)
        out, _ = conv_tile(in_ref, pc_ref, j, live)
        cv_ref[at(j), :] = out
        cl_ref[at(j), :] = out.astype(BF16)

    point(2)
    low = cl_ref[...]
    dp_ref[...] = dot_nn(low, pairs[0]) + pc_ref[DB : DB + 1, :]
    ip_ref[...] = dot_nn(low, pairs[1]) + pc_ref[OB : OB + 1, :]

    def scanned(j):
        _, opening, a, square = gates(dp_ref[at(j), :], ip_ref[at(j), :], pc_ref[C8 : C8 + 1, :])
        b = (square * lax.rsqrt(square)) * opening * cv_ref[at(j), :]
        return scan_tile(a, b, False)

    width = gp_ref.shape[1]

    def long_step(i, carry):
        state, reach = carry
        a, b = scanned(1 + i)
        s = b + a * state
        r = a * reach
        st_ref[at(1 + i), :] = s
        pr_ref[at(1 + i), :] = r
        return s[TILE - 1 : TILE], r[TILE - 1 : TILE]

    state, reach = lax.fori_loop(
        0, ltiles, long_step, (jnp.zeros((1, width), F32), jnp.ones((1, width), F32))
    )
    end_ref[...] = jnp.concatenate([reach, state, jnp.zeros((6, width), F32)], axis=0)

    def short_step(i, state):
        j = 1 + ltiles + i
        a, b = scanned(j)
        s = b + a * state
        st_ref[at(j), :] = s
        mix_ref[at(i), :] = (s * gelu(gp_ref[at(j), :])).astype(BF16)
        return s[TILE - 1 : TILE]

    lax.fori_loop(0, tiles - 1 - ltiles, short_step, jnp.zeros((1, width), F32))


def mlp_kernel(ltiles, tiles, links, *refs):
    resid_ref, n2_ref, cot_ref, gain_ref, w1_ref, w2_ref = refs[:6]
    refs = refs[6:]
    point, gather = no_point, None
    step = pl.program_id(0)
    last = pl.num_programs(0) - 1
    if links is not None:
        zcount, chunks, lags, plan, sum_chunks, sum_lags, sum_plan = links
        owns = [w2_ref, *refs[:2]]
        refs = refs[2:]
    outl_ref, outs_ref, dres_ref, rlow_ref, gain_grad_ref, dw_hbm = refs[:6]
    refs = refs[6:]
    if links is not None:
        w2_ref, early_ref = refs[:2]
        halved = (refs[-9], None, *refs[-8:-5])
        buffers = [None, None, None, halved]
        scatter = Scatter(zcount, [dw_hbm], [early_ref], buffers, refs[-5:], sum_chunks, sum_lags)
        refs = refs[2:-9]
        gather = Gather(zcount, owns, [w2_ref], refs[-3:], chunks, lags)
        got_ref, sems, credit = refs[-6], refs[-5], refs[-4]
        refs = refs[:-6]
        gather_point = in_turn(gather, step, plan)
        scatter_point = in_turn(scatter, step, sum_plan)

        def point(k):
            gather_point(k)
            scatter_point(k)

    (
        acc_o, acc_n, gu_ref, d_ref, h_ref, dgu_ref, wbuf, dwbuf, wsem, dsem
    ) = refs
    lrows = ltiles * TILE
    hid = h_ref.shape[1]
    half = hid // 2
    share = wbuf.shape[-2]
    rows = 3 * share
    ready = w1_ref.shape[-2] // rows
    steps = ready + w2_ref.shape[-2] // rows

    def load(s):
        source, part = (w1_ref, s) if s < ready else (w2_ref, s - ready)
        return [
            pltpu.make_async_copy(
                source.at[:, :, :, :, pl.ds(part * rows + k * share, share)],
                wbuf.at[s % 2, k],
                wsem.at[s % 2, k],
            )
            for k in range(3)
        ]

    def start_load(s):
        for copy in load(s):
            copy.start()

    def wait_load(s):
        for copy in load(s):
            copy.wait()

    def load_next(s):
        if s + 1 < steps and s + 1 >= min(2, ready):
            start_load(s + 1)

    def each(todo, first=0):
        for s in range(first, steps):

            @pl.when(step == s)
            def _(s=s):
                todo(s)

    if gather is not None:
        y, x, c, z = gather.peers.place

    def store(s):
        mine = dwbuf if gather is None else dwbuf.at[:, :, :, c]
        return pltpu.make_async_copy(mine, dw_hbm.at[s], dsem)

    def swap():
        return remote(
            dwbuf.at[:, :, :, 1 - c], got_ref, sems.at[0], sems.at[1], gather.peers.other
        )

    def settle(s):
        if gather is not None:
            swap().wait_recv()

            @pl.loop(0, SLOTS // 2)
            def _(k):
                i, j, m = k // (2 * GRID[3]), (k // GRID[3]) % 2, k % GRID[3]
                for n in range(3):
                    both = dwbuf[n, i, j, c, m].astype(F32) + got_ref[n, i, j, m].astype(F32)
                    dwbuf[n, i, j, c, m] = both.astype(BF16)

            if s < steps - 1:
                pl.semaphore_signal(
                    credit,
                    inc=1,
                    device_id=gather.peers.other,
                    device_id_type=pl.DeviceIdType.MESH,
                )
        store(s).start()

    def clear(s):
        store(s).wait()
        if gather is not None:
            swap().wait_send()

    @pl.when(step == 0)
    def _():
        for s in range(min(2, ready)):
            start_load(s)
        if gather is not None:
            gather.peers.meet()

    point(0)

    @pl.when(step == 0)
    def _():
        acc_o[...] = resid_ref[...]
        acc_n[...] = jnp.zeros_like(acc_n)

    point(1)

    each(wait_load)
    slot = lax.rem(step, 2)

    def gate_up():
        return flat(wbuf[slot, 0:2])

    def down():
        return flat(wbuf[slot, 2])

    gu_ref[...] = dot_nt(n2_ref[...], gate_up())
    point(2)
    d_ref[...] = dot_nt(cot_ref[...], down())
    each(lambda s: settle(s - 1), 1)
    point(3)

    @pl.loop(0, tiles)
    def _(i):
        for k in range(2):
            cols = slice(k * half, (k + 1) * half)
            more = slice(hid + k * half, hid + (k + 1) * half)
            ge, slope = gelu_pair(gu_ref[at(i), cols])
            u = gu_ref[at(i), more]
            d = d_ref[at(i), cols]
            h_ref[at(i), cols] = (ge * u).astype(BF16)
            dgu_ref[at(i), cols] = (d * u * slope).astype(BF16)
            dgu_ref[at(i), more] = (d * ge).astype(BF16)

    point(4)
    acc_o[...] += dot_nn(h_ref[...], down())
    point(5)
    acc_n[...] += dot_nn(dgu_ref[...], gate_up())
    point(6)
    each(lambda s: clear(s - 1), 1)
    dwbuf[2] = dot_tn(h_ref[...], cot_ref[...]).astype(BF16).reshape(dwbuf.shape[1:])
    point(7)
    each(load_next)
    grad = dot_tn(dgu_ref[...], n2_ref[...]).astype(BF16)
    dwbuf[0:2] = grad.reshape((2,) + dwbuf.shape[1:])

    if gather is not None:
        @pl.when(step > 0)
        def _():
            pl.semaphore_wait(credit, 1)

        swap().start()

    @pl.when(step == last)
    def _():
        def one(i, total):
            r = resid_ref[at(i), :]
            dn = acc_n[at(i), :]
            s = lax.rsqrt(jnp.mean(r * r, axis=1, keepdims=True) + EPSILON)
            e = dn * gain_ref[...]
            inner = jnp.mean(e * r, axis=1, keepdims=True)
            dr = cot_ref[at(i), :].astype(F32) + s * e - r * (s * s * s * inner)
            dres_ref[at(i), :] = dr
            rlow_ref[at(i), :] = dr.astype(BF16)
            return total + fold(dn * (r * s))

        gain_grad_ref[...] = lax.fori_loop(0, tiles, one, jnp.zeros(gain_grad_ref.shape, F32))
        outl_ref[...] = acc_o[0:lrows, :].astype(BF16)
        outs_ref[...] = acc_o[lrows:, :].astype(BF16)
        settle(steps - 1)
        clear(steps - 1)

    point(8)
    if gather is not None:

        @pl.when(step == last)
        def _():
            gather.drain()
            scatter.drain()


def back_part(
    ltiles, tiles, point, rlow_ref, wo_ref, mixl_ref, mixs_ref, gp_ref, st_ref, pr_ref, sin_ref,
    dp_ref, pc_ref, dwo_ref, gl_ref, tot_ref, rch_ref, end_ref, bias_ref, dm_ref, free, nm_ref,
    dwg_ref,
):
    point(0)
    lrows = ltiles * TILE
    width = gp_ref.shape[1]
    rlow = rlow_ref[...]
    dm_ref[...] = dot_nt(rlow, flat(wo_ref[...]))
    free()
    grad = dot_tn(mixl_ref[...], rlow_ref[0:lrows, :]) + dot_tn(mixs_ref[...], rlow_ref[lrows:, :])
    dwo_ref[...] = grad.astype(BF16).reshape(dwo_ref.shape)
    point(1)
    gl_ref[0:HALO, :] = jnp.zeros((HALO, width), BF16)
    last = row_iota((TILE, width)) == TILE - 1

    def local(j, states):
        dm = dm_ref[at(j - 1), :]
        ge, slope = gelu_pair(gp_ref[at(j), :])
        dgate = dm * states * slope
        gl_ref[at(j), :] = dgate.astype(BF16)
        ds = dm * ge
        rate = sigmoid(dp_ref[at(j), :])
        decay = jnp.exp(-pc_ref[C8 : C8 + 1, :] * (0.25 + rate))
        a, b = scan_tile(decay, decay * ds, True)
        return a, b, ds, fold(dgate)

    def short_step(i, carry):
        c, bias = carry
        j = tiles - 1 - i
        a, b, ds, part = local(j, st_ref[at(j), :])
        cs = b + a * c
        tot_ref[at(j), :] = ds + jnp.where(last, c, pltpu.roll(cs, TILE - 1, 0))
        return cs[0:1], bias + part

    _, bias = lax.fori_loop(
        0,
        tiles - 1 - ltiles,
        short_step,
        (jnp.zeros((1, width), F32), jnp.zeros((8, width), F32)),
    )
    point(2)
    s_in = sin_ref[0:1, :]

    def long_step(i, carry):
        c, reach, bias = carry
        j = ltiles - i
        a, b, ds, part = local(j, st_ref[at(j), :] + pr_ref[at(j), :] * s_in)
        cs = b + a * c
        rs = a * reach
        tot_ref[at(j), :] = ds + jnp.where(last, c, pltpu.roll(cs, TILE - 1, 0))
        rch_ref[at(j), :] = jnp.where(last, reach, pltpu.roll(rs, TILE - 1, 0))
        return cs[0:1], rs[0:1], bias + part

    c, reach, bias = lax.fori_loop(
        0, ltiles, long_step, (jnp.zeros((1, width), F32), jnp.ones((1, width), F32), bias)
    )
    end_ref[...] = jnp.concatenate([reach, c, jnp.zeros((6, width), F32)], axis=0)
    bias_ref[...] = bias
    dwg_ref[...] = dot_tn(gl_ref[...], nm_ref[...]).astype(BF16).reshape(dwg_ref.shape)


def last_part(
    ltiles, tiles, groups, point, exchange, residual, x_ref, gain_ref, nm_ref, wg_ref, wi_ref,
    wd_ref, wo_ref, pc_ref, in_ref, dp_ref, ip_ref, st_ref, pr_ref, sin_ref, tot_ref, rch_ref,
    gl_ref, bias_ref, dxl_ref, dxs_ref, halo_ref, behind, pairs, gain_grad_ref, dwi_ref,
    gg_ref, small_ref, acc, dc_ref, cl_ref, dl_ref, ol_ref, il_ref, gain2_ref, free, keep,
):
    width = in_ref.shape[1]
    step = pl.program_id(0) - groups
    point(0)
    for g in range(groups):

        @pl.when(step == g)
        def _(g=g):
            dc_ref[0:1, :] = exchange.entering(g, True)

    c_in = dc_ref[0:1, :]

    @pl.when(step == groups - 1)
    def _():
        for copy in residual:
            copy.start()

    first = jnp.where(exchange.place > 0, 1.0, 0.0)
    pair_up(pairs.at[0], wd_ref)
    pair_up(pairs.at[1], wo_ref)
    zero8 = jnp.zeros((8, width), F32)
    cl_ref[0:HALO, :] = jnp.zeros((HALO, width), BF16)
    dl_ref[0:HALO, :] = jnp.zeros((HALO, width), BF16)
    ol_ref[0:HALO, :] = jnp.zeros((HALO, width), BF16)
    dc_ref[0:HALO, :] = jnp.zeros((HALO, width), F32)

    def gate_step(j, states, total, live, carry):
        before, sum_d, sum_o, sum_p = carry
        rows = row_iota((TILE, width))
        prior = jnp.where(rows == 0, before, pltpu.roll(states, 1, 0))
        conv, _ = conv_tile(in_ref, pc_ref, j, live)
        rate, opening, decay, square = gates(
            dp_ref[at(j), :], ip_ref[at(j), :], pc_ref[C8 : C8 + 1, :]
        )
        inv = lax.rsqrt(square)
        mult = square * inv
        weighted = total * opening
        d_open = total * mult * conv
        d_log = decay * (total * prior - (weighted * conv) * (decay * inv))
        d_rate = -pc_ref[C8 : C8 + 1, :] * d_log
        d_dp = d_rate * (rate - rate * rate)
        d_ip = d_open * (opening - opening * opening)
        cl_ref[at(j), :] = conv.astype(BF16)
        dl_ref[at(j), :] = d_dp.astype(BF16)
        ol_ref[at(j), :] = d_ip.astype(BF16)
        dc_ref[at(j), :] = weighted * mult
        return (
            states[TILE - 1 : TILE],
            sum_d + fold(d_dp),
            sum_o + fold(d_ip),
            sum_p - fold((0.25 + rate) * d_log),
        )

    s_in = sin_ref[0:1, :]

    def long_step(i, carry):
        j = 1 + i
        states = st_ref[at(j), :] + pr_ref[at(j), :] * s_in
        total = tot_ref[at(j), :] + rch_ref[at(j), :] * c_in
        return gate_step(j, states, total, 1.0, carry)

    def short_step(i, carry):
        j = 1 + ltiles + i
        return gate_step(j, st_ref[at(j), :], tot_ref[at(j), :], jnp.where(i == 0, 0.0, 1.0), carry)

    carry = lax.fori_loop(0, ltiles, long_step, (s_in, zero8, zero8, zero8))
    carry = lax.fori_loop(
        0, tiles - 1 - ltiles, short_step, (jnp.zeros((1, width), F32),) + carry[1:]
    )
    _, sum_d, sum_o, sum_p = carry
    point(1)

    low, dlow, olow = cl_ref[...], dl_ref[...], ol_ref[...]
    half = width // 2
    for which, grads in ((0, dlow), (1, olow)):
        product = dot_tn(low, grads).astype(BF16)
        shape = (2, half // 2, half)
        place = (which, step // 2, lax.rem(step, 2))
        gg_ref[(*place, slice(0, 2))] = product[:half, :half].reshape(shape)
        gg_ref[(*place, slice(2, 4))] = product[half:, half:].reshape(shape)
    dc_ref[...] += dot_nt(dlow, pairs[0]) + dot_nt(olow, pairs[1])

    point(2)

    def conv_step(j, carry):
        sum_c, sum_i, sums = carry
        live = jnp.where(j == 1 + ltiles, 0.0, 1.0)
        cur = dc_ref[at(j), :]
        up = jnp.where((j == ltiles) | (j == tiles - 1), 0.0, 1.0)
        later = dc_ref[at(jnp.minimum(j + 1, tiles - 1)), :] * up
        _, moved = conv_tile(in_ref, pc_ref, jnp.maximum(j, 1), live)
        d_in = pc_ref[CW : CW + 1, :] * cur
        for k in range(1, 4):
            d_in = d_in + pc_ref[CW + k : CW + k + 1, :] * shift_up(cur, later, k)
        d_in = d_in * jnp.where(j == 0, first, 1.0)
        il_ref[at(j), :] = d_in.astype(BF16)
        return (
            sum_c + fold(cur),
            sum_i + fold(d_in),
            tuple(s + fold(cur * m) for s, m in zip(sums, moved)),
        )

    sum_c, sum_i, sums = lax.fori_loop(0, tiles, conv_step, (zero8, zero8, (zero8,) * 4))
    parts = [sum_i, *sums, sum_c, sum_d, sum_o, sum_p * pc_ref[S8 : S8 + 1, :], bias_ref[...]]
    rows = [jnp.sum(p, axis=0, keepdims=True) for p in parts]
    block = jnp.concatenate(rows + [jnp.zeros((16 - len(rows), width), F32)], axis=0)
    for i in range(width // 128):
        at_block = step * (width // 128) + i
        x, c, z = at_block // 8, lax.rem(at_block // 4, 2), lax.rem(at_block, 4)
        for h in range(2):
            small_ref[h, x, c, z] = block[8 * h : 8 * h + 8, 128 * i : 128 * i + 128]

    point(3)
    free()
    nm = nm_ref[...]
    dwi_ref[...] = dot_tn(il_ref[...], nm).astype(BF16).reshape(dwi_ref.shape)
    keep()
    point(4)
    part = dot_nn(gl_ref[...], flat(wg_ref[...])) + dot_nn(il_ref[...], flat(wi_ref[...]))

    @pl.when(step == 0)
    def _():
        acc[...] = part

    @pl.when(step > 0)
    def _():
        acc[...] += part

    @pl.when(step == groups - 1)
    def _():
        for copy in residual:
            copy.wait()

        def norm_back(j):
            v = x_ref[at(j), :].astype(F32)
            dn = acc[at(j), :]
            s = lax.rsqrt(jnp.mean(v * v, axis=1, keepdims=True) + EPSILON)
            e = dn * gain_ref[...]
            inner = jnp.mean(e * v, axis=1, keepdims=True)
            return s * e - v * (s * s * s * inner), fold(dn * (v * s))

        halo, total = norm_back(0)
        halo_ref[...] = halo
        behind.start()
        done = 1
        for ref in (dxl_ref, dxs_ref):

            def one(i, total, ref=ref, done=done):
                d, part = norm_back(done + i)
                ref[at(i), :] = ref[at(i), :] + d
                return total + part

            total = lax.fori_loop(0, ref.shape[0] // TILE, one, total)
            done += ref.shape[0] // TILE
        gain_grad_ref[...] = total
        zero = jnp.zeros((8, 128), F32)
        for h in range(2):
            for z in range(4):
                small_ref[h, 1, 1, z] = zero
        for z, ref in enumerate((gain_grad_ref, gain2_ref)):
            total = jnp.sum(ref[...], axis=0, keepdims=True)
            for i in range(8):
                small_ref[0, 1, 1, z, i : i + 1, :] = total[:, 128 * i : 128 * i + 128]

    point(5)


def tail_kernel(ltiles, tiles, groups, links, *refs):
    (
        x_ref, gain_ref, nm_ref, dres_hbm, rlow_ref, w_ref, wg_ref, wi_ref, wd_ref, wo_ref, pc_ref,
        mixl_ref, mixs_ref, gp_ref, in_ref, dp_ref, ip_ref, st_ref, pr_ref, sin_ref, gain2_ref,
    ) = refs[:21]
    refs = refs[21:]
    step = pl.program_id(0)
    group = lax.rem(step, groups)
    back_point, last_point, scatter = no_point, no_point, None
    nscratch = 23
    if links is not None:
        zcount, chunks, lags, plan = links
        halved_ref, early_ref, refs = refs[0], refs[1], refs[2:]
        outs, shares = refs[:8], refs[8:14]
        scratch, pool = refs[14 : 14 + nscratch], refs[14 + nscratch :]
    else:
        outs, scratch = refs[:8], refs[8:]
    dxl_ref, dxs_ref, gain_grad_ref, dwo_hbm, dwg_hbm, dwi_hbm, gates_hbm, sums_hbm = outs
    (
        acc, dc_ref, cl_ref, dl_ref, ol_ref, il_ref, gls, tots, rchs, bias_ref, wst, gsrc, ssrc,
        pairs, halo_out, halo_in, hsem, dsem, wsem, *swap
    ) = scratch
    gates_full, sums_full = gsrc, ssrc
    if links is not None:
        *pool, gates_full, sums_full = pool
        main, gate_pool, sum_pool = pool[0:5], pool[5:10], pool[10:15]
        scatter = Scatter(
            zcount,
            [halved_ref, dwo_hbm, dwg_hbm, dwi_hbm, gsrc, ssrc],
            [*shares, gates_full, sums_full],
            [main, gate_pool, sum_pool, main],
            pool[15:],
            chunks,
            lags,
        )
        back_point = in_turn(scatter, step, plan[:groups])
        last_point = in_turn(scatter, step, plan[groups:], groups)

        @pl.when(step == 0)
        def _():
            rows = early_ref.shape[0] // 3
            for k in range(3):
                shares[k][0:rows, :] = early_ref[k * rows : (k + 1) * rows, :]

    def stash(g, k, target):
        return pltpu.make_async_copy(wst.at[k], target.at[g // 2, g % 2], wsem.at[k])

    def stashed(first, what):
        for g in range(groups):

            @pl.when(step == first + g)
            def _(g=g):
                what(g)

    exchange = Exchange(*swap)
    gl_ref, tot_ref, rch_ref = gls.at[group], tots.at[group], rchs.at[group]
    lrows = ltiles * TILE
    residual = [
        pltpu.make_async_copy(dres_hbm.at[pl.ds(0, lrows)], dxl_ref, dsem.at[0]),
        pltpu.make_async_copy(
            dres_hbm.at[pl.ds(lrows, dxs_ref.shape[0])], dxs_ref, dsem.at[1]
        ),
    ]
    behind = remote(
        halo_out, halo_in, hsem.at[0], hsem.at[1], exchange.peer(exchange.count - 1)
    )
    width = gp_ref.shape[1]

    @pl.when(step == 0)
    def _():
        meet_all(exchange, 1 if scatter is None else zcount)

    def freed(g):
        if g > 0:
            stash(g - 1, 0, dwo_hbm).wait()
            stash(g - 1, 1, dwg_hbm).wait()

    def kept(g):
        stash(g, 0, dwo_hbm).start()
        stash(g, 1, dwg_hbm).start()

    @pl.when(step < groups)
    def _():
        back_part(
            ltiles, tiles, back_point, rlow_ref, w_ref, mixl_ref, mixs_ref, gp_ref, st_ref, pr_ref,
            sin_ref, dp_ref, pc_ref, wst.at[0], gl_ref, tot_ref, rch_ref, exchange.mine.at[group],
            bias_ref.at[group], acc.at[0 : rlow_ref.shape[0], 0:width],
            lambda: stashed(0, freed), nm_ref, wst.at[1],
        )
        stashed(0, kept)
        for g in range(groups):

            @pl.when(step == g)
            def _(g=g):
                exchange.theirs[g, exchange.place] = jnp.zeros(exchange.theirs.shape[2:], F32)
                exchange.start(g)

    @pl.when(step >= groups)
    def _():
        @pl.when(step == groups)
        def _():
            stash(groups - 1, 0, dwo_hbm).wait()
            stash(groups - 1, 1, dwg_hbm).wait()

        def before(g):
            if g > 0:
                stash(g - 1, 2, dwi_hbm).wait()

        def after(g):
            stash(g, 2, dwi_hbm).start()
            if g == groups - 1:
                stash(g, 2, dwi_hbm).wait()

        last_part(
            ltiles, tiles, groups, last_point, exchange, residual, x_ref, gain_ref, nm_ref,
            wg_ref, wi_ref, wd_ref, wo_ref, pc_ref, in_ref, dp_ref, ip_ref, st_ref, pr_ref, sin_ref,
            tot_ref, rch_ref, gl_ref, bias_ref.at[group], dxl_ref, dxs_ref, halo_out, behind, pairs,
            gain_grad_ref, wst.at[2], gsrc, ssrc, acc, dc_ref, cl_ref, dl_ref, ol_ref, il_ref, gain2_ref,
            lambda: stashed(groups, before), lambda: stashed(groups, after),
        )

    @pl.when(step == pl.num_programs(0) - 1)
    def _():
        exchange.drain(groups)
        behind.wait()
        rows = slice(lrows - HALO, lrows)
        dxl_ref[rows, :] = dxl_ref[rows, :] + halo_in[...]
        if scatter is not None:
            scatter.drain()
        final = [
            pltpu.make_async_copy(gates_full, gates_hbm, wsem.at[0]),
            pltpu.make_async_copy(sums_full, sums_hbm, wsem.at[1]),
        ]
        for copy in final:
            copy.start()
        for copy in final:
            copy.wait()


def finish_kernel(number, *refs):
    ins, (gates_ref, sums_ref) = refs[:number], refs[number : number + 2]
    outs = refs[number + 2 : 2 * number + 2]
    gd_ref, go_ref, gain1_ref, gain2_ref, conv_ref, *rows = refs[2 * number + 2 : -number - 3]
    *held, table, sem_in, sem_out = refs[-number - 3 :]
    copies = []
    for k, (a, h, b) in enumerate(zip(ins, held, outs)):
        copies.append(
            (
                pltpu.make_async_copy(a, h, sem_in.at[k]),
                pltpu.make_async_copy(h, b, sem_out.at[k]),
            )
        )
        copies[-1][0].start()
    for come, go in copies:
        come.wait()
        go.start()
    gd_ref[...] = gates_ref[0].astype(F32)
    go_ref[...] = gates_ref[1].astype(F32)
    for h in range(2):
        for k in range(16):
            table[8 * h : 8 * h + 8, 128 * k : 128 * k + 128] = sums_ref[h, k]
    chans = conv_ref.shape[1]
    conv_ref[...] = table[1:5, 0:chans]
    for r, ref in zip((0, 5, 6, 7, 8, 9), rows):
        ref[...] = table[r : r + 1, 0:chans].reshape(chans)
    for k, ref in enumerate((gain1_ref, gain2_ref)):
        for i in range(8):
            table[0:1, 128 * i : 128 * i + 128] = sums_ref[0, 12 + k, i : i + 1, :]
        ref[...] = table[0:1, 0:1024].reshape(1024)
    for _, go in copies:
        go.wait()


def shape_of(shape, dtype):
    return jax.ShapeDtypeStruct(shape, dtype)


def whole(shape):
    return pl.BlockSpec(shape, lambda g: (0,) * len(shape), pipeline_mode=pl.Buffered(1))


def params(limit, **more):
    return pltpu.CompilerParams(
        dimension_semantics=("arbitrary",), vmem_limit_bytes=int(limit * MIB), **more
    )


def to_slots(parts, count):
    rows = parts[0].shape[0]
    depth = parts[0].shape[1]
    got = lax.all_gather(jnp.concatenate(parts, axis=0), ("seq", "row"), axis=0, tiled=False)
    if count != SLOTS:
        got = got.reshape(count, len(parts), rows, depth).transpose(1, 0, 2, 3)
        got = got.reshape(len(parts), SLOTS, rows * count // SLOTS, depth).transpose(1, 0, 2, 3)
    return got.reshape(SLOTS, -1, depth)


def scatter_slots(grads, number, count):
    slots, rows, depth = grads.shape
    if count != SLOTS:
        grads = grads.reshape(slots, number, rows // number, depth).transpose(1, 0, 2, 3)
        grads = grads.reshape(number, count, -1, depth).transpose(1, 0, 2, 3)
    flat_grads = grads.reshape(slots * rows, depth)
    own = lax.psum_scatter(flat_grads, ("seq", "row"), scatter_dimension=0, tiled=True)
    own = own.astype(F32).reshape(number, -1, depth)
    return [own[i] for i in range(number)]


def shards(
    long_tokens,
    short_tokens,
    long_length,
    long_cotangent,
    short_cotangent,
    first_gain,
    gate_weight,
    gate_bias,
    input_weight,
    input_bias,
    conv_weight,
    conv_bias,
    decay_gate_weight,
    decay_gate_bias,
    input_gate_weight,
    input_gate_bias,
    decay_param,
    out_weight,
    second_gain,
    mlp_gate_weight,
    mlp_up_weight,
    mlp_down_weight,
):
    count = lax.axis_size("seq") * lax.axis_size("row")
    lrows, srows, depth = long_tokens.shape[1], short_tokens.shape[1], long_tokens.shape[2]
    chans = gate_bias.shape[0]
    units = mlp_gate_weight.shape[1] * count
    tokens = lrows + srows
    total = HALO + tokens
    ltiles, tiles = lrows // TILE, total // TILE
    cshare, ushare = chans // SLOTS, units // SLOTS
    groups = 4
    width = chans // groups
    per = SLOTS // groups

    zcount = lax.axis_size("row")
    seqs = lax.axis_size("seq")
    fast = seqs == 8 and count == SLOTS
    hbm = pl.BlockSpec(memory_space=pl.ANY)
    one_dma = pltpu.SemaphoreType.DMA
    steps = ushare // 16
    ready_parts = max(1, min(steps - 1, FRONT_PARTS))
    blocks, bwidth = decay_gate_weight.shape[0:2]
    mlp_own = [mlp_gate_weight.T, mlp_up_weight.T, mlp_down_weight]
    channel = [
        gate_bias, input_bias, conv_weight, conv_bias, decay_gate_bias, input_gate_bias,
        8.0 * jax.nn.softplus(decay_param), 8.0 * jax.nn.sigmoid(decay_param),
    ]
    gain1 = first_gain[None]
    gain2 = second_gain[None]

    def early(g):
        return jnp.minimum(g, groups - 1)

    def after_one(g):
        return jnp.maximum(g - 1, 0)

    def late(g):
        return jnp.maximum(g - groups, 0)

    def both_times(g):
        return lax.rem(g, groups)

    def slot_at(when, which=0):
        return pl.BlockSpec((per, cshare, depth), lambda g: (when(g), which, 0))

    def blocks_at(when):
        return pl.BlockSpec((2, bwidth, bwidth), lambda g: (when(g), 0, 0))

    def cols_at(nrows, when):
        return pl.BlockSpec((nrows, width), lambda g: (0, when(g)))

    lags = (2, 2, 3, 2)
    if fast:
        front_own = [gate_weight.T, input_weight.T, out_weight, *mlp_own]
        parts = [(0, 0, cshare, 0, 0), (1, 0, cshare, 0, cshare)]
        urgent = len(row_chunks(parts, 16))
        ready = urgent + sum(lags)
        parts += [(2, 0, cshare, 1, 0)]
        parts += [
            (3 + k, 16 * p, 16, 2, 48 * p + 16 * k) for p in range(ready_parts) for k in range(3)
        ]
        chunks = row_chunks(parts, 16)
        waves = len(chunks) + FRONT_DELAY + sum(lags)
        marks = [[4 * g + k for k in range(4)] for g in range(groups)]
        plan = paced(waves - ready - FRONT_LEFT, 1, marks)
        plan = [[]] + plan
        left = list(range(waves - ready - FRONT_LEFT, waves - ready))
        cut = FRONT_LEFT // 3
        plan[-1] += [left[:cut], left[cut : 2 * cut], left[2 * cut :]]
        plan = [[[ready + t for t in p] for p in row] for row in plan]
        front_links = (zcount, chunks, lags, urgent, ready, plan)
        front_shapes = [
            shape_of(GRID + (n, depth), BF16) for n in (2 * cshare, cshare, 48 * ready_parts)
        ]
        front_scratch = gather_sems(len(chunks), zcount)
    else:
        pairw = to_slots([gate_weight.T, input_weight.T], count)
        outw = to_slots([out_weight], count)
        mlpw = to_slots(mlp_own, count).reshape(GRID + (3, steps, 16, depth))
        mlpw = jnp.swapaxes(mlpw, 4, 5).reshape(GRID + (48 * steps, depth))
        w_first, w_second = jnp.split(mlpw, [48 * ready_parts], axis=4)
        front_own = [w.reshape(GRID + (-1, depth)) for w in (pairw, outw)]
        front_links, front_shapes, front_scratch = None, [], []

    col = cols_at(total, after_one)
    wide = shape_of((total, chans), F32)
    narrow = shape_of((HALO + lrows, chans), F32)
    (
        gp, inner, dp, ip, states, reach, mix_s, s_in, normed, x, cot, chan, residual, normed2,
        mix_l, *made,
    ) = pl.pallas_call(
        functools.partial(front_kernel, ltiles, tiles, groups, front_links),
        grid=(1 + groups,),
        in_specs=[
            hbm, hbm, hbm, hbm, pl.BlockSpec(memory_space=pltpu.SMEM), whole((1, depth)),
            *[whole(c.shape) for c in channel], blocks_at(after_one),
            blocks_at(after_one), whole((1, depth)),
            *[whole(w.shape) if fast else hbm for w in front_own],
        ],
        out_specs=[
            col, col, col, col, col, cols_at(HALO + lrows, after_one), cols_at(srows, after_one),
            whole((8, chans)), whole((total, depth)), whole((total, depth)),
            whole((tokens, depth)), cols_at(16, after_one), whole((tokens, depth)),
            whole((tokens, depth)), whole((lrows, chans)), *[hbm for _ in front_shapes],
        ],
        out_shape=[
            wide, wide, wide, wide, wide, narrow, shape_of((srows, chans), BF16),
            shape_of((8, chans), F32), shape_of((total, depth), BF16),
            shape_of((total, depth), BF16), shape_of((tokens, depth), BF16),
            shape_of((16, chans), F32), shape_of((tokens, depth), F32),
            shape_of((tokens, depth), BF16), shape_of((lrows, chans), BF16), *front_shapes,
        ],
        scratch_shapes=[
            pltpu.VMEM((total, width), F32), pltpu.VMEM((total, width), BF16),
            pltpu.VMEM((2,) + GRID[2:] + (2 * cshare, depth), BF16),
            pltpu.VMEM((2, width, width), BF16), pltpu.VMEM((HALO, depth), BF16),
            pltpu.VMEM((16, chans), F32), pltpu.VMEM((groups, srows, width), BF16),
            pltpu.VMEM((3, groups, lrows, width), F32), pltpu.VMEM(GRID + (cshare, depth), BF16),
            one_dma((4,)), one_dma((2,)), one_dma((2,)), one_dma, *exchange_scratch(groups, width, seqs),
            *front_scratch,
        ],
        compiler_params=params(56, collective_id=0, has_side_effects=True),
        name="front",
    )(
        long_tokens.reshape(lrows, depth), short_tokens.reshape(srows, depth),
        long_cotangent.reshape(lrows, depth), short_cotangent.reshape(srows, depth), long_length,
        gain1, *channel, decay_gate_weight, input_gate_weight, gain2, *front_own,
    )
    if fast:
        pairw, outw, w_first = made
    outw = outw.reshape(SLOTS, -1, depth)
    pairw = pairw.reshape(SLOTS, -1, depth)

    hid = units // steps
    block = (3,) + GRID + (16, depth)
    wbuf = pltpu.VMEM((2,) + block, BF16)
    dwbuf = pltpu.VMEM(block, BF16)
    if fast:
        chunks = [
            (k, 16 * (ready_parts + p), 16, 0, 48 * p + 16 * k)
            for p in range(steps - ready_parts)
            for k in range(3)
        ]
        plan = [[[] for _ in range(8)] for _ in range(steps)]
        todo = list(range(len(chunks) + sum(lags)))
        for s in range(ready_parts - 1, steps - 1):
            due = 3 * (s - ready_parts + 1) + 3 + sum(lags)
            now, todo = [t for t in todo if t < due], [t for t in todo if t >= due]
            first = 0 if s == ready_parts - 1 else s
            spots = [(q, k) for q in range(first, s + 1) for k in range(8)]
            for n, t in enumerate(now):
                lead = min(MLP_AHEAD, len(now) - 1) if first == 0 else 0
                share = max(0, n - lead) / max(1, len(now) - lead)
                q, k = spots[int(share * len(spots))]
                plan[q][k].append(t)
        soon = [(p, k) for p in range(EARLY_PARTS) for k in range(3)]
        early_chunks = [
            (HALVED, n, 0, (p, k), (0, 16), 0, 16 * (k * EARLY_PARTS + p))
            for n, (p, k) in enumerate(soon)
        ]
        early_lags = (1, 2, 2, 2)
        early_plan = [[[] for _ in range(9)] for _ in range(steps)]
        spot = 0
        for t in range(len(soon) + sum(early_lags)):
            after = 8 * (t // 3 + 1) + 7 if t < len(soon) else 0
            spot = max(after, spot + EARLY_GAP)
            q, k = divmod(min(spot, 8 * steps), 8)
            q, k = (q, k) if q < steps else (steps - 1, 8)
            early_plan[q][k].append(t)
        mlp_links = (zcount, chunks, lags, plan, early_chunks, early_lags, early_plan)
        w_last, more_specs = mlp_own, [hbm, whole((16 * len(soon), depth))]
        more_shapes = [
            shape_of(GRID + (48 * (steps - ready_parts), depth), BF16),
            shape_of((16 * len(soon), depth), F32),
        ]
        half_block = block[:3] + block[4:]
        more_scratch = [
            pltpu.VMEM(half_block, BF16), one_dma((2,)), pltpu.SemaphoreType.REGULAR,
            *gather_sems(len(chunks), zcount), *halved_scratch(len(soon), len(soon), depth, zcount),
        ]
        dw_shape = (steps,) + half_block
        more_params = dict(collective_id=3, has_side_effects=True)
    else:
        mlp_links, w_last, more_specs, more_shapes, more_scratch = None, [w_second], [], [], []
        dw_shape, more_params = (steps,) + block, {}
    out_l, out_s, d_res, rlow, gain2_grad, dmlp, *more_out = pl.pallas_call(
        functools.partial(mlp_kernel, ltiles, tokens // TILE, mlp_links),
        grid=(steps,),
        in_specs=[
            whole((tokens, depth)), whole((tokens, depth)), whole((tokens, depth)),
            whole((1, depth)), hbm,
            *[whole(w.shape) if fast else hbm for w in w_last],
        ],
        out_specs=[
            whole((lrows, depth)), whole((srows, depth)), whole((tokens, depth)), whole((tokens, depth)),
            whole((8, depth)), hbm, *more_specs,
        ],
        out_shape=[
            shape_of((lrows, depth), BF16), shape_of((srows, depth), BF16),
            shape_of((tokens, depth), F32), shape_of((tokens, depth), BF16),
            shape_of((8, depth), F32), shape_of(dw_shape, BF16), *more_shapes,
        ],
        scratch_shapes=[
            pltpu.VMEM((tokens, depth), F32), pltpu.VMEM((tokens, depth), F32),
            pltpu.VMEM((tokens, 2 * hid), F32),
            pltpu.VMEM((tokens, hid), F32), pltpu.VMEM((tokens, hid), BF16),
            pltpu.VMEM((tokens, 2 * hid), BF16), wbuf, dwbuf, one_dma((2, 3)), one_dma, *more_scratch,
        ],
        compiler_params=params(62, **more_params),
        name="mlp",
    )(residual, normed2, cot, gain2, w_first, *w_last)

    gate_shape, sum_shape = GRID + (bwidth // 2, bwidth), GRID + (8, 128)
    grads_shape = shape_of(GRID + (cshare, depth), BF16)
    tail_links, tail_in, tail_specs, tail_shapes, tail_scratch = None, [], [], [], []
    if fast:
        size = 16
        tail_chunks = []
        number = 0
        for p in range(EARLY_PARTS, steps):
            for k in range(3):
                tail_chunks.append(
                    (HALVED, number % TAIL_SLOTS, 0, (p, k), (0, size), k, 16 * p)
                )
                number += 1
        for which in (1, 2, 3):
            if which == 3:
                tail_chunks.append((SUMS, 0, 5, None, (0, 8), 7, 0))
                tail_chunks.append((GATES, 0, 4, None, (0, bwidth // 2), 6, 0))
                during = len(tail_chunks) - 2
            for start in range(0, cshare, size):
                tail_chunks.append(
                    (CORE, number % TAIL_SLOTS, which, None, (start, size), 2 + which, start)
                )
                number += 1
        tail_lags = (1, 3, 3, 3, 1, 1, 1, 1)
        marks = [[6.0 * g + t for t in (0.0, 1.5, 4.0)] for g in range(groups)]
        marks += [
            [6.0 * groups + 11.5 * g + t for t in (0.0, 5.0, 6.0, 9.0, 9.5, 11.5)] for g in range(groups)
        ]
        plan = paced(during, 3, marks)
        plan[-1][-1] += range(during, len(tail_chunks) + sum(tail_lags) + 1)
        tail_links = (zcount, tail_chunks, tail_lags, plan)
        early_sums = more_out[1]
        tail_in, tail_specs = [dmlp, early_sums], [whole((ushare, depth))] * 3 + [whole((cshare, depth))] * 3
        tail_shapes = [shape_of((ushare, depth), F32)] * 3 + [shape_of((cshare, depth), F32)] * 3
        lone = five(TAIL_SLOTS, (size, depth), BF16, zcount)
        lone[1] = five(CORE_SLOTS, (size, depth), BF16, zcount)[1]
        n = len(tail_chunks)
        links = one_dma((n, zcount + 2))
        tail_scratch = [
            *lone,
            *five(1, gate_shape[4:], BF16, zcount),
            *five(1, sum_shape[4:], F32, zcount),
            one_dma((n,)), links, links, links, links,
            pltpu.VMEM(gate_shape, BF16), pltpu.VMEM(sum_shape, F32),
        ]
    dx_l, dx_s, _, d_out, d_gate, d_input, gate_sums, sums, *shares = pl.pallas_call(
        functools.partial(tail_kernel, ltiles, tiles, groups, tail_links),
        grid=(2 * groups,),
        in_specs=[
            whole((total, depth)), whole((1, depth)), whole((total, depth)), hbm,
            whole((tokens, depth)), slot_at(early), slot_at(late, 0), slot_at(late, 1),
            blocks_at(late), blocks_at(late), cols_at(16, both_times), cols_at(lrows, early),
            cols_at(srows, early), cols_at(total, early), cols_at(total, late),
            cols_at(total, both_times), cols_at(total, late), cols_at(total, both_times),
            cols_at(HALO + lrows, both_times), cols_at(8, both_times), whole((8, depth)),
            *([hbm, whole(early_sums.shape)] if fast else []),
        ],
        out_specs=[
            whole((lrows, depth)), whole((srows, depth)), whole((8, depth)), hbm, hbm, hbm, hbm, hbm,
            *tail_specs,
        ],
        out_shape=[
            shape_of((lrows, depth), F32), shape_of((srows, depth), F32), shape_of((8, depth), F32),
            grads_shape, grads_shape, grads_shape, shape_of(gate_shape, BF16),
            shape_of(sum_shape, F32), *tail_shapes,
        ],
        scratch_shapes=[
            pltpu.VMEM((total, depth), F32), pltpu.VMEM((total, width), F32),
            pltpu.VMEM((total, width), BF16), pltpu.VMEM((total, width), BF16),
            pltpu.VMEM((total, width), BF16), pltpu.VMEM((total, width), BF16),
            pltpu.VMEM((groups, total, width), BF16), pltpu.VMEM((groups, total, width), F32),
            pltpu.VMEM((groups, HALO + lrows, width), F32), pltpu.VMEM((groups, 8, width), F32),
            pltpu.VMEM((3,) + GRID[2:] + (cshare, depth), BF16), pltpu.VMEM(gate_shape, BF16),
            pltpu.VMEM(sum_shape, F32), pltpu.VMEM((2, width, width), BF16),
            pltpu.VMEM((HALO, depth), F32), pltpu.VMEM((HALO, depth), F32), one_dma((2,)),
            one_dma((2,)), one_dma((3,)), *exchange_scratch(groups, width, seqs), *tail_scratch,
        ],
        compiler_params=params(63, collective_id=4, has_side_effects=True),
        name="tail",
    )(
        x, gain1, normed, d_res, rlow, outw, pairw, pairw, decay_gate_weight, input_gate_weight, chan,
        mix_l, mix_s, gp, inner, dp, ip, states, reach, s_in, gain2_grad, *tail_in,
    )

    if fast:
        g_mgate, g_mup, g_down, g_out, g_gate, g_input = shares
    else:
        dmlp = dmlp.reshape(steps, 3, SLOTS, -1, depth).transpose(2, 1, 0, 3, 4)
        g_mgate, g_mup, g_down = scatter_slots(dmlp.reshape(SLOTS, -1, depth), 3, count)
        dmix = jnp.concatenate([d_gate, d_input, d_out], axis=4).reshape(SLOTS, -1, depth)
        g_gate, g_input, g_out = scatter_slots(dmix, 3, count)
        gate_sums, sums = lax.psum((gate_sums.astype(F32), sums), ("seq", "row"))
    large = [out_l, out_s, dx_l, dx_s, g_gate, g_input, g_out, g_mgate, g_mup, g_down]
    vector = shape_of((chans,), F32)
    gate_grad = shape_of((blocks, bwidth, bwidth), F32)
    gain_grad = shape_of((depth,), F32)
    vmem = pl.BlockSpec(memory_space=pltpu.VMEM)
    (
        out_l, out_s, dx_l, dx_s, g_gate, g_input, g_out, g_mgate, g_mup, g_down, decay_grad,
        open_grad, gain1_grad, gain2_grad, conv_grad, input_bias_grad, conv_bias_grad,
        decay_bias_grad, open_bias_grad, param_grad, gate_bias_grad,
    ) = pl.pallas_call(
        functools.partial(finish_kernel, len(large)),
        in_specs=[hbm] * len(large) + [vmem, vmem],
        out_specs=[hbm] * len(large) + [vmem] * 11,
        out_shape=[shape_of(a.shape, a.dtype) for a in large]
        + [gate_grad, gate_grad, gain_grad, gain_grad, shape_of(conv_weight.shape, F32)]
        + [vector] * 6,
        scratch_shapes=[
            *[pltpu.VMEM(a.shape, a.dtype) for a in large], pltpu.VMEM((16, 2048), F32),
            one_dma((len(large),)), one_dma((len(large),)),
        ],
        compiler_params=pltpu.CompilerParams(vmem_limit_bytes=62 * MIB),
        name="finish",
    )(*large, gate_sums.reshape(2, blocks, bwidth, bwidth), sums.reshape(2, 16, 8, 128))
    return (
        out_l.reshape(long_tokens.shape),
        out_s.reshape(short_tokens.shape),
        dx_l.reshape(long_tokens.shape),
        dx_s.reshape(short_tokens.shape),
        gain1_grad,
        g_gate.T,
        gate_bias_grad,
        g_input.T,
        input_bias_grad,
        conv_grad,
        conv_bias_grad,
        decay_grad,
        decay_bias_grad,
        open_grad,
        open_bias_grad,
        param_grad,
        g_out,
        gain2_grad,
        g_mgate.T,
        g_mup.T,
        g_down,
    )


def solution(mesh):
    both = ("seq", "row")
    long_spec = P("row", "seq", None)
    short_spec = P(both, None, None)
    cols = P(None, both)
    rows = P(both, None)
    return jax.shard_map(
        shards,
        mesh=mesh,
        in_specs=(
            long_spec, short_spec, P("row"), long_spec, short_spec, P(), cols, P(), cols, P(),
            P(), P(), P(), P(), P(), P(), P(), rows, P(), cols, cols, rows,
        ),
        out_specs=(
            long_spec, short_spec, long_spec, short_spec, P(), cols, P(), cols, P(), P(), P(),
            P(), P(), P(), P(), P(), rows, P(), cols, cols, rows,
        ),
        check_vma=False,
    )
```

```python
import functools

import jax
import jax.numpy as jnp
from jax import lax
from jax.experimental import pallas as pl
from jax.experimental.pallas import tpu as pltpu
from jax.sharding import PartitionSpec as P

EPSILON = 1e-06
F32 = jnp.float32
BF16 = jnp.bfloat16
GRID = (2, 2, 2, 4)
SLOTS = 32
TILE = 16
HALO = 16
MIB = 1024 * 1024
MLP_AHEAD = 1
EARLY_PARTS = 2
EARLY_GAP = 3
FRONT_LEFT = 9
FRONT_DELAY = 3
FRONT_PARTS = 3
TAIL_SLOTS = 11
CORE_SLOTS = 5
GELU_A = 0.7978845608028654
GELU_B = 0.044715


def dot_nn(a, b):
    return lax.dot_general(a, b, (((1,), (0,)), ((), ())), preferred_element_type=F32)


def dot_nt(a, b):
    return lax.dot_general(a, b, (((1,), (1,)), ((), ())), preferred_element_type=F32)


def dot_tn(a, b):
    return lax.dot_general(a, b, (((0,), (0,)), ((), ())), preferred_element_type=F32)


def sigmoid(v):
    return 0.5 * jnp.tanh(0.5 * v) + 0.5


def gelu(v):
    t = jnp.tanh(v * (GELU_A + (GELU_A * GELU_B) * (v * v)))
    h = 0.5 * v
    return h + h * t


def gelu_pair(v):
    w = v * v
    t = jnp.tanh(v * (GELU_A + (GELU_A * GELU_B) * w))
    h = 0.5 * v
    slope = 0.5 + 0.5 * t + (h - h * (t * t)) * (GELU_A + (3.0 * GELU_A * GELU_B) * w)
    return h + h * t, slope


def row_iota(shape):
    return lax.broadcasted_iota(jnp.int32, shape, 0)


def at(j):
    return pl.ds(pl.multiple_of(j * TILE, TILE), TILE)


def scan_tile(a, b, reverse):
    rows = row_iota(a.shape)
    step = 1
    while step < TILE:
        if reverse:
            keep, shift = rows < TILE - step, TILE - step
        else:
            keep, shift = rows >= step, step
        b = jnp.where(keep, a * pltpu.roll(b, shift, 0) + b, b)
        a = jnp.where(keep, a * pltpu.roll(a, shift, 0), a)
        step *= 2
    return a, b


def shift_down(cur, prev, k):
    if k == 0:
        return cur
    rows = row_iota(cur.shape)
    return jnp.where(rows < k, pltpu.roll(prev, k, 0), pltpu.roll(cur, k, 0))


def shift_up(cur, later, k):
    if k == 0:
        return cur
    rows = row_iota(cur.shape)
    return jnp.where(
        rows >= TILE - k, pltpu.roll(later, TILE - k, 0), pltpu.roll(cur, TILE - k, 0)
    )


def fold(v):
    return v[0:8] + v[8:16]


def flat(block):
    return block.reshape(-1, block.shape[-1])


def gates(dp, ip, c8):
    rate = sigmoid(dp)
    opening = sigmoid(ip)
    log_decay = -c8 * (0.25 + rate)
    decay = jnp.exp(log_decay)
    square = -jnp.tanh(log_decay) * (1.0 + decay * decay)
    return rate, opening, decay, square


GB, IB, CW, CB, DB, OB, C8, S8 = 0, 1, 2, 6, 7, 8, 9, 10


def conv_tile(in_ref, pc_ref, j, live):
    cur = in_ref[at(j), :]
    prev = in_ref[at(j - 1), :] * live
    out = pc_ref[CB : CB + 1, :] + pc_ref[CW : CW + 1, :] * cur
    moved = [cur]
    for k in range(1, 4):
        m = shift_down(cur, prev, k)
        moved.append(m)
        out = out + pc_ref[CW + k : CW + k + 1, :] * m
    return out, moved


def place_of():
    s = lax.axis_index("seq")
    return s // 4, (s // 2) % 2, s % 2, lax.axis_index("row")


def device_at(y, x, c, z):
    return ((y * 2 + x) * 2 + c, z)


class Peers:
    def __init__(self, zcount):
        y, x, c, z = self.place = place_of()
        self.far = [(z + k) % zcount for k in range(1, zcount)]
        self.along = [device_at(y, x, c, q) for q in self.far]
        self.near = ((y + c) % 2, (x + 1 - c) % 2)
        self.first = device_at(*self.near, c, z)
        self.second = device_at((y + 1 - c) % 2, (x + c) % 2, c, z)
        self.other = device_at(y, x, 1 - c, z)

    def meet(self):
        everyone = [*self.along, self.first, self.second, self.other]
        barrier = pltpu.get_barrier_semaphore()
        for peer in everyone:
            pl.semaphore_signal(
                barrier, inc=1, device_id=peer, device_id_type=pl.DeviceIdType.MESH
            )
        pl.semaphore_wait(barrier, len(everyone))


def remote(source, target, send, recv, device):
    return pltpu.make_async_remote_copy(
        src_ref=source,
        dst_ref=target,
        send_sem=send,
        recv_sem=recv,
        device_id=device,
        device_id_type=pl.DeviceIdType.MESH,
    )


class Spread:
    def __init__(self, peers, own, full, send, recv):
        self.peers, self.own, self.full, self.send, self.recv = peers, own, full, send, recv

    def go(self, stage, act):
        y, x, c, z = self.peers.place
        p, full = self.peers, self.full
        if stage == 0:
            for k, device in enumerate(p.along):
                act(remote(self.own, full(y, x, c, z), self.send(k), self.recv(k), device))
            return
        k = len(p.along) + stage - 1
        if stage == 2:

            @pl.when(c == 0)
            def _():
                part = full(y, slice(None), c, slice(None))
                act(remote(part, part, self.send(k), self.recv(k), p.second))

            @pl.when(c == 1)
            def _():
                part = full(slice(None), x, c, slice(None))
                act(remote(part, part, self.send(k), self.recv(k), p.second))

            return
        if stage == 1:
            part, device = full(y, x, c, slice(None)), p.first
        else:
            part, device = full(slice(None), slice(None), c, slice(None)), p.other
        act(remote(part, part, self.send(k), self.recv(k), device))

    def start(self, stage):
        self.go(stage, lambda d: d.start())

    def arrive(self, stage):
        self.go(stage, lambda d: d.wait_recv())

    def drain(self):
        for stage in range(4):
            self.go(stage, lambda d: d.wait_send())


def wave_of(t, count, lags, urgent=None, delay=0):
    urgent = count if urgent is None else urgent
    for stage in range(len(lags), -1, -1):
        piece = t - sum(lags[:stage])
        if 0 <= piece < urgent:
            yield piece, stage
        elif urgent <= piece - delay < count:
            yield piece - delay, stage


class Gather:
    def __init__(self, zcount, ins, outs, sems, chunks, lags, urgent=None, delay=0):
        self.order = (len(chunks), lags, urgent, delay)
        self.csem, self.ssem, self.rsem = sems
        self.peers = Peers(zcount)
        y, x, c, z = self.peers.place
        self.spreads, self.copies = [], []
        for i, (which, start, size, target, offset) in enumerate(chunks):
            own = ins[which].at[pl.ds(start, size)]
            rows = pl.ds(offset, size)

            def full(a, b, d, e, ref=outs[target], rows=rows):
                return ref.at[a, b, d, e, rows]

            def send(k, i=i):
                return self.ssem.at[i, k]

            def recv(k, i=i):
                return self.rsem.at[i, k]

            self.spreads.append(Spread(self.peers, own, full, send, recv))
            self.copies.append(pltpu.make_async_copy(own, full(y, x, c, z), self.csem.at[i]))

    def wave(self, t):
        for i, stage in wave_of(t, *self.order):
            if stage == 0:
                self.copies[i].start()
            elif stage == 1:
                self.copies[i].wait()
            if stage > 0:
                self.spreads[i].arrive(stage - 1)
            if stage < 4:
                self.spreads[i].start(stage)

    def drain(self):
        for spread in self.spreads:
            spread.drain()


def in_turn(weave, step, plan, first=0):
    def point(k):
        for s, points in enumerate(plan, first):
            if k < len(points) and points[k]:

                @pl.when(step == s)
                def _(todo=points[k]):
                    for t in todo:
                        weave.wave(t)

    return point


def spread_out(waves, ahead, steps, points):
    todo = list(range(waves))
    plan = []
    for s in range(steps):
        row = []
        for k in range(points):
            take = ahead if s == 0 and k == 0 else 1
            if s == steps - 1 and k == points - 1:
                take = len(todo)
            row.append(todo[:take])
            todo = todo[take:]
        plan.append(row)
    return plan


def paced(waves, ahead, marks):
    last = marks[-1][-1]
    plan = [[[] for _ in row] for row in marks]
    spots = [(t, s, k) for s, row in enumerate(marks) for k, t in enumerate(row)]
    for w in range(waves):
        due = last * max(0, w - ahead) / max(1, waves - ahead)
        _, s, k = next(spot for spot in spots if spot[0] >= due)
        plan[s][k].append(w)
    return plan


def row_chunks(parts, size):
    return [
        (which, start + i, size, target, offset + i)
        for which, start, count, target, offset in parts
        for i in range(0, count, size)
    ]


def gather_sems(count, zcount):
    links = pltpu.SemaphoreType.DMA((count, zcount + 2))
    return [pltpu.SemaphoreType.DMA((count,)), links, links]


CORE, GATES, SUMS, HALVED = 0, 1, 2, 3


class Scatter:
    def __init__(self, zcount, ins, outs, buffers, sems, chunks, lags):
        self.peers = Peers(zcount)
        self.zcount, self.chunks, self.lags = zcount, chunks, lags
        self.ins, self.outs, self.buffers = ins, outs, buffers
        self.csem, self.ssem, self.rsem = sems[:3]
        self.pieces = [Piece(self, i, sems[3:], *chunk) for i, chunk in enumerate(chunks)]
        self.waves = len(chunks) + sum(lags) + 1

    def wave(self, t):
        for i, stage in wave_of(t, len(self.pieces), self.lags):
            if stage <= 4 or self.pieces[i].spread is not None:
                self.pieces[i].step(stage)

    def drain(self):
        for piece in self.pieces:
            piece.drain()


def slot_of_core(i, slots):
    return i % slots


def add_into(into, i, part, j):
    into[i] = into[i] + part[j]


class Piece:
    def __init__(self, owner, i, sems, kind, slot, which, source, span, target, place):
        self.o, self.i, self.kind, self.slot = owner, i, kind, slot
        self.a, self.r0, self.r1, self.r2, self.r3 = owner.buffers[kind]
        self.from_core = 0 if self.r0 is None else slot_of_core(i, self.r0.shape[0])
        self.source, self.lead, self.rows = owner.ins[which], source, pl.ds(*span)
        self.target, self.place = owner.outs[target], place
        self.spread, self.drained = None, False
        if kind in (GATES, SUMS):
            y, x, c, z = owner.peers.place

            def full(*at_place):
                return self.target.at[at_place]

            def send(k):
                return sems[0].at[i, k]

            def recv(k):
                return sems[1].at[i, k]

            self.spread = Spread(owner.peers, full(y, x, c, z), full, send, recv)

    def local(self):
        c = self.o.peers.place[2]
        if self.kind == HALVED:
            mine = self.source.at[self.lead]
        else:
            mine = self.source.at[:, :, c, :, self.rows]
        return pltpu.make_async_copy(mine, self.a.at[self.slot], self.o.csem.at[self.i])

    def send(self, stage, act):
        s, peers = self.slot, self.o.peers
        y, x, c, z = peers.place

        def go(source, target, k, device):
            act(remote(source, target, self.o.ssem.at[self.i, k], self.o.rsem.at[self.i, k], device))

        if stage == 0:
            if self.kind != HALVED:
                theirs = self.source.at[:, :, 1 - c, :, self.rows]
                go(theirs, self.r0.at[self.from_core], 0, peers.other)
        elif stage == 1:

            @pl.when(c == 0)
            def _():
                go(self.a.at[s, 1 - y], self.r1.at[s], 1, peers.second)

            @pl.when(c == 1)
            def _():
                go(self.a.at[s, :, 1 - x], self.r1.at[s], 1, peers.second)

        elif stage == 2:
            go(self.a.at[(s, *peers.near)], self.r2.at[s], 2, peers.first)
        else:
            for k, device in enumerate(peers.along):
                go(self.a.at[s, y, x, peers.far[k]], self.r3.at[s, k], 3 + k, device)

    def step(self, stage):
        s, zcount = self.slot, self.o.zcount
        y, x, c, z = self.o.peers.place
        if stage == 0:
            for earlier in self.o.pieces[: self.i]:
                if earlier.a is self.a and earlier.slot == s:
                    earlier.drain()
            self.local().start()
        elif stage <= 4:
            self.send(stage - 1, lambda d: d.wait_recv())
        else:
            self.spread.arrive(stage - 5)
        if stage == 1:
            self.local().wait()
            if self.kind != HALVED:

                @pl.loop(0, 4 * zcount)
                def _(q):
                    i = (q // (2 * zcount), (q // zcount) % 2, q % zcount)
                    add_into(self.a, (s, *i), self.r0, (self.from_core, *i))

        elif stage == 2:

            @pl.loop(0, 2 * zcount)
            def _(q):
                h = q // zcount
                i = (s, y * (1 - c) + h * c, h * (1 - c) + x * c, q % zcount)
                add_into(self.a, i, self.r1, (s, h, q % zcount))

        elif stage == 3:

            @pl.loop(0, zcount)
            def _(q):
                add_into(self.a, (s, y, x, q), self.r2, (s, q))

        elif stage == 4:
            total = self.a[s, y, x, z].astype(F32)
            for k in range(zcount - 1):
                total = total + self.r3[s, k].astype(F32)
            if self.spread is None:
                self.target[self.place : self.place + total.shape[0]] = total
            else:
                self.target[y, x, c, z] = total.astype(self.target.dtype)
        if stage < 4:
            self.send(stage, lambda d: d.start())
        elif stage < 8 and self.spread is not None:
            self.spread.start(stage - 4)

    def drain(self):
        if self.drained:
            return
        self.drained = True
        for stage in range(4):
            self.send(stage, lambda d: d.wait_send())
        if self.spread is not None:
            self.spread.drain()


def five(number, shape, dtype, zcount):
    lead = [(2, 2, zcount), (2, 2, zcount), (2, zcount), (zcount,), (zcount - 1,)]
    return [pltpu.VMEM((number, *d, *shape), dtype) for d in lead]


def halved_scratch(count, slots, depth, zcount):
    lone = five(slots, (16, depth), BF16, zcount)
    links = pltpu.SemaphoreType.DMA((count, zcount + 2))
    return [lone[0], *lone[2:], pltpu.SemaphoreType.DMA((count,)), links, links, links, links]


def no_point(k):
    pass


class Exchange:
    def __init__(self, mine, theirs, ssem, rsem):
        self.mine, self.theirs, self.ssem, self.rsem = mine, theirs, ssem, rsem
        self.count = lax.axis_size("seq")
        self.place = lax.axis_index("seq")

    def peer(self, k):
        return (lax.rem(self.place + k, self.count), lax.axis_index("row"))

    def go(self, g, act):
        for k in range(1, self.count):
            act(
                remote(
                    self.mine.at[g],
                    self.theirs.at[g, self.place],
                    self.ssem.at[g, k - 1],
                    self.rsem.at[g, k - 1],
                    self.peer(k),
                )
            )

    def start(self, g):
        self.go(g, lambda d: d.start())

    def entering(self, g, reverse):
        self.go(g, lambda d: d.wait_recv())
        state = jnp.zeros((1, self.mine.shape[-1]), F32)
        for hop in range(self.count - 1):
            source = self.count - 1 - hop if reverse else hop
            ahead = source > self.place if reverse else source < self.place
            reach = self.theirs[g, source, 0:1, :]
            drive = self.theirs[g, source, 1:2, :]
            state = jnp.where(ahead, reach * state + drive, state)
        return state

    def drain(self, groups):
        for g in range(groups):
            self.go(g, lambda d: d.wait_send())


def exchange_scratch(groups, width, count):
    links = pltpu.SemaphoreType.DMA((groups, count - 1))
    return [
        pltpu.VMEM((groups, 8, width), F32),
        pltpu.VMEM((groups, count, 8, width), F32),
        links, links,
    ]


def meet_all(exchange, zcount):
    place, row = exchange.place, lax.axis_index("row")
    everyone = [exchange.peer(k) for k in range(1, exchange.count)]
    everyone += [(place, lax.rem(row + k, zcount)) for k in range(1, zcount)]
    barrier = pltpu.get_barrier_semaphore()
    for peer in everyone:
        pl.semaphore_signal(barrier, inc=1, device_id=peer, device_id_type=pl.DeviceIdType.MESH)
    pl.semaphore_wait(barrier, len(everyone))


def pair_up(pair, blocks):
    half = blocks.shape[1]
    pair[...] = jnp.zeros_like(pair)
    pair[0:half, 0:half] = blocks[0]
    pair[half:, half:] = blocks[1]


def front_kernel(ltiles, tiles, groups, links, *refs):
    (
        long_ref, short_ref, lcot_ref, scot_ref, length_ref, gain_ref, *channel_refs
    ) = refs[:14]
    wd_ref, wo_ref, gain2_ref = refs[14:17]
    refs = refs[17:]
    step = pl.program_id(0)
    point, gather = no_point, None
    zcount = 1
    if links is None:
        pairw, outw, refs = refs[0], refs[1], refs[2:]
    else:
        zcount, chunks, lags, urgent, ready, plan = links
        owns, made = refs[:6], refs[21:24]
        pairw, outw = made[:2]
        gather = Gather(zcount, owns, made, refs[-3:], chunks, lags, urgent, FRONT_DELAY)
        refs = refs[6:21] + refs[24:-3]
        point = in_turn(gather, step, plan)
    gp, inn, dp, ip, st, pr, mix, sin_ref, nm_ref, x_ref, cot_ref, pc_ref = refs[:12]
    resid_ref, n2_ref, mixl_ref = refs[12:15]
    (
        cv_ref, cl_ref, wbuf, pairs, halo, all_pc, mixes, longs, wobuf, isem, wsem, hsem, osem, *swap
    ) = refs[15:]
    exchange = Exchange(*swap)
    lrows = ltiles * TILE
    place = exchange.place

    def load(g):
        return pltpu.make_async_copy(pairw.at[g // 2, g % 2], wbuf.at[g % 2], wsem.at[g % 2])

    @pl.when(step == 0)
    def _():
        srows = short_ref.shape[0]
        copies = [
            pltpu.make_async_copy(source, target, isem.at[k])
            for k, (source, target) in enumerate(
                [
                    (long_ref, x_ref.at[pl.ds(HALO, lrows)]),
                    (short_ref, x_ref.at[pl.ds(HALO + lrows, srows)]),
                    (lcot_ref, cot_ref.at[pl.ds(0, lrows)]),
                    (scot_ref, cot_ref.at[pl.ds(lrows, srows)]),
                ]
            )
        ]
        for copy in copies:
            copy.start()
        meet_all(exchange, zcount)
        ahead = remote(
            long_ref.at[pl.ds(lrows - HALO, HALO)], halo, hsem.at[0], hsem.at[1], exchange.peer(1)
        )
        ahead.start()
        row = 0
        for ref in channel_refs:
            value = ref[...] if len(ref.shape) == 2 else ref[...].reshape(1, ref.shape[0])
            all_pc[row : row + value.shape[0], :] = value
            row += value.shape[0]
        all_pc[row:, :] = jnp.zeros((16 - row, all_pc.shape[1]), F32)
        todo = [] if gather is None else list(range(ready))

        def some(count):
            for t in todo[:count]:
                gather.wave(t)
            del todo[:count]

        some(4)
        for copy in copies:
            copy.wait()

        @pl.loop(0, ltiles)
        def _(i):
            rows = row_iota((TILE, 1)) + (place * lrows + i * TILE)
            keep = jnp.where(rows < length_ref[0], 1.0, 0.0)
            cot_ref[at(i), :] = (cot_ref[at(i), :].astype(F32) * keep).astype(BF16)

        some(1)
        ahead.wait_recv()
        x_ref[0:HALO, :] = halo[...]

        def norm(j):
            v = x_ref[at(j), :].astype(F32)
            s = lax.rsqrt(jnp.mean(v * v, axis=1, keepdims=True) + EPSILON)
            nm_ref[at(j), :] = (v * s * gain_ref[...]).astype(BF16)

        pl.loop(0, tiles // 2)(norm)
        some(1)
        pl.loop(tiles // 2, tiles)(norm)
        some(len(todo))
        ahead.wait_send()
        load(0).start()
        load(1).start()

    @pl.when(step > 0)
    def _():
        for g in range(groups):

            @pl.when(step == g + 1)
            def _(g=g):
                load(g).wait()
                width = pc_ref.shape[1]
                pc_ref[...] = all_pc[:, g * width : (g + 1) * width]

        pair_up(pairs.at[0], wd_ref)
        pair_up(pairs.at[1], wo_ref)
        slot = lax.rem(step - 1, 2)
        share = wbuf.shape[-2] // 2
        front_part(
            ltiles, tiles, point, place, nm_ref, wbuf.at[slot, :, :, 0:share],
            wbuf.at[slot, :, :, share : 2 * share], pairs, pc_ref, gp, inn, dp, ip, st, pr, mix,
            exchange.mine.at[step - 1], cv_ref, cl_ref,
        )
        for g in range(groups):

            @pl.when(step == g + 1)
            def _(g=g):
                if g + 2 < groups:
                    load(g + 2).start()
                exchange.theirs[g, place] = jnp.zeros(exchange.theirs.shape[2:], F32)
                exchange.start(g)

        point(3)

    @pl.when(step > 0)
    def _():
        g = step - 1
        mixes[g] = mix[...]
        for k, ref in enumerate((st, pr, gp)):
            longs[k, g] = ref[HALO : HALO + lrows, :]

    whole_out = pltpu.make_async_copy(outw, wobuf, osem)

    @pl.when(step == groups)
    def _():
        whole_out.start()
        width = gp.shape[1]
        for g in range(groups):
            cols = slice(g * width, (g + 1) * width)
            state = exchange.entering(g, False)
            sin_ref[:, cols] = jnp.broadcast_to(state, (8, width))
            states = longs[0, g] + longs[1, g] * state
            mixl_ref[:, cols] = (states * gelu(longs[2, g])).astype(BF16)
        whole_out.wait()

    point(4)

    @pl.when(step == groups)
    def _():
        width = gp.shape[1]
        for g in range(groups):
            part = flat(wobuf[g // 2, g % 2])
            top = dot_nn(mixl_ref[:, g * width : (g + 1) * width], part)
            low = dot_nn(mixes[g], part)
            if g == 0:
                resid_ref[0:lrows, :] = top
                resid_ref[lrows:, :] = low
            else:
                resid_ref[0:lrows, :] += top
                resid_ref[lrows:, :] += low

    point(5)

    @pl.when(step == groups)
    def _():
        @pl.loop(0, tiles - 1)
        def _(i):
            r = resid_ref[at(i), :] + x_ref[at(1 + i), :].astype(F32)
            resid_ref[at(i), :] = r
            s = lax.rsqrt(jnp.mean(r * r, axis=1, keepdims=True) + EPSILON)
            n2_ref[at(i), :] = (r * s * gain2_ref[...]).astype(BF16)

    point(6)

    @pl.when(step == groups)
    def _():
        exchange.drain(groups)
        if gather is not None:
            gather.drain()


def front_part(
    ltiles, tiles, point, place, nm_ref, wg_ref, wi_ref, pairs, pc_ref, gp_ref, in_ref, dp_ref,
    ip_ref, st_ref, pr_ref, mix_ref, end_ref, cv_ref, cl_ref,
):
    point(0)
    nm = nm_ref[...]
    gp_ref[...] = dot_nt(nm, flat(wg_ref[...])) + pc_ref[GB : GB + 1, :]
    in_ref[...] = dot_nt(nm, flat(wi_ref[...])) + pc_ref[IB : IB + 1, :]
    point(1)
    in_ref[0:HALO, :] = in_ref[0:HALO, :] * jnp.where(place > 0, 1.0, 0.0)
    cl_ref[0:HALO, :] = jnp.zeros((HALO, cl_ref.shape[1]), BF16)

    @pl.loop(1, tiles)
    def _(j):
        live = jnp.where(j == 1 + ltiles, 0.0, 1.0)
        out, _ = conv_tile(in_ref, pc_ref, j, live)
        cv_ref[at(j), :] = out
        cl_ref[at(j), :] = out.astype(BF16)

    point(2)
    low = cl_ref[...]
    dp_ref[...] = dot_nn(low, pairs[0]) + pc_ref[DB : DB + 1, :]
    ip_ref[...] = dot_nn(low, pairs[1]) + pc_ref[OB : OB + 1, :]

    def scanned(j):
        _, opening, a, square = gates(dp_ref[at(j), :], ip_ref[at(j), :], pc_ref[C8 : C8 + 1, :])
        b = (square * lax.rsqrt(square)) * opening * cv_ref[at(j), :]
        return scan_tile(a, b, False)

    width = gp_ref.shape[1]

    def long_step(i, carry):
        state, reach = carry
        a, b = scanned(1 + i)
        s = b + a * state
        r = a * reach
        st_ref[at(1 + i), :] = s
        pr_ref[at(1 + i), :] = r
        return s[TILE - 1 : TILE], r[TILE - 1 : TILE]

    state, reach = lax.fori_loop(
        0, ltiles, long_step, (jnp.zeros((1, width), F32), jnp.ones((1, width), F32))
    )
    end_ref[...] = jnp.concatenate([reach, state, jnp.zeros((6, width), F32)], axis=0)

    def short_step(i, state):
        j = 1 + ltiles + i
        a, b = scanned(j)
        s = b + a * state
        st_ref[at(j), :] = s
        mix_ref[at(i), :] = (s * gelu(gp_ref[at(j), :])).astype(BF16)
        return s[TILE - 1 : TILE]

    lax.fori_loop(0, tiles - 1 - ltiles, short_step, jnp.zeros((1, width), F32))


def mlp_kernel(ltiles, tiles, links, *refs):
    resid_ref, n2_ref, cot_ref, gain_ref, w1_ref, w2_ref = refs[:6]
    refs = refs[6:]
    point, gather = no_point, None
    step = pl.program_id(0)
    last = pl.num_programs(0) - 1
    if links is not None:
        zcount, chunks, lags, plan, sum_chunks, sum_lags, sum_plan = links
        owns = [w2_ref, *refs[:2]]
        refs = refs[2:]
    outl_ref, outs_ref, dres_ref, rlow_ref, gain_grad_ref, dw_hbm = refs[:6]
    refs = refs[6:]
    if links is not None:
        w2_ref, early_ref = refs[:2]
        halved = (refs[-9], None, *refs[-8:-5])
        buffers = [None, None, None, halved]
        scatter = Scatter(zcount, [dw_hbm], [early_ref], buffers, refs[-5:], sum_chunks, sum_lags)
        refs = refs[2:-9]
        gather = Gather(zcount, owns, [w2_ref], refs[-3:], chunks, lags)
        got_ref, sems, credit = refs[-6], refs[-5], refs[-4]
        refs = refs[:-6]
        gather_point = in_turn(gather, step, plan)
        scatter_point = in_turn(scatter, step, sum_plan)

        def point(k):
            gather_point(k)
            scatter_point(k)

    (
        acc_o, acc_n, gu_ref, d_ref, h_ref, dgu_ref, wbuf, dwbuf, wsem, dsem
    ) = refs
    lrows = ltiles * TILE
    hid = h_ref.shape[1]
    half = hid // 2
    share = wbuf.shape[-2]
    rows = 3 * share
    ready = w1_ref.shape[-2] // rows
    steps = ready + w2_ref.shape[-2] // rows

    def load(s):
        source, part = (w1_ref, s) if s < ready else (w2_ref, s - ready)
        return [
            pltpu.make_async_copy(
                source.at[:, :, :, :, pl.ds(part * rows + k * share, share)],
                wbuf.at[s % 2, k],
                wsem.at[s % 2, k],
            )
            for k in range(3)
        ]

    def start_load(s):
        for copy in load(s):
            copy.start()

    def wait_load(s):
        for copy in load(s):
            copy.wait()

    def load_next(s):
        if s + 1 < steps and s + 1 >= min(2, ready):
            start_load(s + 1)

    def each(todo, first=0):
        for s in range(first, steps):

            @pl.when(step == s)
            def _(s=s):
                todo(s)

    if gather is not None:
        y, x, c, z = gather.peers.place

    def store(s):
        mine = dwbuf if gather is None else dwbuf.at[:, :, :, c]
        return pltpu.make_async_copy(mine, dw_hbm.at[s], dsem)

    def swap():
        return remote(
            dwbuf.at[:, :, :, 1 - c], got_ref, sems.at[0], sems.at[1], gather.peers.other
        )

    def settle(s):
        if gather is not None:
            swap().wait_recv()

            @pl.loop(0, SLOTS // 2)
            def _(k):
                i, j, m = k // (2 * GRID[3]), (k // GRID[3]) % 2, k % GRID[3]
                for n in range(3):
                    dwbuf[n, i, j, c, m] = dwbuf[n, i, j, c, m] + got_ref[n, i, j, m]

            if s < steps - 1:
                pl.semaphore_signal(
                    credit,
                    inc=1,
                    device_id=gather.peers.other,
                    device_id_type=pl.DeviceIdType.MESH,
                )
        store(s).start()

    def clear(s):
        store(s).wait()
        if gather is not None:
            swap().wait_send()

    @pl.when(step == 0)
    def _():
        for s in range(min(2, ready)):
            start_load(s)
        if gather is not None:
            gather.peers.meet()

    point(0)

    @pl.when(step == 0)
    def _():
        acc_o[...] = resid_ref[...]
        acc_n[...] = jnp.zeros_like(acc_n)

    point(1)

    each(wait_load)
    slot = lax.rem(step, 2)

    def gate_up():
        return flat(wbuf[slot, 0:2])

    def down():
        return flat(wbuf[slot, 2])

    gu_ref[...] = dot_nt(n2_ref[...], gate_up())
    point(2)
    d_ref[...] = dot_nt(cot_ref[...], down())
    each(lambda s: settle(s - 1), 1)
    point(3)

    @pl.loop(0, tiles)
    def _(i):
        for k in range(2):
            cols = slice(k * half, (k + 1) * half)
            more = slice(hid + k * half, hid + (k + 1) * half)
            ge, slope = gelu_pair(gu_ref[at(i), cols])
            u = gu_ref[at(i), more]
            d = d_ref[at(i), cols]
            h_ref[at(i), cols] = (ge * u).astype(BF16)
            dgu_ref[at(i), cols] = (d * u * slope).astype(BF16)
            dgu_ref[at(i), more] = (d * ge).astype(BF16)

    point(4)
    acc_o[...] += dot_nn(h_ref[...], down())
    point(5)
    acc_n[...] += dot_nn(dgu_ref[...], gate_up())
    point(6)
    each(lambda s: clear(s - 1), 1)
    dwbuf[2] = dot_tn(h_ref[...], cot_ref[...]).astype(BF16).reshape(dwbuf.shape[1:])
    point(7)
    each(load_next)
    grad = dot_tn(dgu_ref[...], n2_ref[...]).astype(BF16)
    dwbuf[0:2] = grad.reshape((2,) + dwbuf.shape[1:])

    if gather is not None:
        @pl.when(step > 0)
        def _():
            pl.semaphore_wait(credit, 1)

        swap().start()

    @pl.when(step == last)
    def _():
        def one(i, total):
            r = resid_ref[at(i), :]
            dn = acc_n[at(i), :]
            s = lax.rsqrt(jnp.mean(r * r, axis=1, keepdims=True) + EPSILON)
            e = dn * gain_ref[...]
            inner = jnp.mean(e * r, axis=1, keepdims=True)
            dr = cot_ref[at(i), :].astype(F32) + s * e - r * (s * s * s * inner)
            dres_ref[at(i), :] = dr
            rlow_ref[at(i), :] = dr.astype(BF16)
            return total + fold(dn * (r * s))

        gain_grad_ref[...] = lax.fori_loop(0, tiles, one, jnp.zeros(gain_grad_ref.shape, F32))
        outl_ref[...] = acc_o[0:lrows, :].astype(BF16)
        outs_ref[...] = acc_o[lrows:, :].astype(BF16)
        settle(steps - 1)
        clear(steps - 1)

    point(8)
    if gather is not None:

        @pl.when(step == last)
        def _():
            gather.drain()
            scatter.drain()


def back_part(
    ltiles, tiles, point, rlow_ref, wo_ref, mixl_ref, mixs_ref, gp_ref, st_ref, pr_ref, sin_ref,
    dp_ref, pc_ref, dwo_ref, gl_ref, tot_ref, rch_ref, end_ref, bias_ref, dm_ref, free, nm_ref,
    dwg_ref,
):
    point(0)
    lrows = ltiles * TILE
    width = gp_ref.shape[1]
    rlow = rlow_ref[...]
    dm_ref[...] = dot_nt(rlow, flat(wo_ref[...]))
    free()
    grad = dot_tn(mixl_ref[...], rlow_ref[0:lrows, :]) + dot_tn(mixs_ref[...], rlow_ref[lrows:, :])
    dwo_ref[...] = grad.astype(BF16).reshape(dwo_ref.shape)
    point(1)
    gl_ref[0:HALO, :] = jnp.zeros((HALO, width), BF16)
    last = row_iota((TILE, width)) == TILE - 1

    def local(j, states):
        dm = dm_ref[at(j - 1), :]
        ge, slope = gelu_pair(gp_ref[at(j), :])
        dgate = dm * states * slope
        gl_ref[at(j), :] = dgate.astype(BF16)
        ds = dm * ge
        rate = sigmoid(dp_ref[at(j), :])
        decay = jnp.exp(-pc_ref[C8 : C8 + 1, :] * (0.25 + rate))
        a, b = scan_tile(decay, decay * ds, True)
        return a, b, ds, fold(dgate)

    def short_step(i, carry):
        c, bias = carry
        j = tiles - 1 - i
        a, b, ds, part = local(j, st_ref[at(j), :])
        cs = b + a * c
        tot_ref[at(j), :] = ds + jnp.where(last, c, pltpu.roll(cs, TILE - 1, 0))
        return cs[0:1], bias + part

    _, bias = lax.fori_loop(
        0,
        tiles - 1 - ltiles,
        short_step,
        (jnp.zeros((1, width), F32), jnp.zeros((8, width), F32)),
    )
    point(2)
    s_in = sin_ref[0:1, :]

    def long_step(i, carry):
        c, reach, bias = carry
        j = ltiles - i
        a, b, ds, part = local(j, st_ref[at(j), :] + pr_ref[at(j), :] * s_in)
        cs = b + a * c
        rs = a * reach
        tot_ref[at(j), :] = ds + jnp.where(last, c, pltpu.roll(cs, TILE - 1, 0))
        rch_ref[at(j), :] = jnp.where(last, reach, pltpu.roll(rs, TILE - 1, 0))
        return cs[0:1], rs[0:1], bias + part

    c, reach, bias = lax.fori_loop(
        0, ltiles, long_step, (jnp.zeros((1, width), F32), jnp.ones((1, width), F32), bias)
    )
    end_ref[...] = jnp.concatenate([reach, c, jnp.zeros((6, width), F32)], axis=0)
    bias_ref[...] = bias
    dwg_ref[...] = dot_tn(gl_ref[...], nm_ref[...]).astype(BF16).reshape(dwg_ref.shape)


def last_part(
    ltiles, tiles, groups, point, exchange, residual, x_ref, gain_ref, nm_ref, wg_ref, wi_ref,
    wd_ref, wo_ref, pc_ref, in_ref, dp_ref, ip_ref, st_ref, pr_ref, sin_ref, tot_ref, rch_ref,
    gl_ref, bias_ref, dxl_ref, dxs_ref, halo_ref, behind, pairs, gain_grad_ref, dwi_ref,
    gg_ref, small_ref, acc, dc_ref, cl_ref, dl_ref, ol_ref, il_ref, gain2_ref, free, keep,
):
    width = in_ref.shape[1]
    step = pl.program_id(0) - groups
    point(0)
    for g in range(groups):

        @pl.when(step == g)
        def _(g=g):
            dc_ref[0:1, :] = exchange.entering(g, True)

    c_in = dc_ref[0:1, :]

    @pl.when(step == groups - 1)
    def _():
        for copy in residual:
            copy.start()

    first = jnp.where(exchange.place > 0, 1.0, 0.0)
    pair_up(pairs.at[0], wd_ref)
    pair_up(pairs.at[1], wo_ref)
    zero8 = jnp.zeros((8, width), F32)
    cl_ref[0:HALO, :] = jnp.zeros((HALO, width), BF16)
    dl_ref[0:HALO, :] = jnp.zeros((HALO, width), BF16)
    ol_ref[0:HALO, :] = jnp.zeros((HALO, width), BF16)
    dc_ref[0:HALO, :] = jnp.zeros((HALO, width), F32)

    def gate_step(j, states, total, live, carry):
        before, sum_d, sum_o, sum_p = carry
        rows = row_iota((TILE, width))
        prior = jnp.where(rows == 0, before, pltpu.roll(states, 1, 0))
        conv, _ = conv_tile(in_ref, pc_ref, j, live)
        rate, opening, decay, square = gates(
            dp_ref[at(j), :], ip_ref[at(j), :], pc_ref[C8 : C8 + 1, :]
        )
        inv = lax.rsqrt(square)
        mult = square * inv
        weighted = total * opening
        d_open = total * mult * conv
        d_log = decay * (total * prior - (weighted * conv) * (decay * inv))
        d_rate = -pc_ref[C8 : C8 + 1, :] * d_log
        d_dp = d_rate * (rate - rate * rate)
        d_ip = d_open * (opening - opening * opening)
        cl_ref[at(j), :] = conv.astype(BF16)
        dl_ref[at(j), :] = d_dp.astype(BF16)
        ol_ref[at(j), :] = d_ip.astype(BF16)
        dc_ref[at(j), :] = weighted * mult
        return (
            states[TILE - 1 : TILE],
            sum_d + fold(d_dp),
            sum_o + fold(d_ip),
            sum_p - fold((0.25 + rate) * d_log),
        )

    s_in = sin_ref[0:1, :]

    def long_step(i, carry):
        j = 1 + i
        states = st_ref[at(j), :] + pr_ref[at(j), :] * s_in
        total = tot_ref[at(j), :] + rch_ref[at(j), :] * c_in
        return gate_step(j, states, total, 1.0, carry)

    def short_step(i, carry):
        j = 1 + ltiles + i
        return gate_step(j, st_ref[at(j), :], tot_ref[at(j), :], jnp.where(i == 0, 0.0, 1.0), carry)

    carry = lax.fori_loop(0, ltiles, long_step, (s_in, zero8, zero8, zero8))
    carry = lax.fori_loop(
        0, tiles - 1 - ltiles, short_step, (jnp.zeros((1, width), F32),) + carry[1:]
    )
    _, sum_d, sum_o, sum_p = carry
    point(1)

    low, dlow, olow = cl_ref[...], dl_ref[...], ol_ref[...]
    half = width // 2
    for which, grads in ((0, dlow), (1, olow)):
        product = dot_tn(low, grads).astype(BF16)
        shape = (2, half // 2, half)
        place = (which, step // 2, lax.rem(step, 2))
        gg_ref[(*place, slice(0, 2))] = product[:half, :half].reshape(shape)
        gg_ref[(*place, slice(2, 4))] = product[half:, half:].reshape(shape)
    dc_ref[...] += dot_nt(dlow, pairs[0]) + dot_nt(olow, pairs[1])

    point(2)

    def conv_step(j, carry):
        sum_c, sum_i, sums = carry
        live = jnp.where(j == 1 + ltiles, 0.0, 1.0)
        cur = dc_ref[at(j), :]
        up = jnp.where((j == ltiles) | (j == tiles - 1), 0.0, 1.0)
        later = dc_ref[at(jnp.minimum(j + 1, tiles - 1)), :] * up
        _, moved = conv_tile(in_ref, pc_ref, jnp.maximum(j, 1), live)
        d_in = pc_ref[CW : CW + 1, :] * cur
        for k in range(1, 4):
            d_in = d_in + pc_ref[CW + k : CW + k + 1, :] * shift_up(cur, later, k)
        d_in = d_in * jnp.where(j == 0, first, 1.0)
        il_ref[at(j), :] = d_in.astype(BF16)
        return (
            sum_c + fold(cur),
            sum_i + fold(d_in),
            tuple(s + fold(cur * m) for s, m in zip(sums, moved)),
        )

    sum_c, sum_i, sums = lax.fori_loop(0, tiles, conv_step, (zero8, zero8, (zero8,) * 4))
    parts = [sum_i, *sums, sum_c, sum_d, sum_o, sum_p * pc_ref[S8 : S8 + 1, :], bias_ref[...]]
    rows = [jnp.sum(p, axis=0, keepdims=True) for p in parts]
    block = jnp.concatenate(rows + [jnp.zeros((16 - len(rows), width), F32)], axis=0)
    for i in range(width // 128):
        at_block = step * (width // 128) + i
        x, c, z = at_block // 8, lax.rem(at_block // 4, 2), lax.rem(at_block, 4)
        for h in range(2):
            small_ref[h, x, c, z] = block[8 * h : 8 * h + 8, 128 * i : 128 * i + 128]

    point(3)
    free()
    nm = nm_ref[...]
    dwi_ref[...] = dot_tn(il_ref[...], nm).astype(BF16).reshape(dwi_ref.shape)
    keep()
    point(4)
    part = dot_nn(gl_ref[...], flat(wg_ref[...])) + dot_nn(il_ref[...], flat(wi_ref[...]))

    @pl.when(step == 0)
    def _():
        acc[...] = part

    @pl.when(step > 0)
    def _():
        acc[...] += part

    @pl.when(step == groups - 1)
    def _():
        for copy in residual:
            copy.wait()

        def norm_back(j):
            v = x_ref[at(j), :].astype(F32)
            dn = acc[at(j), :]
            s = lax.rsqrt(jnp.mean(v * v, axis=1, keepdims=True) + EPSILON)
            e = dn * gain_ref[...]
            inner = jnp.mean(e * v, axis=1, keepdims=True)
            return s * e - v * (s * s * s * inner), fold(dn * (v * s))

        halo, total = norm_back(0)
        halo_ref[...] = halo
        behind.start()
        done = 1
        for ref in (dxl_ref, dxs_ref):

            def one(i, total, ref=ref, done=done):
                d, part = norm_back(done + i)
                ref[at(i), :] = ref[at(i), :] + d
                return total + part

            total = lax.fori_loop(0, ref.shape[0] // TILE, one, total)
            done += ref.shape[0] // TILE
        gain_grad_ref[...] = total
        zero = jnp.zeros((8, 128), F32)
        for h in range(2):
            for z in range(4):
                small_ref[h, 1, 1, z] = zero
        for z, ref in enumerate((gain_grad_ref, gain2_ref)):
            total = jnp.sum(ref[...], axis=0, keepdims=True)
            for i in range(8):
                small_ref[0, 1, 1, z, i : i + 1, :] = total[:, 128 * i : 128 * i + 128]

    point(5)


def tail_kernel(ltiles, tiles, groups, links, *refs):
    (
        x_ref, gain_ref, nm_ref, dres_hbm, rlow_ref, w_ref, wg_ref, wi_ref, wd_ref, wo_ref, pc_ref,
        mixl_ref, mixs_ref, gp_ref, in_ref, dp_ref, ip_ref, st_ref, pr_ref, sin_ref, gain2_ref,
    ) = refs[:21]
    refs = refs[21:]
    step = pl.program_id(0)
    group = lax.rem(step, groups)
    back_point, last_point, scatter = no_point, no_point, None
    nscratch = 23
    if links is not None:
        zcount, chunks, lags, plan = links
        halved_ref, early_ref, refs = refs[0], refs[1], refs[2:]
        outs, shares = refs[:8], refs[8:14]
        scratch, pool = refs[14 : 14 + nscratch], refs[14 + nscratch :]
    else:
        outs, scratch = refs[:8], refs[8:]
    dxl_ref, dxs_ref, gain_grad_ref, dwo_hbm, dwg_hbm, dwi_hbm, gates_hbm, sums_hbm = outs
    (
        acc, dc_ref, cl_ref, dl_ref, ol_ref, il_ref, gls, tots, rchs, bias_ref, wst, gsrc, ssrc,
        pairs, halo_out, halo_in, hsem, dsem, wsem, *swap
    ) = scratch
    gates_full, sums_full = gsrc, ssrc
    if links is not None:
        *pool, gates_full, sums_full = pool
        main, gate_pool, sum_pool = pool[0:5], pool[5:10], pool[10:15]
        scatter = Scatter(
            zcount,
            [halved_ref, dwo_hbm, dwg_hbm, dwi_hbm, gsrc, ssrc],
            [*shares, gates_full, sums_full],
            [main, gate_pool, sum_pool, main],
            pool[15:],
            chunks,
            lags,
        )
        back_point = in_turn(scatter, step, plan[:groups])
        last_point = in_turn(scatter, step, plan[groups:], groups)

        @pl.when(step == 0)
        def _():
            rows = early_ref.shape[0] // 3
            for k in range(3):
                shares[k][0:rows, :] = early_ref[k * rows : (k + 1) * rows, :]

    def stash(g, k, target):
        return pltpu.make_async_copy(wst.at[k], target.at[g // 2, g % 2], wsem.at[k])

    def stashed(first, what):
        for g in range(groups):

            @pl.when(step == first + g)
            def _(g=g):
                what(g)

    exchange = Exchange(*swap)
    gl_ref, tot_ref, rch_ref = gls.at[group], tots.at[group], rchs.at[group]
    lrows = ltiles * TILE
    residual = [
        pltpu.make_async_copy(dres_hbm.at[pl.ds(0, lrows)], dxl_ref, dsem.at[0]),
        pltpu.make_async_copy(
            dres_hbm.at[pl.ds(lrows, dxs_ref.shape[0])], dxs_ref, dsem.at[1]
        ),
    ]
    behind = remote(
        halo_out, halo_in, hsem.at[0], hsem.at[1], exchange.peer(exchange.count - 1)
    )
    width = gp_ref.shape[1]

    @pl.when(step == 0)
    def _():
        meet_all(exchange, 1 if scatter is None else zcount)

    def freed(g):
        if g > 0:
            stash(g - 1, 0, dwo_hbm).wait()
            stash(g - 1, 1, dwg_hbm).wait()

    def kept(g):
        stash(g, 0, dwo_hbm).start()
        stash(g, 1, dwg_hbm).start()

    @pl.when(step < groups)
    def _():
        back_part(
            ltiles, tiles, back_point, rlow_ref, w_ref, mixl_ref, mixs_ref, gp_ref, st_ref, pr_ref,
            sin_ref, dp_ref, pc_ref, wst.at[0], gl_ref, tot_ref, rch_ref, exchange.mine.at[group],
            bias_ref.at[group], acc.at[0 : rlow_ref.shape[0], 0:width],
            lambda: stashed(0, freed), nm_ref, wst.at[1],
        )
        stashed(0, kept)
        for g in range(groups):

            @pl.when(step == g)
            def _(g=g):
                exchange.theirs[g, exchange.place] = jnp.zeros(exchange.theirs.shape[2:], F32)
                exchange.start(g)

    @pl.when(step >= groups)
    def _():
        @pl.when(step == groups)
        def _():
            stash(groups - 1, 0, dwo_hbm).wait()
            stash(groups - 1, 1, dwg_hbm).wait()

        def before(g):
            if g > 0:
                stash(g - 1, 2, dwi_hbm).wait()

        def after(g):
            stash(g, 2, dwi_hbm).start()
            if g == groups - 1:
                stash(g, 2, dwi_hbm).wait()

        last_part(
            ltiles, tiles, groups, last_point, exchange, residual, x_ref, gain_ref, nm_ref,
            wg_ref, wi_ref, wd_ref, wo_ref, pc_ref, in_ref, dp_ref, ip_ref, st_ref, pr_ref, sin_ref,
            tot_ref, rch_ref, gl_ref, bias_ref.at[group], dxl_ref, dxs_ref, halo_out, behind, pairs,
            gain_grad_ref, wst.at[2], gsrc, ssrc, acc, dc_ref, cl_ref, dl_ref, ol_ref, il_ref, gain2_ref,
            lambda: stashed(groups, before), lambda: stashed(groups, after),
        )

    @pl.when(step == pl.num_programs(0) - 1)
    def _():
        exchange.drain(groups)
        behind.wait()
        rows = slice(lrows - HALO, lrows)
        dxl_ref[rows, :] = dxl_ref[rows, :] + halo_in[...]
        if scatter is not None:
            scatter.drain()
        final = [
            pltpu.make_async_copy(gates_full, gates_hbm, wsem.at[0]),
            pltpu.make_async_copy(sums_full, sums_hbm, wsem.at[1]),
        ]
        for copy in final:
            copy.start()
        for copy in final:
            copy.wait()


def finish_kernel(number, *refs):
    ins, (gates_ref, sums_ref) = refs[:number], refs[number : number + 2]
    outs = refs[number + 2 : 2 * number + 2]
    gd_ref, go_ref, gain1_ref, gain2_ref, conv_ref, *rows = refs[2 * number + 2 : -number - 3]
    *held, table, sem_in, sem_out = refs[-number - 3 :]
    copies = []
    for k, (a, h, b) in enumerate(zip(ins, held, outs)):
        copies.append(
            (
                pltpu.make_async_copy(a, h, sem_in.at[k]),
                pltpu.make_async_copy(h, b, sem_out.at[k]),
            )
        )
        copies[-1][0].start()
    for come, go in copies:
        come.wait()
        go.start()
    gd_ref[...] = gates_ref[0].astype(F32)
    go_ref[...] = gates_ref[1].astype(F32)
    for h in range(2):
        for k in range(16):
            table[8 * h : 8 * h + 8, 128 * k : 128 * k + 128] = sums_ref[h, k]
    chans = conv_ref.shape[1]
    conv_ref[...] = table[1:5, 0:chans]
    for r, ref in zip((0, 5, 6, 7, 8, 9), rows):
        ref[...] = table[r : r + 1, 0:chans].reshape(chans)
    for k, ref in enumerate((gain1_ref, gain2_ref)):
        for i in range(8):
            table[0:1, 128 * i : 128 * i + 128] = sums_ref[0, 12 + k, i : i + 1, :]
        ref[...] = table[0:1, 0:1024].reshape(1024)
    for _, go in copies:
        go.wait()


def shape_of(shape, dtype):
    return jax.ShapeDtypeStruct(shape, dtype)


def whole(shape):
    return pl.BlockSpec(shape, lambda g: (0,) * len(shape), pipeline_mode=pl.Buffered(1))


def params(limit, **more):
    return pltpu.CompilerParams(
        dimension_semantics=("arbitrary",), vmem_limit_bytes=int(limit * MIB), **more
    )


def to_slots(parts, count):
    rows = parts[0].shape[0]
    depth = parts[0].shape[1]
    got = lax.all_gather(jnp.concatenate(parts, axis=0), ("seq", "row"), axis=0, tiled=False)
    if count != SLOTS:
        got = got.reshape(count, len(parts), rows, depth).transpose(1, 0, 2, 3)
        got = got.reshape(len(parts), SLOTS, rows * count // SLOTS, depth).transpose(1, 0, 2, 3)
    return got.reshape(SLOTS, -1, depth)


def scatter_slots(grads, number, count):
    slots, rows, depth = grads.shape
    if count != SLOTS:
        grads = grads.reshape(slots, number, rows // number, depth).transpose(1, 0, 2, 3)
        grads = grads.reshape(number, count, -1, depth).transpose(1, 0, 2, 3)
    flat_grads = grads.reshape(slots * rows, depth)
    own = lax.psum_scatter(flat_grads, ("seq", "row"), scatter_dimension=0, tiled=True)
    own = own.astype(F32).reshape(number, -1, depth)
    return [own[i] for i in range(number)]


def shards(
    long_tokens,
    short_tokens,
    long_length,
    long_cotangent,
    short_cotangent,
    first_gain,
    gate_weight,
    gate_bias,
    input_weight,
    input_bias,
    conv_weight,
    conv_bias,
    decay_gate_weight,
    decay_gate_bias,
    input_gate_weight,
    input_gate_bias,
    decay_param,
    out_weight,
    second_gain,
    mlp_gate_weight,
    mlp_up_weight,
    mlp_down_weight,
):
    count = lax.axis_size("seq") * lax.axis_size("row")
    lrows, srows, depth = long_tokens.shape[1], short_tokens.shape[1], long_tokens.shape[2]
    chans = gate_bias.shape[0]
    units = mlp_gate_weight.shape[1] * count
    tokens = lrows + srows
    total = HALO + tokens
    ltiles, tiles = lrows // TILE, total // TILE
    cshare, ushare = chans // SLOTS, units // SLOTS
    groups = 4
    width = chans // groups
    per = SLOTS // groups

    zcount = lax.axis_size("row")
    seqs = lax.axis_size("seq")
    fast = seqs == 8 and count == SLOTS
    hbm = pl.BlockSpec(memory_space=pl.ANY)
    one_dma = pltpu.SemaphoreType.DMA
    steps = ushare // 16
    ready_parts = max(1, min(steps - 1, FRONT_PARTS))
    blocks, bwidth = decay_gate_weight.shape[0:2]
    mlp_own = [mlp_gate_weight.T, mlp_up_weight.T, mlp_down_weight]
    channel = [
        gate_bias, input_bias, conv_weight, conv_bias, decay_gate_bias, input_gate_bias,
        8.0 * jax.nn.softplus(decay_param), 8.0 * jax.nn.sigmoid(decay_param),
    ]
    gain1 = first_gain[None]
    gain2 = second_gain[None]

    def early(g):
        return jnp.minimum(g, groups - 1)

    def after_one(g):
        return jnp.maximum(g - 1, 0)

    def late(g):
        return jnp.maximum(g - groups, 0)

    def both_times(g):
        return lax.rem(g, groups)

    def slot_at(when, which=0):
        return pl.BlockSpec((per, cshare, depth), lambda g: (when(g), which, 0))

    def blocks_at(when):
        return pl.BlockSpec((2, bwidth, bwidth), lambda g: (when(g), 0, 0))

    def cols_at(nrows, when):
        return pl.BlockSpec((nrows, width), lambda g: (0, when(g)))

    lags = (2, 2, 3, 2)
    if fast:
        front_own = [gate_weight.T, input_weight.T, out_weight, *mlp_own]
        parts = [(0, 0, cshare, 0, 0), (1, 0, cshare, 0, cshare)]
        urgent = len(row_chunks(parts, 16))
        ready = urgent + sum(lags)
        parts += [(2, 0, cshare, 1, 0)]
        parts += [
            (3 + k, 16 * p, 16, 2, 48 * p + 16 * k) for p in range(ready_parts) for k in range(3)
        ]
        chunks = row_chunks(parts, 16)
        waves = len(chunks) + FRONT_DELAY + sum(lags)
        marks = [[4 * g + k for k in range(4)] for g in range(groups)]
        plan = paced(waves - ready - FRONT_LEFT, 1, marks)
        plan = [[]] + plan
        left = list(range(waves - ready - FRONT_LEFT, waves - ready))
        cut = FRONT_LEFT // 3
        plan[-1] += [left[:cut], left[cut : 2 * cut], left[2 * cut :]]
        plan = [[[ready + t for t in p] for p in row] for row in plan]
        front_links = (zcount, chunks, lags, urgent, ready, plan)
        front_shapes = [
            shape_of(GRID + (n, depth), BF16) for n in (2 * cshare, cshare, 48 * ready_parts)
        ]
        front_scratch = gather_sems(len(chunks), zcount)
    else:
        pairw = to_slots([gate_weight.T, input_weight.T], count)
        outw = to_slots([out_weight], count)
        mlpw = to_slots(mlp_own, count).reshape(GRID + (3, steps, 16, depth))
        mlpw = jnp.swapaxes(mlpw, 4, 5).reshape(GRID + (48 * steps, depth))
        w_first, w_second = jnp.split(mlpw, [48 * ready_parts], axis=4)
        front_own = [w.reshape(GRID + (-1, depth)) for w in (pairw, outw)]
        front_links, front_shapes, front_scratch = None, [], []

    col = cols_at(total, after_one)
    wide = shape_of((total, chans), F32)
    narrow = shape_of((HALO + lrows, chans), F32)
    (
        gp, inner, dp, ip, states, reach, mix_s, s_in, normed, x, cot, chan, residual, normed2,
        mix_l, *made,
    ) = pl.pallas_call(
        functools.partial(front_kernel, ltiles, tiles, groups, front_links),
        grid=(1 + groups,),
        in_specs=[
            hbm, hbm, hbm, hbm, pl.BlockSpec(memory_space=pltpu.SMEM), whole((1, depth)),
            *[whole(c.shape) for c in channel], blocks_at(after_one),
            blocks_at(after_one), whole((1, depth)),
            *[whole(w.shape) if fast else hbm for w in front_own],
        ],
        out_specs=[
            col, col, col, col, col, cols_at(HALO + lrows, after_one), cols_at(srows, after_one),
            whole((8, chans)), whole((total, depth)), whole((total, depth)),
            whole((tokens, depth)), cols_at(16, after_one), whole((tokens, depth)),
            whole((tokens, depth)), whole((lrows, chans)), *[hbm for _ in front_shapes],
        ],
        out_shape=[
            wide, wide, wide, wide, wide, narrow, shape_of((srows, chans), BF16),
            shape_of((8, chans), F32), shape_of((total, depth), BF16),
            shape_of((total, depth), BF16), shape_of((tokens, depth), BF16),
            shape_of((16, chans), F32), shape_of((tokens, depth), F32),
            shape_of((tokens, depth), BF16), shape_of((lrows, chans), BF16), *front_shapes,
        ],
        scratch_shapes=[
            pltpu.VMEM((total, width), F32), pltpu.VMEM((total, width), BF16),
            pltpu.VMEM((2,) + GRID[2:] + (2 * cshare, depth), BF16),
            pltpu.VMEM((2, width, width), BF16), pltpu.VMEM((HALO, depth), BF16),
            pltpu.VMEM((16, chans), F32), pltpu.VMEM((groups, srows, width), BF16),
            pltpu.VMEM((3, groups, lrows, width), F32), pltpu.VMEM(GRID + (cshare, depth), BF16),
            one_dma((4,)), one_dma((2,)), one_dma((2,)), one_dma, *exchange_scratch(groups, width, seqs),
            *front_scratch,
        ],
        compiler_params=params(56, collective_id=0, has_side_effects=True),
        name="front",
    )(
        long_tokens.reshape(lrows, depth), short_tokens.reshape(srows, depth),
        long_cotangent.reshape(lrows, depth), short_cotangent.reshape(srows, depth), long_length,
        gain1, *channel, decay_gate_weight, input_gate_weight, gain2, *front_own,
    )
    if fast:
        pairw, outw, w_first = made
    outw = outw.reshape(SLOTS, -1, depth)
    pairw = pairw.reshape(SLOTS, -1, depth)

    hid = units // steps
    block = (3,) + GRID + (16, depth)
    wbuf = pltpu.VMEM((2,) + block, BF16)
    dwbuf = pltpu.VMEM(block, BF16)
    if fast:
        chunks = [
            (k, 16 * (ready_parts + p), 16, 0, 48 * p + 16 * k)
            for p in range(steps - ready_parts)
            for k in range(3)
        ]
        plan = [[[] for _ in range(8)] for _ in range(steps)]
        todo = list(range(len(chunks) + sum(lags)))
        for s in range(ready_parts - 1, steps - 1):
            due = 3 * (s - ready_parts + 1) + 3 + sum(lags)
            now, todo = [t for t in todo if t < due], [t for t in todo if t >= due]
            first = 0 if s == ready_parts - 1 else s
            spots = [(q, k) for q in range(first, s + 1) for k in range(8)]
            for n, t in enumerate(now):
                lead = min(MLP_AHEAD, len(now) - 1) if first == 0 else 0
                share = max(0, n - lead) / max(1, len(now) - lead)
                q, k = spots[int(share * len(spots))]
                plan[q][k].append(t)
        soon = [(p, k) for p in range(EARLY_PARTS) for k in range(3)]
        early_chunks = [
            (HALVED, n, 0, (p, k), (0, 16), 0, 16 * (k * EARLY_PARTS + p))
            for n, (p, k) in enumerate(soon)
        ]
        early_lags = (1, 2, 2, 2)
        early_plan = [[[] for _ in range(9)] for _ in range(steps)]
        spot = 0
        for t in range(len(soon) + sum(early_lags)):
            after = 8 * (t // 3 + 1) + 7 if t < len(soon) else 0
            spot = max(after, spot + EARLY_GAP)
            q, k = divmod(min(spot, 8 * steps), 8)
            q, k = (q, k) if q < steps else (steps - 1, 8)
            early_plan[q][k].append(t)
        mlp_links = (zcount, chunks, lags, plan, early_chunks, early_lags, early_plan)
        w_last, more_specs = mlp_own, [hbm, whole((16 * len(soon), depth))]
        more_shapes = [
            shape_of(GRID + (48 * (steps - ready_parts), depth), BF16),
            shape_of((16 * len(soon), depth), F32),
        ]
        half_block = block[:3] + block[4:]
        more_scratch = [
            pltpu.VMEM(half_block, BF16), one_dma((2,)), pltpu.SemaphoreType.REGULAR,
            *gather_sems(len(chunks), zcount), *halved_scratch(len(soon), len(soon), depth, zcount),
        ]
        dw_shape = (steps,) + half_block
        more_params = dict(collective_id=3, has_side_effects=True)
    else:
        mlp_links, w_last, more_specs, more_shapes, more_scratch = None, [w_second], [], [], []
        dw_shape, more_params = (steps,) + block, {}
    out_l, out_s, d_res, rlow, gain2_grad, dmlp, *more_out = pl.pallas_call(
        functools.partial(mlp_kernel, ltiles, tokens // TILE, mlp_links),
        grid=(steps,),
        in_specs=[
            whole((tokens, depth)), whole((tokens, depth)), whole((tokens, depth)),
            whole((1, depth)), hbm,
            *[whole(w.shape) if fast else hbm for w in w_last],
        ],
        out_specs=[
            whole((lrows, depth)), whole((srows, depth)), whole((tokens, depth)), whole((tokens, depth)),
            whole((8, depth)), hbm, *more_specs,
        ],
        out_shape=[
            shape_of((lrows, depth), BF16), shape_of((srows, depth), BF16),
            shape_of((tokens, depth), F32), shape_of((tokens, depth), BF16),
            shape_of((8, depth), F32), shape_of(dw_shape, BF16), *more_shapes,
        ],
        scratch_shapes=[
            pltpu.VMEM((tokens, depth), F32), pltpu.VMEM((tokens, depth), F32),
            pltpu.VMEM((tokens, 2 * hid), F32),
            pltpu.VMEM((tokens, hid), F32), pltpu.VMEM((tokens, hid), BF16),
            pltpu.VMEM((tokens, 2 * hid), BF16), wbuf, dwbuf, one_dma((2, 3)), one_dma, *more_scratch,
        ],
        compiler_params=params(62, **more_params),
        name="mlp",
    )(residual, normed2, cot, gain2, w_first, *w_last)

    gate_shape, sum_shape = GRID + (bwidth // 2, bwidth), GRID + (8, 128)
    grads_shape = shape_of(GRID + (cshare, depth), BF16)
    tail_links, tail_in, tail_specs, tail_shapes, tail_scratch = None, [], [], [], []
    if fast:
        size = 16
        tail_chunks = []
        number = 0
        for p in range(EARLY_PARTS, steps):
            for k in range(3):
                tail_chunks.append(
                    (HALVED, number % TAIL_SLOTS, 0, (p, k), (0, size), k, 16 * p)
                )
                number += 1
        for which in (1, 2, 3):
            if which == 3:
                tail_chunks.append((SUMS, 0, 5, None, (0, 8), 7, 0))
                tail_chunks.append((GATES, 0, 4, None, (0, bwidth // 2), 6, 0))
                during = len(tail_chunks) - 2
            for start in range(0, cshare, size):
                tail_chunks.append(
                    (CORE, number % TAIL_SLOTS, which, None, (start, size), 2 + which, start)
                )
                number += 1
        tail_lags = (1, 3, 3, 3, 1, 1, 1, 1)
        marks = [[6.0 * g + t for t in (0.0, 1.5, 4.0)] for g in range(groups)]
        marks += [
            [6.0 * groups + 11.5 * g + t for t in (0.0, 5.0, 6.0, 9.0, 9.5, 11.5)] for g in range(groups)
        ]
        plan = paced(during, 3, marks)
        plan[-1][-1] += range(during, len(tail_chunks) + sum(tail_lags) + 1)
        tail_links = (zcount, tail_chunks, tail_lags, plan)
        early_sums = more_out[1]
        tail_in, tail_specs = [dmlp, early_sums], [whole((ushare, depth))] * 3 + [whole((cshare, depth))] * 3
        tail_shapes = [shape_of((ushare, depth), F32)] * 3 + [shape_of((cshare, depth), F32)] * 3
        lone = five(TAIL_SLOTS, (size, depth), BF16, zcount)
        lone[1] = five(CORE_SLOTS, (size, depth), BF16, zcount)[1]
        n = len(tail_chunks)
        links = one_dma((n, zcount + 2))
        tail_scratch = [
            *lone,
            *five(1, gate_shape[4:], BF16, zcount),
            *five(1, sum_shape[4:], F32, zcount),
            one_dma((n,)), links, links, links, links,
            pltpu.VMEM(gate_shape, BF16), pltpu.VMEM(sum_shape, F32),
        ]
    dx_l, dx_s, _, d_out, d_gate, d_input, gate_sums, sums, *shares = pl.pallas_call(
        functools.partial(tail_kernel, ltiles, tiles, groups, tail_links),
        grid=(2 * groups,),
        in_specs=[
            whole((total, depth)), whole((1, depth)), whole((total, depth)), hbm,
            whole((tokens, depth)), slot_at(early), slot_at(late, 0), slot_at(late, 1),
            blocks_at(late), blocks_at(late), cols_at(16, both_times), cols_at(lrows, early),
            cols_at(srows, early), cols_at(total, early), cols_at(total, late),
            cols_at(total, both_times), cols_at(total, late), cols_at(total, both_times),
            cols_at(HALO + lrows, both_times), cols_at(8, both_times), whole((8, depth)),
            *([hbm, whole(early_sums.shape)] if fast else []),
        ],
        out_specs=[
            whole((lrows, depth)), whole((srows, depth)), whole((8, depth)), hbm, hbm, hbm, hbm, hbm,
            *tail_specs,
        ],
        out_shape=[
            shape_of((lrows, depth), F32), shape_of((srows, depth), F32), shape_of((8, depth), F32),
            grads_shape, grads_shape, grads_shape, shape_of(gate_shape, BF16),
            shape_of(sum_shape, F32), *tail_shapes,
        ],
        scratch_shapes=[
            pltpu.VMEM((total, depth), F32), pltpu.VMEM((total, width), F32),
            pltpu.VMEM((total, width), BF16), pltpu.VMEM((total, width), BF16),
            pltpu.VMEM((total, width), BF16), pltpu.VMEM((total, width), BF16),
            pltpu.VMEM((groups, total, width), BF16), pltpu.VMEM((groups, total, width), F32),
            pltpu.VMEM((groups, HALO + lrows, width), F32), pltpu.VMEM((groups, 8, width), F32),
            pltpu.VMEM((3,) + GRID[2:] + (cshare, depth), BF16), pltpu.VMEM(gate_shape, BF16),
            pltpu.VMEM(sum_shape, F32), pltpu.VMEM((2, width, width), BF16),
            pltpu.VMEM((HALO, depth), F32), pltpu.VMEM((HALO, depth), F32), one_dma((2,)),
            one_dma((2,)), one_dma((3,)), *exchange_scratch(groups, width, seqs), *tail_scratch,
        ],
        compiler_params=params(63, collective_id=4, has_side_effects=True),
        name="tail",
    )(
        x, gain1, normed, d_res, rlow, outw, pairw, pairw, decay_gate_weight, input_gate_weight, chan,
        mix_l, mix_s, gp, inner, dp, ip, states, reach, s_in, gain2_grad, *tail_in,
    )

    if fast:
        g_mgate, g_mup, g_down, g_out, g_gate, g_input = shares
    else:
        dmlp = dmlp.reshape(steps, 3, SLOTS, -1, depth).transpose(2, 1, 0, 3, 4)
        g_mgate, g_mup, g_down = scatter_slots(dmlp.reshape(SLOTS, -1, depth), 3, count)
        dmix = jnp.concatenate([d_gate, d_input, d_out], axis=4).reshape(SLOTS, -1, depth)
        g_gate, g_input, g_out = scatter_slots(dmix, 3, count)
        gate_sums, sums = lax.psum((gate_sums.astype(F32), sums), ("seq", "row"))
    large = [out_l, out_s, dx_l, dx_s, g_gate, g_input, g_out, g_mgate, g_mup, g_down]
    vector = shape_of((chans,), F32)
    gate_grad = shape_of((blocks, bwidth, bwidth), F32)
    gain_grad = shape_of((depth,), F32)
    vmem = pl.BlockSpec(memory_space=pltpu.VMEM)
    (
        out_l, out_s, dx_l, dx_s, g_gate, g_input, g_out, g_mgate, g_mup, g_down, decay_grad,
        open_grad, gain1_grad, gain2_grad, conv_grad, input_bias_grad, conv_bias_grad,
        decay_bias_grad, open_bias_grad, param_grad, gate_bias_grad,
    ) = pl.pallas_call(
        functools.partial(finish_kernel, len(large)),
        in_specs=[hbm] * len(large) + [vmem, vmem],
        out_specs=[hbm] * len(large) + [vmem] * 11,
        out_shape=[shape_of(a.shape, a.dtype) for a in large]
        + [gate_grad, gate_grad, gain_grad, gain_grad, shape_of(conv_weight.shape, F32)]
        + [vector] * 6,
        scratch_shapes=[
            *[pltpu.VMEM(a.shape, a.dtype) for a in large], pltpu.VMEM((16, 2048), F32),
            one_dma((len(large),)), one_dma((len(large),)),
        ],
        compiler_params=pltpu.CompilerParams(vmem_limit_bytes=62 * MIB),
        name="finish",
    )(*large, gate_sums.reshape(2, blocks, bwidth, bwidth), sums.reshape(2, 16, 8, 128))
    return (
        out_l.reshape(long_tokens.shape),
        out_s.reshape(short_tokens.shape),
        dx_l.reshape(long_tokens.shape),
        dx_s.reshape(short_tokens.shape),
        gain1_grad,
        g_gate.T,
        gate_bias_grad,
        g_input.T,
        input_bias_grad,
        conv_grad,
        conv_bias_grad,
        decay_grad,
        decay_bias_grad,
        open_grad,
        open_bias_grad,
        param_grad,
        g_out,
        gain2_grad,
        g_mgate.T,
        g_mup.T,
        g_down,
    )


def solution(mesh):
    both = ("seq", "row")
    long_spec = P("row", "seq", None)
    short_spec = P(both, None, None)
    cols = P(None, both)
    rows = P(both, None)
    return jax.shard_map(
        shards,
        mesh=mesh,
        in_specs=(
            long_spec, short_spec, P("row"), long_spec, short_spec, P(), cols, P(), cols, P(),
            P(), P(), P(), P(), P(), P(), P(), rows, P(), cols, cols, rows,
        ),
        out_specs=(
            long_spec, short_spec, long_spec, short_spec, P(), cols, P(), cols, P(), P(), P(),
            P(), P(), P(), P(), P(), rows, P(), cols, cols, rows,
        ),
        check_vma=False,
    )
```
